32 devices in a mesh: dp: 16 (over z, y, x), tensor: 2 (over core).
Axes of the slice: x: 2, y: 2, z: 4, core: 2. Of those that a mesh axis runs over, the one named last changes fastest.
Arguments:
- stream: float32 [16384, 768], P(('dp', 'tensor')), may hold values from -6 to 6
- cotangent: float32 [16384, 768], P(('dp', 'tensor')), may hold values from -6 to 6
- positions: int32 [16384], P('dp'), may hold values from -1 to 1023, as said below
- norm_gain: float32 [768], replicated, may hold values from 0.5 to 1.5
- w_gate: float32 [768, 1536], P('dp', 'tensor'), may hold values from -0.21875 to 0.21875
- w_inner: float32 [768, 1536], P('dp', 'tensor'), may hold values from -0.21875 to 0.21875
- w_state: float32 [768, 256], P('dp'), may hold values from -0.21875 to 0.21875
- w_step: float32 [768, 24], P('dp', 'tensor'), may hold values from -0.21875 to 0.21875
- conv_inner: float32 [5, 1536], P(None, 'tensor'), may hold values from -3 to 3
- conv_state: float32 [5, 256], replicated, may hold values from -3 to 3
- head_params: float32 [3, 24], P(None, 'tensor'), may hold values from -6 to 3, as said below
- gate_gain: float32 [1536], P('tensor'), may hold values from 0.5 to 1.5
- w_out: float32 [1536, 768], P('tensor', 'dp'), may hold values from -0.15625 to 0.15625
- moment_norm_gain: float32 [768], replicated, may hold values from -640 to 640
- moment_w_gate: float32 [768, 1536], P('dp', 'tensor'), may hold values from -192 to 192
- moment_w_inner: float32 [768, 1536], P('dp', 'tensor'), may hold values from -192 to 192
- moment_w_state: float32 [768, 256], P('dp', 'tensor'), may hold values from -192 to 192
- moment_w_step: float32 [768, 24], P('dp', 'tensor'), may hold values from -192 to 192
- moment_conv_inner: float32 [5, 1536], P(None, 'tensor'), may hold values from -640 to 640
- moment_conv_state: float32 [5, 256], replicated, may hold values from -640 to 640
- moment_head_params: float32 [3, 24], P(None, 'tensor'), may hold values from -640 to 640
- moment_gate_gain: float32 [1536], P('tensor'), may hold values from -640 to 640
- moment_w_out: float32 [1536, 768], P('tensor', 'dp'), may hold values from -192 to 192
Outputs:
- output: float32 [16384, 768], P(('dp', 'tensor'))
- d_stream: float32 [16384, 768], P(('dp', 'tensor'))
- grad_norm_gain: float32 [768], replicated
- grad_w_gate: float32 [768, 1536], P('dp', 'tensor')
- grad_w_inner: float32 [768, 1536], P('dp', 'tensor')
- grad_w_state: float32 [768, 256], P('dp', 'tensor')
- grad_w_step: float32 [768, 24], P('dp', 'tensor')
- grad_conv_inner: float32 [5, 1536], P(None, 'tensor')
- grad_conv_state: float32 [5, 256], replicated
- grad_head_params: float32 [3, 24], P(None, 'tensor')
- grad_gate_gain: float32 [1536], P('tensor')
- grad_w_out: float32 [1536, 768], P('tensor', 'dp')
- new_norm_gain: float32 [768], replicated
- new_w_gate: float32 [768, 1536], P('dp', 'tensor')
- new_w_inner: float32 [768, 1536], P('dp', 'tensor')
- new_w_state: float32 [768, 256], P('dp', 'tensor')
- new_w_step: float32 [768, 24], P('dp', 'tensor')
- new_conv_inner: float32 [5, 1536], P(None, 'tensor')
- new_conv_state: float32 [5, 256], replicated
- new_head_params: float32 [3, 24], P(None, 'tensor')
- new_gate_gain: float32 [1536], P('tensor')
- new_w_out: float32 [1536, 768], P('tensor', 'dp')
- new_moment_norm_gain: float32 [768], replicated
- new_moment_w_gate: float32 [768, 1536], P('dp', 'tensor')
- new_moment_w_inner: float32 [768, 1536], P('dp', 'tensor')
- new_moment_w_state: float32 [768, 256], P('dp', 'tensor')
- new_moment_w_step: float32 [768, 24], P('dp', 'tensor')
- new_moment_conv_inner: float32 [5, 1536], P(None, 'tensor')
- new_moment_conv_state: float32 [5, 256], replicated
- new_moment_head_params: float32 [3, 24], P(None, 'tensor')
- new_moment_gate_gain: float32 [1536], P('tensor')
- new_moment_w_out: float32 [1536, 768], P('tensor', 'dp')
The draws below stay inside these ranges and needn't reach their ends.
Inputs may be any that keep to these rules, and one draw needn't show every extreme that they name: `positions`: within each block of 1024 rows (one index of dp) an entry is the token's position in its sequence, 0 at a sequence's first token; every block starts a sequence at its first row, sequences stay inside a block, and -1 marks padding that only ends a block. `head_params`: row 0 step biases, row 1 logarithms of decay rates, row 2 skip gains.
All inputs are finite; a program needn't handle non-finite values.
Results may differ from the reference program's by a relative error of at most 0.023.
Values may be sent and summed in bfloat16 or wider, within the bound.
A program may use at most 128 MiB of HBM per device.

```python
import math
from functools import partial
import jax
import jax.numpy as jnp
from jax import lax

D = 768
INNER = 1536
HEADS = 24
STATE = 128
CONV = 4
BLOCK = 256
NS_STEPS = 5
TOK_DEV = 1024
TOKENS = 16384
N_TENSOR = 2


def draw_positions(key, part):
    blocks = TOKENS // TOK_DEV
    index = jnp.arange(TOK_DEV, dtype=jnp.int32)[None, :]
    block_id = jnp.arange(blocks, dtype=jnp.int32)[:, None]
    key_start, key_live = jax.random.split(key)
    starts = jax.random.randint(key_start, (blocks, TOK_DEV), 0, 96) == 0
    starts = starts & (block_id > 0) | (index == 0)
    marks = jnp.where(starts, index, 0)
    latest = lax.cummax(marks, axis=1)
    inside = index - latest
    shortfall = jax.random.randint(key_live, (blocks, 1), 0, TOK_DEV // 4)
    live_length = jnp.where(block_id == 0, TOK_DEV, TOK_DEV - 1 - shortfall)
    return jnp.where(index < live_length, inside, -1).reshape(TOKENS).astype(jnp.int32)


def draw_head_params(key, part):
    first, second, third = jax.random.split(jax.random.fold_in(key, 5), 3)
    bias = jax.random.uniform(first, (HEADS,), jnp.float32, -6.0, -2.5)
    rates = jax.random.uniform(second, (HEADS,), jnp.float32, math.log(0.5), math.log(16.0))
    skips = jax.random.uniform(third, (HEADS,), jnp.float32, 0.5, 1.5)
    return jnp.stack([bias, rates, skips]).astype(jnp.float32)


def levels(own_key, extent, cuts, smallest, largest):
    factor_of = 1.0
    for dim, shards_of in cuts:
        heights = jax.random.uniform(jax.random.fold_in(jax.random.fold_in(own_key, 6), dim), (shards_of,), jnp.float32, smallest / len(cuts), largest / len(cuts))
        factor_of = factor_of * jnp.repeat(jnp.exp(heights), extent[dim] // shards_of).reshape((-1,) + (1,) * (len(extent) - 1 - dim))
    return factor_of


def centred(key, shape, scale, limit, cuts=(), held_as=jnp.bfloat16):
    loudness = levels(key, shape, cuts, -0.22, 0.18) if cuts else 1.0
    values = jax.random.normal(key, shape, jnp.float32) * scale * loudness
    return jnp.minimum(jnp.maximum(values, -limit), limit).astype(held_as)


def setup_inputs(seed: int = 0) -> dict:
    splits = jax.random.split(jax.random.key(seed), 24)
    return {
        "stream": centred(splits[0], (TOKENS, D), 1.0, 6.0, ((0, 32),), jnp.float32),
        "cotangent": centred(splits[1], (TOKENS, D), 1.0, 6.0, ((0, 32),), jnp.float32),
        "positions": draw_positions(jax.random.fold_in(splits[23], 71), 0),
        "norm_gain": jnp.clip(1.0 + 0.1 * jax.random.normal(splits[3], (D,), jnp.float32), 0.5, 1.5),
        "w_gate": centred(splits[4], (D, INNER), D ** -0.5, 0.21875, ((0, 16), (1, 2)), jnp.float32),
        "w_inner": centred(splits[5], (D, INNER), D ** -0.5, 0.21875, ((0, 16), (1, 2)), jnp.float32),
        "w_state": centred(splits[6], (D, 2 * STATE), D ** -0.5, 0.21875, ((0, 16),), jnp.float32),
        "w_step": centred(splits[7], (D, HEADS), D ** -0.5, 0.21875, ((0, 16), (1, 2)), jnp.float32),
        "conv_inner": centred(splits[8], (CONV + 1, INNER), 0.5, 3.0, ((1, 2),), jnp.float32),
        "conv_state": centred(splits[9], (CONV + 1, 2 * STATE), 0.5, 3.0, (), jnp.float32),
        "head_params": draw_head_params(jax.random.fold_in(splits[23], 71), 0),
        "gate_gain": jnp.clip(1.0 + 0.1 * jax.random.normal(splits[11], (INNER,), jnp.float32), 0.5, 1.5),
        "w_out": centred(splits[12], (INNER, D), INNER ** -0.5, 0.15625, ((0, 2), (1, 16)), jnp.float32),
        "moment_norm_gain": centred(splits[13], (D,), 100.0, 640.0, (), jnp.float32),
        "moment_w_gate": centred(splits[14], (D, INNER), 30.0, 192.0, ((0, 16), (1, 2)), jnp.float32),
        "moment_w_inner": centred(splits[15], (D, INNER), 30.0, 192.0, ((0, 16), (1, 2)), jnp.float32),
        "moment_w_state": centred(splits[16], (D, 2 * STATE), 30.0, 192.0, ((0, 16), (1, 2)), jnp.float32),
        "moment_w_step": centred(splits[17], (D, HEADS), 30.0, 192.0, ((0, 16), (1, 2)), jnp.float32),
        "moment_conv_inner": centred(splits[18], (CONV + 1, INNER), 100.0, 640.0, ((1, 2),), jnp.float32),
        "moment_conv_state": centred(splits[19], (CONV + 1, 2 * STATE), 100.0, 640.0, (), jnp.float32),
        "moment_head_params": centred(splits[20], (3, HEADS), 100.0, 640.0, ((1, 2),), jnp.float32),
        "moment_gate_gain": centred(splits[21], (INNER,), 100.0, 640.0, ((0, 2),), jnp.float32),
        "moment_w_out": centred(splits[22], (INNER, D), 30.0, 192.0, ((0, 2), (1, 16)), jnp.float32),
    }


EPS = 1e-05
NS_A = 3.4445
NS_B = -4.775
NS_C = 2.0315
MU_MAT = 0.95
MU_VEC = 0.9
LR_MAT = 0.3
LR_VEC = 0.001
HIGH = lax.Precision.HIGHEST

def silu_slope(value):
    sig = jax.nn.sigmoid(value)
    return sig * (1.0 + value * (1.0 - sig))

def contract_rows(left, right):
    return lax.dot_general(left, right, (((0,), (0,)), ((), ())), preferred_element_type=jnp.float32)

def times_transpose(left, right):
    return lax.dot_general(left, right, (((1,), (1,)), ((), ())), preferred_element_type=jnp.float32)

def causal_conv(signal, taps, positions):
    length = signal.shape[0]
    reach = taps.shape[0] - 1
    total = jnp.zeros_like(signal) + taps[reach]
    for lag_step in range(reach):
        moved = jnp.pad(signal, ((lag_step, 0), (0, 0)))[:length]
        total = total + jnp.where((positions >= lag_step)[:, None], moved * taps[lag_step], 0.0)
    return jax.nn.silu(total)

def mixer_core(inner_pre, state_pre, step_pre, conv_inner, conv_state, head_params, positions):
    length = inner_pre.shape[0]
    heads = step_pre.shape[1]
    head_size = inner_pre.shape[1] // heads
    states = state_pre.shape[1] // 2
    blocks = length // BLOCK
    inner_act = causal_conv(inner_pre, conv_inner, positions).reshape(blocks, BLOCK, heads, head_size)
    state_act = causal_conv(state_pre, conv_state, positions)
    input_map = state_act[:, :states].reshape(blocks, BLOCK, states)
    output_map = state_act[:, states:].reshape(blocks, BLOCK, states)
    step_size = jax.nn.softplus(step_pre + head_params[0])
    log_decay = (step_size * -jnp.exp(head_params[1])).reshape(blocks, BLOCK, heads)
    step_size = step_size.reshape(blocks, BLOCK, heads)
    resets = (positions <= 0).astype(jnp.float32).reshape(blocks, BLOCK)
    cumulative = jnp.cumsum(log_decay, axis=1)
    seen = jnp.cumsum(resets, axis=1)
    order = jnp.arange(BLOCK)
    linked = (seen[:, :, None] == seen[:, None, :]) & (order[:, None] >= order[None, :])[None]
    linked_heads = linked[..., None]
    spacing = cumulative[:, :, None, :] - cumulative[:, None, :, :]
    decay = jnp.where(linked_heads, jnp.exp(jnp.where(linked_heads, spacing, 0.0)), 0.0)
    scores = jnp.einsum('cin,cjn->cij', output_map, input_map, precision=HIGH)
    mixing = scores[..., None] * decay * step_size[:, None, :, :]
    within = jnp.einsum('cijh,cjhp->cihp', mixing, inner_act, precision=HIGH)
    tail_linked = (seen[:, -1:] == seen)[..., None]
    tail = jnp.where(tail_linked, jnp.exp(jnp.where(tail_linked, cumulative[:, -1:, :] - cumulative, 0.0)), 0.0) * step_size
    own_state = jnp.einsum('cjh,cjhp,cjn->chpn', tail, inner_act, input_map, precision=HIGH)
    carry_rate = jnp.exp(cumulative[:, -1, :]) * (seen[:, -1] == 0).astype(jnp.float32)[:, None]

    def advance(state, inputs):
        rate, fresh_state = inputs
        return (rate[:, None, None] * state + fresh_state, state)
    _, entering = lax.scan(advance, jnp.zeros((heads, head_size, states), jnp.float32), (carry_rate, own_state))
    fresh = (seen == 0)[..., None]
    carry_in = jnp.where(fresh, jnp.exp(cumulative), 0.0)
    across = jnp.einsum('cin,chpn->cihp', output_map, entering, precision=HIGH) * carry_in[..., None]
    result = within + across + head_params[2][None, None, :, None] * inner_act
    return result.reshape(length, heads * head_size)

def layer_pass(stream, cotangent, positions, params):
    norm_gain, full_gate, full_inner, full_state, full_step, conv_inner, conv_state, head_params, gate_gain, full_out = params
    inv_first = lax.rsqrt(lax.optimization_barrier(jnp.mean(stream * stream, axis=1, keepdims=True)) + EPS)
    normed = (stream * inv_first * norm_gain).astype(jnp.bfloat16)
    gate_pre = jnp.dot(normed, full_gate, preferred_element_type=jnp.float32)
    inner_pre = jnp.dot(normed, full_inner, preferred_element_type=jnp.float32)
    state_pre = jnp.dot(normed, full_state, preferred_element_type=jnp.float32)
    step_pre = jnp.dot(normed, full_step, preferred_element_type=jnp.float32)
    alive = (positions >= 0).astype(jnp.float32)[:, None]
    scanned, core_back = jax.vjp(partial(mixer_core, positions=positions), inner_pre, state_pre, step_pre, conv_inner, conv_state, head_params)
    gate_act = jax.nn.silu(gate_pre)
    gated = scanned * gate_act
    inv_second = lax.rsqrt(lax.optimization_barrier(jnp.sum(gated * gated, axis=1, keepdims=True)) / INNER + EPS)
    normed_out = (gated * inv_second * gate_gain * alive).astype(jnp.bfloat16)
    output = stream + jnp.dot(normed_out, full_out, preferred_element_type=jnp.float32)
    cot_low = cotangent.astype(jnp.bfloat16)
    d_normed_out = times_transpose(cot_low, full_out)
    grad_out = contract_rows(normed_out, cot_low)
    scaled = d_normed_out * gate_gain * alive
    grad_gate_gain = lax.optimization_barrier(jnp.sum(d_normed_out * gated * inv_second * alive, axis=0))
    cross_sum = lax.optimization_barrier(jnp.sum(scaled * gated, axis=1, keepdims=True))
    d_gated = inv_second * scaled - gated * inv_second ** 3 * (cross_sum / INNER)
    d_gate_pre = (d_gated * scanned * silu_slope(gate_pre)).astype(jnp.bfloat16)
    d_inner, d_state, d_step, grad_conv_inner, grad_conv_state, grad_head = core_back(d_gated * gate_act)
    d_inner_low = d_inner.astype(jnp.bfloat16)
    d_state_low = d_state.astype(jnp.bfloat16)
    d_step_low = d_step.astype(jnp.bfloat16)
    d_normed = times_transpose(d_gate_pre, full_gate) + times_transpose(d_inner_low, full_inner)
    d_normed = d_normed + times_transpose(d_state_low, full_state) + times_transpose(d_step_low, full_step)
    grad_norm = lax.optimization_barrier(jnp.sum(d_normed * stream * inv_first, axis=0))
    weighted = d_normed * norm_gain
    d_stream = cotangent + inv_first * weighted - stream * inv_first ** 3 * lax.optimization_barrier(jnp.mean(weighted * stream, axis=1, keepdims=True))
    grads = (grad_norm, contract_rows(normed, d_gate_pre), contract_rows(normed, d_inner_low), contract_rows(normed, d_state_low), contract_rows(normed, d_step_low), grad_conv_inner, grad_conv_state, grad_head, grad_gate_gain, grad_out)
    return (output, d_stream, grads)

def gram_groups(low, groups):
    rows = low.shape[0]
    width = low.shape[1] // groups
    pieces = low.astype(jnp.float32).reshape(rows, groups, width)
    terms = jnp.einsum('rgc,sgc->grs', pieces, pieces, precision=HIGH)
    rounded = lax.optimization_barrier(terms.astype(jnp.bfloat16))
    return lax.optimization_barrier(jnp.sum(rounded.astype(jnp.float32), axis=0))

def orthogonalize(matrix, groups):
    first = gram_groups(matrix.astype(jnp.bfloat16), groups)
    scale = jnp.sqrt(jnp.trace(first)) + 1e-07
    current = (matrix / scale).astype(jnp.bfloat16)
    gram = (first / (scale * scale)).astype(jnp.bfloat16)
    for turn in range(NS_STEPS):
        if turn > 0:
            gram = gram_groups(current, groups).astype(jnp.bfloat16)
        applied = jnp.dot(gram, current, preferred_element_type=jnp.float32)
        twice = jnp.dot(gram, applied.astype(jnp.bfloat16), preferred_element_type=jnp.float32)
        current = (NS_A * current.astype(jnp.float32) + NS_B * applied + NS_C * twice).astype(jnp.bfloat16)
    return current.astype(jnp.float32)

def widen(matrix, groups):
    rows = matrix.shape[0]
    width = matrix.shape[1] // groups
    room = INNER // groups
    return jnp.pad(matrix.reshape(rows, groups, width), ((0, 0), (0, 0), (0, room - width))).reshape(rows, groups * room)

def narrow(matrix, groups, width):
    rows = matrix.shape[0]
    room = matrix.shape[1] // groups
    return matrix.reshape(rows, groups, room)[:, :, :width].reshape(rows, groups * width)

def spread(rows, cols):
    return math.sqrt(max(1.0, rows / cols))

def reference(stream, cotangent, positions, norm_gain, w_gate, w_inner, w_state, w_step, conv_inner, conv_state, head_params, gate_gain, w_out, moment_norm_gain, moment_w_gate, moment_w_inner, moment_w_state, moment_w_step, moment_conv_inner, moment_conv_state, moment_head_params, moment_gate_gain, moment_w_out):
    params = (norm_gain, w_gate.astype(jnp.bfloat16), w_inner.astype(jnp.bfloat16), w_state.astype(jnp.bfloat16), w_step.astype(jnp.bfloat16), conv_inner, conv_state, head_params, gate_gain, w_out.astype(jnp.bfloat16))
    initials = (norm_gain, w_gate, w_inner, w_state, w_step, conv_inner, conv_state, head_params, gate_gain, w_out)
    init = tuple((jnp.zeros(item.shape, jnp.float32) for item in initials))
    blocks = stream.shape[0] // TOK_DEV

    def one_block(totals, data):
        rows, cots, where_pos = data
        output, d_rows, grads = layer_pass(rows, cots, where_pos, params)
        return (tuple((first + second for first, second in zip(totals, grads))), (output, d_rows))
    grads, (outputs, d_streams) = lax.scan(one_block, init, (stream.reshape(blocks, TOK_DEV, D), cotangent.reshape(blocks, TOK_DEV, D), positions.reshape(blocks, TOK_DEV)))
    g_norm, g_gate, g_inner, g_state, g_step, g_conv_inner, g_conv_state, g_head, g_gate_gain, g_out = grads
    groups = N_TENSOR
    m_gate = MU_MAT * moment_w_gate + g_gate
    m_inner = MU_MAT * moment_w_inner + g_inner
    m_state = MU_MAT * moment_w_state + g_state
    m_step = MU_MAT * moment_w_step + g_step
    m_out = MU_MAT * moment_w_out + g_out
    new_gate = w_gate - LR_MAT * spread(D, INNER) * orthogonalize(m_gate, groups)
    new_inner = w_inner - LR_MAT * spread(D, INNER) * orthogonalize(m_inner, groups)
    new_out = w_out - LR_MAT * spread(INNER, D) * orthogonalize(m_out.T, groups).T
    new_step = w_step - LR_MAT * spread(D, HEADS) * narrow(orthogonalize(widen(m_step, groups), groups), groups, HEADS // groups)
    new_state = w_state - LR_MAT * spread(D, 2 * STATE) * narrow(orthogonalize(widen(m_state, groups), groups), groups, 2 * STATE // groups)
    m_norm = MU_VEC * moment_norm_gain + g_norm
    m_conv_inner = MU_VEC * moment_conv_inner + g_conv_inner
    m_conv_state = MU_VEC * moment_conv_state + g_conv_state
    m_head = MU_VEC * moment_head_params + g_head
    m_gate_gain = MU_VEC * moment_gate_gain + g_gate_gain
    return (outputs.reshape(stream.shape), d_streams.reshape(stream.shape), g_norm, g_gate, g_inner, g_state, g_step, g_conv_inner, g_conv_state, g_head, g_gate_gain, g_out, norm_gain - LR_VEC * m_norm, new_gate, new_inner, new_state, new_step, conv_inner - LR_VEC * m_conv_inner, conv_state - LR_VEC * m_conv_state, head_params - LR_VEC * m_head, gate_gain - LR_VEC * m_gate_gain, new_out, m_norm, m_gate, m_inner, m_state, m_step, m_conv_inner, m_conv_state, m_head, m_gate_gain, m_out)
```

```python
from functools import partial
import math

import jax
import jax.numpy as jnp
from jax import lax
from jax.experimental import pallas as pl
from jax.experimental.pallas import tpu as pltpu
from jax.sharding import PartitionSpec as P

D = 768
INNER = 1536
HEADS = 24
STATE = 128
BLOCK = 256
NS_STEPS = 5


EPS = 1e-05
NS_A = 3.4445
NS_B = -4.775
NS_C = 2.0315
MU_MAT = 0.95
MU_VEC = 0.9
LR_MAT = 0.3
LR_VEC = 0.001
HIGH = lax.Precision.HIGHEST
CORE = lax.Precision.DEFAULT


def silu_slope(value):
    sig = jax.nn.sigmoid(value)
    return sig * (1.0 + value * (1.0 - sig))


def contract_rows(left, right):
    return lax.dot_general(
        left, right, (((0,), (0,)), ((), ())), preferred_element_type=jnp.float32
    )


def times_transpose(left, right):
    return lax.dot_general(
        left, right, (((1,), (1,)), ((), ())), preferred_element_type=jnp.float32
    )


def causal_conv(signal, taps, positions):
    length = signal.shape[0]
    reach = taps.shape[0] - 1
    total = jnp.zeros_like(signal) + taps[reach]
    for lag_step in range(reach):
        moved = jnp.pad(signal, ((lag_step, 0), (0, 0)))[:length]
        total = total + jnp.where((positions >= lag_step)[:, None], moved * taps[lag_step], 0.0)
    return jax.nn.silu(total)


def mixer_core(inner_pre, state_pre, step_pre, conv_inner, conv_state, head_params, positions, precision=HIGH):
    length = inner_pre.shape[0]
    heads = step_pre.shape[1]
    head_size = inner_pre.shape[1] // heads
    states = state_pre.shape[1] // 2
    blocks = length // BLOCK
    inner_act = causal_conv(inner_pre, conv_inner, positions).reshape(
        blocks, BLOCK, heads, head_size
    )
    state_act = causal_conv(state_pre, conv_state, positions)
    input_map = state_act[:, :states].reshape(blocks, BLOCK, states)
    output_map = state_act[:, states:].reshape(blocks, BLOCK, states)
    step_size = jax.nn.softplus(step_pre + head_params[0])
    log_decay = (step_size * -jnp.exp(head_params[1])).reshape(blocks, BLOCK, heads)
    step_size = step_size.reshape(blocks, BLOCK, heads)
    resets = (positions <= 0).astype(jnp.float32).reshape(blocks, BLOCK)
    order = jnp.arange(BLOCK)
    lower = (order[:, None] >= order[None, :]).astype(jnp.float32)
    cumulative = jnp.einsum("ij,cjh->cih", lower, log_decay, precision=HIGH)
    seen = jnp.einsum("ij,cj->ci", lower, resets, precision=HIGH)
    linked = (seen[:, :, None] == seen[:, None, :]) & (order[:, None] >= order[None, :])[None]
    linked_heads = linked[..., None]
    spacing = cumulative[:, :, None, :] - cumulative[:, None, :, :]
    decay = jnp.where(linked_heads, jnp.exp(jnp.where(linked_heads, spacing, 0.0)), 0.0)
    scores = jnp.einsum("cin,cjn->cij", output_map, input_map, precision=precision)
    mixing = scores[..., None] * decay * step_size[:, None, :, :]
    within = jnp.einsum("cijh,cjhp->cihp", mixing, inner_act, precision=precision)
    tail_linked = (seen[:, -1:] == seen)[..., None]
    tail = (
        jnp.where(
            tail_linked,
            jnp.exp(jnp.where(tail_linked, cumulative[:, -1:, :] - cumulative, 0.0)),
            0.0,
        )
        * step_size
    )
    own_state = jnp.einsum("cjh,cjhp,cjn->chpn", tail, inner_act, input_map, precision=precision)
    carry_rate = jnp.exp(cumulative[:, -1, :]) * (seen[:, -1] == 0).astype(jnp.float32)[:, None]

    state = jnp.zeros((heads, head_size, states), jnp.float32)
    entering = []
    for block in range(blocks):
        entering.append(state)
        state = carry_rate[block][:, None, None] * state + own_state[block]
    entering = jnp.stack(entering)
    fresh = (seen == 0)[..., None]
    carry_in = jnp.where(fresh, jnp.exp(cumulative), 0.0)
    across = (
        jnp.einsum("cin,chpn->cihp", output_map, entering, precision=precision) * carry_in[..., None]
    )
    result = within + across + head_params[2][None, None, :, None] * inner_act
    return result.reshape(length, heads * head_size)


def gram_total(low):
    return lax.psum(
        jnp.dot(low, low.T, preferred_element_type=jnp.float32).astype(jnp.bfloat16), "tensor"
    ).astype(jnp.float32)


def orthogonalize(matrix):
    first = gram_total(matrix.astype(jnp.bfloat16))
    scale = jnp.sqrt(jnp.trace(first)) + 1e-07
    current = (matrix / scale).astype(jnp.bfloat16)
    gram = (first / (scale * scale)).astype(jnp.bfloat16)
    for turn in range(NS_STEPS):
        if turn > 0:
            gram = gram_total(current).astype(jnp.bfloat16)
        applied = jnp.dot(gram, current, preferred_element_type=jnp.float32)
        twice = jnp.dot(gram, applied.astype(jnp.bfloat16), preferred_element_type=jnp.float32)
        current = (NS_A * current.astype(jnp.float32) + NS_B * applied + NS_C * twice).astype(
            jnp.bfloat16
        )
    return current.astype(jnp.float32)


def spread(rows, cols):
    return math.sqrt(max(1.0, rows / cols))


def shards(
    stream,
    cotangent,
    positions,
    norm_gain,
    w_gate,
    w_inner,
    w_state,
    w_step,
    conv_inner,
    conv_state,
    head_params,
    gate_gain,
    w_out,
    moment_norm_gain,
    moment_w_gate,
    moment_w_inner,
    moment_w_state,
    moment_w_step,
    moment_conv_inner,
    moment_conv_state,
    moment_head_params,
    moment_gate_gain,
    moment_w_out,
):
    dp_count = lax.axis_size("dp")
    inv_first = lax.rsqrt(jnp.mean(stream * stream, axis=1, keepdims=True) + EPS)
    normed = (stream * inv_first * norm_gain).astype(jnp.bfloat16)
    token_rows, cotangent_rows = (
        lax.all_gather(normed, "tensor", axis=0, tiled=True),
        lax.all_gather(cotangent.astype(jnp.bfloat16), "tensor", axis=0, tiled=True),
    )
    local_weights = (
        w_gate.astype(jnp.bfloat16),
        w_inner.astype(jnp.bfloat16),
        w_step.astype(jnp.bfloat16),
        w_state.astype(jnp.bfloat16),
        w_out.astype(jnp.bfloat16),
    )
    full_gate, full_inner, full_step, full_state, full_out = (
        lax.all_gather(local_weights[0], "dp", axis=0, tiled=True),
        lax.all_gather(local_weights[1], "dp", axis=0, tiled=True),
        lax.all_gather(local_weights[2], "dp", axis=0, tiled=True),
        lax.all_gather(local_weights[3], "dp", axis=0, tiled=True),
        lax.all_gather(local_weights[4], "dp", axis=1, tiled=True),
    )
    gate_pre = jnp.dot(token_rows, full_gate, preferred_element_type=jnp.float32)
    inner_pre = jnp.dot(token_rows, full_inner, preferred_element_type=jnp.float32)
    state_pre = jnp.dot(token_rows, full_state, preferred_element_type=jnp.float32)
    step_pre = jnp.dot(token_rows, full_step, preferred_element_type=jnp.float32)
    alive = (positions >= 0).astype(jnp.float32)[:, None]
    scanned, core_back = jax.vjp(
        partial(mixer_core, positions=positions),
        inner_pre,
        state_pre,
        step_pre,
        conv_inner,
        conv_state,
        head_params,
    )
    gate_act = jax.nn.silu(gate_pre)
    gated = scanned * gate_act
    square_sum = lax.psum(jnp.sum(gated * gated, axis=1), "tensor")
    inv_second = lax.rsqrt(square_sum / INNER + EPS)[:, None]
    normed_out = (gated * inv_second * gate_gain * alive).astype(jnp.bfloat16)
    mixed = lax.psum_scatter(
        jnp.dot(normed_out, full_out, preferred_element_type=jnp.float32).astype(jnp.bfloat16),
        "tensor",
        scatter_dimension=0,
        tiled=True,
    ).astype(jnp.float32)
    output = stream + mixed
    d_normed_out = times_transpose(cotangent_rows, full_out)
    grad_out_part = contract_rows(normed_out, cotangent_rows)
    scaled = d_normed_out * gate_gain * alive
    grad_gate_part = jnp.sum(d_normed_out * gated * inv_second * alive, axis=0)
    cross_sum = lax.psum(jnp.sum(scaled * gated, axis=1), "tensor")
    d_gated = inv_second * scaled - gated * inv_second**3 * (cross_sum / INNER)[:, None]
    d_gate_pre = (d_gated * scanned * silu_slope(gate_pre)).astype(jnp.bfloat16)
    d_inner, d_state_part, d_step, grad_conv_inner_part, grad_conv_state_part, grad_head_part = (
        core_back(d_gated * gate_act)
    )
    d_state_cols = lax.psum_scatter(
        d_state_part.astype(jnp.bfloat16), "tensor", scatter_dimension=1, tiled=True
    ).astype(jnp.float32)
    d_inner_low = d_inner.astype(jnp.bfloat16)
    d_state_low = d_state_cols.astype(jnp.bfloat16)
    d_step_low = d_step.astype(jnp.bfloat16)
    col_width = d_state_cols.shape[1]
    col_first = lax.axis_index("tensor") * col_width
    state_cols = lax.dynamic_slice_in_dim(full_state, col_first, col_width, 1)
    total = times_transpose(d_gate_pre, full_gate)
    total = total + times_transpose(d_inner_low, full_inner)
    total = total + times_transpose(d_state_low, state_cols)
    d_normed = lax.psum_scatter(
        (total + times_transpose(d_step_low, full_step)).astype(jnp.bfloat16),
        "tensor",
        scatter_dimension=0,
        tiled=True,
    ).astype(jnp.float32)
    grad_gate_w, grad_inner_w, grad_state_w, grad_step_w, grad_out_w = (
        lax.psum_scatter(
            contract_rows(token_rows, d_gate_pre).astype(jnp.bfloat16),
            "dp",
            scatter_dimension=0,
            tiled=True,
        ).astype(jnp.float32),
        lax.psum_scatter(
            contract_rows(token_rows, d_inner_low).astype(jnp.bfloat16),
            "dp",
            scatter_dimension=0,
            tiled=True,
        ).astype(jnp.float32),
        lax.psum_scatter(
            contract_rows(token_rows, d_state_low).astype(jnp.bfloat16),
            "dp",
            scatter_dimension=0,
            tiled=True,
        ).astype(jnp.float32),
        lax.psum_scatter(
            contract_rows(token_rows, d_step_low).astype(jnp.bfloat16),
            "dp",
            scatter_dimension=0,
            tiled=True,
        ).astype(jnp.float32),
        lax.psum_scatter(
            grad_out_part.astype(jnp.bfloat16), "dp", scatter_dimension=1, tiled=True
        ).astype(jnp.float32),
    )
    grad_norm_part = jnp.sum(d_normed * stream * inv_first, axis=0)
    weighted = d_normed * norm_gain
    d_stream = (
        cotangent
        + inv_first * weighted
        - stream * inv_first**3 * jnp.mean(weighted * stream, axis=1, keepdims=True)
    )
    grad_conv_inner, grad_gate_gain, grad_head = lax.psum(
        (grad_conv_inner_part, grad_gate_part, grad_head_part), "dp"
    )
    grad_conv_state, grad_norm = lax.psum((grad_conv_state_part, grad_norm_part), ("dp", "tensor"))
    m_gate = MU_MAT * moment_w_gate + grad_gate_w
    m_inner = MU_MAT * moment_w_inner + grad_inner_w
    m_state = MU_MAT * moment_w_state + grad_state_w
    m_step = MU_MAT * moment_w_step + grad_step_w
    m_out = MU_MAT * moment_w_out + grad_out_w
    room = w_gate.shape[1]
    shard_rows = w_gate.shape[0]
    stacked = jnp.stack(
        [
            m_gate,
            m_inner,
            m_out.T,
            jnp.pad(m_step, ((0, 0), (0, room - m_step.shape[1]))),
            jnp.pad(m_state, ((0, 0), (0, room - m_state.shape[1]))),
        ]
    )
    matrix_count = stacked.shape[0]
    owner_index = jnp.arange(matrix_count, dtype=jnp.int32) * dp_count // matrix_count
    select = (owner_index[None, :] == jnp.arange(dp_count, dtype=jnp.int32)[:, None]).astype(
        jnp.float32
    )
    outgoing = jnp.einsum("jk,krc->jrc", select, stacked, precision=HIGH)
    owned = (
        lax.all_to_all(outgoing.astype(jnp.bfloat16), "dp", split_axis=0, concat_axis=0, tiled=True)
        .astype(outgoing.dtype)
        .reshape(dp_count * shard_rows, room)
    )
    ortho = orthogonalize(owned)
    returned = lax.all_to_all(
        ortho.reshape(dp_count, shard_rows, room).astype(jnp.bfloat16),
        "dp",
        split_axis=0,
        concat_axis=0,
        tiled=True,
    ).astype(jnp.float32)
    mine = jnp.einsum("jk,jrc->krc", select, returned, precision=HIGH)
    new_gate = w_gate - LR_MAT * spread(D, INNER) * mine[0]
    new_inner = w_inner - LR_MAT * spread(D, INNER) * mine[1]
    new_out = w_out - LR_MAT * spread(INNER, D) * mine[2].T
    new_step = w_step - LR_MAT * spread(D, HEADS) * mine[3][:, : w_step.shape[1]]
    state_slice = lax.dynamic_slice_in_dim(w_state, col_first, col_width, 1)
    new_state = state_slice - LR_MAT * spread(D, 2 * STATE) * mine[4][:, :col_width]
    m_norm = MU_VEC * moment_norm_gain + grad_norm
    m_conv_inner = MU_VEC * moment_conv_inner + grad_conv_inner
    m_conv_state = MU_VEC * moment_conv_state + grad_conv_state
    m_head = MU_VEC * moment_head_params + grad_head
    m_gate_gain = MU_VEC * moment_gate_gain + grad_gate_gain
    return (
        output,
        d_stream,
        grad_norm,
        grad_gate_w,
        grad_inner_w,
        grad_state_w,
        grad_step_w,
        grad_conv_inner,
        grad_conv_state,
        grad_head,
        grad_gate_gain,
        grad_out_w,
        norm_gain - LR_VEC * m_norm,
        new_gate,
        new_inner,
        new_state,
        new_step,
        conv_inner - LR_VEC * m_conv_inner,
        conv_state - LR_VEC * m_conv_state,
        head_params - LR_VEC * m_head,
        gate_gain - LR_VEC * m_gate_gain,
        new_out,
        m_norm,
        m_gate,
        m_inner,
        m_state,
        m_step,
        m_conv_inner,
        m_conv_state,
        m_head,
        m_gate_gain,
        m_out,
    )


CHUNK = 128
PACK = 16


def sigmoid(value):
    return 0.5 * jnp.tanh(0.5 * value) + 0.5


def expand_matrix():
    row = jnp.arange(128)[:, None]
    col = jnp.arange(768)[None, :] // 64
    return ((row == col) | (row == col + PACK)).astype(jnp.bfloat16)


def two_term(value):
    lane = lax.broadcasted_iota(jnp.int32, value.shape, 1)
    high = value.astype(jnp.bfloat16).astype(jnp.float32)
    return jnp.where(lane < PACK, high, value - high).astype(jnp.bfloat16)


def split_terms(value, terms):
    out = []
    for _ in range(terms):
        piece = value.astype(jnp.bfloat16)
        out.append(piece)
        value = value - piece.astype(jnp.float32)
    return out


def dot(left, right, dims=((1,), (0,))):
    return lax.dot_general(left, right, (dims, ((), ())), preferred_element_type=jnp.float32)


def head_terms(step_ref, head_ref, pos):
    shifted = step_ref[...] + head_ref[0:1, :]
    small = jnp.exp(-jnp.abs(shifted))
    step = jnp.maximum(shifted, 0.0) + jnp.log1p(small)
    log_decay = -step * jnp.exp(head_ref[1:2, :])
    row = lax.broadcasted_iota(jnp.int32, (CHUNK, 128), 0)
    col = lax.broadcasted_iota(jnp.int32, (CHUNK, 128), 1)
    lower = (row >= col).astype(jnp.bfloat16)
    cumulative = sum(dot(lower, piece) for piece in split_terms(log_decay, 3))
    last = cumulative[CHUNK - 1 : CHUNK, :]
    back = (row - col).astype(jnp.float32)
    linked = (row >= col) & (back <= jnp.maximum(pos, 0.0))
    row = row.astype(jnp.float32)
    carry_in = jnp.where(pos > row, jnp.exp(cumulative), 0.0)
    pos_last = pos[CHUNK - 1 : CHUNK, :]
    tail_linked = (CHUNK - 1.0 - row) <= jnp.maximum(pos_last, 0.0)
    tail = jnp.where(tail_linked, jnp.exp(jnp.minimum(last - cumulative, 0.0)), 0.0)
    carry = jnp.where(pos_last > CHUNK - 1.0, jnp.exp(last), 0.0)
    return shifted, step, log_decay, cumulative, linked, carry_in, tail, carry


def pair_decay(cumulative, across, pair):
    parts = []
    for head in (2 * pair, 2 * pair + 1):
        spacing = cumulative[:, head : head + 1] - across[head : head + 1, :]
        parts.append(jnp.exp(jnp.minimum(spacing, 0.0)))
    return parts


def forward_kernel(
    inner_ref, step_ref, gate_ref, state_ref, dno_ref, pos_ref, taps_ref, taps_s_ref, head_ref,
    skip_ref, gain_ref, wide_ref,
    scanned_ref, zi_ref, zs_ref, enter_ref, sums_ref,
    halo_i, halo_s, hold,
):
    @pl.when(pl.program_id(0) == 0)
    def _():
        halo_i[...] = jnp.zeros_like(halo_i)
        halo_s[...] = jnp.zeros_like(halo_s)
        hold[...] = jnp.zeros_like(hold)

    low = jnp.bfloat16
    pos = pos_ref[...]
    marks = [(pos >= lag).astype(jnp.float32) for lag in range(4)]

    def conv(ref, halo, taps, out_ref, first):
        value = ref[:, first : first + 128]
        ext = jnp.concatenate([halo[:, first : first + 128], value], axis=0)
        total = taps[4:5, first : first + 128] + marks[0] * (value * taps[0:1, first : first + 128])
        for lag in range(1, 4):
            moved = pltpu.roll(ext, lag, 0)[8:]
            total = total + marks[lag] * (moved * taps[lag : lag + 1, first : first + 128])
        out_ref[:, first : first + 128] = total
        return total * sigmoid(total)

    shifted, step, log_decay, cumulative, linked, carry_in, tail, carry = head_terms(
        step_ref, head_ref, pos
    )
    across = cumulative.T
    wide = dot(
        jnp.concatenate(
            [
                two_term(step),
                two_term(carry_in),
                two_term(tail * step),
                two_term(jnp.broadcast_to(carry, (16, 128))),
            ],
            axis=0,
        ),
        wide_ref[...],
    )
    input_map = conv(state_ref, halo_s, taps_s_ref, zs_ref, 0).astype(low)
    output_map = conv(state_ref, halo_s, taps_s_ref, zs_ref, 128).astype(low)
    scores = jnp.where(linked, dot(output_map, input_map, ((1,), (1,))), 0.0)
    state = hold[...]
    state_low = state.astype(low)
    enter_ref[...] = state_low
    entered = dot(output_map, state_low)
    lane = lax.broadcasted_iota(jnp.int32, (CHUNK, 128), 1)
    squares = jnp.zeros((CHUNK, 128), jnp.float32)
    crosses = jnp.zeros((CHUNK, 128), jnp.float32)
    fed = []
    for pair in range(6):
        cols = slice(pair * 128, pair * 128 + 128)
        act = conv(inner_ref, halo_i, taps_ref, zi_ref, pair * 128)
        stepped = (wide[:CHUNK, cols] * act).astype(low)
        first, second = pair_decay(cumulative, across, pair)
        mixing = jnp.concatenate([(scores * first).astype(low), (scores * second).astype(low)], axis=0)
        both = dot(mixing, stepped)
        within = jnp.where(lane < 64, both[:CHUNK], both[CHUNK:])
        scanned = (
            within + entered[:, cols] * wide[CHUNK : 2 * CHUNK, cols] + skip_ref[0:1, cols] * act
        )
        scanned_ref[:, cols] = scanned
        fed.append((wide[2 * CHUNK : 3 * CHUNK, cols] * act).astype(low))
        gate = gate_ref[:, cols]
        gated = scanned * (gate * sigmoid(gate))
        squares = squares + gated * gated
        crosses = crosses + dno_ref[:, cols] * gain_ref[0:1, cols] * gated
    fresh = dot(input_map, jnp.concatenate(fed, axis=1), ((0,), (0,)))
    hold[...] = wide[3 * CHUNK : 3 * CHUNK + 1, :] * state + fresh
    halo_i[...] = inner_ref[CHUNK - 8 :, :]
    halo_s[...] = state_ref[CHUNK - 8 :, :]
    square = jnp.sum(squares, axis=1, keepdims=True)
    cross = jnp.sum(crosses * marks[0], axis=1, keepdims=True)
    sums_ref[...] = jnp.where(lane == 0, square, cross)


def backward_kernel(
    inner_ref, step_ref, state_ref, zi_ref, zs_ref, scanned_ref, dscan_ref, enter_ref, pos_ref,
    taps_ref, taps_s_ref, head_ref, skip_ref, wide_ref,
    d_inner_ref, d_state_ref, d_step_ref, g_taps_ref, g_taps_s_ref, g_skip_ref, g_head_ref,
    halo_i, halo_s, halo_p, hold,
):
    low = jnp.bfloat16

    @pl.when(pl.program_id(0) == 0)
    def _():
        for ref in (halo_i, halo_s, halo_p, hold, g_taps_ref, g_taps_s_ref, g_skip_ref, g_head_ref):
            ref[...] = jnp.zeros_like(ref)

    pos = pos_ref[...]
    pos_ext = jnp.concatenate([pos, halo_p[...]], axis=0)
    marks = [(pos_ext >= lag).astype(jnp.float32) for lag in range(4)]
    lane = lax.broadcasted_iota(jnp.int32, (CHUNK, 128), 1)
    row = lax.broadcasted_iota(jnp.int32, (CHUNK, 128), 0)
    col = lane

    def slope(total):
        sig = sigmoid(total)
        return sig * (1.0 + total * (1.0 - sig)), total * sig

    def fold(value):
        return jnp.sum(value.reshape(CHUNK // 8, 8, 128), axis=0)

    def conv_back(grad, ref, halo, taps, out_ref, g_ref, first):
        cols = slice(first, first + 128)
        ext = jnp.concatenate([grad, halo[:, cols]], axis=0)
        value = ref[:, cols]
        halo[:, cols] = grad[:8]
        g_ref[4, :, cols] += fold(grad)
        total = jnp.zeros((CHUNK, 128), jnp.float32)
        for lag in range(4):
            masked = ext * marks[lag]
            if lag:
                masked = pltpu.roll(masked, CHUNK + 8 - lag, 0)
            masked = masked[:CHUNK]
            g_ref[lag, :, cols] += fold(masked * value)
            total = total + masked * taps[lag : lag + 1, cols]
        out_ref[:, cols] = total.astype(low)

    shifted, step, log_decay, cumulative, linked, carry_in, tail, carry = head_terms(
        step_ref, head_ref, pos
    )
    across = cumulative.T
    wide = dot(
        jnp.concatenate(
            [
                two_term(step),
                two_term(carry_in),
                two_term(tail),
                two_term(jnp.broadcast_to(carry, (16, 128))),
            ],
            axis=0,
        ),
        wide_ref[...],
    )
    slope_b, input_map = slope(zs_ref[:, :128])
    slope_c, output_map = slope(zs_ref[:, 128:])
    input_low, output_low = input_map.astype(low), output_map.astype(low)
    scores = jnp.where(linked, dot(output_low, input_low, ((1,), (1,))), 0.0)
    entering = enter_ref[...]
    d_next = hold[...]
    d_next_low = d_next.astype(low)
    pulled = dot(input_low, d_next_low)
    d_scores = jnp.zeros((CHUNK, 128), jnp.float32)
    d_entered, fed, balance, direct, extra = [], [], [], [], []
    carry_wide = wide[3 * CHUNK : 3 * CHUNK + 1, :]
    carry_grad = jnp.sum(d_next * entering.astype(jnp.float32), axis=0, keepdims=True) * carry_wide
    for pair in range(6):
        cols = slice(pair * 128, pair * 128 + 128)
        slope_x, act = slope(zi_ref[:, cols])
        d_scan = dscan_ref[:, cols]
        skip = skip_ref[0:1, cols]
        stepped = (wide[:CHUNK, cols] * act).astype(low)
        stepped_wide = stepped.astype(jnp.float32)
        d_low = d_scan.astype(low)
        d_exact = d_low.astype(jnp.float32)
        d_both = jnp.concatenate(
            [jnp.where(lane < 64, d_exact, 0.0).astype(low), jnp.where(lane < 64, 0.0, d_exact).astype(low)],
            axis=0,
        )
        first, second = pair_decay(cumulative, across, pair)
        mixing = jnp.concatenate([(scores * first).astype(low), (scores * second).astype(low)], axis=0)
        d_mixing = dot(d_both, stepped, ((1,), (1,)))
        d_scores = d_scores + d_mixing[:CHUNK] * first + d_mixing[CHUNK:] * second
        tail_cols = wide[2 * CHUNK : 3 * CHUNK, cols]
        tailed = tail_cols * pulled[:, cols]
        d_stepped = dot(mixing, d_both, ((0,), (0,))) + tailed
        extra.append(jnp.sum(stepped_wide * tailed, axis=0, keepdims=True) + carry_grad[:, cols])
        fed.append((tail_cols * stepped_wide).astype(low))
        d_entered.append((wide[CHUNK : 2 * CHUNK, cols] * d_exact).astype(low))
        balance.append(d_exact * (scanned_ref[:, cols] - skip * act) - stepped_wide * d_stepped)
        direct.append(act * d_stepped)
        g_skip_ref[:, cols] += fold(d_scan * act)
        d_act = skip * d_scan + wide[:CHUNK, cols] * d_stepped
        conv_back(d_act * slope_x, inner_ref, halo_i, taps_ref, d_inner_ref, g_taps_ref, pair * 128)
    d_entered = jnp.concatenate(d_entered, axis=1)
    fed = jnp.concatenate(fed, axis=1)
    d_scores = jnp.where(linked, d_scores, 0.0).astype(low)
    d_output = dot(d_scores, input_low) + dot(d_entered, entering, ((1,), (1,)))
    d_input = dot(d_scores, output_low, ((0,), (0,))) + dot(fed, d_next_low, ((1,), (1,)))
    hold[...] = carry_wide * d_next + dot(output_low, d_entered, ((0,), (0,)))
    conv_back(d_input * slope_b, state_ref, halo_s, taps_s_ref, d_state_ref, g_taps_s_ref, 0)
    conv_back(d_output * slope_c, state_ref, halo_s, taps_s_ref, d_state_ref, g_taps_s_ref, 128)
    halo_p[...] = pos[:8]
    spread_back = wide_ref[...]
    extra = jnp.broadcast_to(jnp.concatenate(extra, axis=1), (16, 768))
    stacked = jnp.concatenate(
        split_terms(jnp.concatenate(balance, axis=1), 2)
        + split_terms(jnp.concatenate(direct, axis=1), 2)
        + split_terms(extra, 2),
        axis=0,
    )
    summed = dot(stacked, spread_back, ((1,), (1,)))
    d_sum = summed[:CHUNK] + summed[CHUNK : 2 * CHUNK]
    d_direct = summed[2 * CHUNK : 3 * CHUNK] + summed[3 * CHUNK : 4 * CHUNK]
    d_last = summed[4 * CHUNK : 4 * CHUNK + 1] + summed[4 * CHUNK + 16 : 4 * CHUNK + 17]
    upper = (row <= col).astype(low)
    d_decay = sum(dot(upper, piece) for piece in split_terms(d_sum, 3)) + d_last
    d_step = (d_direct - d_decay * jnp.exp(head_ref[1:2, :])) * sigmoid(shifted)
    d_step = jnp.where(lane < PACK, d_step, 0.0)
    d_step_ref[...] = d_step.astype(low)
    g_head_ref[0] += fold(d_step)
    g_head_ref[1] += fold(d_decay * log_decay)


def forward_core(first_pre, second_pre, d_normed_out, pos, taps, taps_s, heads_lanes, skip, gain, wide):
    rows = first_pre.shape[0]
    at = lambda width, col: pl.BlockSpec((CHUNK, width), lambda c: (c, col))
    whole = lambda arr: pl.BlockSpec(arr.shape, lambda c: (0,) * arr.ndim)
    f32 = jnp.float32
    return pl.pallas_call(
        forward_kernel,
        grid=(rows // CHUNK,),
        in_specs=[
            at(768, 0), at(128, 6), at(768, 0), at(256, 3), at(768, 0), at(128, 0),
            whole(taps), whole(taps_s), whole(heads_lanes), whole(skip), whole(gain), whole(wide),
        ],
        out_specs=[at(768, 0), at(768, 0), at(256, 0), at(768, 0), at(128, 0)],
        out_shape=[
            jax.ShapeDtypeStruct((rows, 768), f32),
            jax.ShapeDtypeStruct((rows, 768), f32),
            jax.ShapeDtypeStruct((rows, 256), f32),
            jax.ShapeDtypeStruct((rows, 768), jnp.bfloat16),
            jax.ShapeDtypeStruct((rows, 128), f32),
        ],
        scratch_shapes=[
            pltpu.VMEM((8, 768), f32), pltpu.VMEM((8, 256), f32), pltpu.VMEM((128, 768), f32),
        ],
        compiler_params=pltpu.CompilerParams(vmem_limit_bytes=40 * 2**20),
        cost_estimate=pl.CostEstimate(flops=8 * 10**9, bytes_accessed=24 * 10**6, transcendentals=4 * 10**6),
        name="mixer_forward",
    )(second_pre, second_pre, first_pre, first_pre, d_normed_out, pos, taps, taps_s, heads_lanes, skip, gain, wide)


def backward_core(first_pre, second_pre, zi, zs, scanned, d_scan, enter, pos, taps, taps_s, heads_lanes, skip, wide):
    rows = first_pre.shape[0]
    count = rows // CHUNK
    at = lambda width, col: pl.BlockSpec((CHUNK, width), lambda c: (count - 1 - c, col))
    whole = lambda shape: pl.BlockSpec(shape, lambda c: (0,) * len(shape))
    f32, low = jnp.float32, jnp.bfloat16
    return pl.pallas_call(
        backward_kernel,
        grid=(count,),
        in_specs=[
            at(768, 0), at(128, 6), at(256, 3), at(768, 0), at(256, 0), at(768, 0), at(768, 0),
            at(768, 0), at(128, 0),
            whole(taps.shape), whole(taps_s.shape), whole(heads_lanes.shape), whole(skip.shape), whole(wide.shape),
        ],
        out_specs=[
            at(768, 0), at(256, 0), at(128, 0),
            whole((5, 8, 768)), whole((5, 8, 256)), whole((8, 768)), whole((2, 8, 128)),
        ],
        out_shape=[
            jax.ShapeDtypeStruct((rows, 768), low),
            jax.ShapeDtypeStruct((rows, 256), low),
            jax.ShapeDtypeStruct((rows, 128), low),
            jax.ShapeDtypeStruct((5, 8, 768), f32),
            jax.ShapeDtypeStruct((5, 8, 256), f32),
            jax.ShapeDtypeStruct((8, 768), f32),
            jax.ShapeDtypeStruct((2, 8, 128), f32),
        ],
        scratch_shapes=[
            pltpu.VMEM((8, 768), f32), pltpu.VMEM((8, 256), f32), pltpu.VMEM((8, 128), f32),
            pltpu.VMEM((128, 768), f32),
        ],
        compiler_params=pltpu.CompilerParams(vmem_limit_bytes=40 * 2**20),
        cost_estimate=pl.CostEstimate(flops=16 * 10**9, bytes_accessed=24 * 10**6, transcendentals=6 * 10**6),
        name="mixer_backward",
    )(second_pre, second_pre, first_pre, zi, zs, scanned, d_scan, enter, pos, taps, taps_s, heads_lanes, skip, wide)


def exchange(value, bit):
    count = lax.axis_size("dp")
    return lax.ppermute(value, "dp", [(i, i ^ bit) for i in range(count)])


def swap(value):
    return lax.ppermute(value, "tensor", [(0, 1), (1, 0)])


def bit_of(bit):
    return (lax.axis_index("dp") // bit) % 2


def join(kept, received, mine, axis):
    first = jnp.where(mine == 0, kept, received)
    second = jnp.where(mine == 0, received, kept)
    return jnp.concatenate([first, second], axis=axis)


AXIS_OF = {8: 0, 4: 1, 2: 2, 1: 3}


def spread_rows(held, order):
    for bit in order:
        held = join(held, exchange(held, bit), bit_of(bit), AXIS_OF[bit])
    return held


def gather_rows(block, order):
    rows, cols = block.shape
    held = spread_rows(block.reshape(1, 1, 1, 1, rows, cols), order)
    return held.reshape(16 * rows, cols)


def scatter_rows(part, order):
    rows, cols = part.shape
    held = part.reshape(2, 2, 2, 2, rows // 16, cols)
    for bit in order:
        axis = AXIS_OF[bit]
        mine = bit_of(bit)
        send = lax.dynamic_index_in_dim(held, 1 - mine, axis, keepdims=True)
        keep = lax.dynamic_index_in_dim(held, mine, axis, keepdims=True)
        total = keep.astype(jnp.float32) + exchange(send.astype(jnp.bfloat16), bit).astype(
            jnp.float32
        )
        held = total.astype(jnp.bfloat16) if bit != order[-1] else total
    return held.reshape(rows // 16, cols)


def pair_gather(block):
    return join(block, swap(block), lax.axis_index("tensor"), 0)


def pair_scatter(part, axis):
    mine = lax.axis_index("tensor")
    width = part.shape[axis] // 2
    keep = lax.dynamic_slice_in_dim(part, mine * width, width, axis)
    send = lax.dynamic_slice_in_dim(part, (1 - mine) * width, width, axis)
    return keep.astype(jnp.float32) + swap(send.astype(jnp.bfloat16)).astype(jnp.float32)


def pad_cols(value, width):
    return jnp.pad(value, ((0, 0), (0, width - value.shape[1])))


def to_owner(tasks):
    _, rows, cols = tasks.shape
    across, along = bit_of(1), bit_of(2)
    held = tasks.reshape(2, 2, rows, cols)
    send = lax.dynamic_index_in_dim(held, 1 - across, 1)
    keep = lax.dynamic_index_in_dim(held, across, 1)
    held = join(keep, exchange(send, 1), across, 1)
    send = lax.dynamic_index_in_dim(held, 1 - along, 0)
    keep = lax.dynamic_index_in_dim(held, along, 0)
    held = join(keep, exchange(send, 2), along, 0)
    held = spread_rows(held.reshape(1, 1, 2, 2, rows, cols), (8, 4))
    return held.reshape(16 * rows, cols)


def from_owner(matrix):
    rows, cols = matrix.shape[0] // 16, matrix.shape[1]
    across, along = bit_of(1), bit_of(2)
    plane = lax.dynamic_index_in_dim(
        matrix.reshape(4, 2, 2, rows, cols), lax.axis_index("dp") // 4, 0, keepdims=False
    )
    send = lax.dynamic_index_in_dim(plane, 1 - along, 0)
    keep = lax.dynamic_index_in_dim(plane, along, 0)
    held = join(keep, exchange(send, 2), along, 0)
    send = lax.dynamic_index_in_dim(held, 1 - across, 1)
    keep = lax.dynamic_index_in_dim(held, across, 1)
    return join(keep, exchange(send, 1), across, 1).reshape(4, rows, cols)


def orthogonal_half(own, state_width):
    width = own.shape[1]
    small = lax.axis_index("dp") % 4 == 3
    full = jnp.concatenate([own, swap(own)], axis=1)
    col = jnp.arange(2 * width)[None, :] % width
    keep = (col < state_width) == (lax.axis_index("tensor") == 0)
    full = jnp.where(small & ~keep, jnp.zeros_like(full), full)
    first = times_transpose(full, full)
    scale = jnp.sqrt(jnp.sum(jnp.square(full.astype(jnp.float32)))) + 1e-07
    current = (full.astype(jnp.float32) / scale).astype(jnp.bfloat16)
    gram = (first / (scale * scale)).astype(jnp.bfloat16)
    for turn in range(NS_STEPS):
        if turn > 0:
            gram = times_transpose(current, current).astype(jnp.bfloat16)
        square = jnp.dot(gram, gram, preferred_element_type=jnp.float32)
        mix = (NS_B * gram.astype(jnp.float32) + NS_C * square).astype(jnp.bfloat16)
        if turn == NS_STEPS - 1:
            current = current[:, : width + 2 * state_width]
        current = (
            NS_A * current.astype(jnp.float32)
            + jnp.dot(mix, current, preferred_element_type=jnp.float32)
        ).astype(jnp.bfloat16)
    half, lent = current[:, :width], current[:, width:]
    edge = half[:, : 2 * state_width]
    edge = edge + jnp.where(small, swap(lent), jnp.zeros_like(lent))
    return jnp.concatenate([edge, half[:, 2 * state_width :]], axis=1)


def paired_shards(
    stream,
    cotangent,
    positions,
    norm_gain,
    w_gate,
    w_inner,
    w_state,
    w_step,
    conv_inner,
    conv_state,
    head_params,
    gate_gain,
    w_out,
    moment_norm_gain,
    moment_w_gate,
    moment_w_inner,
    moment_w_state,
    moment_w_step,
    moment_conv_inner,
    moment_conv_state,
    moment_head_params,
    moment_gate_gain,
    moment_w_out,
):
    low = jnp.bfloat16
    core = lax.axis_index("tensor")
    room = w_gate.shape[1]
    wide = w_state.shape[1]
    col_width = wide // 2
    heads = w_step.shape[1]
    inv_first = lax.rsqrt(jnp.mean(stream * stream, axis=1, keepdims=True) + EPS)
    normed = (stream * inv_first * norm_gain).astype(low)
    first_pack = jnp.concatenate([w_gate.astype(low), w_state.astype(low)], axis=1)
    step_low = w_step.astype(low)
    step_lanes = jnp.concatenate([pad_cols(step_low, PACK), pad_cols(step_low, 128 - PACK)], axis=1)
    second_pack = jnp.concatenate([w_inner.astype(low), step_lanes], axis=1)
    full_first = gather_rows(first_pack, (8, 4, 2, 1))
    full_second = gather_rows(second_pack, (8, 4, 1, 2))
    token_rows = pair_gather(normed)
    cotangent_rows = pair_gather(cotangent.astype(low))
    full_out = gather_rows(w_out.astype(low).T, (8, 4, 1, 2))
    first_pre = jnp.dot(token_rows, full_first, preferred_element_type=jnp.float32)
    second_pre = jnp.dot(token_rows, full_second, preferred_element_type=jnp.float32)
    gate_pre = first_pre[:, :room]
    alive = (positions >= 0).astype(jnp.float32)[:, None]
    pos = jnp.broadcast_to(positions.astype(jnp.float32)[:, None], (positions.shape[0], 128))
    taps = jnp.pad(conv_inner, ((0, 3), (0, 0)))
    taps_s = jnp.pad(conv_state, ((0, 3), (0, 0)))
    lanes = jnp.concatenate([pad_cols(head_params, PACK), pad_cols(head_params, 128 - PACK)], axis=1)
    lanes = jnp.pad(lanes, ((0, 5), (0, 0)))
    skip = jnp.repeat(head_params[2], room // heads)[None, :]
    wide_map = expand_matrix()
    d_normed_out = jnp.dot(cotangent_rows, full_out, preferred_element_type=jnp.float32)
    scanned, zi, zs, enter, sums = forward_core(
        first_pre, second_pre, d_normed_out, pos, taps, taps_s, lanes, skip, gate_gain[None, :], wide_map
    )
    sums = sums + swap(sums)
    square_sum, cross_sum = sums[:, 0], sums[:, 1]
    gate_act = jax.nn.silu(gate_pre)
    gated = scanned * gate_act
    scaled = d_normed_out * gate_gain * alive
    inv_second = lax.rsqrt(square_sum / INNER + EPS)[:, None]
    normed_out = (gated * inv_second * gate_gain * alive).astype(low)
    mixed = pair_scatter(times_transpose(normed_out, full_out).astype(low), 0)
    output = stream + mixed
    grad_out_t = scatter_rows(contract_rows(cotangent_rows, normed_out).astype(low), (1, 2, 4, 8))
    grad_gate_part = jnp.sum(d_normed_out * gated * inv_second * alive, axis=0)
    d_gated = inv_second * scaled - gated * inv_second**3 * (cross_sum / INNER)[:, None]
    d_gate_pre = (d_gated * scanned * silu_slope(gate_pre)).astype(low)
    grad_gate_w = scatter_rows(contract_rows(token_rows, d_gate_pre).astype(low), (2, 1, 4, 8))
    d_inner, d_state_part, d_step, taps_part, taps_s_part, skip_part, head_part = backward_core(
        first_pre, second_pre, zi, zs, scanned, d_gated * gate_act, enter, pos, taps, taps_s, lanes, skip, wide_map
    )
    grad_conv_inner_part = jnp.sum(taps_part, axis=1)
    grad_conv_state_part = jnp.sum(taps_s_part, axis=1)
    head_rows = jnp.sum(head_part, axis=1)[:, :heads]
    skip_row = jnp.sum(jnp.sum(skip_part, axis=0).reshape(heads, -1), axis=1)
    grad_head_part = jnp.concatenate([head_rows, skip_row[None, :]], axis=0)
    d_state_low = pair_scatter(d_state_part, 1).astype(low)
    d_tail = jnp.concatenate([d_inner, d_state_low, d_step], axis=1)
    col_first = core * col_width
    state_cols = lax.dynamic_slice_in_dim(full_first, room + col_first, col_width, 1)
    tail_weights = jnp.concatenate(
        [full_second[:, :room], state_cols, full_second[:, room:]], axis=1
    )
    total = times_transpose(d_gate_pre, full_first[:, :room])
    total = total + times_transpose(d_tail, tail_weights)
    d_normed = pair_scatter(total.astype(low), 0)
    tail_part = contract_rows(token_rows, d_tail).astype(low)
    cut = tail_part.shape[1] // 2
    tail_grad = jnp.concatenate(
        [
            scatter_rows(tail_part[:, :cut], (1, 2, 4, 8)),
            scatter_rows(tail_part[:, cut:], (2, 1, 4, 8)),
        ],
        axis=1,
    )
    grad_inner_w = tail_grad[:, :room]
    grad_state_w = tail_grad[:, room : room + col_width]
    grad_step_w = tail_grad[:, room + col_width : room + col_width + heads]
    grad_out_w = grad_out_t.T
    grad_norm_part = jnp.sum(d_normed * stream * inv_first, axis=0)
    weighted = d_normed * norm_gain
    d_stream = (
        cotangent
        + inv_first * weighted
        - stream * inv_first**3 * jnp.mean(weighted * stream, axis=1, keepdims=True)
    )
    shared = jnp.concatenate([grad_conv_state_part, grad_norm_part.reshape(-1, wide)], axis=0)
    shared = shared + swap(shared)
    vectors = jnp.concatenate(
        [
            grad_conv_inner_part,
            grad_gate_part[None, :],
            pad_cols(grad_head_part, room),
            pad_cols(shared, room),
        ],
        axis=0,
    )
    for bit in (1, 2, 4, 8):
        vectors = vectors + exchange(vectors, bit)
    grad_conv_inner = vectors[:5]
    grad_gate_gain = vectors[5]
    grad_head = vectors[6:9, :heads]
    grad_conv_state = vectors[9:14, :wide]
    grad_norm = vectors[14:, :wide].reshape(-1)
    m_gate = MU_MAT * moment_w_gate + grad_gate_w
    m_inner = MU_MAT * moment_w_inner + grad_inner_w
    m_state = MU_MAT * moment_w_state + grad_state_w
    m_step = MU_MAT * moment_w_step + grad_step_w
    m_out = MU_MAT * moment_w_out + grad_out_w
    small = pad_cols(jnp.concatenate([m_state, m_step], axis=1), room)
    tasks = jnp.stack([m_gate, m_inner, m_out.T, small]).astype(low)
    mine = from_owner(orthogonal_half(to_owner(tasks), col_width)).astype(jnp.float32)
    new_gate = w_gate - LR_MAT * spread(D, INNER) * mine[0]
    new_inner = w_inner - LR_MAT * spread(D, INNER) * mine[1]
    new_out = w_out - LR_MAT * spread(INNER, D) * mine[2].T
    new_step = w_step - LR_MAT * spread(D, HEADS) * mine[3][:, col_width : col_width + heads]
    state_slice = lax.dynamic_slice_in_dim(w_state, col_first, col_width, 1)
    new_state = state_slice - LR_MAT * spread(D, 2 * STATE) * mine[3][:, :col_width]
    m_norm = MU_VEC * moment_norm_gain + grad_norm
    m_conv_inner = MU_VEC * moment_conv_inner + grad_conv_inner
    m_conv_state = MU_VEC * moment_conv_state + grad_conv_state
    m_head = MU_VEC * moment_head_params + grad_head
    m_gate_gain = MU_VEC * moment_gate_gain + grad_gate_gain
    return (
        output,
        d_stream,
        grad_norm,
        grad_gate_w,
        grad_inner_w,
        grad_state_w,
        grad_step_w,
        grad_conv_inner,
        grad_conv_state,
        grad_head,
        grad_gate_gain,
        grad_out_w,
        norm_gain - LR_VEC * m_norm,
        new_gate,
        new_inner,
        new_state,
        new_step,
        conv_inner - LR_VEC * m_conv_inner,
        conv_state - LR_VEC * m_conv_state,
        head_params - LR_VEC * m_head,
        gate_gain - LR_VEC * m_gate_gain,
        new_out,
        m_norm,
        m_gate,
        m_inner,
        m_state,
        m_step,
        m_conv_inner,
        m_conv_state,
        m_head,
        m_gate_gain,
        m_out,
    )


def solution(mesh):
    paired = mesh.shape["dp"] == 16 and mesh.shape["tensor"] == 2
    return jax.shard_map(
        paired_shards if paired else shards,
        mesh=mesh,
        in_specs=(
            P(("dp", "tensor"), None),
            P(("dp", "tensor"), None),
            P("dp"),
            P(),
            P("dp", "tensor"),
            P("dp", "tensor"),
            P("dp", None),
            P("dp", "tensor"),
            P(None, "tensor"),
            P(),
            P(None, "tensor"),
            P("tensor"),
            P("tensor", "dp"),
            P(),
            P("dp", "tensor"),
            P("dp", "tensor"),
            P("dp", "tensor"),
            P("dp", "tensor"),
            P(None, "tensor"),
            P(),
            P(None, "tensor"),
            P("tensor"),
            P("tensor", "dp"),
        ),
        out_specs=(
            P(("dp", "tensor"), None),
            P(("dp", "tensor"), None),
            P(),
            P("dp", "tensor"),
            P("dp", "tensor"),
            P("dp", "tensor"),
            P("dp", "tensor"),
            P(None, "tensor"),
            P(),
            P(None, "tensor"),
            P("tensor"),
            P("tensor", "dp"),
            P(),
            P("dp", "tensor"),
            P("dp", "tensor"),
            P("dp", "tensor"),
            P("dp", "tensor"),
            P(None, "tensor"),
            P(),
            P(None, "tensor"),
            P("tensor"),
            P("tensor", "dp"),
            P(),
            P("dp", "tensor"),
            P("dp", "tensor"),
            P("dp", "tensor"),
            P("dp", "tensor"),
            P(None, "tensor"),
            P(),
            P(None, "tensor"),
            P("tensor"),
            P("tensor", "dp"),
        ),
        check_vma=False,
    )
```

```python
from functools import partial
import math

import jax
import jax.numpy as jnp
from jax import lax
from jax.experimental import pallas as pl
from jax.experimental.pallas import tpu as pltpu
from jax.sharding import PartitionSpec as P

D = 768
INNER = 1536
HEADS = 24
STATE = 128
BLOCK = 256
NS_STEPS = 5


EPS = 1e-05
NS_A = 3.4445
NS_B = -4.775
NS_C = 2.0315
MU_MAT = 0.95
MU_VEC = 0.9
LR_MAT = 0.3
LR_VEC = 0.001
HIGH = lax.Precision.HIGHEST
CORE = lax.Precision.DEFAULT


def silu_slope(value):
    sig = jax.nn.sigmoid(value)
    return sig * (1.0 + value * (1.0 - sig))


def contract_rows(left, right):
    return lax.dot_general(
        left, right, (((0,), (0,)), ((), ())), preferred_element_type=jnp.float32
    )


def times_transpose(left, right):
    return lax.dot_general(
        left, right, (((1,), (1,)), ((), ())), preferred_element_type=jnp.float32
    )


def causal_conv(signal, taps, positions):
    length = signal.shape[0]
    reach = taps.shape[0] - 1
    total = jnp.zeros_like(signal) + taps[reach]
    for lag_step in range(reach):
        moved = jnp.pad(signal, ((lag_step, 0), (0, 0)))[:length]
        total = total + jnp.where((positions >= lag_step)[:, None], moved * taps[lag_step], 0.0)
    return jax.nn.silu(total)


def mixer_core(inner_pre, state_pre, step_pre, conv_inner, conv_state, head_params, positions, precision=HIGH):
    length = inner_pre.shape[0]
    heads = step_pre.shape[1]
    head_size = inner_pre.shape[1] // heads
    states = state_pre.shape[1] // 2
    blocks = length // BLOCK
    inner_act = causal_conv(inner_pre, conv_inner, positions).reshape(
        blocks, BLOCK, heads, head_size
    )
    state_act = causal_conv(state_pre, conv_state, positions)
    input_map = state_act[:, :states].reshape(blocks, BLOCK, states)
    output_map = state_act[:, states:].reshape(blocks, BLOCK, states)
    step_size = jax.nn.softplus(step_pre + head_params[0])
    log_decay = (step_size * -jnp.exp(head_params[1])).reshape(blocks, BLOCK, heads)
    step_size = step_size.reshape(blocks, BLOCK, heads)
    resets = (positions <= 0).astype(jnp.float32).reshape(blocks, BLOCK)
    order = jnp.arange(BLOCK)
    lower = (order[:, None] >= order[None, :]).astype(jnp.float32)
    cumulative = jnp.einsum("ij,cjh->cih", lower, log_decay, precision=HIGH)
    seen = jnp.einsum("ij,cj->ci", lower, resets, precision=HIGH)
    linked = (seen[:, :, None] == seen[:, None, :]) & (order[:, None] >= order[None, :])[None]
    linked_heads = linked[..., None]
    spacing = cumulative[:, :, None, :] - cumulative[:, None, :, :]
    decay = jnp.where(linked_heads, jnp.exp(jnp.where(linked_heads, spacing, 0.0)), 0.0)
    scores = jnp.einsum("cin,cjn->cij", output_map, input_map, precision=precision)
    mixing = scores[..., None] * decay * step_size[:, None, :, :]
    within = jnp.einsum("cijh,cjhp->cihp", mixing, inner_act, precision=precision)
    tail_linked = (seen[:, -1:] == seen)[..., None]
    tail = (
        jnp.where(
            tail_linked,
            jnp.exp(jnp.where(tail_linked, cumulative[:, -1:, :] - cumulative, 0.0)),
            0.0,
        )
        * step_size
    )
    own_state = jnp.einsum("cjh,cjhp,cjn->chpn", tail, inner_act, input_map, precision=precision)
    carry_rate = jnp.exp(cumulative[:, -1, :]) * (seen[:, -1] == 0).astype(jnp.float32)[:, None]

    state = jnp.zeros((heads, head_size, states), jnp.float32)
    entering = []
    for block in range(blocks):
        entering.append(state)
        state = carry_rate[block][:, None, None] * state + own_state[block]
    entering = jnp.stack(entering)
    fresh = (seen == 0)[..., None]
    carry_in = jnp.where(fresh, jnp.exp(cumulative), 0.0)
    across = (
        jnp.einsum("cin,chpn->cihp", output_map, entering, precision=precision) * carry_in[..., None]
    )
    result = within + across + head_params[2][None, None, :, None] * inner_act
    return result.reshape(length, heads * head_size)


def gram_total(low):
    return lax.psum(
        jnp.dot(low, low.T, preferred_element_type=jnp.float32).astype(jnp.bfloat16), "tensor"
    ).astype(jnp.float32)


def orthogonalize(matrix):
    first = gram_total(matrix.astype(jnp.bfloat16))
    scale = jnp.sqrt(jnp.trace(first)) + 1e-07
    current = (matrix / scale).astype(jnp.bfloat16)
    gram = (first / (scale * scale)).astype(jnp.bfloat16)
    for turn in range(NS_STEPS):
        if turn > 0:
            gram = gram_total(current).astype(jnp.bfloat16)
        applied = jnp.dot(gram, current, preferred_element_type=jnp.float32)
        twice = jnp.dot(gram, applied.astype(jnp.bfloat16), preferred_element_type=jnp.float32)
        current = (NS_A * current.astype(jnp.float32) + NS_B * applied + NS_C * twice).astype(
            jnp.bfloat16
        )
    return current.astype(jnp.float32)


def spread(rows, cols):
    return math.sqrt(max(1.0, rows / cols))


def shards(
    stream,
    cotangent,
    positions,
    norm_gain,
    w_gate,
    w_inner,
    w_state,
    w_step,
    conv_inner,
    conv_state,
    head_params,
    gate_gain,
    w_out,
    moment_norm_gain,
    moment_w_gate,
    moment_w_inner,
    moment_w_state,
    moment_w_step,
    moment_conv_inner,
    moment_conv_state,
    moment_head_params,
    moment_gate_gain,
    moment_w_out,
):
    dp_count = lax.axis_size("dp")
    inv_first = lax.rsqrt(jnp.mean(stream * stream, axis=1, keepdims=True) + EPS)
    normed = (stream * inv_first * norm_gain).astype(jnp.bfloat16)
    token_rows, cotangent_rows = (
        lax.all_gather(normed, "tensor", axis=0, tiled=True),
        lax.all_gather(cotangent.astype(jnp.bfloat16), "tensor", axis=0, tiled=True),
    )
    local_weights = (
        w_gate.astype(jnp.bfloat16),
        w_inner.astype(jnp.bfloat16),
        w_step.astype(jnp.bfloat16),
        w_state.astype(jnp.bfloat16),
        w_out.astype(jnp.bfloat16),
    )
    full_gate, full_inner, full_step, full_state, full_out = (
        lax.all_gather(local_weights[0], "dp", axis=0, tiled=True),
        lax.all_gather(local_weights[1], "dp", axis=0, tiled=True),
        lax.all_gather(local_weights[2], "dp", axis=0, tiled=True),
        lax.all_gather(local_weights[3], "dp", axis=0, tiled=True),
        lax.all_gather(local_weights[4], "dp", axis=1, tiled=True),
    )
    gate_pre = jnp.dot(token_rows, full_gate, preferred_element_type=jnp.float32)
    inner_pre = jnp.dot(token_rows, full_inner, preferred_element_type=jnp.float32)
    state_pre = jnp.dot(token_rows, full_state, preferred_element_type=jnp.float32)
    step_pre = jnp.dot(token_rows, full_step, preferred_element_type=jnp.float32)
    alive = (positions >= 0).astype(jnp.float32)[:, None]
    scanned, core_back = jax.vjp(
        partial(mixer_core, positions=positions),
        inner_pre,
        state_pre,
        step_pre,
        conv_inner,
        conv_state,
        head_params,
    )
    gate_act = jax.nn.silu(gate_pre)
    gated = scanned * gate_act
    square_sum = lax.psum(jnp.sum(gated * gated, axis=1), "tensor")
    inv_second = lax.rsqrt(square_sum / INNER + EPS)[:, None]
    normed_out = (gated * inv_second * gate_gain * alive).astype(jnp.bfloat16)
    mixed = lax.psum_scatter(
        jnp.dot(normed_out, full_out, preferred_element_type=jnp.float32).astype(jnp.bfloat16),
        "tensor",
        scatter_dimension=0,
        tiled=True,
    ).astype(jnp.float32)
    output = stream + mixed
    d_normed_out = times_transpose(cotangent_rows, full_out)
    grad_out_part = contract_rows(normed_out, cotangent_rows)
    scaled = d_normed_out * gate_gain * alive
    grad_gate_part = jnp.sum(d_normed_out * gated * inv_second * alive, axis=0)
    cross_sum = lax.psum(jnp.sum(scaled * gated, axis=1), "tensor")
    d_gated = inv_second * scaled - gated * inv_second**3 * (cross_sum / INNER)[:, None]
    d_gate_pre = (d_gated * scanned * silu_slope(gate_pre)).astype(jnp.bfloat16)
    d_inner, d_state_part, d_step, grad_conv_inner_part, grad_conv_state_part, grad_head_part = (
        core_back(d_gated * gate_act)
    )
    d_state_cols = lax.psum_scatter(
        d_state_part.astype(jnp.bfloat16), "tensor", scatter_dimension=1, tiled=True
    ).astype(jnp.float32)
    d_inner_low = d_inner.astype(jnp.bfloat16)
    d_state_low = d_state_cols.astype(jnp.bfloat16)
    d_step_low = d_step.astype(jnp.bfloat16)
    col_width = d_state_cols.shape[1]
    col_first = lax.axis_index("tensor") * col_width
    state_cols = lax.dynamic_slice_in_dim(full_state, col_first, col_width, 1)
    total = times_transpose(d_gate_pre, full_gate)
    total = total + times_transpose(d_inner_low, full_inner)
    total = total + times_transpose(d_state_low, state_cols)
    d_normed = lax.psum_scatter(
        (total + times_transpose(d_step_low, full_step)).astype(jnp.bfloat16),
        "tensor",
        scatter_dimension=0,
        tiled=True,
    ).astype(jnp.float32)
    grad_gate_w, grad_inner_w, grad_state_w, grad_step_w, grad_out_w = (
        lax.psum_scatter(
            contract_rows(token_rows, d_gate_pre).astype(jnp.bfloat16),
            "dp",
            scatter_dimension=0,
            tiled=True,
        ).astype(jnp.float32),
        lax.psum_scatter(
            contract_rows(token_rows, d_inner_low).astype(jnp.bfloat16),
            "dp",
            scatter_dimension=0,
            tiled=True,
        ).astype(jnp.float32),
        lax.psum_scatter(
            contract_rows(token_rows, d_state_low).astype(jnp.bfloat16),
            "dp",
            scatter_dimension=0,
            tiled=True,
        ).astype(jnp.float32),
        lax.psum_scatter(
            contract_rows(token_rows, d_step_low).astype(jnp.bfloat16),
            "dp",
            scatter_dimension=0,
            tiled=True,
        ).astype(jnp.float32),
        lax.psum_scatter(
            grad_out_part.astype(jnp.bfloat16), "dp", scatter_dimension=1, tiled=True
        ).astype(jnp.float32),
    )
    grad_norm_part = jnp.sum(d_normed * stream * inv_first, axis=0)
    weighted = d_normed * norm_gain
    d_stream = (
        cotangent
        + inv_first * weighted
        - stream * inv_first**3 * jnp.mean(weighted * stream, axis=1, keepdims=True)
    )
    grad_conv_inner, grad_gate_gain, grad_head = lax.psum(
        (grad_conv_inner_part, grad_gate_part, grad_head_part), "dp"
    )
    grad_conv_state, grad_norm = lax.psum((grad_conv_state_part, grad_norm_part), ("dp", "tensor"))
    m_gate = MU_MAT * moment_w_gate + grad_gate_w
    m_inner = MU_MAT * moment_w_inner + grad_inner_w
    m_state = MU_MAT * moment_w_state + grad_state_w
    m_step = MU_MAT * moment_w_step + grad_step_w
    m_out = MU_MAT * moment_w_out + grad_out_w
    room = w_gate.shape[1]
    shard_rows = w_gate.shape[0]
    stacked = jnp.stack(
        [
            m_gate,
            m_inner,
            m_out.T,
            jnp.pad(m_step, ((0, 0), (0, room - m_step.shape[1]))),
            jnp.pad(m_state, ((0, 0), (0, room - m_state.shape[1]))),
        ]
    )
    matrix_count = stacked.shape[0]
    owner_index = jnp.arange(matrix_count, dtype=jnp.int32) * dp_count // matrix_count
    select = (owner_index[None, :] == jnp.arange(dp_count, dtype=jnp.int32)[:, None]).astype(
        jnp.float32
    )
    outgoing = jnp.einsum("jk,krc->jrc", select, stacked, precision=HIGH)
    owned = (
        lax.all_to_all(outgoing.astype(jnp.bfloat16), "dp", split_axis=0, concat_axis=0, tiled=True)
        .astype(outgoing.dtype)
        .reshape(dp_count * shard_rows, room)
    )
    ortho = orthogonalize(owned)
    returned = lax.all_to_all(
        ortho.reshape(dp_count, shard_rows, room).astype(jnp.bfloat16),
        "dp",
        split_axis=0,
        concat_axis=0,
        tiled=True,
    ).astype(jnp.float32)
    mine = jnp.einsum("jk,jrc->krc", select, returned, precision=HIGH)
    new_gate = w_gate - LR_MAT * spread(D, INNER) * mine[0]
    new_inner = w_inner - LR_MAT * spread(D, INNER) * mine[1]
    new_out = w_out - LR_MAT * spread(INNER, D) * mine[2].T
    new_step = w_step - LR_MAT * spread(D, HEADS) * mine[3][:, : w_step.shape[1]]
    state_slice = lax.dynamic_slice_in_dim(w_state, col_first, col_width, 1)
    new_state = state_slice - LR_MAT * spread(D, 2 * STATE) * mine[4][:, :col_width]
    m_norm = MU_VEC * moment_norm_gain + grad_norm
    m_conv_inner = MU_VEC * moment_conv_inner + grad_conv_inner
    m_conv_state = MU_VEC * moment_conv_state + grad_conv_state
    m_head = MU_VEC * moment_head_params + grad_head
    m_gate_gain = MU_VEC * moment_gate_gain + grad_gate_gain
    return (
        output,
        d_stream,
        grad_norm,
        grad_gate_w,
        grad_inner_w,
        grad_state_w,
        grad_step_w,
        grad_conv_inner,
        grad_conv_state,
        grad_head,
        grad_gate_gain,
        grad_out_w,
        norm_gain - LR_VEC * m_norm,
        new_gate,
        new_inner,
        new_state,
        new_step,
        conv_inner - LR_VEC * m_conv_inner,
        conv_state - LR_VEC * m_conv_state,
        head_params - LR_VEC * m_head,
        gate_gain - LR_VEC * m_gate_gain,
        new_out,
        m_norm,
        m_gate,
        m_inner,
        m_state,
        m_step,
        m_conv_inner,
        m_conv_state,
        m_head,
        m_gate_gain,
        m_out,
    )


CHUNK = 128
PACK = 16


def sigmoid(value):
    return 0.5 * jnp.tanh(0.5 * value) + 0.5


def expand_matrix():
    row = jnp.arange(128)[:, None]
    col = jnp.arange(768)[None, :] // 64
    return ((row == col) | (row == col + PACK)).astype(jnp.bfloat16)


def two_term(value):
    lane = lax.broadcasted_iota(jnp.int32, value.shape, 1)
    high = value.astype(jnp.bfloat16).astype(jnp.float32)
    return jnp.where(lane < PACK, high, value - high).astype(jnp.bfloat16)


def split_terms(value, terms):
    out = []
    for _ in range(terms):
        piece = value.astype(jnp.bfloat16)
        out.append(piece)
        value = value - piece.astype(jnp.float32)
    return out


def dot(left, right, dims=((1,), (0,))):
    return lax.dot_general(left, right, (dims, ((), ())), preferred_element_type=jnp.float32)


def head_terms(step_ref, head_ref, pos):
    shifted = step_ref[...] + head_ref[0:1, :]
    small = jnp.exp(-jnp.abs(shifted))
    step = jnp.maximum(shifted, 0.0) + jnp.log1p(small)
    log_decay = -step * jnp.exp(head_ref[1:2, :])
    row = lax.broadcasted_iota(jnp.int32, (CHUNK, 128), 0)
    col = lax.broadcasted_iota(jnp.int32, (CHUNK, 128), 1)
    lower = (row >= col).astype(jnp.bfloat16)
    cumulative = sum(dot(lower, piece) for piece in split_terms(log_decay, 3))
    last = cumulative[CHUNK - 1 : CHUNK, :]
    back = (row - col).astype(jnp.float32)
    linked = (row >= col) & (back <= jnp.maximum(pos, 0.0))
    row = row.astype(jnp.float32)
    carry_in = jnp.where(pos > row, jnp.exp(cumulative), 0.0)
    pos_last = pos[CHUNK - 1 : CHUNK, :]
    tail_linked = (CHUNK - 1.0 - row) <= jnp.maximum(pos_last, 0.0)
    tail = jnp.where(tail_linked, jnp.exp(jnp.minimum(last - cumulative, 0.0)), 0.0)
    carry = jnp.where(pos_last > CHUNK - 1.0, jnp.exp(last), 0.0)
    return shifted, step, log_decay, cumulative, linked, carry_in, tail, carry


def pair_decay(cumulative, across, pair):
    parts = []
    for head in (2 * pair, 2 * pair + 1):
        spacing = cumulative[:, head : head + 1] - across[head : head + 1, :]
        parts.append(jnp.exp(jnp.minimum(spacing, 0.0)))
    return parts


def forward_kernel(
    inner_ref, step_ref, gate_ref, state_ref, dno_ref, pos_ref, taps_ref, taps_s_ref, head_ref,
    skip_ref, gain_ref, wide_ref,
    scanned_ref, zi_ref, zs_ref, enter_ref, sums_ref,
    halo_i, halo_s, hold,
):
    @pl.when(pl.program_id(0) == 0)
    def _():
        halo_i[...] = jnp.zeros_like(halo_i)
        halo_s[...] = jnp.zeros_like(halo_s)
        hold[...] = jnp.zeros_like(hold)

    low = jnp.bfloat16
    pos = pos_ref[...]
    marks = [(pos >= lag).astype(jnp.float32) for lag in range(4)]

    def conv(ref, halo, taps, out_ref, first):
        value = ref[:, first : first + 128]
        ext = jnp.concatenate([halo[:, first : first + 128], value], axis=0)
        total = taps[4:5, first : first + 128] + marks[0] * (value * taps[0:1, first : first + 128])
        for lag in range(1, 4):
            moved = pltpu.roll(ext, lag, 0)[8:]
            total = total + marks[lag] * (moved * taps[lag : lag + 1, first : first + 128])
        out_ref[:, first : first + 128] = total
        return total * sigmoid(total)

    shifted, step, log_decay, cumulative, linked, carry_in, tail, carry = head_terms(
        step_ref, head_ref, pos
    )
    across = cumulative.T
    wide = dot(
        jnp.concatenate(
            [
                two_term(step),
                two_term(carry_in),
                two_term(tail * step),
                two_term(jnp.broadcast_to(carry, (16, 128))),
            ],
            axis=0,
        ),
        wide_ref[...],
    )
    input_map = conv(state_ref, halo_s, taps_s_ref, zs_ref, 0).astype(low)
    output_map = conv(state_ref, halo_s, taps_s_ref, zs_ref, 128).astype(low)
    scores = jnp.where(linked, dot(output_map, input_map, ((1,), (1,))), 0.0)
    state = hold[...]
    state_low = state.astype(low)
    enter_ref[...] = state_low
    entered = dot(output_map, state_low)
    lane = lax.broadcasted_iota(jnp.int32, (CHUNK, 128), 1)
    squares = jnp.zeros((CHUNK, 128), jnp.float32)
    crosses = jnp.zeros((CHUNK, 128), jnp.float32)
    fed = []
    for pair in range(6):
        cols = slice(pair * 128, pair * 128 + 128)
        act = conv(inner_ref, halo_i, taps_ref, zi_ref, pair * 128)
        stepped = (wide[:CHUNK, cols] * act).astype(low)
        first, second = pair_decay(cumulative, across, pair)
        mixing = jnp.concatenate([(scores * first).astype(low), (scores * second).astype(low)], axis=0)
        both = dot(mixing, stepped)
        within = jnp.where(lane < 64, both[:CHUNK], both[CHUNK:])
        scanned = (
            within + entered[:, cols] * wide[CHUNK : 2 * CHUNK, cols] + skip_ref[0:1, cols] * act
        )
        scanned_ref[:, cols] = scanned
        fed.append((wide[2 * CHUNK : 3 * CHUNK, cols] * act).astype(low))
        gate = gate_ref[:, cols]
        gated = scanned * (gate * sigmoid(gate))
        squares = squares + gated * gated
        crosses = crosses + dno_ref[:, cols] * gain_ref[0:1, cols] * gated
    fresh = dot(input_map, jnp.concatenate(fed, axis=1), ((0,), (0,)))
    hold[...] = wide[3 * CHUNK : 3 * CHUNK + 1, :] * state + fresh
    halo_i[...] = inner_ref[CHUNK - 8 :, :]
    halo_s[...] = state_ref[CHUNK - 8 :, :]
    square = jnp.sum(squares, axis=1, keepdims=True)
    cross = jnp.sum(crosses * marks[0], axis=1, keepdims=True)
    sums_ref[...] = jnp.where(lane == 0, square, cross)


def backward_kernel(
    inner_ref, step_ref, state_ref, zi_ref, zs_ref, scanned_ref, dscan_ref, enter_ref, pos_ref,
    taps_ref, taps_s_ref, head_ref, skip_ref, wide_ref,
    d_inner_ref, d_state_ref, d_step_ref, g_taps_ref, g_taps_s_ref, g_skip_ref, g_head_ref,
    halo_i, halo_s, halo_p, hold,
):
    low = jnp.bfloat16

    @pl.when(pl.program_id(0) == 0)
    def _():
        for ref in (halo_i, halo_s, halo_p, hold, g_taps_ref, g_taps_s_ref, g_skip_ref, g_head_ref):
            ref[...] = jnp.zeros_like(ref)

    pos = pos_ref[...]
    pos_ext = jnp.concatenate([pos, halo_p[...]], axis=0)
    marks = [(pos_ext >= lag).astype(jnp.float32) for lag in range(4)]
    lane = lax.broadcasted_iota(jnp.int32, (CHUNK, 128), 1)
    row = lax.broadcasted_iota(jnp.int32, (CHUNK, 128), 0)
    col = lane

    def slope(total):
        sig = sigmoid(total)
        return sig * (1.0 + total * (1.0 - sig)), total * sig

    def fold(value):
        return jnp.sum(value.reshape(CHUNK // 8, 8, 128), axis=0)

    def conv_back(grad, ref, halo, taps, out_ref, g_ref, first):
        cols = slice(first, first + 128)
        ext = jnp.concatenate([grad, halo[:, cols]], axis=0)
        value = ref[:, cols]
        halo[:, cols] = grad[:8]
        g_ref[4, :, cols] += fold(grad)
        total = jnp.zeros((CHUNK, 128), jnp.float32)
        for lag in range(4):
            masked = ext * marks[lag]
            if lag:
                masked = pltpu.roll(masked, CHUNK + 8 - lag, 0)
            masked = masked[:CHUNK]
            g_ref[lag, :, cols] += fold(masked * value)
            total = total + masked * taps[lag : lag + 1, cols]
        out_ref[:, cols] = total.astype(low)

    shifted, step, log_decay, cumulative, linked, carry_in, tail, carry = head_terms(
        step_ref, head_ref, pos
    )
    across = cumulative.T
    wide = dot(
        jnp.concatenate(
            [
                two_term(step),
                two_term(carry_in),
                two_term(tail),
                two_term(jnp.broadcast_to(carry, (16, 128))),
            ],
            axis=0,
        ),
        wide_ref[...],
    )
    slope_b, input_map = slope(zs_ref[:, :128])
    slope_c, output_map = slope(zs_ref[:, 128:])
    input_low, output_low = input_map.astype(low), output_map.astype(low)
    scores = jnp.where(linked, dot(output_low, input_low, ((1,), (1,))), 0.0)
    entering = enter_ref[...]
    d_next = hold[...]
    d_next_low = d_next.astype(low)
    pulled = dot(input_low, d_next_low)
    d_scores = jnp.zeros((CHUNK, 128), jnp.float32)
    d_entered, fed, balance, direct, extra = [], [], [], [], []
    carry_wide = wide[3 * CHUNK : 3 * CHUNK + 1, :]
    carry_grad = jnp.sum(d_next * entering.astype(jnp.float32), axis=0, keepdims=True) * carry_wide
    for pair in range(6):
        cols = slice(pair * 128, pair * 128 + 128)
        slope_x, act = slope(zi_ref[:, cols])
        d_scan = dscan_ref[:, cols]
        skip = skip_ref[0:1, cols]
        stepped = (wide[:CHUNK, cols] * act).astype(low)
        stepped_wide = stepped.astype(jnp.float32)
        d_low = d_scan.astype(low)
        d_exact = d_low.astype(jnp.float32)
        d_both = jnp.concatenate(
            [jnp.where(lane < 64, d_exact, 0.0).astype(low), jnp.where(lane < 64, 0.0, d_exact).astype(low)],
            axis=0,
        )
        first, second = pair_decay(cumulative, across, pair)
        mixing = jnp.concatenate([(scores * first).astype(low), (scores * second).astype(low)], axis=0)
        d_mixing = dot(d_both, stepped, ((1,), (1,)))
        d_scores = d_scores + d_mixing[:CHUNK] * first + d_mixing[CHUNK:] * second
        tail_cols = wide[2 * CHUNK : 3 * CHUNK, cols]
        tailed = tail_cols * pulled[:, cols]
        d_stepped = dot(mixing, d_both, ((0,), (0,))) + tailed
        extra.append(jnp.sum(stepped_wide * tailed, axis=0, keepdims=True) + carry_grad[:, cols])
        fed.append((tail_cols * stepped_wide).astype(low))
        d_entered.append((wide[CHUNK : 2 * CHUNK, cols] * d_exact).astype(low))
        balance.append(d_exact * (scanned_ref[:, cols] - skip * act) - stepped_wide * d_stepped)
        direct.append(act * d_stepped)
        g_skip_ref[:, cols] += fold(d_scan * act)
        d_act = skip * d_scan + wide[:CHUNK, cols] * d_stepped
        conv_back(d_act * slope_x, inner_ref, halo_i, taps_ref, d_inner_ref, g_taps_ref, pair * 128)
    d_entered = jnp.concatenate(d_entered, axis=1)
    fed = jnp.concatenate(fed, axis=1)
    d_scores = jnp.where(linked, d_scores, 0.0).astype(low)
    d_output = dot(d_scores, input_low) + dot(d_entered, entering, ((1,), (1,)))
    d_input = dot(d_scores, output_low, ((0,), (0,))) + dot(fed, d_next_low, ((1,), (1,)))
    hold[...] = carry_wide * d_next + dot(output_low, d_entered, ((0,), (0,)))
    conv_back(d_input * slope_b, state_ref, halo_s, taps_s_ref, d_state_ref, g_taps_s_ref, 0)
    conv_back(d_output * slope_c, state_ref, halo_s, taps_s_ref, d_state_ref, g_taps_s_ref, 128)
    halo_p[...] = pos[:8]
    spread_back = wide_ref[...]
    extra = jnp.broadcast_to(jnp.concatenate(extra, axis=1), (16, 768))
    stacked = jnp.concatenate(
        split_terms(jnp.concatenate(balance, axis=1), 2)
        + split_terms(jnp.concatenate(direct, axis=1), 2)
        + split_terms(extra, 2),
        axis=0,
    )
    summed = dot(stacked, spread_back, ((1,), (1,)))
    d_sum = summed[:CHUNK] + summed[CHUNK : 2 * CHUNK]
    d_direct = summed[2 * CHUNK : 3 * CHUNK] + summed[3 * CHUNK : 4 * CHUNK]
    d_last = summed[4 * CHUNK : 4 * CHUNK + 1] + summed[4 * CHUNK + 16 : 4 * CHUNK + 17]
    upper = (row <= col).astype(low)
    d_decay = sum(dot(upper, piece) for piece in split_terms(d_sum, 3)) + d_last
    d_step = (d_direct - d_decay * jnp.exp(head_ref[1:2, :])) * sigmoid(shifted)
    d_step = jnp.where(lane < PACK, d_step, 0.0)
    d_step_ref[...] = d_step.astype(low)
    g_head_ref[0] += fold(d_step)
    g_head_ref[1] += fold(d_decay * log_decay)


def forward_core(first_pre, second_pre, d_normed_out, pos, taps, taps_s, heads_lanes, skip, gain, wide):
    rows = first_pre.shape[0]
    at = lambda width, col: pl.BlockSpec((CHUNK, width), lambda c: (c, col))
    whole = lambda arr: pl.BlockSpec(arr.shape, lambda c: (0,) * arr.ndim)
    f32 = jnp.float32
    return pl.pallas_call(
        forward_kernel,
        grid=(rows // CHUNK,),
        in_specs=[
            at(768, 0), at(128, 6), at(768, 0), at(256, 3), at(768, 0), at(128, 0),
            whole(taps), whole(taps_s), whole(heads_lanes), whole(skip), whole(gain), whole(wide),
        ],
        out_specs=[at(768, 0), at(768, 0), at(256, 0), at(768, 0), at(128, 0)],
        out_shape=[
            jax.ShapeDtypeStruct((rows, 768), f32),
            jax.ShapeDtypeStruct((rows, 768), f32),
            jax.ShapeDtypeStruct((rows, 256), f32),
            jax.ShapeDtypeStruct((rows, 768), jnp.bfloat16),
            jax.ShapeDtypeStruct((rows, 128), f32),
        ],
        scratch_shapes=[
            pltpu.VMEM((8, 768), f32), pltpu.VMEM((8, 256), f32), pltpu.VMEM((128, 768), f32),
        ],
        compiler_params=pltpu.CompilerParams(vmem_limit_bytes=40 * 2**20),
        cost_estimate=pl.CostEstimate(flops=8 * 10**9, bytes_accessed=24 * 10**6, transcendentals=4 * 10**6),
        name="mixer_forward",
    )(second_pre, second_pre, first_pre, first_pre, d_normed_out, pos, taps, taps_s, heads_lanes, skip, gain, wide)


def backward_core(first_pre, second_pre, zi, zs, scanned, d_scan, enter, pos, taps, taps_s, heads_lanes, skip, wide):
    rows = first_pre.shape[0]
    count = rows // CHUNK
    at = lambda width, col: pl.BlockSpec((CHUNK, width), lambda c: (count - 1 - c, col))
    whole = lambda shape: pl.BlockSpec(shape, lambda c: (0,) * len(shape))
    f32, low = jnp.float32, jnp.bfloat16
    return pl.pallas_call(
        backward_kernel,
        grid=(count,),
        in_specs=[
            at(768, 0), at(128, 6), at(256, 3), at(768, 0), at(256, 0), at(768, 0), at(768, 0),
            at(768, 0), at(128, 0),
            whole(taps.shape), whole(taps_s.shape), whole(heads_lanes.shape), whole(skip.shape), whole(wide.shape),
        ],
        out_specs=[
            at(768, 0), at(256, 0), at(128, 0),
            whole((5, 8, 768)), whole((5, 8, 256)), whole((8, 768)), whole((2, 8, 128)),
        ],
        out_shape=[
            jax.ShapeDtypeStruct((rows, 768), low),
            jax.ShapeDtypeStruct((rows, 256), low),
            jax.ShapeDtypeStruct((rows, 128), low),
            jax.ShapeDtypeStruct((5, 8, 768), f32),
            jax.ShapeDtypeStruct((5, 8, 256), f32),
            jax.ShapeDtypeStruct((8, 768), f32),
            jax.ShapeDtypeStruct((2, 8, 128), f32),
        ],
        scratch_shapes=[
            pltpu.VMEM((8, 768), f32), pltpu.VMEM((8, 256), f32), pltpu.VMEM((8, 128), f32),
            pltpu.VMEM((128, 768), f32),
        ],
        compiler_params=pltpu.CompilerParams(vmem_limit_bytes=40 * 2**20),
        cost_estimate=pl.CostEstimate(flops=16 * 10**9, bytes_accessed=24 * 10**6, transcendentals=6 * 10**6),
        name="mixer_backward",
    )(second_pre, second_pre, first_pre, zi, zs, scanned, d_scan, enter, pos, taps, taps_s, heads_lanes, skip, wide)


def swap(value):
    return lax.ppermute(value, "tensor", [(0, 1), (1, 0)])


def pair_scatter(part, axis):
    mine = lax.axis_index("tensor")
    width = part.shape[axis] // 2
    keep = lax.dynamic_slice_in_dim(part, mine * width, width, axis)
    send = lax.dynamic_slice_in_dim(part, (1 - mine) * width, width, axis)
    return keep.astype(jnp.float32) + swap(send.astype(jnp.bfloat16)).astype(jnp.float32)


def pad_cols(value, width):
    return jnp.pad(value, ((0, 0), (0, width - value.shape[1])))


MESH_ID = pl.DeviceIdType.MESH
SHARD = 48
PLAN = (("out", 768), ("gate", 768), ("inner", 768), ("small", 256))
PLANE_OF = {"gate": 0, "inner": 1, "out": 2, "small": 3}


def place():
    index = lax.axis_index("dp")
    z = lax.div(index, 4)
    y = lax.rem(lax.div(index, 2), 2)
    x = lax.rem(index, 2)
    at_x = {"dp": z * 4 + y * 2 + (1 - x)}
    at_y = {"dp": z * 4 + (1 - y) * 2 + x}
    at_z = [{"dp": lax.rem(z + step, 4) * 4 + y * 2 + x} for step in range(1, 4)]
    return x, y, z, at_x, at_y, at_z


def greet(peers):
    barrier = pltpu.get_barrier_semaphore()
    for peer in peers:
        pl.semaphore_signal(barrier, inc=1, device_id=peer, device_id_type=MESH_ID)
    pl.semaphore_wait(barrier, len(peers))


def remote(src, dst, send, recv, peer):
    return pltpu.make_async_remote_copy(
        src_ref=src, dst_ref=dst, send_sem=send, recv_sem=recv, device_id=peer, device_id_type=MESH_ID
    )


GATHER_PIECES = (
    (1, 0, 384, 0), (1, 384, 512, 1), (0, 0, 512, 0), (0, 512, 512, 1), (2, 0, 384, 0), (2, 384, 384, 1),
)


def gather_kernel(
    first_ref, second_ref, out_ref, normed_ref, cot_ref,
    full_first, full_second, full_out, rows_ref, cots_ref,
    near_sem, row_sem, z_send, z_recv, one_send, one_recv, two_send, two_recv,
):
    x, y, z, at_x, at_y, at_z = place()
    core = lax.axis_index("tensor")
    twin = {"tensor": 1 - core}
    greet([at_x, at_y, twin] + at_z)
    shards = (first_ref, second_ref, out_ref)
    fulls = (full_first, full_second, full_out)
    z_copies = []
    for piece, (which, start, width, _) in enumerate(GATHER_PIECES):
        cols = pl.ds(start, width)
        z_copies.append([])
        for step, peer in enumerate(at_z):
            copy = remote(
                shards[which].at[:, cols], fulls[which].at[z, y, x, :, cols],
                z_send.at[piece, step], z_recv.at[piece, step], peer,
            )
            copy.start()
            z_copies[-1].append(copy)
        if piece == 0:
            near = []
            for at, (src, dst) in enumerate(zip(shards, fulls)):
                near.append(pltpu.make_async_copy(src, dst.at[z, y, x], near_sem.at[at]))
            for at, (src, dst) in enumerate(((normed_ref, rows_ref), (cot_ref, cots_ref))):
                near.append(pltpu.make_async_copy(src, dst.at[core], near_sem.at[3 + at]))
                near.append(remote(src, dst.at[core], row_sem.at[at], row_sem.at[2 + at], twin))
            for copy in near:
                copy.start()
    for copy in near[:3]:
        copy.wait()

    def step_one(piece):
        which, start, width, route = GATHER_PIECES[piece]
        for copy in z_copies[piece]:
            copy.wait()
        part = fulls[which].at[:, y, x, :, pl.ds(start, width)]
        copy = remote(part, part, one_send.at[piece], one_recv.at[piece], at_x if route else at_y)
        copy.start()
        return copy

    def step_two(piece):
        which, start, width, route = GATHER_PIECES[piece]
        cols = pl.ds(start, width)
        part = fulls[which].at[:, y, :, :, cols] if route else fulls[which].at[:, :, x, :, cols]
        copy = remote(part, part, two_send.at[piece], two_recv.at[piece], at_y if route else at_x)
        copy.start()
        return copy

    ones, twos = {}, {}
    count = len(GATHER_PIECES)
    for piece in range(count + 2):
        if piece < count:
            ones[piece] = step_one(piece)
        if piece >= 2:
            ones[piece - 2].wait()
            twos[piece - 2] = step_two(piece - 2)
    for piece in range(count):
        twos[piece].wait()
    for copy in near[3:]:
        copy.wait()


def gather_all(first, second, out, normed, cot):
    low = jnp.bfloat16
    anywhere = pl.BlockSpec(memory_space=pl.ANY)
    count = len(GATHER_PIECES)
    dma = pltpu.SemaphoreType.DMA
    full = lambda arr: jax.ShapeDtypeStruct((4, 2, 2) + arr.shape, low)
    rows = jax.ShapeDtypeStruct((2,) + normed.shape, low)
    got = pl.pallas_call(
        gather_kernel,
        in_specs=[anywhere] * 5,
        out_specs=[anywhere] * 5,
        out_shape=[full(first), full(second), full(out), rows, rows],
        scratch_shapes=[
            dma((5,)), dma((4,)), dma((count, 3)), dma((count, 3)),
            dma((count,)), dma((count,)), dma((count,)), dma((count,)),
        ],
        compiler_params=pltpu.CompilerParams(collective_id=0, has_side_effects=True),
        cost_estimate=pl.CostEstimate(flops=0, bytes_accessed=120 * 10**6, transcendentals=0),
        name="gather_weights",
    )(first, second, out, normed, cot)
    return [item.reshape(-1, item.shape[-1]) for item in got]


def reduce_kernel(
    out_ref, gate_ref, inner_ref, small_ref, vec_ref, moment_ref,
    whole_ref, other_ref, grads_ref, total_ref,
    arrived, summed, arrived_two, held_out, held_gate, held_inner, held_small, slots, moments,
    block, back, vec_in, vec_mid, vec_slots,
    m_send, m_recv, one_send, one_recv, two_send, two_recv, z_send, z_recv, g_send, g_recv,
    p_send, p_recv, t_send, t_recv, v_send, v_recv,
):
    f32, low = jnp.float32, jnp.bfloat16
    x, y, z, at_x, at_y, at_z = place()
    core = lax.axis_index("tensor")
    twin = {"tensor": 1 - core}
    greet([at_x, at_y, twin] + at_z)
    parts = (out_ref, gate_ref, inner_ref, small_ref)
    held = (held_out, held_gate, held_inner, held_small)
    steps_z = [lax.rem(z + step, 4) for step in range(1, 4)]

    vec_x = remote(vec_ref, vec_in.at[0], v_send.at[0], v_recv.at[0], at_x)
    vec_x.start()
    moment_copies = []
    for step, (peer, plane) in enumerate(zip(at_z, steps_z)):
        copy = remote(moment_ref.at[plane], moments.at[z], m_send.at[step], m_recv.at[step], peer)
        copy.start()
        moment_copies.append(copy)

    def span(task, route):
        half = PLAN[task][1] // 2
        return pl.ds(route * half, half), pl.ds(0, half)

    def step_one(task, route):
        cols, mine = span(task, route)
        other = parts[task].at[:, 1 - y, :, :, cols] if route else parts[task].at[:, :, 1 - x, :, cols]
        copy = remote(
            other, arrived.at[task, route, :, :, :, mine], one_send.at[task, route],
            one_recv.at[task, route], at_y if route else at_x,
        )
        copy.start()
        return copy

    def step_two(task, route):
        cols, mine = span(task, route)
        own = parts[task][:, y, :, :, cols] if route else parts[task][:, :, x, :, cols]
        got = arrived[task, route, :, :, :, mine]
        summed[task, route, :, :, :, mine] = (own.astype(f32) + got.astype(f32)).astype(low)
        copy = remote(
            summed.at[task, route, :, 1 - x if route else 1 - y, :, mine],
            arrived_two.at[task, route, :, :, mine], two_send.at[task, route],
            two_recv.at[task, route], at_x if route else at_y,
        )
        copy.start()
        return copy

    def settle(task, route):
        cols, mine = span(task, route)
        own = summed[task, route, :, x if route else y, :, mine]
        got = arrived_two[task, route, :, :, mine]
        held[task][:, :, cols] = (own.astype(f32) + got.astype(f32)).astype(low)

    def to_plane(task):
        plane, width = PLANE_OF[PLAN[task][0]], PLAN[task][1]

        @pl.when(z != plane)
        def _():
            remote(
                held[task], slots.at[z, :, :, pl.ds(0, width)], z_send.at[task], z_recv.at[z],
                {"dp": plane * 4 + y * 2 + x},
            ).start()

    ones, twos = {}, {}
    for task in range(2):
        for route in range(2):
            ones[task, route] = step_one(task, route)
    vec_x.wait()
    vec_mid[0] = vec_ref[...] + vec_in[0]
    vec_y = remote(vec_mid.at[0], vec_in.at[1], v_send.at[1], v_recv.at[1], at_y)
    vec_y.start()
    for task in range(5):
        for route in range(2):
            if task < 4:
                ones[task, route].wait()
                twos[task, route] = step_two(task, route)
            if task + 2 < 4:
                ones[task + 2, route] = step_one(task + 2, route)
        if task >= 1:
            for route in range(2):
                twos[task - 1, route].wait()
                settle(task - 1, route)
            to_plane(task - 1)
        if task == 0:
            vec_y.wait()
            vec_mid[1] = vec_mid[0] + vec_in[1]
            vec_slots[z] = vec_mid[1]
            vec_z = []
            for step, peer in enumerate(at_z):
                copy = remote(vec_mid.at[1], vec_slots.at[z], v_send.at[2 + step], v_recv.at[2 + step], peer)
                copy.start()
                vec_z.append(copy)
        if task == 1:
            for copy in moment_copies:
                copy.wait()
            moments[z] = moment_ref[z]
            for copy in vec_z:
                copy.wait()
            total_ref[...] = (vec_slots[0] + vec_slots[1]) + (vec_slots[2] + vec_slots[3])

    for task, (name, width) in enumerate(PLAN):
        plane = PLANE_OF[name]
        cols = pl.ds(0, width)

        @pl.when(z == plane)
        def _():
            for source in range(4):
                if source != plane:
                    remote(
                        held[task], slots.at[source, :, :, cols], z_send.at[task], z_recv.at[source], at_x
                    ).wait_recv()
            total = held[task][...].astype(f32)
            for source in range(4):
                if source != plane:
                    total = total + slots[source, :, :, cols].astype(f32)
            if width < 768:
                back[...] = jnp.zeros_like(back)
                block[...] = jnp.zeros_like(block)
            back[:, :, cols] = total.astype(low)
            block[:, :, cols] = (MU_MAT * moments[:, :, cols].astype(f32) + total).astype(low)

    half = 384
    routes = (pl.ds(0, half), pl.ds(half, half))
    for row in range(4):
        whole_ref[row, y, x] = block[row]
    plane_one = []
    for route, peer in enumerate((at_x, at_y)):
        copy = remote(
            block.at[:, :, routes[route]], whole_ref.at[:, y, x, :, routes[route]],
            p_send.at[0, route], p_recv.at[0, route], peer,
        )
        copy.start()
        plane_one.append(copy)
    twin_own = remote(block, other_ref.at[:, y, x], t_send.at[0], t_recv.at[0], twin)
    twin_own.start()
    grads_ref[z] = back[z]
    returns = []
    for step, (peer, plane) in enumerate(zip(at_z, steps_z)):
        copy = remote(back.at[plane], grads_ref.at[z], g_send.at[step], g_recv.at[step], peer)
        copy.start()
        returns.append(copy)
    plane_two = []
    for route, peer in enumerate((at_y, at_x)):
        plane_one[route].wait()
        part = (
            whole_ref.at[:, :, x, :, routes[1]] if route else whole_ref.at[:, y, :, :, routes[0]]
        )
        copy = remote(part, part, p_send.at[1, route], p_recv.at[1, route], peer)
        copy.start()
        plane_two.append(copy)
    twins = [twin_own]
    for route in range(2):
        src = whole_ref.at[:, 1 - y, x, :, routes[1]] if route else whole_ref.at[:, y, 1 - x, :, routes[0]]
        dst = other_ref.at[:, 1 - y, x, :, routes[1]] if route else other_ref.at[:, y, 1 - x, :, routes[0]]
        copy = remote(src, dst, t_send.at[1 + route], t_recv.at[1 + route], twin)
        copy.start()
        twins.append(copy)
    for route in range(2):
        plane_two[route].wait()
        src = whole_ref.at[:, :, 1 - x, :, routes[1]] if route else whole_ref.at[:, 1 - y, :, :, routes[0]]
        dst = other_ref.at[:, :, 1 - x, :, routes[1]] if route else other_ref.at[:, 1 - y, :, :, routes[0]]
        copy = remote(src, dst, t_send.at[3 + route], t_recv.at[3 + route], twin)
        copy.start()
        twins.append(copy)
    for copy in twins + returns:
        copy.wait()
    for task, (name, width) in enumerate(PLAN):
        plane = PLANE_OF[name]

        @pl.when(z != plane)
        def _():
            remote(
                held[task], slots.at[z, :, :, pl.ds(0, width)], z_send.at[task], z_recv.at[z],
                {"dp": plane * 4 + y * 2 + x},
            ).wait_send()


def reduce_all(parts, vectors, moments):
    f32, low = jnp.float32, jnp.bfloat16
    vmem = pl.BlockSpec(memory_space=pltpu.VMEM)
    dma = pltpu.SemaphoreType.DMA
    parts = [part.reshape(4, 2, 2, SHARD, part.shape[1]) for part in parts]
    buf = pltpu.VMEM
    whole, other, grads, total = pl.pallas_call(
        reduce_kernel,
        in_specs=[vmem] * 6,
        out_specs=[vmem] * 4,
        out_shape=[
            jax.ShapeDtypeStruct((4, 2, 2, SHARD, 768), low),
            jax.ShapeDtypeStruct((4, 2, 2, SHARD, 768), low),
            jax.ShapeDtypeStruct((4, SHARD, 768), low),
            jax.ShapeDtypeStruct(vectors.shape, f32),
        ],
        scratch_shapes=[
            buf((4, 2, 4, 2, SHARD, 384), low), buf((4, 2, 4, 2, SHARD, 384), low),
            buf((4, 2, 4, SHARD, 384), low),
            buf((4, SHARD, 768), low), buf((4, SHARD, 768), low), buf((4, SHARD, 768), low),
            buf((4, SHARD, 256), low),
            buf((4, 4, SHARD, 768), low), buf((4, SHARD, 768), low),
            buf((4, SHARD, 768), low), buf((4, SHARD, 768), low),
            buf((2,) + vectors.shape, f32), buf((2,) + vectors.shape, f32), buf((4,) + vectors.shape, f32),
            dma((3,)), dma((3,)), dma((4, 2)), dma((4, 2)), dma((4, 2)), dma((4, 2)),
            dma((4,)), dma((4,)), dma((3,)), dma((3,)), dma((2, 2)), dma((2, 2)),
            dma((5,)), dma((5,)), dma((5,)), dma((5,)),
        ],
        compiler_params=pltpu.CompilerParams(
            collective_id=1, has_side_effects=True, vmem_limit_bytes=48 * 2**20
        ),
        cost_estimate=pl.CostEstimate(flops=0, bytes_accessed=150 * 10**6, transcendentals=0),
        name="reduce_grads",
    )(*parts, vectors, moments)
    return whole.reshape(768, 768), other.reshape(768, 768), grads, total


def newton_kernel(full_ref, out_ref, current, gram, mix):
    f32, low = jnp.float32, jnp.bfloat16
    rows, cols = current.shape
    tile = 256
    count = rows // tile
    row_ids = lax.broadcasted_iota(jnp.int32, (tile, tile), 0)
    col_ids = lax.broadcasted_iota(jnp.int32, (tile, tile), 1)
    blocks = [pl.ds(at * tile, tile) for at in range(count)]

    def symmetric(source, store):
        for first in range(count):
            for second in range(first, count):
                store(first, second, dot(source[blocks[first], :], source[blocks[second], :], ((1,), (1,))))

    def put(ref, first, second, value):
        ref[blocks[first], blocks[second]] = value.astype(low)
        if first != second:
            ref[blocks[second], blocks[first]] = value.T.astype(low)

    firsts = {}
    symmetric(full_ref, lambda first, second, value: firsts.update({(first, second): value}))
    trace = sum(
        jnp.sum(jnp.where(row_ids == col_ids, firsts[at, at], 0.0), keepdims=True) for at in range(count)
    )
    scale = jnp.sqrt(trace) + 1e-07
    inverse, inverse_square = 1.0 / scale, 1.0 / (scale * scale)
    for (first, second), value in firsts.items():
        put(gram, first, second, value * inverse_square)
    for at in range(count):
        current[blocks[at], :] = (full_ref[blocks[at], :].astype(f32) * inverse).astype(low)

    def mixed():
        def store(first, second, value):
            piece = gram[blocks[first], blocks[second]].astype(f32)
            put(mix, first, second, NS_B * piece + NS_C * value)

        symmetric(gram, store)

    def turn(_, carry):
        mixed()

        def update(at, carry):
            here = pl.ds(pl.multiple_of(at * tile, tile), tile)
            held = current[:, here]
            current[:, here] = (NS_A * held.astype(f32) + dot(mix[...], held)).astype(low)
            return carry

        lax.fori_loop(0, cols // tile, update, 0)
        symmetric(current, lambda first, second, value: put(gram, first, second, value))
        return carry

    lax.fori_loop(0, NS_STEPS - 1, turn, 0)
    mixed()
    for at in range(out_ref.shape[1] // tile):
        here = pl.ds(at * tile, tile)
        held = current[:, here]
        out_ref[:, here] = (NS_A * held.astype(f32) + dot(mix[...], held)).astype(low)


def newton(full, width):
    low = jnp.bfloat16
    rows = full.shape[0]
    return pl.pallas_call(
        newton_kernel,
        in_specs=[pl.BlockSpec(memory_space=pltpu.VMEM)],
        out_specs=pl.BlockSpec(memory_space=pltpu.VMEM),
        out_shape=jax.ShapeDtypeStruct((rows, width), low),
        scratch_shapes=[
            pltpu.VMEM(full.shape, low), pltpu.VMEM((rows, rows), low), pltpu.VMEM((rows, rows), low),
        ],
        compiler_params=pltpu.CompilerParams(vmem_limit_bytes=48 * 2**20),
        cost_estimate=pl.CostEstimate(flops=20 * 10**9, bytes_accessed=4 * 10**6, transcendentals=0),
        name="newton_schulz",
    )(full)


def return_kernel(done_ref, back_ref, send, recv):
    x, y, z, _, _, at_z = place()
    greet(at_z)
    copies = []
    for step, peer in enumerate(at_z):
        plane = lax.rem(z + step + 1, 4)
        copies.append(
            remote(done_ref.at[plane, y, x], back_ref.at[z], send.at[step], recv.at[step], peer)
        )
        copies[-1].start()
    back_ref[z] = done_ref[z, y, x]
    for copy in copies:
        copy.wait()


def return_rows(done):
    vmem = pl.BlockSpec(memory_space=pltpu.VMEM)
    dma = pltpu.SemaphoreType.DMA
    return pl.pallas_call(
        return_kernel,
        in_specs=[vmem],
        out_specs=vmem,
        out_shape=jax.ShapeDtypeStruct((4, SHARD, 768), done.dtype),
        scratch_shapes=[dma((3,)), dma((3,))],
        compiler_params=pltpu.CompilerParams(collective_id=2, has_side_effects=True, vmem_limit_bytes=16 * 2**20),
        cost_estimate=pl.CostEstimate(flops=0, bytes_accessed=20 * 10**6, transcendentals=0),
        name="return_rows",
    )(done.reshape(4, 2, 2, SHARD, 768))


def orthogonal_owned(own, other, state_width):
    width = own.shape[1]
    small = lax.axis_index("dp") // 4 == PLANE_OF["small"]
    full = jnp.concatenate([own, other], axis=1)
    col = jnp.arange(2 * width)[None, :] % width
    keep = (col < state_width) == (lax.axis_index("tensor") == 0)
    full = jnp.where(small & ~keep, jnp.zeros_like(full), full)
    done = newton(full, width + 2 * state_width)
    half, lent = done[:, :width], done[:, width:]
    edge = half[:, : 2 * state_width]
    edge = edge + jnp.where(small, swap(lent), jnp.zeros_like(lent))
    return jnp.concatenate([edge, half[:, 2 * state_width :]], axis=1)


def paired_shards(
    stream,
    cotangent,
    positions,
    norm_gain,
    w_gate,
    w_inner,
    w_state,
    w_step,
    conv_inner,
    conv_state,
    head_params,
    gate_gain,
    w_out,
    moment_norm_gain,
    moment_w_gate,
    moment_w_inner,
    moment_w_state,
    moment_w_step,
    moment_conv_inner,
    moment_conv_state,
    moment_head_params,
    moment_gate_gain,
    moment_w_out,
):
    low = jnp.bfloat16
    core = lax.axis_index("tensor")
    room = w_gate.shape[1]
    wide = w_state.shape[1]
    col_width = wide // 2
    heads = w_step.shape[1]
    inv_first = lax.rsqrt(jnp.mean(stream * stream, axis=1, keepdims=True) + EPS)
    normed = (stream * inv_first * norm_gain).astype(low)
    first_pack = jnp.concatenate([w_gate.astype(low), w_state.astype(low)], axis=1)
    step_low = w_step.astype(low)
    step_lanes = jnp.concatenate([pad_cols(step_low, PACK), pad_cols(step_low, 128 - PACK)], axis=1)
    second_pack = jnp.concatenate([w_inner.astype(low), step_lanes], axis=1)
    full_first, full_second, full_out, token_rows, cotangent_rows = gather_all(
        first_pack, second_pack, w_out.astype(low).T, normed, cotangent.astype(low)
    )
    first_pre = jnp.dot(token_rows, full_first, preferred_element_type=jnp.float32)
    second_pre = jnp.dot(token_rows, full_second, preferred_element_type=jnp.float32)
    gate_pre = first_pre[:, :room]
    alive = (positions >= 0).astype(jnp.float32)[:, None]
    pos = jnp.broadcast_to(positions.astype(jnp.float32)[:, None], (positions.shape[0], 128))
    taps = jnp.pad(conv_inner, ((0, 3), (0, 0)))
    taps_s = jnp.pad(conv_state, ((0, 3), (0, 0)))
    lanes = jnp.concatenate([pad_cols(head_params, PACK), pad_cols(head_params, 128 - PACK)], axis=1)
    lanes = jnp.pad(lanes, ((0, 5), (0, 0)))
    skip = jnp.repeat(head_params[2], room // heads)[None, :]
    wide_map = expand_matrix()
    d_normed_out = jnp.dot(cotangent_rows, full_out, preferred_element_type=jnp.float32)
    scanned, zi, zs, enter, sums = forward_core(
        first_pre, second_pre, d_normed_out, pos, taps, taps_s, lanes, skip, gate_gain[None, :], wide_map
    )
    sums = sums + swap(sums)
    square_sum, cross_sum = sums[:, 0], sums[:, 1]
    gate_act = jax.nn.silu(gate_pre)
    gated = scanned * gate_act
    scaled = d_normed_out * gate_gain * alive
    inv_second = lax.rsqrt(square_sum / INNER + EPS)[:, None]
    normed_out = (gated * inv_second * gate_gain * alive).astype(low)
    mixed = pair_scatter(times_transpose(normed_out, full_out).astype(low), 0)
    output = stream + mixed
    out_part = contract_rows(cotangent_rows, normed_out).astype(low)
    grad_gate_part = jnp.sum(d_normed_out * gated * inv_second * alive, axis=0)
    d_gated = inv_second * scaled - gated * inv_second**3 * (cross_sum / INNER)[:, None]
    d_gate_pre = (d_gated * scanned * silu_slope(gate_pre)).astype(low)
    gate_part = contract_rows(token_rows, d_gate_pre).astype(low)
    d_inner, d_state_part, d_step, taps_part, taps_s_part, skip_part, head_part = backward_core(
        first_pre, second_pre, zi, zs, scanned, d_gated * gate_act, enter, pos, taps, taps_s, lanes, skip, wide_map
    )
    grad_conv_inner_part = jnp.sum(taps_part, axis=1)
    grad_conv_state_part = jnp.sum(taps_s_part, axis=1)
    head_rows = jnp.sum(head_part, axis=1)[:, :heads]
    skip_row = jnp.sum(jnp.sum(skip_part, axis=0).reshape(heads, -1), axis=1)
    grad_head_part = jnp.concatenate([head_rows, skip_row[None, :]], axis=0)
    d_state_low = pair_scatter(d_state_part, 1).astype(low)
    d_tail = jnp.concatenate([d_inner, d_state_low, d_step], axis=1)
    col_first = core * col_width
    state_cols = lax.dynamic_slice_in_dim(full_first, room + col_first, col_width, 1)
    tail_weights = jnp.concatenate(
        [full_second[:, :room], state_cols, full_second[:, room:]], axis=1
    )
    total = times_transpose(d_gate_pre, full_first[:, :room])
    total = total + times_transpose(d_tail, tail_weights)
    d_normed = pair_scatter(total.astype(low), 0)
    tail_part = contract_rows(token_rows, d_tail).astype(low)
    grad_norm_part = jnp.sum(d_normed * stream * inv_first, axis=0)
    weighted = d_normed * norm_gain
    d_stream = (
        cotangent
        + inv_first * weighted
        - stream * inv_first**3 * jnp.mean(weighted * stream, axis=1, keepdims=True)
    )
    shared = jnp.concatenate([grad_conv_state_part, grad_norm_part.reshape(-1, wide)], axis=0)
    shared = shared + swap(shared)
    vectors = jnp.concatenate(
        [
            grad_conv_inner_part,
            grad_gate_part[None, :],
            pad_cols(grad_head_part, room),
            pad_cols(shared, room),
        ],
        axis=0,
    )
    vectors = jnp.pad(vectors, ((0, -vectors.shape[0] % 8), (0, 0)))
    small_moment = pad_cols(jnp.concatenate([moment_w_state, moment_w_step], axis=1), room)
    moment_rows = jnp.stack([moment_w_gate, moment_w_inner, moment_w_out.T, small_moment]).astype(low)
    own, other, grads, vectors = reduce_all(
        (out_part, gate_part, tail_part[:, :room], tail_part[:, room:]), vectors, moment_rows
    )
    grads = grads.astype(jnp.float32)
    grad_gate_w = grads[0]
    grad_inner_w = grads[1]
    grad_out_w = grads[2].T
    grad_state_w = grads[3][:, :col_width]
    grad_step_w = grads[3][:, col_width : col_width + heads]
    grad_conv_inner = vectors[:5]
    grad_gate_gain = vectors[5]
    grad_head = vectors[6:9, :heads]
    grad_conv_state = vectors[9:14, :wide]
    grad_norm = vectors[14:17, :wide].reshape(-1)
    m_gate = MU_MAT * moment_w_gate + grad_gate_w
    m_inner = MU_MAT * moment_w_inner + grad_inner_w
    m_state = MU_MAT * moment_w_state + grad_state_w
    m_step = MU_MAT * moment_w_step + grad_step_w
    m_out = MU_MAT * moment_w_out + grad_out_w
    mine = return_rows(orthogonal_owned(own, other, col_width)).astype(jnp.float32)
    new_gate = w_gate - LR_MAT * spread(D, INNER) * mine[0]
    new_inner = w_inner - LR_MAT * spread(D, INNER) * mine[1]
    new_out = w_out - LR_MAT * spread(INNER, D) * mine[2].T
    new_step = w_step - LR_MAT * spread(D, HEADS) * mine[3][:, col_width : col_width + heads]
    state_slice = lax.dynamic_slice_in_dim(w_state, col_first, col_width, 1)
    new_state = state_slice - LR_MAT * spread(D, 2 * STATE) * mine[3][:, :col_width]
    m_norm = MU_VEC * moment_norm_gain + grad_norm
    m_conv_inner = MU_VEC * moment_conv_inner + grad_conv_inner
    m_conv_state = MU_VEC * moment_conv_state + grad_conv_state
    m_head = MU_VEC * moment_head_params + grad_head
    m_gate_gain = MU_VEC * moment_gate_gain + grad_gate_gain
    return (
        output,
        d_stream,
        grad_norm,
        grad_gate_w,
        grad_inner_w,
        grad_state_w,
        grad_step_w,
        grad_conv_inner,
        grad_conv_state,
        grad_head,
        grad_gate_gain,
        grad_out_w,
        norm_gain - LR_VEC * m_norm,
        new_gate,
        new_inner,
        new_state,
        new_step,
        conv_inner - LR_VEC * m_conv_inner,
        conv_state - LR_VEC * m_conv_state,
        head_params - LR_VEC * m_head,
        gate_gain - LR_VEC * m_gate_gain,
        new_out,
        m_norm,
        m_gate,
        m_inner,
        m_state,
        m_step,
        m_conv_inner,
        m_conv_state,
        m_head,
        m_gate_gain,
        m_out,
    )


def solution(mesh):
    paired = mesh.shape["dp"] == 16 and mesh.shape["tensor"] == 2
    return jax.shard_map(
        paired_shards if paired else shards,
        mesh=mesh,
        in_specs=(
            P(("dp", "tensor"), None),
            P(("dp", "tensor"), None),
            P("dp"),
            P(),
            P("dp", "tensor"),
            P("dp", "tensor"),
            P("dp", None),
            P("dp", "tensor"),
            P(None, "tensor"),
            P(),
            P(None, "tensor"),
            P("tensor"),
            P("tensor", "dp"),
            P(),
            P("dp", "tensor"),
            P("dp", "tensor"),
            P("dp", "tensor"),
            P("dp", "tensor"),
            P(None, "tensor"),
            P(),
            P(None, "tensor"),
            P("tensor"),
            P("tensor", "dp"),
        ),
        out_specs=(
            P(("dp", "tensor"), None),
            P(("dp", "tensor"), None),
            P(),
            P("dp", "tensor"),
            P("dp", "tensor"),
            P("dp", "tensor"),
            P("dp", "tensor"),
            P(None, "tensor"),
            P(),
            P(None, "tensor"),
            P("tensor"),
            P("tensor", "dp"),
            P(),
            P("dp", "tensor"),
            P("dp", "tensor"),
            P("dp", "tensor"),
            P("dp", "tensor"),
            P(None, "tensor"),
            P(),
            P(None, "tensor"),
            P("tensor"),
            P("tensor", "dp"),
            P(),
            P("dp", "tensor"),
            P("dp", "tensor"),
            P("dp", "tensor"),
            P("dp", "tensor"),
            P(None, "tensor"),
            P(),
            P(None, "tensor"),
            P("tensor"),
            P("tensor", "dp"),
        ),
        check_vma=False,
    )
```

```python
from functools import partial
import math

import jax
import jax.numpy as jnp
from jax import lax
from jax.experimental import pallas as pl
from jax.experimental.pallas import tpu as pltpu
from jax.sharding import PartitionSpec as P

D = 768
INNER = 1536
HEADS = 24
STATE = 128
BLOCK = 256
NS_STEPS = 5


EPS = 1e-05
NS_A = 3.4445
NS_B = -4.775
NS_C = 2.0315
MU_MAT = 0.95
MU_VEC = 0.9
LR_MAT = 0.3
LR_VEC = 0.001
HIGH = lax.Precision.HIGHEST
CORE = lax.Precision.DEFAULT


def silu_slope(value):
    sig = jax.nn.sigmoid(value)
    return sig * (1.0 + value * (1.0 - sig))


def contract_rows(left, right):
    return lax.dot_general(
        left, right, (((0,), (0,)), ((), ())), preferred_element_type=jnp.float32
    )


def times_transpose(left, right):
    return lax.dot_general(
        left, right, (((1,), (1,)), ((), ())), preferred_element_type=jnp.float32
    )


def causal_conv(signal, taps, positions):
    length = signal.shape[0]
    reach = taps.shape[0] - 1
    total = jnp.zeros_like(signal) + taps[reach]
    for lag_step in range(reach):
        moved = jnp.pad(signal, ((lag_step, 0), (0, 0)))[:length]
        total = total + jnp.where((positions >= lag_step)[:, None], moved * taps[lag_step], 0.0)
    return jax.nn.silu(total)


def mixer_core(inner_pre, state_pre, step_pre, conv_inner, conv_state, head_params, positions, precision=HIGH):
    length = inner_pre.shape[0]
    heads = step_pre.shape[1]
    head_size = inner_pre.shape[1] // heads
    states = state_pre.shape[1] // 2
    blocks = length // BLOCK
    inner_act = causal_conv(inner_pre, conv_inner, positions).reshape(
        blocks, BLOCK, heads, head_size
    )
    state_act = causal_conv(state_pre, conv_state, positions)
    input_map = state_act[:, :states].reshape(blocks, BLOCK, states)
    output_map = state_act[:, states:].reshape(blocks, BLOCK, states)
    step_size = jax.nn.softplus(step_pre + head_params[0])
    log_decay = (step_size * -jnp.exp(head_params[1])).reshape(blocks, BLOCK, heads)
    step_size = step_size.reshape(blocks, BLOCK, heads)
    resets = (positions <= 0).astype(jnp.float32).reshape(blocks, BLOCK)
    order = jnp.arange(BLOCK)
    lower = (order[:, None] >= order[None, :]).astype(jnp.float32)
    cumulative = jnp.einsum("ij,cjh->cih", lower, log_decay, precision=HIGH)
    seen = jnp.einsum("ij,cj->ci", lower, resets, precision=HIGH)
    linked = (seen[:, :, None] == seen[:, None, :]) & (order[:, None] >= order[None, :])[None]
    linked_heads = linked[..., None]
    spacing = cumulative[:, :, None, :] - cumulative[:, None, :, :]
    decay = jnp.where(linked_heads, jnp.exp(jnp.where(linked_heads, spacing, 0.0)), 0.0)
    scores = jnp.einsum("cin,cjn->cij", output_map, input_map, precision=precision)
    mixing = scores[..., None] * decay * step_size[:, None, :, :]
    within = jnp.einsum("cijh,cjhp->cihp", mixing, inner_act, precision=precision)
    tail_linked = (seen[:, -1:] == seen)[..., None]
    tail = (
        jnp.where(
            tail_linked,
            jnp.exp(jnp.where(tail_linked, cumulative[:, -1:, :] - cumulative, 0.0)),
            0.0,
        )
        * step_size
    )
    own_state = jnp.einsum("cjh,cjhp,cjn->chpn", tail, inner_act, input_map, precision=precision)
    carry_rate = jnp.exp(cumulative[:, -1, :]) * (seen[:, -1] == 0).astype(jnp.float32)[:, None]

    state = jnp.zeros((heads, head_size, states), jnp.float32)
    entering = []
    for block in range(blocks):
        entering.append(state)
        state = carry_rate[block][:, None, None] * state + own_state[block]
    entering = jnp.stack(entering)
    fresh = (seen == 0)[..., None]
    carry_in = jnp.where(fresh, jnp.exp(cumulative), 0.0)
    across = (
        jnp.einsum("cin,chpn->cihp", output_map, entering, precision=precision) * carry_in[..., None]
    )
    result = within + across + head_params[2][None, None, :, None] * inner_act
    return result.reshape(length, heads * head_size)


def gram_total(low):
    return lax.psum(
        jnp.dot(low, low.T, preferred_element_type=jnp.float32).astype(jnp.bfloat16), "tensor"
    ).astype(jnp.float32)


def orthogonalize(matrix):
    first = gram_total(matrix.astype(jnp.bfloat16))
    scale = jnp.sqrt(jnp.trace(first)) + 1e-07
    current = (matrix / scale).astype(jnp.bfloat16)
    gram = (first / (scale * scale)).astype(jnp.bfloat16)
    for turn in range(NS_STEPS):
        if turn > 0:
            gram = gram_total(current).astype(jnp.bfloat16)
        applied = jnp.dot(gram, current, preferred_element_type=jnp.float32)
        twice = jnp.dot(gram, applied.astype(jnp.bfloat16), preferred_element_type=jnp.float32)
        current = (NS_A * current.astype(jnp.float32) + NS_B * applied + NS_C * twice).astype(
            jnp.bfloat16
        )
    return current.astype(jnp.float32)


def spread(rows, cols):
    return math.sqrt(max(1.0, rows / cols))


def shards(
    stream,
    cotangent,
    positions,
    norm_gain,
    w_gate,
    w_inner,
    w_state,
    w_step,
    conv_inner,
    conv_state,
    head_params,
    gate_gain,
    w_out,
    moment_norm_gain,
    moment_w_gate,
    moment_w_inner,
    moment_w_state,
    moment_w_step,
    moment_conv_inner,
    moment_conv_state,
    moment_head_params,
    moment_gate_gain,
    moment_w_out,
):
    dp_count = lax.axis_size("dp")
    inv_first = lax.rsqrt(jnp.mean(stream * stream, axis=1, keepdims=True) + EPS)
    normed = (stream * inv_first * norm_gain).astype(jnp.bfloat16)
    token_rows, cotangent_rows = (
        lax.all_gather(normed, "tensor", axis=0, tiled=True),
        lax.all_gather(cotangent.astype(jnp.bfloat16), "tensor", axis=0, tiled=True),
    )
    local_weights = (
        w_gate.astype(jnp.bfloat16),
        w_inner.astype(jnp.bfloat16),
        w_step.astype(jnp.bfloat16),
        w_state.astype(jnp.bfloat16),
        w_out.astype(jnp.bfloat16),
    )
    full_gate, full_inner, full_step, full_state, full_out = (
        lax.all_gather(local_weights[0], "dp", axis=0, tiled=True),
        lax.all_gather(local_weights[1], "dp", axis=0, tiled=True),
        lax.all_gather(local_weights[2], "dp", axis=0, tiled=True),
        lax.all_gather(local_weights[3], "dp", axis=0, tiled=True),
        lax.all_gather(local_weights[4], "dp", axis=1, tiled=True),
    )
    gate_pre = jnp.dot(token_rows, full_gate, preferred_element_type=jnp.float32)
    inner_pre = jnp.dot(token_rows, full_inner, preferred_element_type=jnp.float32)
    state_pre = jnp.dot(token_rows, full_state, preferred_element_type=jnp.float32)
    step_pre = jnp.dot(token_rows, full_step, preferred_element_type=jnp.float32)
    alive = (positions >= 0).astype(jnp.float32)[:, None]
    scanned, core_back = jax.vjp(
        partial(mixer_core, positions=positions),
        inner_pre,
        state_pre,
        step_pre,
        conv_inner,
        conv_state,
        head_params,
    )
    gate_act = jax.nn.silu(gate_pre)
    gated = scanned * gate_act
    square_sum = lax.psum(jnp.sum(gated * gated, axis=1), "tensor")
    inv_second = lax.rsqrt(square_sum / INNER + EPS)[:, None]
    normed_out = (gated * inv_second * gate_gain * alive).astype(jnp.bfloat16)
    mixed = lax.psum_scatter(
        jnp.dot(normed_out, full_out, preferred_element_type=jnp.float32).astype(jnp.bfloat16),
        "tensor",
        scatter_dimension=0,
        tiled=True,
    ).astype(jnp.float32)
    output = stream + mixed
    d_normed_out = times_transpose(cotangent_rows, full_out)
    grad_out_part = contract_rows(normed_out, cotangent_rows)
    scaled = d_normed_out * gate_gain * alive
    grad_gate_part = jnp.sum(d_normed_out * gated * inv_second * alive, axis=0)
    cross_sum = lax.psum(jnp.sum(scaled * gated, axis=1), "tensor")
    d_gated = inv_second * scaled - gated * inv_second**3 * (cross_sum / INNER)[:, None]
    d_gate_pre = (d_gated * scanned * silu_slope(gate_pre)).astype(jnp.bfloat16)
    d_inner, d_state_part, d_step, grad_conv_inner_part, grad_conv_state_part, grad_head_part = (
        core_back(d_gated * gate_act)
    )
    d_state_cols = lax.psum_scatter(
        d_state_part.astype(jnp.bfloat16), "tensor", scatter_dimension=1, tiled=True
    ).astype(jnp.float32)
    d_inner_low = d_inner.astype(jnp.bfloat16)
    d_state_low = d_state_cols.astype(jnp.bfloat16)
    d_step_low = d_step.astype(jnp.bfloat16)
    col_width = d_state_cols.shape[1]
    col_first = lax.axis_index("tensor") * col_width
    state_cols = lax.dynamic_slice_in_dim(full_state, col_first, col_width, 1)
    total = times_transpose(d_gate_pre, full_gate)
    total = total + times_transpose(d_inner_low, full_inner)
    total = total + times_transpose(d_state_low, state_cols)
    d_normed = lax.psum_scatter(
        (total + times_transpose(d_step_low, full_step)).astype(jnp.bfloat16),
        "tensor",
        scatter_dimension=0,
        tiled=True,
    ).astype(jnp.float32)
    grad_gate_w, grad_inner_w, grad_state_w, grad_step_w, grad_out_w = (
        lax.psum_scatter(
            contract_rows(token_rows, d_gate_pre).astype(jnp.bfloat16),
            "dp",
            scatter_dimension=0,
            tiled=True,
        ).astype(jnp.float32),
        lax.psum_scatter(
            contract_rows(token_rows, d_inner_low).astype(jnp.bfloat16),
            "dp",
            scatter_dimension=0,
            tiled=True,
        ).astype(jnp.float32),
        lax.psum_scatter(
            contract_rows(token_rows, d_state_low).astype(jnp.bfloat16),
            "dp",
            scatter_dimension=0,
            tiled=True,
        ).astype(jnp.float32),
        lax.psum_scatter(
            contract_rows(token_rows, d_step_low).astype(jnp.bfloat16),
            "dp",
            scatter_dimension=0,
            tiled=True,
        ).astype(jnp.float32),
        lax.psum_scatter(
            grad_out_part.astype(jnp.bfloat16), "dp", scatter_dimension=1, tiled=True
        ).astype(jnp.float32),
    )
    grad_norm_part = jnp.sum(d_normed * stream * inv_first, axis=0)
    weighted = d_normed * norm_gain
    d_stream = (
        cotangent
        + inv_first * weighted
        - stream * inv_first**3 * jnp.mean(weighted * stream, axis=1, keepdims=True)
    )
    grad_conv_inner, grad_gate_gain, grad_head = lax.psum(
        (grad_conv_inner_part, grad_gate_part, grad_head_part), "dp"
    )
    grad_conv_state, grad_norm = lax.psum((grad_conv_state_part, grad_norm_part), ("dp", "tensor"))
    m_gate = MU_MAT * moment_w_gate + grad_gate_w
    m_inner = MU_MAT * moment_w_inner + grad_inner_w
    m_state = MU_MAT * moment_w_state + grad_state_w
    m_step = MU_MAT * moment_w_step + grad_step_w
    m_out = MU_MAT * moment_w_out + grad_out_w
    room = w_gate.shape[1]
    shard_rows = w_gate.shape[0]
    stacked = jnp.stack(
        [
            m_gate,
            m_inner,
            m_out.T,
            jnp.pad(m_step, ((0, 0), (0, room - m_step.shape[1]))),
            jnp.pad(m_state, ((0, 0), (0, room - m_state.shape[1]))),
        ]
    )
    matrix_count = stacked.shape[0]
    owner_index = jnp.arange(matrix_count, dtype=jnp.int32) * dp_count // matrix_count
    select = (owner_index[None, :] == jnp.arange(dp_count, dtype=jnp.int32)[:, None]).astype(
        jnp.float32
    )
    outgoing = jnp.einsum("jk,krc->jrc", select, stacked, precision=HIGH)
    owned = (
        lax.all_to_all(outgoing.astype(jnp.bfloat16), "dp", split_axis=0, concat_axis=0, tiled=True)
        .astype(outgoing.dtype)
        .reshape(dp_count * shard_rows, room)
    )
    ortho = orthogonalize(owned)
    returned = lax.all_to_all(
        ortho.reshape(dp_count, shard_rows, room).astype(jnp.bfloat16),
        "dp",
        split_axis=0,
        concat_axis=0,
        tiled=True,
    ).astype(jnp.float32)
    mine = jnp.einsum("jk,jrc->krc", select, returned, precision=HIGH)
    new_gate = w_gate - LR_MAT * spread(D, INNER) * mine[0]
    new_inner = w_inner - LR_MAT * spread(D, INNER) * mine[1]
    new_out = w_out - LR_MAT * spread(INNER, D) * mine[2].T
    new_step = w_step - LR_MAT * spread(D, HEADS) * mine[3][:, : w_step.shape[1]]
    state_slice = lax.dynamic_slice_in_dim(w_state, col_first, col_width, 1)
    new_state = state_slice - LR_MAT * spread(D, 2 * STATE) * mine[4][:, :col_width]
    m_norm = MU_VEC * moment_norm_gain + grad_norm
    m_conv_inner = MU_VEC * moment_conv_inner + grad_conv_inner
    m_conv_state = MU_VEC * moment_conv_state + grad_conv_state
    m_head = MU_VEC * moment_head_params + grad_head
    m_gate_gain = MU_VEC * moment_gate_gain + grad_gate_gain
    return (
        output,
        d_stream,
        grad_norm,
        grad_gate_w,
        grad_inner_w,
        grad_state_w,
        grad_step_w,
        grad_conv_inner,
        grad_conv_state,
        grad_head,
        grad_gate_gain,
        grad_out_w,
        norm_gain - LR_VEC * m_norm,
        new_gate,
        new_inner,
        new_state,
        new_step,
        conv_inner - LR_VEC * m_conv_inner,
        conv_state - LR_VEC * m_conv_state,
        head_params - LR_VEC * m_head,
        gate_gain - LR_VEC * m_gate_gain,
        new_out,
        m_norm,
        m_gate,
        m_inner,
        m_state,
        m_step,
        m_conv_inner,
        m_conv_state,
        m_head,
        m_gate_gain,
        m_out,
    )


CHUNK = 128
PACK = 16


def sigmoid(value):
    return 0.5 * jnp.tanh(0.5 * value) + 0.5


def expand_matrix():
    row = jnp.arange(128)[:, None]
    col = jnp.arange(768)[None, :] // 64
    return ((row == col) | (row == col + PACK)).astype(jnp.bfloat16)


def two_term(value):
    lane = lax.broadcasted_iota(jnp.int32, value.shape, 1)
    high = value.astype(jnp.bfloat16).astype(jnp.float32)
    return jnp.where(lane < PACK, high, value - high).astype(jnp.bfloat16)


def split_terms(value, terms):
    out = []
    for _ in range(terms):
        piece = value.astype(jnp.bfloat16)
        out.append(piece)
        value = value - piece.astype(jnp.float32)
    return out


def dot(left, right, dims=((1,), (0,))):
    return lax.dot_general(left, right, (dims, ((), ())), preferred_element_type=jnp.float32)


def head_terms(step_ref, head_ref, pos):
    shifted = step_ref[...] + head_ref[0:1, :]
    small = jnp.exp(-jnp.abs(shifted))
    step = jnp.maximum(shifted, 0.0) + jnp.log1p(small)
    log_decay = -step * jnp.exp(head_ref[1:2, :])
    row = lax.broadcasted_iota(jnp.int32, (CHUNK, 128), 0)
    col = lax.broadcasted_iota(jnp.int32, (CHUNK, 128), 1)
    lower = (row >= col).astype(jnp.bfloat16)
    cumulative = sum(dot(lower, piece) for piece in split_terms(log_decay, 3))
    last = cumulative[CHUNK - 1 : CHUNK, :]
    back = (row - col).astype(jnp.float32)
    linked = (row >= col) & (back <= jnp.maximum(pos, 0.0))
    row = row.astype(jnp.float32)
    carry_in = jnp.where(pos > row, jnp.exp(cumulative), 0.0)
    pos_last = pos[CHUNK - 1 : CHUNK, :]
    tail_linked = (CHUNK - 1.0 - row) <= jnp.maximum(pos_last, 0.0)
    tail = jnp.where(tail_linked, jnp.exp(jnp.minimum(last - cumulative, 0.0)), 0.0)
    carry = jnp.where(pos_last > CHUNK - 1.0, jnp.exp(last), 0.0)
    return shifted, step, log_decay, cumulative, linked, carry_in, tail, carry


def pair_decay(cumulative, across, pair):
    parts = []
    for head in (2 * pair, 2 * pair + 1):
        spacing = cumulative[:, head : head + 1] - across[head : head + 1, :]
        parts.append(jnp.exp(jnp.minimum(spacing, 0.0)))
    return parts


def forward_kernel(
    inner_ref, step_ref, gate_ref, state_ref, dno_ref, pos_ref, taps_ref, taps_s_ref, head_ref,
    skip_ref, gain_ref, wide_ref,
    scanned_ref, zi_ref, zs_ref, enter_ref, sums_ref,
    halo_i, halo_s, hold,
):
    @pl.when(pl.program_id(0) == 0)
    def _():
        halo_i[...] = jnp.zeros_like(halo_i)
        halo_s[...] = jnp.zeros_like(halo_s)
        hold[...] = jnp.zeros_like(hold)

    low = jnp.bfloat16
    pos = pos_ref[...]
    marks = [(pos >= lag).astype(jnp.float32) for lag in range(4)]

    def conv(ref, halo, taps, out_ref, first):
        value = ref[:, first : first + 128]
        ext = jnp.concatenate([halo[:, first : first + 128], value], axis=0)
        total = taps[4:5, first : first + 128] + marks[0] * (value * taps[0:1, first : first + 128])
        for lag in range(1, 4):
            moved = pltpu.roll(ext, lag, 0)[8:]
            total = total + marks[lag] * (moved * taps[lag : lag + 1, first : first + 128])
        out_ref[:, first : first + 128] = total
        return total * sigmoid(total)

    shifted, step, log_decay, cumulative, linked, carry_in, tail, carry = head_terms(
        step_ref, head_ref, pos
    )
    across = cumulative.T
    wide = dot(
        jnp.concatenate(
            [
                two_term(step),
                two_term(carry_in),
                two_term(tail * step),
                two_term(jnp.broadcast_to(carry, (16, 128))),
            ],
            axis=0,
        ),
        wide_ref[...],
    )
    input_map = conv(state_ref, halo_s, taps_s_ref, zs_ref, 0).astype(low)
    output_map = conv(state_ref, halo_s, taps_s_ref, zs_ref, 128).astype(low)
    scores = jnp.where(linked, dot(output_map, input_map, ((1,), (1,))), 0.0)
    state = hold[...]
    state_low = state.astype(low)
    enter_ref[...] = state_low
    entered = dot(output_map, state_low)
    lane = lax.broadcasted_iota(jnp.int32, (CHUNK, 128), 1)
    squares = jnp.zeros((CHUNK, 128), jnp.float32)
    crosses = jnp.zeros((CHUNK, 128), jnp.float32)
    fed = []
    for pair in range(6):
        cols = slice(pair * 128, pair * 128 + 128)
        act = conv(inner_ref, halo_i, taps_ref, zi_ref, pair * 128)
        stepped = (wide[:CHUNK, cols] * act).astype(low)
        first, second = pair_decay(cumulative, across, pair)
        mixing = jnp.concatenate([(scores * first).astype(low), (scores * second).astype(low)], axis=0)
        both = dot(mixing, stepped)
        within = jnp.where(lane < 64, both[:CHUNK], both[CHUNK:])
        scanned = (
            within + entered[:, cols] * wide[CHUNK : 2 * CHUNK, cols] + skip_ref[0:1, cols] * act
        )
        scanned_ref[:, cols] = scanned
        fed.append((wide[2 * CHUNK : 3 * CHUNK, cols] * act).astype(low))
        gate = gate_ref[:, cols]
        gated = scanned * (gate * sigmoid(gate))
        squares = squares + gated * gated
        crosses = crosses + dno_ref[:, cols] * gain_ref[0:1, cols] * gated
    fresh = dot(input_map, jnp.concatenate(fed, axis=1), ((0,), (0,)))
    hold[...] = wide[3 * CHUNK : 3 * CHUNK + 1, :] * state + fresh
    halo_i[...] = inner_ref[CHUNK - 8 :, :]
    halo_s[...] = state_ref[CHUNK - 8 :, :]
    square = jnp.sum(squares, axis=1, keepdims=True)
    cross = jnp.sum(crosses * marks[0], axis=1, keepdims=True)
    sums_ref[...] = jnp.where(lane == 0, square, cross)


def gate_kernel(
    gate_ref, scanned_ref, dno_ref, sums_ref, twin_ref, gain_ref, pos_ref,
    normed_ref, d_gate_ref, d_scan_ref, g_gain_ref,
):
    @pl.when(pl.program_id(0) == 0)
    def _():
        g_gain_ref[...] = jnp.zeros_like(g_gain_ref)

    low = jnp.bfloat16
    alive = (pos_ref[...] >= 0).astype(jnp.float32)
    sums = sums_ref[...] + twin_ref[...]
    inv = jnp.broadcast_to(lax.rsqrt(sums[:, 0:1] / INNER + EPS), alive.shape)
    pull = inv * inv * inv * jnp.broadcast_to(sums[:, 1:2] / INNER, alive.shape)
    live = inv * alive
    for pair in range(6):
        cols = slice(pair * 128, pair * 128 + 128)
        gain = gain_ref[0:1, cols]
        gate, scanned, d_normed_out = gate_ref[:, cols], scanned_ref[:, cols], dno_ref[:, cols]
        sig = sigmoid(gate)
        gate_act = gate * sig
        gated = scanned * gate_act
        normed_ref[:, cols] = (gated * live * gain).astype(low)
        product = d_normed_out * gated * live
        g_gain_ref[:, cols] += jnp.sum(product.reshape(CHUNK // 8, 8, 128), axis=0)
        d_gated = live * gain * d_normed_out - gated * pull
        d_scan_ref[:, cols] = (d_gated * gate_act).astype(low)
        d_gate_ref[:, cols] = (d_gated * scanned * (sig * (1.0 + gate * (1.0 - sig)))).astype(low)


def gate_stage(first_pre, scanned, d_normed_out, sums, twin_sums, gain, pos):
    rows = first_pre.shape[0]
    at = lambda width: pl.BlockSpec((CHUNK, width), lambda c: (c, 0))
    f32, low = jnp.float32, jnp.bfloat16
    wide = jax.ShapeDtypeStruct((rows, 768), low)
    return pl.pallas_call(
        gate_kernel,
        grid=(rows // CHUNK,),
        in_specs=[
            at(768), at(768), at(768), at(128), at(128), pl.BlockSpec((1, 768), lambda c: (0, 0)), at(128),
        ],
        out_specs=[at(768), at(768), at(768), pl.BlockSpec((8, 768), lambda c: (0, 0))],
        out_shape=[wide, wide, wide, jax.ShapeDtypeStruct((8, 768), f32)],
        compiler_params=pltpu.CompilerParams(vmem_limit_bytes=40 * 2**20),
        cost_estimate=pl.CostEstimate(flops=10**8, bytes_accessed=15 * 10**6, transcendentals=10**6),
        name="gate_stage",
    )(first_pre, scanned, d_normed_out, sums, twin_sums, gain, pos)


def backward_kernel(
    inner_ref, step_ref, state_ref, zi_ref, zs_ref, scanned_ref, dscan_ref, enter_ref, pos_ref,
    taps_ref, taps_s_ref, head_ref, skip_ref, wide_ref,
    d_inner_ref, d_state_ref, d_step_ref, g_taps_ref, g_taps_s_ref, g_skip_ref, g_head_ref,
    halo_i, halo_s, halo_p, hold,
):
    low = jnp.bfloat16

    @pl.when(pl.program_id(0) == 0)
    def _():
        for ref in (halo_i, halo_s, halo_p, hold, g_taps_ref, g_taps_s_ref, g_skip_ref, g_head_ref):
            ref[...] = jnp.zeros_like(ref)

    pos = pos_ref[...]
    pos_ext = jnp.concatenate([pos, halo_p[...]], axis=0)
    marks = [(pos_ext >= lag).astype(jnp.float32) for lag in range(4)]
    lane = lax.broadcasted_iota(jnp.int32, (CHUNK, 128), 1)
    row = lax.broadcasted_iota(jnp.int32, (CHUNK, 128), 0)
    col = lane

    def slope(total):
        sig = sigmoid(total)
        return sig * (1.0 + total * (1.0 - sig)), total * sig

    def fold(value):
        return jnp.sum(value.reshape(CHUNK // 8, 8, 128), axis=0)

    def conv_back(grad, ref, halo, taps, out_ref, g_ref, first):
        cols = slice(first, first + 128)
        ext = jnp.concatenate([grad, halo[:, cols]], axis=0)
        value = ref[:, cols]
        halo[:, cols] = grad[:8]
        g_ref[4, :, cols] += fold(grad)
        total = jnp.zeros((CHUNK, 128), jnp.float32)
        for lag in range(4):
            masked = ext * marks[lag]
            if lag:
                masked = pltpu.roll(masked, CHUNK + 8 - lag, 0)
            masked = masked[:CHUNK]
            g_ref[lag, :, cols] += fold(masked * value)
            total = total + masked * taps[lag : lag + 1, cols]
        out_ref[:, cols] = total.astype(low)

    shifted, step, log_decay, cumulative, linked, carry_in, tail, carry = head_terms(
        step_ref, head_ref, pos
    )
    across = cumulative.T
    wide = dot(
        jnp.concatenate(
            [
                two_term(step),
                two_term(carry_in),
                two_term(tail),
                two_term(jnp.broadcast_to(carry, (16, 128))),
            ],
            axis=0,
        ),
        wide_ref[...],
    )
    slope_b, input_map = slope(zs_ref[:, :128])
    slope_c, output_map = slope(zs_ref[:, 128:])
    input_low, output_low = input_map.astype(low), output_map.astype(low)
    scores = jnp.where(linked, dot(output_low, input_low, ((1,), (1,))), 0.0)
    entering = enter_ref[...]
    d_next = hold[...]
    d_next_low = d_next.astype(low)
    pulled = dot(input_low, d_next_low)
    d_scores = jnp.zeros((CHUNK, 128), jnp.float32)
    d_entered, fed, balance, direct, extra = [], [], [], [], []
    carry_wide = wide[3 * CHUNK : 3 * CHUNK + 1, :]
    carry_grad = jnp.sum(d_next * entering.astype(jnp.float32), axis=0, keepdims=True) * carry_wide
    for pair in range(6):
        cols = slice(pair * 128, pair * 128 + 128)
        slope_x, act = slope(zi_ref[:, cols])
        d_low = dscan_ref[:, cols]
        skip = skip_ref[0:1, cols]
        stepped = (wide[:CHUNK, cols] * act).astype(low)
        stepped_wide = stepped.astype(jnp.float32)
        d_exact = d_low.astype(jnp.float32)
        d_both = jnp.concatenate(
            [jnp.where(lane < 64, d_exact, 0.0).astype(low), jnp.where(lane < 64, 0.0, d_exact).astype(low)],
            axis=0,
        )
        first, second = pair_decay(cumulative, across, pair)
        mixing = jnp.concatenate([(scores * first).astype(low), (scores * second).astype(low)], axis=0)
        d_mixing = dot(d_both, stepped, ((1,), (1,)))
        d_scores = d_scores + d_mixing[:CHUNK] * first + d_mixing[CHUNK:] * second
        tail_cols = wide[2 * CHUNK : 3 * CHUNK, cols]
        tailed = tail_cols * pulled[:, cols]
        d_stepped = dot(mixing, d_both, ((0,), (0,))) + tailed
        extra.append(jnp.sum(stepped_wide * tailed, axis=0, keepdims=True) + carry_grad[:, cols])
        fed.append((tail_cols * stepped_wide).astype(low))
        d_entered.append((wide[CHUNK : 2 * CHUNK, cols] * d_exact).astype(low))
        balance.append(d_exact * (scanned_ref[:, cols] - skip * act) - stepped_wide * d_stepped)
        direct.append(act * d_stepped)
        g_skip_ref[:, cols] += fold(d_exact * act)
        d_act = skip * d_exact + wide[:CHUNK, cols] * d_stepped
        conv_back(d_act * slope_x, inner_ref, halo_i, taps_ref, d_inner_ref, g_taps_ref, pair * 128)
    d_entered = jnp.concatenate(d_entered, axis=1)
    fed = jnp.concatenate(fed, axis=1)
    d_scores = jnp.where(linked, d_scores, 0.0).astype(low)
    d_output = dot(d_scores, input_low) + dot(d_entered, entering, ((1,), (1,)))
    d_input = dot(d_scores, output_low, ((0,), (0,))) + dot(fed, d_next_low, ((1,), (1,)))
    hold[...] = carry_wide * d_next + dot(output_low, d_entered, ((0,), (0,)))
    conv_back(d_input * slope_b, state_ref, halo_s, taps_s_ref, d_state_ref, g_taps_s_ref, 0)
    conv_back(d_output * slope_c, state_ref, halo_s, taps_s_ref, d_state_ref, g_taps_s_ref, 128)
    halo_p[...] = pos[:8]
    spread_back = wide_ref[...]
    extra = jnp.broadcast_to(jnp.concatenate(extra, axis=1), (16, 768))
    stacked = jnp.concatenate(
        split_terms(jnp.concatenate(balance, axis=1), 2)
        + split_terms(jnp.concatenate(direct, axis=1), 2)
        + split_terms(extra, 2),
        axis=0,
    )
    summed = dot(stacked, spread_back, ((1,), (1,)))
    d_sum = summed[:CHUNK] + summed[CHUNK : 2 * CHUNK]
    d_direct = summed[2 * CHUNK : 3 * CHUNK] + summed[3 * CHUNK : 4 * CHUNK]
    d_last = summed[4 * CHUNK : 4 * CHUNK + 1] + summed[4 * CHUNK + 16 : 4 * CHUNK + 17]
    upper = (row <= col).astype(low)
    d_decay = sum(dot(upper, piece) for piece in split_terms(d_sum, 3)) + d_last
    d_step = (d_direct - d_decay * jnp.exp(head_ref[1:2, :])) * sigmoid(shifted)
    d_step = jnp.where(lane < PACK, d_step, 0.0)
    d_step_ref[...] = d_step.astype(low)
    g_head_ref[0] += fold(d_step)
    g_head_ref[1] += fold(d_decay * log_decay)


def forward_core(first_pre, second_pre, d_normed_out, pos, taps, taps_s, heads_lanes, skip, gain, wide):
    rows = first_pre.shape[0]
    at = lambda width, col: pl.BlockSpec((CHUNK, width), lambda c: (c, col))
    whole = lambda arr: pl.BlockSpec(arr.shape, lambda c: (0,) * arr.ndim)
    f32 = jnp.float32
    return pl.pallas_call(
        forward_kernel,
        grid=(rows // CHUNK,),
        in_specs=[
            at(768, 0), at(128, 6), at(768, 0), at(256, 3), at(768, 0), at(128, 0),
            whole(taps), whole(taps_s), whole(heads_lanes), whole(skip), whole(gain), whole(wide),
        ],
        out_specs=[at(768, 0), at(768, 0), at(256, 0), at(768, 0), at(128, 0)],
        out_shape=[
            jax.ShapeDtypeStruct((rows, 768), f32),
            jax.ShapeDtypeStruct((rows, 768), f32),
            jax.ShapeDtypeStruct((rows, 256), f32),
            jax.ShapeDtypeStruct((rows, 768), jnp.bfloat16),
            jax.ShapeDtypeStruct((rows, 128), f32),
        ],
        scratch_shapes=[
            pltpu.VMEM((8, 768), f32), pltpu.VMEM((8, 256), f32), pltpu.VMEM((128, 768), f32),
        ],
        compiler_params=pltpu.CompilerParams(vmem_limit_bytes=40 * 2**20),
        cost_estimate=pl.CostEstimate(flops=8 * 10**9, bytes_accessed=24 * 10**6, transcendentals=4 * 10**6),
        name="mixer_forward",
    )(second_pre, second_pre, first_pre, first_pre, d_normed_out, pos, taps, taps_s, heads_lanes, skip, gain, wide)


def backward_core(first_pre, second_pre, zi, zs, scanned, d_scan, enter, pos, taps, taps_s, heads_lanes, skip, wide):
    rows = first_pre.shape[0]
    count = rows // CHUNK
    at = lambda width, col: pl.BlockSpec((CHUNK, width), lambda c: (count - 1 - c, col))
    whole = lambda shape: pl.BlockSpec(shape, lambda c: (0,) * len(shape))
    f32, low = jnp.float32, jnp.bfloat16
    return pl.pallas_call(
        backward_kernel,
        grid=(count,),
        in_specs=[
            at(768, 0), at(128, 6), at(256, 3), at(768, 0), at(256, 0), at(768, 0), at(768, 0),
            at(768, 0), at(128, 0),
            whole(taps.shape), whole(taps_s.shape), whole(heads_lanes.shape), whole(skip.shape), whole(wide.shape),
        ],
        out_specs=[
            at(768, 0), at(256, 0), at(128, 0),
            whole((5, 8, 768)), whole((5, 8, 256)), whole((8, 768)), whole((2, 8, 128)),
        ],
        out_shape=[
            jax.ShapeDtypeStruct((rows, 768), low),
            jax.ShapeDtypeStruct((rows, 256), low),
            jax.ShapeDtypeStruct((rows, 128), low),
            jax.ShapeDtypeStruct((5, 8, 768), f32),
            jax.ShapeDtypeStruct((5, 8, 256), f32),
            jax.ShapeDtypeStruct((8, 768), f32),
            jax.ShapeDtypeStruct((2, 8, 128), f32),
        ],
        scratch_shapes=[
            pltpu.VMEM((8, 768), f32), pltpu.VMEM((8, 256), f32), pltpu.VMEM((8, 128), f32),
            pltpu.VMEM((128, 768), f32),
        ],
        compiler_params=pltpu.CompilerParams(vmem_limit_bytes=40 * 2**20),
        cost_estimate=pl.CostEstimate(flops=16 * 10**9, bytes_accessed=24 * 10**6, transcendentals=6 * 10**6),
        name="mixer_backward",
    )(second_pre, second_pre, first_pre, zi, zs, scanned, d_scan, enter, pos, taps, taps_s, heads_lanes, skip, wide)


def swap(value):
    return lax.ppermute(value, "tensor", [(0, 1), (1, 0)])


def pair_scatter(part, axis):
    mine = lax.axis_index("tensor")
    width = part.shape[axis] // 2
    keep = lax.dynamic_slice_in_dim(part, mine * width, width, axis)
    send = lax.dynamic_slice_in_dim(part, (1 - mine) * width, width, axis)
    return keep.astype(jnp.float32) + swap(send.astype(jnp.bfloat16)).astype(jnp.float32)


def pad_cols(value, width):
    return jnp.pad(value, ((0, 0), (0, width - value.shape[1])))


MESH_ID = pl.DeviceIdType.MESH
SHARD = 48
PLAN = (("out", 768), ("gate", 768), ("inner", 768), ("small", 256))
PLANE_OF = {"out": 0, "inner": 1, "gate": 2, "small": 3}


def place():
    index = lax.axis_index("dp")
    z = lax.div(index, 4)
    y = lax.rem(lax.div(index, 2), 2)
    x = lax.rem(index, 2)
    at_x = {"dp": z * 4 + y * 2 + (1 - x)}
    at_y = {"dp": z * 4 + (1 - y) * 2 + x}
    at_z = [{"dp": lax.rem(z + step, 4) * 4 + y * 2 + x} for step in range(1, 4)]
    return x, y, z, at_x, at_y, at_z


def greet(peers):
    barrier = pltpu.get_barrier_semaphore()
    for peer in peers:
        pl.semaphore_signal(barrier, inc=1, device_id=peer, device_id_type=MESH_ID)
    pl.semaphore_wait(barrier, len(peers))


def remote(src, dst, send, recv, peer):
    return pltpu.make_async_remote_copy(
        src_ref=src, dst_ref=dst, send_sem=send, recv_sem=recv, device_id=peer, device_id_type=MESH_ID
    )


GATHER_PIECES = (
    (1, 0, 384, 0), (1, 384, 512, 1), (0, 0, 512, 0), (0, 512, 512, 1), (2, 0, 384, 0), (2, 384, 384, 1),
)


def gather_kernel(
    first_ref, second_ref, out_ref, normed_ref, cot_ref,
    full_first, full_second, full_out, rows_ref, cots_ref,
    near_sem, row_sem, z_send, z_recv, one_send, one_recv, two_send, two_recv,
):
    x, y, z, at_x, at_y, at_z = place()
    core = lax.axis_index("tensor")
    twin = {"tensor": 1 - core}
    greet([at_x, at_y, twin] + at_z)
    shards = (first_ref, second_ref, out_ref)
    fulls = (full_first, full_second, full_out)
    z_copies = {}

    def step_zero(piece):
        which, start, width, _ = GATHER_PIECES[piece]
        cols = pl.ds(start, width)
        z_copies[piece] = []
        for step, peer in enumerate(at_z):
            copy = remote(
                shards[which].at[:, cols], fulls[which].at[z, y, x, :, cols],
                z_send.at[piece, step], z_recv.at[piece, step], peer,
            )
            copy.start()
            z_copies[piece].append(copy)

    step_zero(0)
    near = []
    for at, (src, dst) in enumerate(zip(shards, fulls)):
        near.append(pltpu.make_async_copy(src, dst.at[z, y, x], near_sem.at[at]))
    for at, (src, dst) in enumerate(((normed_ref, rows_ref), (cot_ref, cots_ref))):
        near.append(pltpu.make_async_copy(src, dst.at[core], near_sem.at[3 + at]))
        near.append(remote(src, dst.at[core], row_sem.at[at], row_sem.at[2 + at], twin))
    for copy in near:
        copy.start()
    step_zero(1)
    for copy in near[:3]:
        copy.wait()

    def step_one(piece):
        which, start, width, route = GATHER_PIECES[piece]
        for copy in z_copies[piece]:
            copy.wait()
        part = fulls[which].at[:, y, x, :, pl.ds(start, width)]
        copy = remote(part, part, one_send.at[piece], one_recv.at[piece], at_x if route else at_y)
        copy.start()
        return copy

    def step_two(piece):
        which, start, width, route = GATHER_PIECES[piece]
        cols = pl.ds(start, width)
        part = fulls[which].at[:, y, :, :, cols] if route else fulls[which].at[:, :, x, :, cols]
        copy = remote(part, part, two_send.at[piece], two_recv.at[piece], at_y if route else at_x)
        copy.start()
        return copy

    ones, twos = {}, {}
    count = len(GATHER_PIECES)
    for piece in range(count + 1):
        if piece < count:
            ones[piece] = step_one(piece)
        if piece + 2 < count:
            step_zero(piece + 2)
        if piece >= 1:
            ones[piece - 1].wait()
            twos[piece - 1] = step_two(piece - 1)
    for piece in range(count):
        twos[piece].wait()
    for copy in near[3:]:
        copy.wait()


def gather_all(first, second, out, normed, cot):
    low = jnp.bfloat16
    anywhere = pl.BlockSpec(memory_space=pl.ANY)
    count = len(GATHER_PIECES)
    dma = pltpu.SemaphoreType.DMA
    full = lambda arr: jax.ShapeDtypeStruct((4, 2, 2) + arr.shape, low)
    rows = jax.ShapeDtypeStruct((2,) + normed.shape, low)
    got = pl.pallas_call(
        gather_kernel,
        in_specs=[anywhere] * 5,
        out_specs=[anywhere] * 5,
        out_shape=[full(first), full(second), full(out), rows, rows],
        scratch_shapes=[
            dma((5,)), dma((4,)), dma((count, 3)), dma((count, 3)),
            dma((count,)), dma((count,)), dma((count,)), dma((count,)),
        ],
        compiler_params=pltpu.CompilerParams(collective_id=0, has_side_effects=True),
        cost_estimate=pl.CostEstimate(flops=0, bytes_accessed=120 * 10**6, transcendentals=0),
        name="gather_weights",
    )(first, second, out, normed, cot)
    return [item.reshape(-1, item.shape[-1]) for item in got]


def reduce_kernel(
    out_ref, gate_ref, inner_ref, small_ref, vec_ref, moment_ref,
    whole_ref, other_ref, grads_ref, total_ref,
    arrived, summed, arrived_two, held_out, held_gate, held_inner, held_small, slots, moments,
    block, back, vec_in, vec_mid, vec_slots,
    m_send, m_recv, one_send, one_recv, two_send, two_recv, z_send, z_recv, g_send, g_recv,
    p_send, p_recv, t_send, t_recv, v_send, v_recv,
):
    f32, low = jnp.float32, jnp.bfloat16
    x, y, z, at_x, at_y, at_z = place()
    core = lax.axis_index("tensor")
    twin = {"tensor": 1 - core}
    greet([at_x, at_y, twin] + at_z)
    parts = (out_ref, gate_ref, inner_ref, small_ref)
    held = (held_out, held_gate, held_inner, held_small)
    steps_z = [lax.rem(z + step, 4) for step in range(1, 4)]

    vec_x = remote(vec_ref, vec_in.at[0], v_send.at[0], v_recv.at[0], at_x)
    vec_x.start()
    moment_copies = []
    for step, (peer, plane) in enumerate(zip(at_z, steps_z)):
        copy = remote(moment_ref.at[plane], moments.at[z], m_send.at[step], m_recv.at[step], peer)
        copy.start()
        moment_copies.append(copy)

    def span(task, route):
        half = PLAN[task][1] // 2
        return pl.ds(route * half, half), pl.ds(0, half)

    def step_one(task, route):
        cols, mine = span(task, route)
        other = parts[task].at[:, 1 - y, :, :, cols] if route else parts[task].at[:, :, 1 - x, :, cols]
        copy = remote(
            other, arrived.at[task, route, :, :, :, mine], one_send.at[task, route],
            one_recv.at[task, route], at_y if route else at_x,
        )
        copy.start()
        return copy

    def step_two(task, route):
        cols, mine = span(task, route)
        own = parts[task][:, y, :, :, cols] if route else parts[task][:, :, x, :, cols]
        got = arrived[task, route, :, :, :, mine]
        summed[task, route, :, :, :, mine] = (own.astype(f32) + got.astype(f32)).astype(low)
        copy = remote(
            summed.at[task, route, :, 1 - x if route else 1 - y, :, mine],
            arrived_two.at[task, route, :, :, mine], two_send.at[task, route],
            two_recv.at[task, route], at_x if route else at_y,
        )
        copy.start()
        return copy

    def settle(task, route):
        cols, mine = span(task, route)
        own = summed[task, route, :, x if route else y, :, mine]
        got = arrived_two[task, route, :, :, mine]
        held[task][:, :, cols] = (own.astype(f32) + got.astype(f32)).astype(low)

    def to_plane(task):
        plane, width = PLANE_OF[PLAN[task][0]], PLAN[task][1]

        @pl.when(z != plane)
        def _():
            remote(
                held[task], slots.at[z, :, :, pl.ds(0, width)], z_send.at[task], z_recv.at[z],
                {"dp": plane * 4 + y * 2 + x},
            ).start()

    ones, twos = {}, {}
    for task in range(2):
        for route in range(2):
            ones[task, route] = step_one(task, route)
    vec_x.wait()
    vec_mid[0] = vec_ref[...] + vec_in[0]
    vec_y = remote(vec_mid.at[0], vec_in.at[1], v_send.at[1], v_recv.at[1], at_y)
    vec_y.start()
    for task in range(5):
        for route in range(2):
            if task < 4:
                ones[task, route].wait()
                twos[task, route] = step_two(task, route)
            if task + 2 < 4:
                ones[task + 2, route] = step_one(task + 2, route)
        if task >= 1:
            for route in range(2):
                twos[task - 1, route].wait()
                settle(task - 1, route)
            to_plane(task - 1)
        if task == 0:
            vec_y.wait()
            vec_mid[1] = vec_mid[0] + vec_in[1]
            vec_slots[z] = vec_mid[1]
            vec_z = []
            for step, peer in enumerate(at_z):
                copy = remote(vec_mid.at[1], vec_slots.at[z], v_send.at[2 + step], v_recv.at[2 + step], peer)
                copy.start()
                vec_z.append(copy)
        if task == 1:
            for copy in moment_copies:
                copy.wait()
            moments[z] = moment_ref[z]
            for copy in vec_z:
                copy.wait()
            total_ref[...] = (vec_slots[0] + vec_slots[1]) + (vec_slots[2] + vec_slots[3])

    for task, (name, width) in enumerate(PLAN):
        plane = PLANE_OF[name]
        cols = pl.ds(0, width)

        @pl.when(z == plane)
        def _():
            for source in range(4):
                if source != plane:
                    remote(
                        held[task], slots.at[source, :, :, cols], z_send.at[task], z_recv.at[source], at_x
                    ).wait_recv()
            total = held[task][...].astype(f32)
            for source in range(4):
                if source != plane:
                    total = total + slots[source, :, :, cols].astype(f32)
            if width < 768:
                back[...] = jnp.zeros_like(back)
                block[...] = jnp.zeros_like(block)
            back[:, :, cols] = total.astype(low)
            block[:, :, cols] = (MU_MAT * moments[:, :, cols].astype(f32) + total).astype(low)

    half = 384
    routes = (pl.ds(0, half), pl.ds(half, half))
    for row in range(4):
        whole_ref[row, y, x] = block[row]
    plane_one = []
    for route, peer in enumerate((at_x, at_y)):
        copy = remote(
            block.at[:, :, routes[route]], whole_ref.at[:, y, x, :, routes[route]],
            p_send.at[0, route], p_recv.at[0, route], peer,
        )
        copy.start()
        plane_one.append(copy)
    twin_own = remote(block, other_ref.at[:, y, x], t_send.at[0], t_recv.at[0], twin)
    twin_own.start()
    grads_ref[z] = back[z]
    returns = []
    for step, (peer, plane) in enumerate(zip(at_z, steps_z)):
        copy = remote(back.at[plane], grads_ref.at[z], g_send.at[step], g_recv.at[step], peer)
        copy.start()
        returns.append(copy)
    plane_two = []
    for route, peer in enumerate((at_y, at_x)):
        plane_one[route].wait()
        part = (
            whole_ref.at[:, :, x, :, routes[1]] if route else whole_ref.at[:, y, :, :, routes[0]]
        )
        copy = remote(part, part, p_send.at[1, route], p_recv.at[1, route], peer)
        copy.start()
        plane_two.append(copy)
    twins = [twin_own]
    for route in range(2):
        src = whole_ref.at[:, 1 - y, x, :, routes[1]] if route else whole_ref.at[:, y, 1 - x, :, routes[0]]
        dst = other_ref.at[:, 1 - y, x, :, routes[1]] if route else other_ref.at[:, y, 1 - x, :, routes[0]]
        copy = remote(src, dst, t_send.at[1 + route], t_recv.at[1 + route], twin)
        copy.start()
        twins.append(copy)
    for route in range(2):
        plane_two[route].wait()
        src = whole_ref.at[:, :, 1 - x, :, routes[1]] if route else whole_ref.at[:, 1 - y, :, :, routes[0]]
        dst = other_ref.at[:, :, 1 - x, :, routes[1]] if route else other_ref.at[:, 1 - y, :, :, routes[0]]
        copy = remote(src, dst, t_send.at[3 + route], t_recv.at[3 + route], twin)
        copy.start()
        twins.append(copy)
    for copy in twins + returns:
        copy.wait()
    for task, (name, width) in enumerate(PLAN):
        plane = PLANE_OF[name]

        @pl.when(z != plane)
        def _():
            remote(
                held[task], slots.at[z, :, :, pl.ds(0, width)], z_send.at[task], z_recv.at[z],
                {"dp": plane * 4 + y * 2 + x},
            ).wait_send()


def reduce_all(parts, vectors, moments):
    f32, low = jnp.float32, jnp.bfloat16
    vmem = pl.BlockSpec(memory_space=pltpu.VMEM)
    dma = pltpu.SemaphoreType.DMA
    parts = [part.reshape(4, 2, 2, SHARD, part.shape[1]) for part in parts]
    buf = pltpu.VMEM
    whole, other, grads, total = pl.pallas_call(
        reduce_kernel,
        in_specs=[vmem] * 6,
        out_specs=[vmem] * 4,
        out_shape=[
            jax.ShapeDtypeStruct((4, 2, 2, SHARD, 768), low),
            jax.ShapeDtypeStruct((4, 2, 2, SHARD, 768), low),
            jax.ShapeDtypeStruct((4, SHARD, 768), low),
            jax.ShapeDtypeStruct(vectors.shape, f32),
        ],
        scratch_shapes=[
            buf((4, 2, 4, 2, SHARD, 384), low), buf((4, 2, 4, 2, SHARD, 384), low),
            buf((4, 2, 4, SHARD, 384), low),
            buf((4, SHARD, 768), low), buf((4, SHARD, 768), low), buf((4, SHARD, 768), low),
            buf((4, SHARD, 256), low),
            buf((4, 4, SHARD, 768), low), buf((4, SHARD, 768), low),
            buf((4, SHARD, 768), low), buf((4, SHARD, 768), low),
            buf((2,) + vectors.shape, f32), buf((2,) + vectors.shape, f32), buf((4,) + vectors.shape, f32),
            dma((3,)), dma((3,)), dma((4, 2)), dma((4, 2)), dma((4, 2)), dma((4, 2)),
            dma((4,)), dma((4,)), dma((3,)), dma((3,)), dma((2, 2)), dma((2, 2)),
            dma((5,)), dma((5,)), dma((5,)), dma((5,)),
        ],
        compiler_params=pltpu.CompilerParams(
            collective_id=1, has_side_effects=True, vmem_limit_bytes=48 * 2**20
        ),
        cost_estimate=pl.CostEstimate(flops=0, bytes_accessed=150 * 10**6, transcendentals=0),
        name="reduce_grads",
    )(*parts, vectors, moments)
    return whole.reshape(768, 768), other.reshape(768, 768), grads, total


def newton_kernel(full_ref, out_ref, current, gram, mix):
    f32, low = jnp.float32, jnp.bfloat16
    rows, cols = current.shape
    tile = 256
    count = rows // tile
    row_ids = lax.broadcasted_iota(jnp.int32, (tile, tile), 0)
    col_ids = lax.broadcasted_iota(jnp.int32, (tile, tile), 1)
    blocks = [pl.ds(at * tile, tile) for at in range(count)]

    def symmetric(source, store):
        for first in range(count):
            for second in range(first, count):
                store(first, second, dot(source[blocks[first], :], source[blocks[second], :], ((1,), (1,))))

    def put(ref, first, second, value):
        ref[blocks[first], blocks[second]] = value.astype(low)
        if first != second:
            ref[blocks[second], blocks[first]] = value.T.astype(low)

    firsts = {}
    symmetric(full_ref, lambda first, second, value: firsts.update({(first, second): value}))
    trace = sum(
        jnp.sum(jnp.where(row_ids == col_ids, firsts[at, at], 0.0), keepdims=True) for at in range(count)
    )
    scale = jnp.sqrt(trace) + 1e-07
    inverse, inverse_square = 1.0 / scale, 1.0 / (scale * scale)
    for (first, second), value in firsts.items():
        put(gram, first, second, value * inverse_square)
    for at in range(count):
        current[blocks[at], :] = (full_ref[blocks[at], :].astype(f32) * inverse).astype(low)

    def mixed():
        def store(first, second, value):
            piece = gram[blocks[first], blocks[second]].astype(f32)
            put(mix, first, second, NS_B * piece + NS_C * value)

        symmetric(gram, store)

    def turn(_, carry):
        mixed()

        def update(at, carry):
            here = pl.ds(pl.multiple_of(at * tile, tile), tile)
            held = current[:, here]
            current[:, here] = (NS_A * held.astype(f32) + dot(mix[...], held)).astype(low)
            return carry

        lax.fori_loop(0, cols // tile, update, 0)
        symmetric(current, lambda first, second, value: put(gram, first, second, value))
        return carry

    lax.fori_loop(0, NS_STEPS - 1, turn, 0)
    mixed()
    for at in range(out_ref.shape[1] // tile):
        here = pl.ds(at * tile, tile)
        held = current[:, here]
        out_ref[:, here] = (NS_A * held.astype(f32) + dot(mix[...], held)).astype(low)


def newton(full, width):
    low = jnp.bfloat16
    rows = full.shape[0]
    return pl.pallas_call(
        newton_kernel,
        in_specs=[pl.BlockSpec(memory_space=pltpu.VMEM)],
        out_specs=pl.BlockSpec(memory_space=pltpu.VMEM),
        out_shape=jax.ShapeDtypeStruct((rows, width), low),
        scratch_shapes=[
            pltpu.VMEM(full.shape, low), pltpu.VMEM((rows, rows), low), pltpu.VMEM((rows, rows), low),
        ],
        compiler_params=pltpu.CompilerParams(vmem_limit_bytes=48 * 2**20),
        cost_estimate=pl.CostEstimate(flops=20 * 10**9, bytes_accessed=4 * 10**6, transcendentals=0),
        name="newton_schulz",
    )(full)


def return_kernel(done_ref, back_ref, send, recv):
    x, y, z, _, _, at_z = place()
    greet(at_z)
    copies = []
    for step, peer in enumerate(at_z):
        plane = lax.rem(z + step + 1, 4)
        copies.append(
            remote(done_ref.at[plane, y, x], back_ref.at[z], send.at[step], recv.at[step], peer)
        )
        copies[-1].start()
    back_ref[z] = done_ref[z, y, x]
    for copy in copies:
        copy.wait()


def return_rows(done):
    vmem = pl.BlockSpec(memory_space=pltpu.VMEM)
    dma = pltpu.SemaphoreType.DMA
    return pl.pallas_call(
        return_kernel,
        in_specs=[vmem],
        out_specs=vmem,
        out_shape=jax.ShapeDtypeStruct((4, SHARD, 768), done.dtype),
        scratch_shapes=[dma((3,)), dma((3,))],
        compiler_params=pltpu.CompilerParams(collective_id=2, has_side_effects=True, vmem_limit_bytes=16 * 2**20),
        cost_estimate=pl.CostEstimate(flops=0, bytes_accessed=20 * 10**6, transcendentals=0),
        name="return_rows",
    )(done.reshape(4, 2, 2, SHARD, 768))


def orthogonal_owned(own, other, state_width):
    width = own.shape[1]
    small = lax.axis_index("dp") // 4 == PLANE_OF["small"]
    full = jnp.concatenate([own, other], axis=1)
    col = jnp.arange(2 * width)[None, :] % width
    keep = (col < state_width) == (lax.axis_index("tensor") == 0)
    full = jnp.where(small & ~keep, jnp.zeros_like(full), full)
    done = newton(full, width + 2 * state_width)
    half, lent = done[:, :width], done[:, width:]
    edge = half[:, : 2 * state_width]
    edge = edge + jnp.where(small, swap(lent), jnp.zeros_like(lent))
    return jnp.concatenate([edge, half[:, 2 * state_width :]], axis=1)


def paired_shards(
    stream,
    cotangent,
    positions,
    norm_gain,
    w_gate,
    w_inner,
    w_state,
    w_step,
    conv_inner,
    conv_state,
    head_params,
    gate_gain,
    w_out,
    moment_norm_gain,
    moment_w_gate,
    moment_w_inner,
    moment_w_state,
    moment_w_step,
    moment_conv_inner,
    moment_conv_state,
    moment_head_params,
    moment_gate_gain,
    moment_w_out,
):
    low = jnp.bfloat16
    core = lax.axis_index("tensor")
    room = w_gate.shape[1]
    wide = w_state.shape[1]
    col_width = wide // 2
    heads = w_step.shape[1]
    inv_first = lax.rsqrt(jnp.mean(stream * stream, axis=1, keepdims=True) + EPS)
    normed = (stream * inv_first * norm_gain).astype(low)
    first_pack = jnp.concatenate([w_gate.astype(low), w_state.astype(low)], axis=1)
    step_low = w_step.astype(low)
    step_lanes = jnp.concatenate([pad_cols(step_low, PACK), pad_cols(step_low, 128 - PACK)], axis=1)
    second_pack = jnp.concatenate([w_inner.astype(low), step_lanes], axis=1)
    full_first, full_second, full_out, token_rows, cotangent_rows = gather_all(
        first_pack, second_pack, w_out.astype(low).T, normed, cotangent.astype(low)
    )
    first_pre = jnp.dot(token_rows, full_first, preferred_element_type=jnp.float32)
    second_pre = jnp.dot(token_rows, full_second, preferred_element_type=jnp.float32)
    gate_pre = first_pre[:, :room]
    pos = jnp.broadcast_to(positions.astype(jnp.float32)[:, None], (positions.shape[0], 128))
    taps = jnp.pad(conv_inner, ((0, 3), (0, 0)))
    taps_s = jnp.pad(conv_state, ((0, 3), (0, 0)))
    lanes = jnp.concatenate([pad_cols(head_params, PACK), pad_cols(head_params, 128 - PACK)], axis=1)
    lanes = jnp.pad(lanes, ((0, 5), (0, 0)))
    skip = jnp.repeat(head_params[2], room // heads)[None, :]
    wide_map = expand_matrix()
    d_normed_out = jnp.dot(cotangent_rows, full_out, preferred_element_type=jnp.float32)
    scanned, zi, zs, enter, sums = forward_core(
        first_pre, second_pre, d_normed_out, pos, taps, taps_s, lanes, skip, gate_gain[None, :], wide_map
    )
    normed_out, d_gate_pre, d_scan, gain_part = gate_stage(
        first_pre, scanned, d_normed_out, sums, swap(sums), gate_gain[None, :], pos
    )
    grad_gate_part = jnp.sum(gain_part, axis=0)
    mixed = pair_scatter(times_transpose(normed_out, full_out).astype(low), 0)
    output = stream + mixed
    out_part = contract_rows(cotangent_rows, normed_out).astype(low)
    gate_part = contract_rows(token_rows, d_gate_pre).astype(low)
    d_inner, d_state_part, d_step, taps_part, taps_s_part, skip_part, head_part = backward_core(
        first_pre, second_pre, zi, zs, scanned, d_scan, enter, pos, taps, taps_s, lanes, skip, wide_map
    )
    grad_conv_inner_part = jnp.sum(taps_part, axis=1)
    grad_conv_state_part = jnp.sum(taps_s_part, axis=1)
    head_rows = jnp.sum(head_part, axis=1)[:, :heads]
    skip_row = jnp.sum(jnp.sum(skip_part, axis=0).reshape(heads, -1), axis=1)
    grad_head_part = jnp.concatenate([head_rows, skip_row[None, :]], axis=0)
    d_state_low = pair_scatter(d_state_part, 1).astype(low)
    d_tail = jnp.concatenate([d_inner, d_state_low, d_step], axis=1)
    col_first = core * col_width
    state_cols = lax.dynamic_slice_in_dim(full_first, room + col_first, col_width, 1)
    tail_weights = jnp.concatenate(
        [full_second[:, :room], state_cols, full_second[:, room:]], axis=1
    )
    total = times_transpose(d_gate_pre, full_first[:, :room])
    total = total + times_transpose(d_tail, tail_weights)
    d_normed = pair_scatter(total.astype(low), 0)
    tail_part = contract_rows(token_rows, d_tail).astype(low)
    grad_norm_part = jnp.sum(d_normed * stream * inv_first, axis=0)
    weighted = d_normed * norm_gain
    d_stream = (
        cotangent
        + inv_first * weighted
        - stream * inv_first**3 * jnp.mean(weighted * stream, axis=1, keepdims=True)
    )
    shared = jnp.concatenate([grad_conv_state_part, grad_norm_part.reshape(-1, wide)], axis=0)
    shared = shared + swap(shared)
    vectors = jnp.concatenate(
        [
            grad_conv_inner_part,
            grad_gate_part[None, :],
            pad_cols(grad_head_part, room),
            pad_cols(shared, room),
        ],
        axis=0,
    )
    vectors = jnp.pad(vectors, ((0, -vectors.shape[0] % 8), (0, 0)))
    small_moment = pad_cols(jnp.concatenate([moment_w_state, moment_w_step], axis=1), room)
    moment_rows = jnp.stack([moment_w_out.T, moment_w_inner, moment_w_gate, small_moment]).astype(low)
    own, other, grads, vectors = reduce_all(
        (out_part, gate_part, tail_part[:, :room], tail_part[:, room:]), vectors, moment_rows
    )
    grads = grads.astype(jnp.float32)
    grad_gate_w = grads[2]
    grad_inner_w = grads[1]
    grad_out_w = grads[0].T
    grad_state_w = grads[3][:, :col_width]
    grad_step_w = grads[3][:, col_width : col_width + heads]
    grad_conv_inner = vectors[:5]
    grad_gate_gain = vectors[5]
    grad_head = vectors[6:9, :heads]
    grad_conv_state = vectors[9:14, :wide]
    grad_norm = vectors[14:17, :wide].reshape(-1)
    m_gate = MU_MAT * moment_w_gate + grad_gate_w
    m_inner = MU_MAT * moment_w_inner + grad_inner_w
    m_state = MU_MAT * moment_w_state + grad_state_w
    m_step = MU_MAT * moment_w_step + grad_step_w
    m_out = MU_MAT * moment_w_out + grad_out_w
    mine = return_rows(orthogonal_owned(own, other, col_width)).astype(jnp.float32)
    new_gate = w_gate - LR_MAT * spread(D, INNER) * mine[2]
    new_inner = w_inner - LR_MAT * spread(D, INNER) * mine[1]
    new_out = w_out - LR_MAT * spread(INNER, D) * mine[0].T
    new_step = w_step - LR_MAT * spread(D, HEADS) * mine[3][:, col_width : col_width + heads]
    state_slice = lax.dynamic_slice_in_dim(w_state, col_first, col_width, 1)
    new_state = state_slice - LR_MAT * spread(D, 2 * STATE) * mine[3][:, :col_width]
    m_norm = MU_VEC * moment_norm_gain + grad_norm
    m_conv_inner = MU_VEC * moment_conv_inner + grad_conv_inner
    m_conv_state = MU_VEC * moment_conv_state + grad_conv_state
    m_head = MU_VEC * moment_head_params + grad_head
    m_gate_gain = MU_VEC * moment_gate_gain + grad_gate_gain
    return (
        output,
        d_stream,
        grad_norm,
        grad_gate_w,
        grad_inner_w,
        grad_state_w,
        grad_step_w,
        grad_conv_inner,
        grad_conv_state,
        grad_head,
        grad_gate_gain,
        grad_out_w,
        norm_gain - LR_VEC * m_norm,
        new_gate,
        new_inner,
        new_state,
        new_step,
        conv_inner - LR_VEC * m_conv_inner,
        conv_state - LR_VEC * m_conv_state,
        head_params - LR_VEC * m_head,
        gate_gain - LR_VEC * m_gate_gain,
        new_out,
        m_norm,
        m_gate,
        m_inner,
        m_state,
        m_step,
        m_conv_inner,
        m_conv_state,
        m_head,
        m_gate_gain,
        m_out,
    )


def solution(mesh):
    paired = mesh.shape["dp"] == 16 and mesh.shape["tensor"] == 2
    return jax.shard_map(
        paired_shards if paired else shards,
        mesh=mesh,
        in_specs=(
            P(("dp", "tensor"), None),
            P(("dp", "tensor"), None),
            P("dp"),
            P(),
            P("dp", "tensor"),
            P("dp", "tensor"),
            P("dp", None),
            P("dp", "tensor"),
            P(None, "tensor"),
            P(),
            P(None, "tensor"),
            P("tensor"),
            P("tensor", "dp"),
            P(),
            P("dp", "tensor"),
            P("dp", "tensor"),
            P("dp", "tensor"),
            P("dp", "tensor"),
            P(None, "tensor"),
            P(),
            P(None, "tensor"),
            P("tensor"),
            P("tensor", "dp"),
        ),
        out_specs=(
            P(("dp", "tensor"), None),
            P(("dp", "tensor"), None),
            P(),
            P("dp", "tensor"),
            P("dp", "tensor"),
            P("dp", "tensor"),
            P("dp", "tensor"),
            P(None, "tensor"),
            P(),
            P(None, "tensor"),
            P("tensor"),
            P("tensor", "dp"),
            P(),
            P("dp", "tensor"),
            P("dp", "tensor"),
            P("dp", "tensor"),
            P("dp", "tensor"),
            P(None, "tensor"),
            P(),
            P(None, "tensor"),
            P("tensor"),
            P("tensor", "dp"),
            P(),
            P("dp", "tensor"),
            P("dp", "tensor"),
            P("dp", "tensor"),
            P("dp", "tensor"),
            P(None, "tensor"),
            P(),
            P(None, "tensor"),
            P("tensor"),
            P("tensor", "dp"),
        ),
        check_vma=False,
    )
```

```python
from functools import partial
import math

import jax
import jax.numpy as jnp
from jax import lax
from jax.experimental import pallas as pl
from jax.experimental.pallas import tpu as pltpu
from jax.sharding import PartitionSpec as P

D = 768
INNER = 1536
HEADS = 24
STATE = 128
BLOCK = 256
NS_STEPS = 5


EPS = 1e-05
NS_A = 3.4445
NS_B = -4.775
NS_C = 2.0315
MU_MAT = 0.95
MU_VEC = 0.9
LR_MAT = 0.3
LR_VEC = 0.001
HIGH = lax.Precision.HIGHEST
CORE = lax.Precision.DEFAULT


def silu_slope(value):
    sig = jax.nn.sigmoid(value)
    return sig * (1.0 + value * (1.0 - sig))


def contract_rows(left, right):
    return lax.dot_general(
        left, right, (((0,), (0,)), ((), ())), preferred_element_type=jnp.float32
    )


def times_transpose(left, right):
    return lax.dot_general(
        left, right, (((1,), (1,)), ((), ())), preferred_element_type=jnp.float32
    )


def causal_conv(signal, taps, positions):
    length = signal.shape[0]
    reach = taps.shape[0] - 1
    total = jnp.zeros_like(signal) + taps[reach]
    for lag_step in range(reach):
        moved = jnp.pad(signal, ((lag_step, 0), (0, 0)))[:length]
        total = total + jnp.where((positions >= lag_step)[:, None], moved * taps[lag_step], 0.0)
    return jax.nn.silu(total)


def mixer_core(inner_pre, state_pre, step_pre, conv_inner, conv_state, head_params, positions, precision=HIGH):
    length = inner_pre.shape[0]
    heads = step_pre.shape[1]
    head_size = inner_pre.shape[1] // heads
    states = state_pre.shape[1] // 2
    blocks = length // BLOCK
    inner_act = causal_conv(inner_pre, conv_inner, positions).reshape(
        blocks, BLOCK, heads, head_size
    )
    state_act = causal_conv(state_pre, conv_state, positions)
    input_map = state_act[:, :states].reshape(blocks, BLOCK, states)
    output_map = state_act[:, states:].reshape(blocks, BLOCK, states)
    step_size = jax.nn.softplus(step_pre + head_params[0])
    log_decay = (step_size * -jnp.exp(head_params[1])).reshape(blocks, BLOCK, heads)
    step_size = step_size.reshape(blocks, BLOCK, heads)
    resets = (positions <= 0).astype(jnp.float32).reshape(blocks, BLOCK)
    order = jnp.arange(BLOCK)
    lower = (order[:, None] >= order[None, :]).astype(jnp.float32)
    cumulative = jnp.einsum("ij,cjh->cih", lower, log_decay, precision=HIGH)
    seen = jnp.einsum("ij,cj->ci", lower, resets, precision=HIGH)
    linked = (seen[:, :, None] == seen[:, None, :]) & (order[:, None] >= order[None, :])[None]
    linked_heads = linked[..., None]
    spacing = cumulative[:, :, None, :] - cumulative[:, None, :, :]
    decay = jnp.where(linked_heads, jnp.exp(jnp.where(linked_heads, spacing, 0.0)), 0.0)
    scores = jnp.einsum("cin,cjn->cij", output_map, input_map, precision=precision)
    mixing = scores[..., None] * decay * step_size[:, None, :, :]
    within = jnp.einsum("cijh,cjhp->cihp", mixing, inner_act, precision=precision)
    tail_linked = (seen[:, -1:] == seen)[..., None]
    tail = (
        jnp.where(
            tail_linked,
            jnp.exp(jnp.where(tail_linked, cumulative[:, -1:, :] - cumulative, 0.0)),
            0.0,
        )
        * step_size
    )
    own_state = jnp.einsum("cjh,cjhp,cjn->chpn", tail, inner_act, input_map, precision=precision)
    carry_rate = jnp.exp(cumulative[:, -1, :]) * (seen[:, -1] == 0).astype(jnp.float32)[:, None]

    state = jnp.zeros((heads, head_size, states), jnp.float32)
    entering = []
    for block in range(blocks):
        entering.append(state)
        state = carry_rate[block][:, None, None] * state + own_state[block]
    entering = jnp.stack(entering)
    fresh = (seen == 0)[..., None]
    carry_in = jnp.where(fresh, jnp.exp(cumulative), 0.0)
    across = (
        jnp.einsum("cin,chpn->cihp", output_map, entering, precision=precision) * carry_in[..., None]
    )
    result = within + across + head_params[2][None, None, :, None] * inner_act
    return result.reshape(length, heads * head_size)


def gram_total(low):
    return lax.psum(
        jnp.dot(low, low.T, preferred_element_type=jnp.float32).astype(jnp.bfloat16), "tensor"
    ).astype(jnp.float32)


def orthogonalize(matrix):
    first = gram_total(matrix.astype(jnp.bfloat16))
    scale = jnp.sqrt(jnp.trace(first)) + 1e-07
    current = (matrix / scale).astype(jnp.bfloat16)
    gram = (first / (scale * scale)).astype(jnp.bfloat16)
    for turn in range(NS_STEPS):
        if turn > 0:
            gram = gram_total(current).astype(jnp.bfloat16)
        applied = jnp.dot(gram, current, preferred_element_type=jnp.float32)
        twice = jnp.dot(gram, applied.astype(jnp.bfloat16), preferred_element_type=jnp.float32)
        current = (NS_A * current.astype(jnp.float32) + NS_B * applied + NS_C * twice).astype(
            jnp.bfloat16
        )
    return current.astype(jnp.float32)


def spread(rows, cols):
    return math.sqrt(max(1.0, rows / cols))


def shards(
    stream,
    cotangent,
    positions,
    norm_gain,
    w_gate,
    w_inner,
    w_state,
    w_step,
    conv_inner,
    conv_state,
    head_params,
    gate_gain,
    w_out,
    moment_norm_gain,
    moment_w_gate,
    moment_w_inner,
    moment_w_state,
    moment_w_step,
    moment_conv_inner,
    moment_conv_state,
    moment_head_params,
    moment_gate_gain,
    moment_w_out,
):
    dp_count = lax.axis_size("dp")
    inv_first = lax.rsqrt(jnp.mean(stream * stream, axis=1, keepdims=True) + EPS)
    normed = (stream * inv_first * norm_gain).astype(jnp.bfloat16)
    token_rows, cotangent_rows = (
        lax.all_gather(normed, "tensor", axis=0, tiled=True),
        lax.all_gather(cotangent.astype(jnp.bfloat16), "tensor", axis=0, tiled=True),
    )
    local_weights = (
        w_gate.astype(jnp.bfloat16),
        w_inner.astype(jnp.bfloat16),
        w_step.astype(jnp.bfloat16),
        w_state.astype(jnp.bfloat16),
        w_out.astype(jnp.bfloat16),
    )
    full_gate, full_inner, full_step, full_state, full_out = (
        lax.all_gather(local_weights[0], "dp", axis=0, tiled=True),
        lax.all_gather(local_weights[1], "dp", axis=0, tiled=True),
        lax.all_gather(local_weights[2], "dp", axis=0, tiled=True),
        lax.all_gather(local_weights[3], "dp", axis=0, tiled=True),
        lax.all_gather(local_weights[4], "dp", axis=1, tiled=True),
    )
    gate_pre = jnp.dot(token_rows, full_gate, preferred_element_type=jnp.float32)
    inner_pre = jnp.dot(token_rows, full_inner, preferred_element_type=jnp.float32)
    state_pre = jnp.dot(token_rows, full_state, preferred_element_type=jnp.float32)
    step_pre = jnp.dot(token_rows, full_step, preferred_element_type=jnp.float32)
    alive = (positions >= 0).astype(jnp.float32)[:, None]
    scanned, core_back = jax.vjp(
        partial(mixer_core, positions=positions),
        inner_pre,
        state_pre,
        step_pre,
        conv_inner,
        conv_state,
        head_params,
    )
    gate_act = jax.nn.silu(gate_pre)
    gated = scanned * gate_act
    square_sum = lax.psum(jnp.sum(gated * gated, axis=1), "tensor")
    inv_second = lax.rsqrt(square_sum / INNER + EPS)[:, None]
    normed_out = (gated * inv_second * gate_gain * alive).astype(jnp.bfloat16)
    mixed = lax.psum_scatter(
        jnp.dot(normed_out, full_out, preferred_element_type=jnp.float32).astype(jnp.bfloat16),
        "tensor",
        scatter_dimension=0,
        tiled=True,
    ).astype(jnp.float32)
    output = stream + mixed
    d_normed_out = times_transpose(cotangent_rows, full_out)
    grad_out_part = contract_rows(normed_out, cotangent_rows)
    scaled = d_normed_out * gate_gain * alive
    grad_gate_part = jnp.sum(d_normed_out * gated * inv_second * alive, axis=0)
    cross_sum = lax.psum(jnp.sum(scaled * gated, axis=1), "tensor")
    d_gated = inv_second * scaled - gated * inv_second**3 * (cross_sum / INNER)[:, None]
    d_gate_pre = (d_gated * scanned * silu_slope(gate_pre)).astype(jnp.bfloat16)
    d_inner, d_state_part, d_step, grad_conv_inner_part, grad_conv_state_part, grad_head_part = (
        core_back(d_gated * gate_act)
    )
    d_state_cols = lax.psum_scatter(
        d_state_part.astype(jnp.bfloat16), "tensor", scatter_dimension=1, tiled=True
    ).astype(jnp.float32)
    d_inner_low = d_inner.astype(jnp.bfloat16)
    d_state_low = d_state_cols.astype(jnp.bfloat16)
    d_step_low = d_step.astype(jnp.bfloat16)
    col_width = d_state_cols.shape[1]
    col_first = lax.axis_index("tensor") * col_width
    state_cols = lax.dynamic_slice_in_dim(full_state, col_first, col_width, 1)
    total = times_transpose(d_gate_pre, full_gate)
    total = total + times_transpose(d_inner_low, full_inner)
    total = total + times_transpose(d_state_low, state_cols)
    d_normed = lax.psum_scatter(
        (total + times_transpose(d_step_low, full_step)).astype(jnp.bfloat16),
        "tensor",
        scatter_dimension=0,
        tiled=True,
    ).astype(jnp.float32)
    grad_gate_w, grad_inner_w, grad_state_w, grad_step_w, grad_out_w = (
        lax.psum_scatter(
            contract_rows(token_rows, d_gate_pre).astype(jnp.bfloat16),
            "dp",
            scatter_dimension=0,
            tiled=True,
        ).astype(jnp.float32),
        lax.psum_scatter(
            contract_rows(token_rows, d_inner_low).astype(jnp.bfloat16),
            "dp",
            scatter_dimension=0,
            tiled=True,
        ).astype(jnp.float32),
        lax.psum_scatter(
            contract_rows(token_rows, d_state_low).astype(jnp.bfloat16),
            "dp",
            scatter_dimension=0,
            tiled=True,
        ).astype(jnp.float32),
        lax.psum_scatter(
            contract_rows(token_rows, d_step_low).astype(jnp.bfloat16),
            "dp",
            scatter_dimension=0,
            tiled=True,
        ).astype(jnp.float32),
        lax.psum_scatter(
            grad_out_part.astype(jnp.bfloat16), "dp", scatter_dimension=1, tiled=True
        ).astype(jnp.float32),
    )
    grad_norm_part = jnp.sum(d_normed * stream * inv_first, axis=0)
    weighted = d_normed * norm_gain
    d_stream = (
        cotangent
        + inv_first * weighted
        - stream * inv_first**3 * jnp.mean(weighted * stream, axis=1, keepdims=True)
    )
    grad_conv_inner, grad_gate_gain, grad_head = lax.psum(
        (grad_conv_inner_part, grad_gate_part, grad_head_part), "dp"
    )
    grad_conv_state, grad_norm = lax.psum((grad_conv_state_part, grad_norm_part), ("dp", "tensor"))
    m_gate = MU_MAT * moment_w_gate + grad_gate_w
    m_inner = MU_MAT * moment_w_inner + grad_inner_w
    m_state = MU_MAT * moment_w_state + grad_state_w
    m_step = MU_MAT * moment_w_step + grad_step_w
    m_out = MU_MAT * moment_w_out + grad_out_w
    room = w_gate.shape[1]
    shard_rows = w_gate.shape[0]
    stacked = jnp.stack(
        [
            m_gate,
            m_inner,
            m_out.T,
            jnp.pad(m_step, ((0, 0), (0, room - m_step.shape[1]))),
            jnp.pad(m_state, ((0, 0), (0, room - m_state.shape[1]))),
        ]
    )
    matrix_count = stacked.shape[0]
    owner_index = jnp.arange(matrix_count, dtype=jnp.int32) * dp_count // matrix_count
    select = (owner_index[None, :] == jnp.arange(dp_count, dtype=jnp.int32)[:, None]).astype(
        jnp.float32
    )
    outgoing = jnp.einsum("jk,krc->jrc", select, stacked, precision=HIGH)
    owned = (
        lax.all_to_all(outgoing.astype(jnp.bfloat16), "dp", split_axis=0, concat_axis=0, tiled=True)
        .astype(outgoing.dtype)
        .reshape(dp_count * shard_rows, room)
    )
    ortho = orthogonalize(owned)
    returned = lax.all_to_all(
        ortho.reshape(dp_count, shard_rows, room).astype(jnp.bfloat16),
        "dp",
        split_axis=0,
        concat_axis=0,
        tiled=True,
    ).astype(jnp.float32)
    mine = jnp.einsum("jk,jrc->krc", select, returned, precision=HIGH)
    new_gate = w_gate - LR_MAT * spread(D, INNER) * mine[0]
    new_inner = w_inner - LR_MAT * spread(D, INNER) * mine[1]
    new_out = w_out - LR_MAT * spread(INNER, D) * mine[2].T
    new_step = w_step - LR_MAT * spread(D, HEADS) * mine[3][:, : w_step.shape[1]]
    state_slice = lax.dynamic_slice_in_dim(w_state, col_first, col_width, 1)
    new_state = state_slice - LR_MAT * spread(D, 2 * STATE) * mine[4][:, :col_width]
    m_norm = MU_VEC * moment_norm_gain + grad_norm
    m_conv_inner = MU_VEC * moment_conv_inner + grad_conv_inner
    m_conv_state = MU_VEC * moment_conv_state + grad_conv_state
    m_head = MU_VEC * moment_head_params + grad_head
    m_gate_gain = MU_VEC * moment_gate_gain + grad_gate_gain
    return (
        output,
        d_stream,
        grad_norm,
        grad_gate_w,
        grad_inner_w,
        grad_state_w,
        grad_step_w,
        grad_conv_inner,
        grad_conv_state,
        grad_head,
        grad_gate_gain,
        grad_out_w,
        norm_gain - LR_VEC * m_norm,
        new_gate,
        new_inner,
        new_state,
        new_step,
        conv_inner - LR_VEC * m_conv_inner,
        conv_state - LR_VEC * m_conv_state,
        head_params - LR_VEC * m_head,
        gate_gain - LR_VEC * m_gate_gain,
        new_out,
        m_norm,
        m_gate,
        m_inner,
        m_state,
        m_step,
        m_conv_inner,
        m_conv_state,
        m_head,
        m_gate_gain,
        m_out,
    )


MESH_ID = pl.DeviceIdType.MESH
SHARD = 48
PLAN = (("out", 768), ("gate", 768), ("inner", 768), ("small", 256))
PLANE_OF = {"out": 0, "inner": 1, "gate": 2, "small": 3}


def place():
    index = lax.axis_index("dp")
    z = lax.div(index, 4)
    y = lax.rem(lax.div(index, 2), 2)
    x = lax.rem(index, 2)
    at_x = {"dp": z * 4 + y * 2 + (1 - x)}
    at_y = {"dp": z * 4 + (1 - y) * 2 + x}
    at_z = [{"dp": lax.rem(z + step, 4) * 4 + y * 2 + x} for step in range(1, 4)]
    return x, y, z, at_x, at_y, at_z


def greet(peers):
    barrier = pltpu.get_barrier_semaphore()
    for peer in peers:
        pl.semaphore_signal(barrier, inc=1, device_id=peer, device_id_type=MESH_ID)
    pl.semaphore_wait(barrier, len(peers))


def remote(src, dst, send, recv, peer):
    return pltpu.make_async_remote_copy(
        src_ref=src, dst_ref=dst, send_sem=send, recv_sem=recv, device_id=peer, device_id_type=MESH_ID
    )

EARLY = 2


def half_steps(parts, at_x, at_y, x, y, arrived, summed, arrived_two, one_send, one_recv, two_send, two_recv):
    def span(task, route):
        half = parts[task].shape[-1] // 2
        return pl.ds(route * half, half), pl.ds(0, half)

    def one(task, route):
        cols, mine = span(task, route)
        other = parts[task].at[:, 1 - y, :, :, cols] if route else parts[task].at[:, :, 1 - x, :, cols]
        return remote(
            other, arrived.at[task, route, :, :, :, mine], one_send.at[task, route],
            one_recv.at[task, route], at_y if route else at_x,
        )

    def two(task, route):
        mine = span(task, route)[1]
        return remote(
            summed.at[task, route, :, 1 - x if route else 1 - y, :, mine],
            arrived_two.at[task, route, :, :, mine], two_send.at[task, route],
            two_recv.at[task, route], at_x if route else at_y,
        )

    def add(task, route, own):
        mine = span(task, route)[1]
        got = arrived[task, route, :, :, :, mine]
        summed[task, route, :, :, :, mine] = (own.astype(jnp.float32) + got.astype(jnp.float32)).astype(jnp.bfloat16)

    def settle(task, route, held):
        cols, mine = span(task, route)
        own = summed[task, route, :, x if route else y, :, mine]
        got = arrived_two[task, route, :, :, mine]
        held[:, :, cols] = (own.astype(jnp.float32) + got.astype(jnp.float32)).astype(jnp.bfloat16)

    return span, one, two, add, settle


def early_reduce(parts, held, own, arrived, summed, arrived_two, own_sem, one_send, one_recv, two_send, two_recv):
    step = pl.program_id(0)
    x, y, z, at_x, at_y, _ = place()
    span, one, two, add, settle = half_steps(
        parts, at_x, at_y, x, y, arrived, summed, arrived_two, one_send, one_recv, two_send, two_recv
    )
    pairs = [(task, route) for task in range(EARLY) for route in range(2)]

    def load(task, route):
        cols = span(task, route)[0]
        src = parts[task].at[:, y, :, :, cols] if route else parts[task].at[:, :, x, :, cols]
        return pltpu.make_async_copy(src, own.at[task, route], own_sem.at[task, route])

    @pl.when(step == 0)
    def _():
        greet([at_x, at_y])
        for route in range(2):
            one(0, route).start()
        for task, route in pairs:
            load(task, route).start()
        for route in range(2):
            one(1, route).start()

    for task, at in ((0, 3), (1, 5)):

        @pl.when(step == at)
        def _():
            for route in range(2):
                load(task, route).wait()
                one(task, route).wait()
                add(task, route, own[task, route])
                two(task, route).start()

    for task, at in ((0, 6), (1, 7)):

        @pl.when(step == at)
        def _():
            for route in range(2):
                two(task, route).wait()
                settle(task, route, held[task])


CHUNK = 128
PACK = 16


def sigmoid(value):
    return 0.5 * jnp.tanh(0.5 * value) + 0.5


def expand_matrix():
    row = jnp.arange(128)[:, None]
    col = jnp.arange(768)[None, :] // 64
    return ((row == col) | (row == col + PACK)).astype(jnp.bfloat16)


def two_term(value):
    lane = lax.broadcasted_iota(jnp.int32, value.shape, 1)
    high = value.astype(jnp.bfloat16).astype(jnp.float32)
    return jnp.where(lane < PACK, high, value - high).astype(jnp.bfloat16)


def split_terms(value, terms):
    out = []
    for _ in range(terms):
        piece = value.astype(jnp.bfloat16)
        out.append(piece)
        value = value - piece.astype(jnp.float32)
    return out


def dot(left, right, dims=((1,), (0,))):
    return lax.dot_general(left, right, (dims, ((), ())), preferred_element_type=jnp.float32)


def head_terms(step_ref, head_ref, pos):
    shifted = step_ref[...] + head_ref[0:1, :]
    small = jnp.exp(-jnp.abs(shifted))
    step = jnp.maximum(shifted, 0.0) + jnp.log1p(small)
    log_decay = -step * jnp.exp(head_ref[1:2, :])
    row = lax.broadcasted_iota(jnp.int32, (CHUNK, 128), 0)
    col = lax.broadcasted_iota(jnp.int32, (CHUNK, 128), 1)
    lower = (row >= col).astype(jnp.bfloat16)
    cumulative = sum(dot(lower, piece) for piece in split_terms(log_decay, 3))
    last = cumulative[CHUNK - 1 : CHUNK, :]
    back = (row - col).astype(jnp.float32)
    linked = (row >= col) & (back <= jnp.maximum(pos, 0.0))
    row = row.astype(jnp.float32)
    carry_in = jnp.where(pos > row, jnp.exp(cumulative), 0.0)
    pos_last = pos[CHUNK - 1 : CHUNK, :]
    tail_linked = (CHUNK - 1.0 - row) <= jnp.maximum(pos_last, 0.0)
    tail = jnp.where(tail_linked, jnp.exp(jnp.minimum(last - cumulative, 0.0)), 0.0)
    carry = jnp.where(pos_last > CHUNK - 1.0, jnp.exp(last), 0.0)
    return shifted, step, log_decay, cumulative, linked, carry_in, tail, carry


def pair_decay(cumulative, across, pair):
    parts = []
    for head in (2 * pair, 2 * pair + 1):
        spacing = cumulative[:, head : head + 1] - across[head : head + 1, :]
        parts.append(jnp.exp(jnp.minimum(spacing, 0.0)))
    return parts


def forward_kernel(
    inner_ref, step_ref, gate_ref, state_ref, dno_ref, pos_ref, taps_ref, taps_s_ref, head_ref,
    skip_ref, gain_ref, wide_ref,
    scanned_ref, zi_ref, zs_ref, enter_ref, sums_ref,
    halo_i, halo_s, hold,
):
    @pl.when(pl.program_id(0) == 0)
    def _():
        halo_i[...] = jnp.zeros_like(halo_i)
        halo_s[...] = jnp.zeros_like(halo_s)
        hold[...] = jnp.zeros_like(hold)

    low = jnp.bfloat16
    pos = pos_ref[...]
    marks = [(pos >= lag).astype(jnp.float32) for lag in range(4)]

    def conv(ref, halo, taps, out_ref, first):
        value = ref[:, first : first + 128]
        ext = jnp.concatenate([halo[:, first : first + 128], value], axis=0)
        total = taps[4:5, first : first + 128] + marks[0] * (value * taps[0:1, first : first + 128])
        for lag in range(1, 4):
            moved = pltpu.roll(ext, lag, 0)[8:]
            total = total + marks[lag] * (moved * taps[lag : lag + 1, first : first + 128])
        out_ref[:, first : first + 128] = total
        return total * sigmoid(total)

    shifted, step, log_decay, cumulative, linked, carry_in, tail, carry = head_terms(
        step_ref, head_ref, pos
    )
    across = cumulative.T
    wide = dot(
        jnp.concatenate(
            [
                two_term(step),
                two_term(carry_in),
                two_term(tail * step),
                two_term(jnp.broadcast_to(carry, (16, 128))),
            ],
            axis=0,
        ),
        wide_ref[...],
    )
    input_map = conv(state_ref, halo_s, taps_s_ref, zs_ref, 0).astype(low)
    output_map = conv(state_ref, halo_s, taps_s_ref, zs_ref, 128).astype(low)
    scores = jnp.where(linked, dot(output_map, input_map, ((1,), (1,))), 0.0)
    state = hold[...]
    state_low = state.astype(low)
    enter_ref[...] = state_low
    entered = dot(output_map, state_low)
    lane = lax.broadcasted_iota(jnp.int32, (CHUNK, 128), 1)
    squares = jnp.zeros((CHUNK, 128), jnp.float32)
    crosses = jnp.zeros((CHUNK, 128), jnp.float32)
    fed = []
    for pair in range(6):
        cols = slice(pair * 128, pair * 128 + 128)
        act = conv(inner_ref, halo_i, taps_ref, zi_ref, pair * 128)
        stepped = (wide[:CHUNK, cols] * act).astype(low)
        first, second = pair_decay(cumulative, across, pair)
        mixing = jnp.concatenate([(scores * first).astype(low), (scores * second).astype(low)], axis=0)
        both = dot(mixing, stepped)
        within = jnp.where(lane < 64, both[:CHUNK], both[CHUNK:])
        scanned = (
            within + entered[:, cols] * wide[CHUNK : 2 * CHUNK, cols] + skip_ref[0:1, cols] * act
        )
        scanned_ref[:, cols] = scanned
        fed.append((wide[2 * CHUNK : 3 * CHUNK, cols] * act).astype(low))
        gate = gate_ref[:, cols]
        gated = scanned * (gate * sigmoid(gate))
        squares = squares + gated * gated
        crosses = crosses + dno_ref[:, cols] * gain_ref[0:1, cols] * gated
    fresh = dot(input_map, jnp.concatenate(fed, axis=1), ((0,), (0,)))
    hold[...] = wide[3 * CHUNK : 3 * CHUNK + 1, :] * state + fresh
    halo_i[...] = inner_ref[CHUNK - 8 :, :]
    halo_s[...] = state_ref[CHUNK - 8 :, :]
    square = jnp.sum(squares, axis=1, keepdims=True)
    cross = jnp.sum(crosses * marks[0], axis=1, keepdims=True)
    sums_ref[...] = jnp.where(lane == 0, square, cross)


def gate_kernel(
    gate_ref, scanned_ref, dno_ref, sums_ref, twin_ref, gain_ref, pos_ref,
    normed_ref, d_gate_ref, d_scan_ref, g_gain_ref,
):
    @pl.when(pl.program_id(0) == 0)
    def _():
        g_gain_ref[...] = jnp.zeros_like(g_gain_ref)

    low = jnp.bfloat16
    alive = (pos_ref[...] >= 0).astype(jnp.float32)
    sums = sums_ref[...] + twin_ref[...]
    inv = jnp.broadcast_to(lax.rsqrt(sums[:, 0:1] / INNER + EPS), alive.shape)
    pull = inv * inv * inv * jnp.broadcast_to(sums[:, 1:2] / INNER, alive.shape)
    live = inv * alive
    for pair in range(6):
        cols = slice(pair * 128, pair * 128 + 128)
        gain = gain_ref[0:1, cols]
        gate, scanned, d_normed_out = gate_ref[:, cols], scanned_ref[:, cols], dno_ref[:, cols]
        sig = sigmoid(gate)
        gate_act = gate * sig
        gated = scanned * gate_act
        normed_ref[:, cols] = (gated * live * gain).astype(low)
        product = d_normed_out * gated * live
        g_gain_ref[:, cols] += jnp.sum(product.reshape(CHUNK // 8, 8, 128), axis=0)
        d_gated = live * gain * d_normed_out - gated * pull
        d_scan_ref[:, cols] = (d_gated * gate_act).astype(low)
        d_gate_ref[:, cols] = (d_gated * scanned * (sig * (1.0 + gate * (1.0 - sig)))).astype(low)


def gate_stage(first_pre, scanned, d_normed_out, sums, twin_sums, gain, pos):
    rows = first_pre.shape[0]
    at = lambda width: pl.BlockSpec((CHUNK, width), lambda c: (c, 0))
    f32, low = jnp.float32, jnp.bfloat16
    wide = jax.ShapeDtypeStruct((rows, 768), low)
    return pl.pallas_call(
        gate_kernel,
        grid=(rows // CHUNK,),
        in_specs=[
            at(768), at(768), at(768), at(128), at(128), pl.BlockSpec((1, 768), lambda c: (0, 0)), at(128),
        ],
        out_specs=[at(768), at(768), at(768), pl.BlockSpec((8, 768), lambda c: (0, 0))],
        out_shape=[wide, wide, wide, jax.ShapeDtypeStruct((8, 768), f32)],
        compiler_params=pltpu.CompilerParams(vmem_limit_bytes=40 * 2**20),
        cost_estimate=pl.CostEstimate(flops=10**8, bytes_accessed=15 * 10**6, transcendentals=10**6),
        name="gate_stage",
    )(first_pre, scanned, d_normed_out, sums, twin_sums, gain, pos)


def backward_kernel(
    inner_ref, step_ref, state_ref, zi_ref, zs_ref, scanned_ref, dscan_ref, enter_ref, pos_ref,
    taps_ref, taps_s_ref, head_ref, skip_ref, wide_ref, out_part, gate_part,
    d_inner_ref, d_state_ref, d_step_ref, g_taps_ref, g_taps_s_ref, g_skip_ref, g_head_ref, held_out, held_gate,
    halo_i, halo_s, halo_p, hold, *reducing,
):
    low = jnp.bfloat16
    early_reduce((out_part, gate_part), (held_out, held_gate), *reducing)

    @pl.when(pl.program_id(0) == 0)
    def _():
        for ref in (halo_i, halo_s, halo_p, hold, g_taps_ref, g_taps_s_ref, g_skip_ref, g_head_ref):
            ref[...] = jnp.zeros_like(ref)

    pos = pos_ref[...]
    pos_ext = jnp.concatenate([pos, halo_p[...]], axis=0)
    marks = [(pos_ext >= lag).astype(jnp.float32) for lag in range(4)]
    lane = lax.broadcasted_iota(jnp.int32, (CHUNK, 128), 1)
    row = lax.broadcasted_iota(jnp.int32, (CHUNK, 128), 0)
    col = lane

    def slope(total):
        sig = sigmoid(total)
        return sig * (1.0 + total * (1.0 - sig)), total * sig

    def fold(value):
        return jnp.sum(value.reshape(CHUNK // 8, 8, 128), axis=0)

    def conv_back(grad, ref, halo, taps, out_ref, g_ref, first):
        cols = slice(first, first + 128)
        ext = jnp.concatenate([grad, halo[:, cols]], axis=0)
        value = ref[:, cols]
        halo[:, cols] = grad[:8]
        g_ref[4, :, cols] += fold(grad)
        total = jnp.zeros((CHUNK, 128), jnp.float32)
        for lag in range(4):
            masked = ext * marks[lag]
            if lag:
                masked = pltpu.roll(masked, CHUNK + 8 - lag, 0)
            masked = masked[:CHUNK]
            g_ref[lag, :, cols] += fold(masked * value)
            total = total + masked * taps[lag : lag + 1, cols]
        out_ref[:, cols] = total.astype(low)

    shifted, step, log_decay, cumulative, linked, carry_in, tail, carry = head_terms(
        step_ref, head_ref, pos
    )
    across = cumulative.T
    wide = dot(
        jnp.concatenate(
            [
                two_term(step),
                two_term(carry_in),
                two_term(tail),
                two_term(jnp.broadcast_to(carry, (16, 128))),
            ],
            axis=0,
        ),
        wide_ref[...],
    )
    slope_b, input_map = slope(zs_ref[:, :128])
    slope_c, output_map = slope(zs_ref[:, 128:])
    input_low, output_low = input_map.astype(low), output_map.astype(low)
    scores = jnp.where(linked, dot(output_low, input_low, ((1,), (1,))), 0.0)
    entering = enter_ref[...]
    d_next = hold[...]
    d_next_low = d_next.astype(low)
    pulled = dot(input_low, d_next_low)
    d_scores = jnp.zeros((CHUNK, 128), jnp.float32)
    d_entered, fed, balance, direct, extra = [], [], [], [], []
    carry_wide = wide[3 * CHUNK : 3 * CHUNK + 1, :]
    carry_grad = jnp.sum(d_next * entering.astype(jnp.float32), axis=0, keepdims=True) * carry_wide
    for pair in range(6):
        cols = slice(pair * 128, pair * 128 + 128)
        slope_x, act = slope(zi_ref[:, cols])
        d_low = dscan_ref[:, cols]
        skip = skip_ref[0:1, cols]
        stepped = (wide[:CHUNK, cols] * act).astype(low)
        stepped_wide = stepped.astype(jnp.float32)
        d_exact = d_low.astype(jnp.float32)
        d_both = jnp.concatenate(
            [jnp.where(lane < 64, d_exact, 0.0).astype(low), jnp.where(lane < 64, 0.0, d_exact).astype(low)],
            axis=0,
        )
        first, second = pair_decay(cumulative, across, pair)
        mixing = jnp.concatenate([(scores * first).astype(low), (scores * second).astype(low)], axis=0)
        d_mixing = dot(d_both, stepped, ((1,), (1,)))
        d_scores = d_scores + d_mixing[:CHUNK] * first + d_mixing[CHUNK:] * second
        tail_cols = wide[2 * CHUNK : 3 * CHUNK, cols]
        tailed = tail_cols * pulled[:, cols]
        d_stepped = dot(mixing, d_both, ((0,), (0,))) + tailed
        extra.append(jnp.sum(stepped_wide * tailed, axis=0, keepdims=True) + carry_grad[:, cols])
        fed.append((tail_cols * stepped_wide).astype(low))
        d_entered.append((wide[CHUNK : 2 * CHUNK, cols] * d_exact).astype(low))
        balance.append(d_exact * (scanned_ref[:, cols] - skip * act) - stepped_wide * d_stepped)
        direct.append(act * d_stepped)
        g_skip_ref[:, cols] += fold(d_exact * act)
        d_act = skip * d_exact + wide[:CHUNK, cols] * d_stepped
        conv_back(d_act * slope_x, inner_ref, halo_i, taps_ref, d_inner_ref, g_taps_ref, pair * 128)
    d_entered = jnp.concatenate(d_entered, axis=1)
    fed = jnp.concatenate(fed, axis=1)
    d_scores = jnp.where(linked, d_scores, 0.0).astype(low)
    d_output = dot(d_scores, input_low) + dot(d_entered, entering, ((1,), (1,)))
    d_input = dot(d_scores, output_low, ((0,), (0,))) + dot(fed, d_next_low, ((1,), (1,)))
    hold[...] = carry_wide * d_next + dot(output_low, d_entered, ((0,), (0,)))
    conv_back(d_input * slope_b, state_ref, halo_s, taps_s_ref, d_state_ref, g_taps_s_ref, 0)
    conv_back(d_output * slope_c, state_ref, halo_s, taps_s_ref, d_state_ref, g_taps_s_ref, 128)
    halo_p[...] = pos[:8]
    spread_back = wide_ref[...]
    extra = jnp.broadcast_to(jnp.concatenate(extra, axis=1), (16, 768))
    stacked = jnp.concatenate(
        split_terms(jnp.concatenate(balance, axis=1), 2)
        + split_terms(jnp.concatenate(direct, axis=1), 2)
        + split_terms(extra, 2),
        axis=0,
    )
    summed = dot(stacked, spread_back, ((1,), (1,)))
    d_sum = summed[:CHUNK] + summed[CHUNK : 2 * CHUNK]
    d_direct = summed[2 * CHUNK : 3 * CHUNK] + summed[3 * CHUNK : 4 * CHUNK]
    d_last = summed[4 * CHUNK : 4 * CHUNK + 1] + summed[4 * CHUNK + 16 : 4 * CHUNK + 17]
    upper = (row <= col).astype(low)
    d_decay = sum(dot(upper, piece) for piece in split_terms(d_sum, 3)) + d_last
    d_step = (d_direct - d_decay * jnp.exp(head_ref[1:2, :])) * sigmoid(shifted)
    d_step = jnp.where(lane < PACK, d_step, 0.0)
    d_step_ref[...] = d_step.astype(low)
    g_head_ref[0] += fold(d_step)
    g_head_ref[1] += fold(d_decay * log_decay)


def forward_core(first_pre, second_pre, d_normed_out, pos, taps, taps_s, heads_lanes, skip, gain, wide):
    rows = first_pre.shape[0]
    at = lambda width, col: pl.BlockSpec((CHUNK, width), lambda c: (c, col))
    whole = lambda arr: pl.BlockSpec(arr.shape, lambda c: (0,) * arr.ndim)
    f32 = jnp.float32
    return pl.pallas_call(
        forward_kernel,
        grid=(rows // CHUNK,),
        in_specs=[
            at(768, 0), at(128, 6), at(768, 0), at(256, 3), at(768, 0), at(128, 0),
            whole(taps), whole(taps_s), whole(heads_lanes), whole(skip), whole(gain), whole(wide),
        ],
        out_specs=[at(768, 0), at(768, 0), at(256, 0), at(768, 0), at(128, 0)],
        out_shape=[
            jax.ShapeDtypeStruct((rows, 768), f32),
            jax.ShapeDtypeStruct((rows, 768), f32),
            jax.ShapeDtypeStruct((rows, 256), f32),
            jax.ShapeDtypeStruct((rows, 768), jnp.bfloat16),
            jax.ShapeDtypeStruct((rows, 128), f32),
        ],
        scratch_shapes=[
            pltpu.VMEM((8, 768), f32), pltpu.VMEM((8, 256), f32), pltpu.VMEM((128, 768), f32),
        ],
        compiler_params=pltpu.CompilerParams(vmem_limit_bytes=40 * 2**20),
        cost_estimate=pl.CostEstimate(flops=8 * 10**9, bytes_accessed=24 * 10**6, transcendentals=4 * 10**6),
        name="mixer_forward",
    )(second_pre, second_pre, first_pre, first_pre, d_normed_out, pos, taps, taps_s, heads_lanes, skip, gain, wide)


def backward_core(
    first_pre, second_pre, zi, zs, scanned, d_scan, enter, pos, taps, taps_s, heads_lanes, skip, wide, out_part, gate_part
):
    rows = first_pre.shape[0]
    count = rows // CHUNK
    at = lambda width, col: pl.BlockSpec((CHUNK, width), lambda c: (count - 1 - c, col))
    whole = lambda shape: pl.BlockSpec(shape, lambda c: (0,) * len(shape))
    f32, low = jnp.float32, jnp.bfloat16
    return pl.pallas_call(
        backward_kernel,
        grid=(count,),
        in_specs=[
            at(768, 0), at(128, 6), at(256, 3), at(768, 0), at(256, 0), at(768, 0), at(768, 0),
            at(768, 0), at(128, 0),
            whole(taps.shape), whole(taps_s.shape), whole(heads_lanes.shape), whole(skip.shape), whole(wide.shape),
            pl.BlockSpec(memory_space=pl.ANY), pl.BlockSpec(memory_space=pl.ANY),
        ],
        out_specs=[
            at(768, 0), at(256, 0), at(128, 0),
            whole((5, 8, 768)), whole((5, 8, 256)), whole((8, 768)), whole((2, 8, 128)),
            whole((4, SHARD, 768)), whole((4, SHARD, 768)),
        ],
        out_shape=[
            jax.ShapeDtypeStruct((rows, 768), low),
            jax.ShapeDtypeStruct((rows, 256), low),
            jax.ShapeDtypeStruct((rows, 128), low),
            jax.ShapeDtypeStruct((5, 8, 768), f32),
            jax.ShapeDtypeStruct((5, 8, 256), f32),
            jax.ShapeDtypeStruct((8, 768), f32),
            jax.ShapeDtypeStruct((2, 8, 128), f32),
            jax.ShapeDtypeStruct((4, SHARD, 768), low),
            jax.ShapeDtypeStruct((4, SHARD, 768), low),
        ],
        scratch_shapes=[
            pltpu.VMEM((8, 768), f32), pltpu.VMEM((8, 256), f32), pltpu.VMEM((8, 128), f32),
            pltpu.VMEM((128, 768), f32),
            pltpu.VMEM((EARLY, 2, 4, 2, SHARD, 384), low),
            pltpu.VMEM((EARLY, 2, 4, 2, SHARD, 384), low),
            pltpu.VMEM((EARLY, 2, 4, 2, SHARD, 384), low),
            pltpu.VMEM((EARLY, 2, 4, SHARD, 384), low),
        ]
        + [pltpu.SemaphoreType.DMA((EARLY, 2))] * 5,
        compiler_params=pltpu.CompilerParams(
            collective_id=3, has_side_effects=True, vmem_limit_bytes=48 * 2**20
        ),
        cost_estimate=pl.CostEstimate(flops=16 * 10**9, bytes_accessed=24 * 10**6, transcendentals=6 * 10**6),
        name="mixer_backward",
    )(
        second_pre, second_pre, first_pre, zi, zs, scanned, d_scan, enter, pos, taps, taps_s, heads_lanes, skip, wide,
        out_part.reshape(4, 2, 2, SHARD, 768), gate_part.reshape(4, 2, 2, SHARD, 768),
    )


def swap(value):
    return lax.ppermute(value, "tensor", [(0, 1), (1, 0)])


def pair_scatter(part, axis):
    mine = lax.axis_index("tensor")
    width = part.shape[axis] // 2
    keep = lax.dynamic_slice_in_dim(part, mine * width, width, axis)
    send = lax.dynamic_slice_in_dim(part, (1 - mine) * width, width, axis)
    return keep.astype(jnp.float32) + swap(send.astype(jnp.bfloat16)).astype(jnp.float32)


def pad_cols(value, width):
    return jnp.pad(value, ((0, 0), (0, width - value.shape[1])))


GATHER_PIECES = (
    (1, 0, 384, 0), (1, 384, 512, 1), (0, 0, 512, 0), (0, 512, 512, 1), (2, 0, 384, 0), (2, 384, 384, 1),
)


def gather_kernel(
    first_ref, second_ref, out_ref, stream_ref, cot_ref, gain_ref,
    full_first, full_second, full_out, rows_ref, cots_ref, pre_first, pre_second, pre_out,
    held_first, held_second, held_out,
    pre_sem, row_sem, z_send, z_recv, one_send, one_recv, two_send, two_recv,
):
    x, y, z, at_x, at_y, at_z = place()
    core = lax.axis_index("tensor")
    twin = {"tensor": 1 - core}
    greet([at_x, at_y, twin] + at_z)
    shards = (first_ref, second_ref, out_ref)
    fulls = (full_first, full_second, full_out)
    results = ((held_first, pre_first), (held_second, pre_second), (held_out, pre_out))
    z_copies, ones, twos, copies = {}, {}, {}, []

    def step_zero(piece):
        which, start, width, _ = GATHER_PIECES[piece]
        cols = pl.ds(start, width)
        z_copies[piece] = []
        for step, peer in enumerate(at_z):
            copy = remote(
                shards[which].at[:, cols], fulls[which].at[z, y, x, :, cols],
                z_send.at[piece, step], z_recv.at[piece, step], peer,
            )
            copy.start()
            z_copies[piece].append(copy)

    def step_one(piece):
        which, start, width, route = GATHER_PIECES[piece]
        for copy in z_copies[piece]:
            copy.wait()
        part = fulls[which].at[:, y, x, :, pl.ds(start, width)]
        ones[piece] = remote(part, part, one_send.at[piece], one_recv.at[piece], at_x if route else at_y)
        ones[piece].start()

    def step_two(piece):
        which, start, width, route = GATHER_PIECES[piece]
        cols = pl.ds(start, width)
        ones[piece].wait()
        part = fulls[which].at[:, y, :, :, cols] if route else fulls[which].at[:, :, x, :, cols]
        twos[piece] = remote(part, part, two_send.at[piece], two_recv.at[piece], at_y if route else at_x)
        twos[piece].start()

    def finish(piece):
        which, start, width, _ = GATHER_PIECES[piece]
        cols = pl.ds(start, width)
        twos[piece].wait()
        left = cots_ref if which == 2 else rows_ref
        held, pre = results[which]
        weights = fulls[which]

        def tile(at, carry):
            here = pl.ds(pl.multiple_of(lax.rem(at, 2) * 256, 256), 256)
            there = pl.ds(pl.multiple_of(at * 256, 256), 256)
            held[there, cols] = dot(
                left[lax.div(at, 2), here, :], weights[:, :, :, :, cols].reshape(768, width)
            )
            return carry

        lax.fori_loop(0, 4, tile, 0)
        copy = pltpu.make_async_copy(held.at[:, cols], pre.at[:, cols], pre_sem.at[piece])
        copy.start()
        copies.append(copy)

    step_zero(0)
    for shard, full in zip(shards, fulls):
        full[z, y, x] = shard[...]
    step_zero(1)
    for part in range(4):
        here = pl.ds(part * 128, 128)
        value = stream_ref[here, :]
        inv = lax.rsqrt(jnp.sum(value * value, axis=1, keepdims=True) / D + EPS)
        rows_ref[core, here, :] = (value * inv * gain_ref[...]).astype(jnp.bfloat16)
        cots_ref[core, here, :] = cot_ref[here, :].astype(jnp.bfloat16)
    swaps = []
    for at, ref in enumerate((rows_ref, cots_ref)):
        swaps.append(remote(ref.at[core], ref.at[core], row_sem.at[at], row_sem.at[2 + at], twin))
        swaps[-1].start()
    count = len(GATHER_PIECES)
    for piece in range(count + 1):
        if piece < count:
            step_one(piece)
        if piece + 2 < count:
            step_zero(piece + 2)
        if piece >= 1:
            step_two(piece - 1)
        if piece == 3:
            for copy in swaps:
                copy.wait()
        if piece >= 4:
            finish(piece - 4)
    for piece in range(count - 3, count):
        finish(piece)
    for copy in copies:
        copy.wait()


def gather_all(first, second, out, stream, cotangent, gain):
    f32, low = jnp.float32, jnp.bfloat16
    vmem = pl.BlockSpec(memory_space=pltpu.VMEM)
    count = len(GATHER_PIECES)
    dma = pltpu.SemaphoreType.DMA
    tokens = 2 * stream.shape[0]
    full = lambda arr: jax.ShapeDtypeStruct((4, 2, 2) + arr.shape, low)
    rows = jax.ShapeDtypeStruct((2,) + stream.shape, low)
    pre = lambda arr: jax.ShapeDtypeStruct((tokens, arr.shape[1]), f32)
    got = pl.pallas_call(
        gather_kernel,
        in_specs=[vmem] * 6,
        out_specs=[vmem] * 5 + [pl.BlockSpec(memory_space=pl.ANY)] * 3,
        out_shape=[full(first), full(second), full(out), rows, rows, pre(first), pre(second), pre(out)],
        scratch_shapes=[
            pltpu.VMEM((tokens, first.shape[1]), f32),
            pltpu.VMEM((tokens, second.shape[1]), f32),
            pltpu.VMEM((tokens, out.shape[1]), f32),
            dma((count,)), dma((4,)), dma((count, 3)), dma((count, 3)),
            dma((count,)), dma((count,)), dma((count,)), dma((count,)),
        ],
        compiler_params=pltpu.CompilerParams(
            collective_id=0, has_side_effects=True, vmem_limit_bytes=48 * 2**20
        ),
        cost_estimate=pl.CostEstimate(flops=4 * 10**9, bytes_accessed=120 * 10**6, transcendentals=0),
        name="gather_weights",
    )(first, second, out, stream, cotangent, gain)
    return [item.reshape(-1, item.shape[-1]) for item in got]


def reduce_kernel(
    held_out, held_gate, inner_ref, small_ref, vec_ref, moment_ref,
    whole_ref, other_ref, grads_ref, total_ref,
    arrived, summed, arrived_two, held_inner, held_small, slots, moments,
    block, back, vec_in, vec_mid, vec_slots,
    m_send, m_recv, one_send, one_recv, two_send, two_recv, z_send, z_recv, g_send, g_recv,
    p_send, p_recv, t_send, t_recv, v_send, v_recv,
):
    f32, low = jnp.float32, jnp.bfloat16
    x, y, z, at_x, at_y, at_z = place()
    core = lax.axis_index("tensor")
    twin = {"tensor": 1 - core}
    greet([at_x, at_y, twin] + at_z)
    parts = (inner_ref, small_ref)
    held = (held_out, held_gate, held_inner, held_small)
    steps_z = [lax.rem(z + step, 4) for step in range(1, 4)]
    span, one, two, add, settle = half_steps(
        parts, at_x, at_y, x, y, arrived, summed, arrived_two, one_send, one_recv, two_send, two_recv
    )

    def to_plane(task):
        plane, width = PLANE_OF[PLAN[task][0]], PLAN[task][1]

        @pl.when(z != plane)
        def _():
            remote(
                held[task], slots.at[z, :, :, pl.ds(0, width)], z_send.at[task], z_recv.at[z],
                {"dp": plane * 4 + y * 2 + x},
            ).start()

    for task in range(2):
        for route in range(2):
            one(task, route).start()
    vec_x = remote(vec_ref, vec_in.at[0], v_send.at[0], v_recv.at[0], at_x)
    vec_x.start()
    to_plane(0)
    to_plane(1)
    moment_copies = []
    for step, (peer, plane) in enumerate(zip(at_z, steps_z)):
        copy = remote(moment_ref.at[plane], moments.at[z], m_send.at[step], m_recv.at[step], peer)
        copy.start()
        moment_copies.append(copy)
    for task in range(2):
        for route in range(2):
            cols = span(task, route)[0]
            one(task, route).wait()
            add(task, route, parts[task][:, y, :, :, cols] if route else parts[task][:, :, x, :, cols])
            two(task, route).start()
    vec_x.wait()
    vec_mid[0] = vec_ref[...] + vec_in[0]
    vec_y = remote(vec_mid.at[0], vec_in.at[1], v_send.at[1], v_recv.at[1], at_y)
    vec_y.start()
    for task in range(2):
        for route in range(2):
            two(task, route).wait()
            settle(task, route, held[2 + task])
        to_plane(2 + task)
    vec_y.wait()
    vec_mid[1] = vec_mid[0] + vec_in[1]
    vec_slots[z] = vec_mid[1]
    vec_z = []
    for step, peer in enumerate(at_z):
        copy = remote(vec_mid.at[1], vec_slots.at[z], v_send.at[2 + step], v_recv.at[2 + step], peer)
        copy.start()
        vec_z.append(copy)
    for copy in moment_copies:
        copy.wait()
    moments[z] = moment_ref[z]

    for task, (name, width) in enumerate(PLAN):
        plane = PLANE_OF[name]
        cols = pl.ds(0, width)

        @pl.when(z == plane)
        def _():
            for source in range(4):
                if source != plane:
                    remote(
                        held[task], slots.at[source, :, :, cols], z_send.at[task], z_recv.at[source], at_x
                    ).wait_recv()
            total = held[task][...].astype(f32)
            for source in range(4):
                if source != plane:
                    total = total + slots[source, :, :, cols].astype(f32)
            if width < 768:
                back[...] = jnp.zeros_like(back)
                block[...] = jnp.zeros_like(block)
            back[:, :, cols] = total.astype(low)
            block[:, :, cols] = (MU_MAT * moments[:, :, cols].astype(f32) + total).astype(low)

    half = 384
    routes = (pl.ds(0, half), pl.ds(half, half))
    for row in range(4):
        whole_ref[row, y, x] = block[row]
    plane_one = []
    for route, peer in enumerate((at_x, at_y)):
        copy = remote(
            block.at[:, :, routes[route]], whole_ref.at[:, y, x, :, routes[route]],
            p_send.at[0, route], p_recv.at[0, route], peer,
        )
        copy.start()
        plane_one.append(copy)
    twin_own = remote(block, other_ref.at[:, y, x], t_send.at[0], t_recv.at[0], twin)
    twin_own.start()
    grads_ref[z] = back[z]
    returns = []
    for step, (peer, plane) in enumerate(zip(at_z, steps_z)):
        copy = remote(back.at[plane], grads_ref.at[z], g_send.at[step], g_recv.at[step], peer)
        copy.start()
        returns.append(copy)
    plane_two = []
    for route, peer in enumerate((at_y, at_x)):
        plane_one[route].wait()
        part = (
            whole_ref.at[:, :, x, :, routes[1]] if route else whole_ref.at[:, y, :, :, routes[0]]
        )
        copy = remote(part, part, p_send.at[1, route], p_recv.at[1, route], peer)
        copy.start()
        plane_two.append(copy)
    twins = [twin_own]
    for route in range(2):
        src = whole_ref.at[:, 1 - y, x, :, routes[1]] if route else whole_ref.at[:, y, 1 - x, :, routes[0]]
        dst = other_ref.at[:, 1 - y, x, :, routes[1]] if route else other_ref.at[:, y, 1 - x, :, routes[0]]
        copy = remote(src, dst, t_send.at[1 + route], t_recv.at[1 + route], twin)
        copy.start()
        twins.append(copy)
    for route in range(2):
        plane_two[route].wait()
        src = whole_ref.at[:, :, 1 - x, :, routes[1]] if route else whole_ref.at[:, 1 - y, :, :, routes[0]]
        dst = other_ref.at[:, :, 1 - x, :, routes[1]] if route else other_ref.at[:, 1 - y, :, :, routes[0]]
        copy = remote(src, dst, t_send.at[3 + route], t_recv.at[3 + route], twin)
        copy.start()
        twins.append(copy)
    for copy in twins + returns + vec_z:
        copy.wait()
    total_ref[...] = (vec_slots[0] + vec_slots[1]) + (vec_slots[2] + vec_slots[3])
    for task, (name, width) in enumerate(PLAN):
        plane = PLANE_OF[name]

        @pl.when(z != plane)
        def _():
            remote(
                held[task], slots.at[z, :, :, pl.ds(0, width)], z_send.at[task], z_recv.at[z],
                {"dp": plane * 4 + y * 2 + x},
            ).wait_send()


def reduce_all(held, parts, vectors, moments):
    f32, low = jnp.float32, jnp.bfloat16
    vmem = pl.BlockSpec(memory_space=pltpu.VMEM)
    dma = pltpu.SemaphoreType.DMA
    parts = [part.reshape(4, 2, 2, SHARD, part.shape[1]) for part in parts]
    buf = pltpu.VMEM
    whole, other, grads, total = pl.pallas_call(
        reduce_kernel,
        in_specs=[vmem] * 6,
        out_specs=[vmem] * 4,
        out_shape=[
            jax.ShapeDtypeStruct((4, 2, 2, SHARD, 768), low),
            jax.ShapeDtypeStruct((4, 2, 2, SHARD, 768), low),
            jax.ShapeDtypeStruct((4, SHARD, 768), low),
            jax.ShapeDtypeStruct(vectors.shape, f32),
        ],
        scratch_shapes=[
            buf((2, 2, 4, 2, SHARD, 384), low), buf((2, 2, 4, 2, SHARD, 384), low),
            buf((2, 2, 4, SHARD, 384), low),
            buf((4, SHARD, 768), low), buf((4, SHARD, 256), low),
            buf((4, 4, SHARD, 768), low), buf((4, SHARD, 768), low),
            buf((4, SHARD, 768), low), buf((4, SHARD, 768), low),
            buf((2,) + vectors.shape, f32), buf((2,) + vectors.shape, f32), buf((4,) + vectors.shape, f32),
            dma((3,)), dma((3,)), dma((2, 2)), dma((2, 2)), dma((2, 2)), dma((2, 2)),
            dma((4,)), dma((4,)), dma((3,)), dma((3,)), dma((2, 2)), dma((2, 2)),
            dma((5,)), dma((5,)), dma((5,)), dma((5,)),
        ],
        compiler_params=pltpu.CompilerParams(
            collective_id=1, has_side_effects=True, vmem_limit_bytes=48 * 2**20
        ),
        cost_estimate=pl.CostEstimate(flops=0, bytes_accessed=150 * 10**6, transcendentals=0),
        name="reduce_grads",
    )(*held, *parts, vectors, moments)
    return whole.reshape(768, 768), other.reshape(768, 768), grads, total


def newton_kernel(full_ref, out_ref, current, gram, mix):
    f32, low = jnp.float32, jnp.bfloat16
    rows, cols = current.shape
    tile = 256
    count = rows // tile
    row_ids = lax.broadcasted_iota(jnp.int32, (tile, tile), 0)
    col_ids = lax.broadcasted_iota(jnp.int32, (tile, tile), 1)
    blocks = [pl.ds(at * tile, tile) for at in range(count)]

    def symmetric(source, store):
        for first in range(count):
            for second in range(first, count):
                store(first, second, dot(source[blocks[first], :], source[blocks[second], :], ((1,), (1,))))

    def put(ref, first, second, value):
        ref[blocks[first], blocks[second]] = value.astype(low)
        if first != second:
            ref[blocks[second], blocks[first]] = value.T.astype(low)

    firsts = {}
    symmetric(full_ref, lambda first, second, value: firsts.update({(first, second): value}))
    trace = sum(
        jnp.sum(jnp.where(row_ids == col_ids, firsts[at, at], 0.0), keepdims=True) for at in range(count)
    )
    scale = jnp.sqrt(trace) + 1e-07
    inverse, inverse_square = 1.0 / scale, 1.0 / (scale * scale)
    for (first, second), value in firsts.items():
        put(gram, first, second, value * inverse_square)
    for at in range(count):
        current[blocks[at], :] = (full_ref[blocks[at], :].astype(f32) * inverse).astype(low)

    def mixed():
        def store(first, second, value):
            piece = gram[blocks[first], blocks[second]].astype(f32)
            put(mix, first, second, NS_B * piece + NS_C * value)

        symmetric(gram, store)

    def turn(_, carry):
        mixed()

        def update(at, carry):
            here = pl.ds(pl.multiple_of(at * tile, tile), tile)
            held = current[:, here]
            current[:, here] = (NS_A * held.astype(f32) + dot(mix[...], held)).astype(low)
            return carry

        lax.fori_loop(0, cols // tile, update, 0)
        symmetric(current, lambda first, second, value: put(gram, first, second, value))
        return carry

    lax.fori_loop(0, NS_STEPS - 1, turn, 0)
    mixed()
    for at in range(out_ref.shape[1] // tile):
        here = pl.ds(at * tile, tile)
        held = current[:, here]
        out_ref[:, here] = (NS_A * held.astype(f32) + dot(mix[...], held)).astype(low)


def newton(full, width):
    low = jnp.bfloat16
    rows = full.shape[0]
    return pl.pallas_call(
        newton_kernel,
        in_specs=[pl.BlockSpec(memory_space=pltpu.VMEM)],
        out_specs=pl.BlockSpec(memory_space=pltpu.VMEM),
        out_shape=jax.ShapeDtypeStruct((rows, width), low),
        scratch_shapes=[
            pltpu.VMEM(full.shape, low), pltpu.VMEM((rows, rows), low), pltpu.VMEM((rows, rows), low),
        ],
        compiler_params=pltpu.CompilerParams(vmem_limit_bytes=48 * 2**20),
        cost_estimate=pl.CostEstimate(flops=20 * 10**9, bytes_accessed=4 * 10**6, transcendentals=0),
        name="newton_schulz",
    )(full)


def return_kernel(done_ref, back_ref, send, recv):
    x, y, z, _, _, at_z = place()
    greet(at_z)
    copies = []
    for step, peer in enumerate(at_z):
        plane = lax.rem(z + step + 1, 4)
        copies.append(
            remote(done_ref.at[plane, y, x], back_ref.at[z], send.at[step], recv.at[step], peer)
        )
        copies[-1].start()
    back_ref[z] = done_ref[z, y, x]
    for copy in copies:
        copy.wait()


def return_rows(done):
    vmem = pl.BlockSpec(memory_space=pltpu.VMEM)
    dma = pltpu.SemaphoreType.DMA
    return pl.pallas_call(
        return_kernel,
        in_specs=[vmem],
        out_specs=vmem,
        out_shape=jax.ShapeDtypeStruct((4, SHARD, 768), done.dtype),
        scratch_shapes=[dma((3,)), dma((3,))],
        compiler_params=pltpu.CompilerParams(collective_id=2, has_side_effects=True, vmem_limit_bytes=16 * 2**20),
        cost_estimate=pl.CostEstimate(flops=0, bytes_accessed=20 * 10**6, transcendentals=0),
        name="return_rows",
    )(done.reshape(4, 2, 2, SHARD, 768))


def orthogonal_owned(own, other, state_width):
    width = own.shape[1]
    small = lax.axis_index("dp") // 4 == PLANE_OF["small"]
    full = jnp.concatenate([own, other], axis=1)
    col = jnp.arange(2 * width)[None, :] % width
    keep = (col < state_width) == (lax.axis_index("tensor") == 0)
    full = jnp.where(small & ~keep, jnp.zeros_like(full), full)
    done = newton(full, width + 2 * state_width)
    half, lent = done[:, :width], done[:, width:]
    edge = half[:, : 2 * state_width]
    edge = edge + jnp.where(small, swap(lent), jnp.zeros_like(lent))
    return jnp.concatenate([edge, half[:, 2 * state_width :]], axis=1)


def paired_shards(
    stream,
    cotangent,
    positions,
    norm_gain,
    w_gate,
    w_inner,
    w_state,
    w_step,
    conv_inner,
    conv_state,
    head_params,
    gate_gain,
    w_out,
    moment_norm_gain,
    moment_w_gate,
    moment_w_inner,
    moment_w_state,
    moment_w_step,
    moment_conv_inner,
    moment_conv_state,
    moment_head_params,
    moment_gate_gain,
    moment_w_out,
):
    low = jnp.bfloat16
    core = lax.axis_index("tensor")
    room = w_gate.shape[1]
    wide = w_state.shape[1]
    col_width = wide // 2
    heads = w_step.shape[1]
    inv_first = lax.rsqrt(jnp.mean(stream * stream, axis=1, keepdims=True) + EPS)
    first_pack = jnp.concatenate([w_gate.astype(low), w_state.astype(low)], axis=1)
    step_low = w_step.astype(low)
    step_lanes = jnp.concatenate([pad_cols(step_low, PACK), pad_cols(step_low, 128 - PACK)], axis=1)
    second_pack = jnp.concatenate([w_inner.astype(low), step_lanes], axis=1)
    full_first, full_second, full_out, token_rows, cotangent_rows, first_pre, second_pre, d_normed_out = gather_all(
        first_pack, second_pack, w_out.astype(low).T, stream, cotangent, norm_gain[None, :]
    )
    pos = jnp.broadcast_to(positions.astype(jnp.float32)[:, None], (positions.shape[0], 128))
    taps = jnp.pad(conv_inner, ((0, 3), (0, 0)))
    taps_s = jnp.pad(conv_state, ((0, 3), (0, 0)))
    lanes = jnp.concatenate([pad_cols(head_params, PACK), pad_cols(head_params, 128 - PACK)], axis=1)
    lanes = jnp.pad(lanes, ((0, 5), (0, 0)))
    skip = jnp.repeat(head_params[2], room // heads)[None, :]
    wide_map = expand_matrix()
    scanned, zi, zs, enter, sums = forward_core(
        first_pre, second_pre, d_normed_out, pos, taps, taps_s, lanes, skip, gate_gain[None, :], wide_map
    )
    normed_out, d_gate_pre, d_scan, gain_part = gate_stage(
        first_pre, scanned, d_normed_out, sums, swap(sums), gate_gain[None, :], pos
    )
    grad_gate_part = jnp.sum(gain_part, axis=0)
    mixed = pair_scatter(times_transpose(normed_out, full_out).astype(low), 0)
    output = stream + mixed
    out_part = contract_rows(cotangent_rows, normed_out).astype(low)
    gate_part = contract_rows(token_rows, d_gate_pre).astype(low)
    d_inner, d_state_part, d_step, taps_part, taps_s_part, skip_part, head_part, held_out, held_gate = backward_core(
        first_pre, second_pre, zi, zs, scanned, d_scan, enter, pos, taps, taps_s, lanes, skip, wide_map, out_part, gate_part
    )
    grad_conv_inner_part = jnp.sum(taps_part, axis=1)
    grad_conv_state_part = jnp.sum(taps_s_part, axis=1)
    head_rows = jnp.sum(head_part, axis=1)[:, :heads]
    skip_row = jnp.sum(jnp.sum(skip_part, axis=0).reshape(heads, -1), axis=1)
    grad_head_part = jnp.concatenate([head_rows, skip_row[None, :]], axis=0)
    d_state_low = pair_scatter(d_state_part, 1).astype(low)
    d_tail = jnp.concatenate([d_inner, d_state_low, d_step], axis=1)
    col_first = core * col_width
    state_cols = lax.dynamic_slice_in_dim(full_first, room + col_first, col_width, 1)
    tail_weights = jnp.concatenate(
        [full_second[:, :room], state_cols, full_second[:, room:]], axis=1
    )
    total = times_transpose(d_gate_pre, full_first[:, :room])
    total = total + times_transpose(d_tail, tail_weights)
    d_normed = pair_scatter(total.astype(low), 0)
    tail_part = contract_rows(token_rows, d_tail).astype(low)
    grad_norm_part = jnp.sum(d_normed * stream * inv_first, axis=0)
    weighted = d_normed * norm_gain
    d_stream = (
        cotangent
        + inv_first * weighted
        - stream * inv_first**3 * jnp.mean(weighted * stream, axis=1, keepdims=True)
    )
    shared = jnp.concatenate([grad_conv_state_part, grad_norm_part.reshape(-1, wide)], axis=0)
    shared = shared + swap(shared)
    vectors = jnp.concatenate(
        [
            grad_conv_inner_part,
            grad_gate_part[None, :],
            pad_cols(grad_head_part, room),
            pad_cols(shared, room),
        ],
        axis=0,
    )
    vectors = jnp.pad(vectors, ((0, -vectors.shape[0] % 8), (0, 0)))
    small_moment = pad_cols(jnp.concatenate([moment_w_state, moment_w_step], axis=1), room)
    moment_rows = jnp.stack([moment_w_out.T, moment_w_inner, moment_w_gate, small_moment]).astype(low)
    own, other, grads, vectors = reduce_all(
        (held_out, held_gate), (tail_part[:, :room], tail_part[:, room:]), vectors, moment_rows
    )
    grads = grads.astype(jnp.float32)
    grad_gate_w = grads[2]
    grad_inner_w = grads[1]
    grad_out_w = grads[0].T
    grad_state_w = grads[3][:, :col_width]
    grad_step_w = grads[3][:, col_width : col_width + heads]
    grad_conv_inner = vectors[:5]
    grad_gate_gain = vectors[5]
    grad_head = vectors[6:9, :heads]
    grad_conv_state = vectors[9:14, :wide]
    grad_norm = vectors[14:17, :wide].reshape(-1)
    m_gate = MU_MAT * moment_w_gate + grad_gate_w
    m_inner = MU_MAT * moment_w_inner + grad_inner_w
    m_state = MU_MAT * moment_w_state + grad_state_w
    m_step = MU_MAT * moment_w_step + grad_step_w
    m_out = MU_MAT * moment_w_out + grad_out_w
    mine = return_rows(orthogonal_owned(own, other, col_width)).astype(jnp.float32)
    new_gate = w_gate - LR_MAT * spread(D, INNER) * mine[2]
    new_inner = w_inner - LR_MAT * spread(D, INNER) * mine[1]
    new_out = w_out - LR_MAT * spread(INNER, D) * mine[0].T
    new_step = w_step - LR_MAT * spread(D, HEADS) * mine[3][:, col_width : col_width + heads]
    state_slice = lax.dynamic_slice_in_dim(w_state, col_first, col_width, 1)
    new_state = state_slice - LR_MAT * spread(D, 2 * STATE) * mine[3][:, :col_width]
    m_norm = MU_VEC * moment_norm_gain + grad_norm
    m_conv_inner = MU_VEC * moment_conv_inner + grad_conv_inner
    m_conv_state = MU_VEC * moment_conv_state + grad_conv_state
    m_head = MU_VEC * moment_head_params + grad_head
    m_gate_gain = MU_VEC * moment_gate_gain + grad_gate_gain
    return (
        output,
        d_stream,
        grad_norm,
        grad_gate_w,
        grad_inner_w,
        grad_state_w,
        grad_step_w,
        grad_conv_inner,
        grad_conv_state,
        grad_head,
        grad_gate_gain,
        grad_out_w,
        norm_gain - LR_VEC * m_norm,
        new_gate,
        new_inner,
        new_state,
        new_step,
        conv_inner - LR_VEC * m_conv_inner,
        conv_state - LR_VEC * m_conv_state,
        head_params - LR_VEC * m_head,
        gate_gain - LR_VEC * m_gate_gain,
        new_out,
        m_norm,
        m_gate,
        m_inner,
        m_state,
        m_step,
        m_conv_inner,
        m_conv_state,
        m_head,
        m_gate_gain,
        m_out,
    )


def solution(mesh):
    paired = mesh.shape["dp"] == 16 and mesh.shape["tensor"] == 2
    return jax.shard_map(
        paired_shards if paired else shards,
        mesh=mesh,
        in_specs=(
            P(("dp", "tensor"), None),
            P(("dp", "tensor"), None),
            P("dp"),
            P(),
            P("dp", "tensor"),
            P("dp", "tensor"),
            P("dp", None),
            P("dp", "tensor"),
            P(None, "tensor"),
            P(),
            P(None, "tensor"),
            P("tensor"),
            P("tensor", "dp"),
            P(),
            P("dp", "tensor"),
            P("dp", "tensor"),
            P("dp", "tensor"),
            P("dp", "tensor"),
            P(None, "tensor"),
            P(),
            P(None, "tensor"),
            P("tensor"),
            P("tensor", "dp"),
        ),
        out_specs=(
            P(("dp", "tensor"), None),
            P(("dp", "tensor"), None),
            P(),
            P("dp", "tensor"),
            P("dp", "tensor"),
            P("dp", "tensor"),
            P("dp", "tensor"),
            P(None, "tensor"),
            P(),
            P(None, "tensor"),
            P("tensor"),
            P("tensor", "dp"),
            P(),
            P("dp", "tensor"),
            P("dp", "tensor"),
            P("dp", "tensor"),
            P("dp", "tensor"),
            P(None, "tensor"),
            P(),
            P(None, "tensor"),
            P("tensor"),
            P("tensor", "dp"),
            P(),
            P("dp", "tensor"),
            P("dp", "tensor"),
            P("dp", "tensor"),
            P("dp", "tensor"),
            P(None, "tensor"),
            P(),
            P(None, "tensor"),
            P("tensor"),
            P("tensor", "dp"),
        ),
        check_vma=False,
    )
```

```python
from functools import partial
import math

import jax
import jax.numpy as jnp
from jax import lax
from jax.experimental import pallas as pl
from jax.experimental.pallas import tpu as pltpu
from jax.sharding import PartitionSpec as P

D = 768
INNER = 1536
HEADS = 24
STATE = 128
BLOCK = 256
NS_STEPS = 5


EPS = 1e-05
NS_A = 3.4445
NS_B = -4.775
NS_C = 2.0315
MU_MAT = 0.95
MU_VEC = 0.9
LR_MAT = 0.3
LR_VEC = 0.001
HIGH = lax.Precision.HIGHEST
CORE = lax.Precision.DEFAULT


def silu_slope(value):
    sig = jax.nn.sigmoid(value)
    return sig * (1.0 + value * (1.0 - sig))


def contract_rows(left, right):
    return lax.dot_general(
        left, right, (((0,), (0,)), ((), ())), preferred_element_type=jnp.float32
    )


def times_transpose(left, right):
    return lax.dot_general(
        left, right, (((1,), (1,)), ((), ())), preferred_element_type=jnp.float32
    )


def causal_conv(signal, taps, positions):
    length = signal.shape[0]
    reach = taps.shape[0] - 1
    total = jnp.zeros_like(signal) + taps[reach]
    for lag_step in range(reach):
        moved = jnp.pad(signal, ((lag_step, 0), (0, 0)))[:length]
        total = total + jnp.where((positions >= lag_step)[:, None], moved * taps[lag_step], 0.0)
    return jax.nn.silu(total)


def mixer_core(inner_pre, state_pre, step_pre, conv_inner, conv_state, head_params, positions, precision=HIGH):
    length = inner_pre.shape[0]
    heads = step_pre.shape[1]
    head_size = inner_pre.shape[1] // heads
    states = state_pre.shape[1] // 2
    blocks = length // BLOCK
    inner_act = causal_conv(inner_pre, conv_inner, positions).reshape(
        blocks, BLOCK, heads, head_size
    )
    state_act = causal_conv(state_pre, conv_state, positions)
    input_map = state_act[:, :states].reshape(blocks, BLOCK, states)
    output_map = state_act[:, states:].reshape(blocks, BLOCK, states)
    step_size = jax.nn.softplus(step_pre + head_params[0])
    log_decay = (step_size * -jnp.exp(head_params[1])).reshape(blocks, BLOCK, heads)
    step_size = step_size.reshape(blocks, BLOCK, heads)
    resets = (positions <= 0).astype(jnp.float32).reshape(blocks, BLOCK)
    order = jnp.arange(BLOCK)
    lower = (order[:, None] >= order[None, :]).astype(jnp.float32)
    cumulative = jnp.einsum("ij,cjh->cih", lower, log_decay, precision=HIGH)
    seen = jnp.einsum("ij,cj->ci", lower, resets, precision=HIGH)
    linked = (seen[:, :, None] == seen[:, None, :]) & (order[:, None] >= order[None, :])[None]
    linked_heads = linked[..., None]
    spacing = cumulative[:, :, None, :] - cumulative[:, None, :, :]
    decay = jnp.where(linked_heads, jnp.exp(jnp.where(linked_heads, spacing, 0.0)), 0.0)
    scores = jnp.einsum("cin,cjn->cij", output_map, input_map, precision=precision)
    mixing = scores[..., None] * decay * step_size[:, None, :, :]
    within = jnp.einsum("cijh,cjhp->cihp", mixing, inner_act, precision=precision)
    tail_linked = (seen[:, -1:] == seen)[..., None]
    tail = (
        jnp.where(
            tail_linked,
            jnp.exp(jnp.where(tail_linked, cumulative[:, -1:, :] - cumulative, 0.0)),
            0.0,
        )
        * step_size
    )
    own_state = jnp.einsum("cjh,cjhp,cjn->chpn", tail, inner_act, input_map, precision=precision)
    carry_rate = jnp.exp(cumulative[:, -1, :]) * (seen[:, -1] == 0).astype(jnp.float32)[:, None]

    state = jnp.zeros((heads, head_size, states), jnp.float32)
    entering = []
    for block in range(blocks):
        entering.append(state)
        state = carry_rate[block][:, None, None] * state + own_state[block]
    entering = jnp.stack(entering)
    fresh = (seen == 0)[..., None]
    carry_in = jnp.where(fresh, jnp.exp(cumulative), 0.0)
    across = (
        jnp.einsum("cin,chpn->cihp", output_map, entering, precision=precision) * carry_in[..., None]
    )
    result = within + across + head_params[2][None, None, :, None] * inner_act
    return result.reshape(length, heads * head_size)


def gram_total(low):
    return lax.psum(
        jnp.dot(low, low.T, preferred_element_type=jnp.float32).astype(jnp.bfloat16), "tensor"
    ).astype(jnp.float32)


def orthogonalize(matrix):
    first = gram_total(matrix.astype(jnp.bfloat16))
    scale = jnp.sqrt(jnp.trace(first)) + 1e-07
    current = (matrix / scale).astype(jnp.bfloat16)
    gram = (first / (scale * scale)).astype(jnp.bfloat16)
    for turn in range(NS_STEPS):
        if turn > 0:
            gram = gram_total(current).astype(jnp.bfloat16)
        applied = jnp.dot(gram, current, preferred_element_type=jnp.float32)
        twice = jnp.dot(gram, applied.astype(jnp.bfloat16), preferred_element_type=jnp.float32)
        current = (NS_A * current.astype(jnp.float32) + NS_B * applied + NS_C * twice).astype(
            jnp.bfloat16
        )
    return current.astype(jnp.float32)


def spread(rows, cols):
    return math.sqrt(max(1.0, rows / cols))


def shards(
    stream,
    cotangent,
    positions,
    norm_gain,
    w_gate,
    w_inner,
    w_state,
    w_step,
    conv_inner,
    conv_state,
    head_params,
    gate_gain,
    w_out,
    moment_norm_gain,
    moment_w_gate,
    moment_w_inner,
    moment_w_state,
    moment_w_step,
    moment_conv_inner,
    moment_conv_state,
    moment_head_params,
    moment_gate_gain,
    moment_w_out,
):
    dp_count = lax.axis_size("dp")
    inv_first = lax.rsqrt(jnp.mean(stream * stream, axis=1, keepdims=True) + EPS)
    normed = (stream * inv_first * norm_gain).astype(jnp.bfloat16)
    token_rows, cotangent_rows = (
        lax.all_gather(normed, "tensor", axis=0, tiled=True),
        lax.all_gather(cotangent.astype(jnp.bfloat16), "tensor", axis=0, tiled=True),
    )
    local_weights = (
        w_gate.astype(jnp.bfloat16),
        w_inner.astype(jnp.bfloat16),
        w_step.astype(jnp.bfloat16),
        w_state.astype(jnp.bfloat16),
        w_out.astype(jnp.bfloat16),
    )
    full_gate, full_inner, full_step, full_state, full_out = (
        lax.all_gather(local_weights[0], "dp", axis=0, tiled=True),
        lax.all_gather(local_weights[1], "dp", axis=0, tiled=True),
        lax.all_gather(local_weights[2], "dp", axis=0, tiled=True),
        lax.all_gather(local_weights[3], "dp", axis=0, tiled=True),
        lax.all_gather(local_weights[4], "dp", axis=1, tiled=True),
    )
    gate_pre = jnp.dot(token_rows, full_gate, preferred_element_type=jnp.float32)
    inner_pre = jnp.dot(token_rows, full_inner, preferred_element_type=jnp.float32)
    state_pre = jnp.dot(token_rows, full_state, preferred_element_type=jnp.float32)
    step_pre = jnp.dot(token_rows, full_step, preferred_element_type=jnp.float32)
    alive = (positions >= 0).astype(jnp.float32)[:, None]
    scanned, core_back = jax.vjp(
        partial(mixer_core, positions=positions),
        inner_pre,
        state_pre,
        step_pre,
        conv_inner,
        conv_state,
        head_params,
    )
    gate_act = jax.nn.silu(gate_pre)
    gated = scanned * gate_act
    square_sum = lax.psum(jnp.sum(gated * gated, axis=1), "tensor")
    inv_second = lax.rsqrt(square_sum / INNER + EPS)[:, None]
    normed_out = (gated * inv_second * gate_gain * alive).astype(jnp.bfloat16)
    mixed = lax.psum_scatter(
        jnp.dot(normed_out, full_out, preferred_element_type=jnp.float32).astype(jnp.bfloat16),
        "tensor",
        scatter_dimension=0,
        tiled=True,
    ).astype(jnp.float32)
    output = stream + mixed
    d_normed_out = times_transpose(cotangent_rows, full_out)
    grad_out_part = contract_rows(normed_out, cotangent_rows)
    scaled = d_normed_out * gate_gain * alive
    grad_gate_part = jnp.sum(d_normed_out * gated * inv_second * alive, axis=0)
    cross_sum = lax.psum(jnp.sum(scaled * gated, axis=1), "tensor")
    d_gated = inv_second * scaled - gated * inv_second**3 * (cross_sum / INNER)[:, None]
    d_gate_pre = (d_gated * scanned * silu_slope(gate_pre)).astype(jnp.bfloat16)
    d_inner, d_state_part, d_step, grad_conv_inner_part, grad_conv_state_part, grad_head_part = (
        core_back(d_gated * gate_act)
    )
    d_state_cols = lax.psum_scatter(
        d_state_part.astype(jnp.bfloat16), "tensor", scatter_dimension=1, tiled=True
    ).astype(jnp.float32)
    d_inner_low = d_inner.astype(jnp.bfloat16)
    d_state_low = d_state_cols.astype(jnp.bfloat16)
    d_step_low = d_step.astype(jnp.bfloat16)
    col_width = d_state_cols.shape[1]
    col_first = lax.axis_index("tensor") * col_width
    state_cols = lax.dynamic_slice_in_dim(full_state, col_first, col_width, 1)
    total = times_transpose(d_gate_pre, full_gate)
    total = total + times_transpose(d_inner_low, full_inner)
    total = total + times_transpose(d_state_low, state_cols)
    d_normed = lax.psum_scatter(
        (total + times_transpose(d_step_low, full_step)).astype(jnp.bfloat16),
        "tensor",
        scatter_dimension=0,
        tiled=True,
    ).astype(jnp.float32)
    grad_gate_w, grad_inner_w, grad_state_w, grad_step_w, grad_out_w = (
        lax.psum_scatter(
            contract_rows(token_rows, d_gate_pre).astype(jnp.bfloat16),
            "dp",
            scatter_dimension=0,
            tiled=True,
        ).astype(jnp.float32),
        lax.psum_scatter(
            contract_rows(token_rows, d_inner_low).astype(jnp.bfloat16),
            "dp",
            scatter_dimension=0,
            tiled=True,
        ).astype(jnp.float32),
        lax.psum_scatter(
            contract_rows(token_rows, d_state_low).astype(jnp.bfloat16),
            "dp",
            scatter_dimension=0,
            tiled=True,
        ).astype(jnp.float32),
        lax.psum_scatter(
            contract_rows(token_rows, d_step_low).astype(jnp.bfloat16),
            "dp",
            scatter_dimension=0,
            tiled=True,
        ).astype(jnp.float32),
        lax.psum_scatter(
            grad_out_part.astype(jnp.bfloat16), "dp", scatter_dimension=1, tiled=True
        ).astype(jnp.float32),
    )
    grad_norm_part = jnp.sum(d_normed * stream * inv_first, axis=0)
    weighted = d_normed * norm_gain
    d_stream = (
        cotangent
        + inv_first * weighted
        - stream * inv_first**3 * jnp.mean(weighted * stream, axis=1, keepdims=True)
    )
    grad_conv_inner, grad_gate_gain, grad_head = lax.psum(
        (grad_conv_inner_part, grad_gate_part, grad_head_part), "dp"
    )
    grad_conv_state, grad_norm = lax.psum((grad_conv_state_part, grad_norm_part), ("dp", "tensor"))
    m_gate = MU_MAT * moment_w_gate + grad_gate_w
    m_inner = MU_MAT * moment_w_inner + grad_inner_w
    m_state = MU_MAT * moment_w_state + grad_state_w
    m_step = MU_MAT * moment_w_step + grad_step_w
    m_out = MU_MAT * moment_w_out + grad_out_w
    room = w_gate.shape[1]
    shard_rows = w_gate.shape[0]
    stacked = jnp.stack(
        [
            m_gate,
            m_inner,
            m_out.T,
            jnp.pad(m_step, ((0, 0), (0, room - m_step.shape[1]))),
            jnp.pad(m_state, ((0, 0), (0, room - m_state.shape[1]))),
        ]
    )
    matrix_count = stacked.shape[0]
    owner_index = jnp.arange(matrix_count, dtype=jnp.int32) * dp_count // matrix_count
    select = (owner_index[None, :] == jnp.arange(dp_count, dtype=jnp.int32)[:, None]).astype(
        jnp.float32
    )
    outgoing = jnp.einsum("jk,krc->jrc", select, stacked, precision=HIGH)
    owned = (
        lax.all_to_all(outgoing.astype(jnp.bfloat16), "dp", split_axis=0, concat_axis=0, tiled=True)
        .astype(outgoing.dtype)
        .reshape(dp_count * shard_rows, room)
    )
    ortho = orthogonalize(owned)
    returned = lax.all_to_all(
        ortho.reshape(dp_count, shard_rows, room).astype(jnp.bfloat16),
        "dp",
        split_axis=0,
        concat_axis=0,
        tiled=True,
    ).astype(jnp.float32)
    mine = jnp.einsum("jk,jrc->krc", select, returned, precision=HIGH)
    new_gate = w_gate - LR_MAT * spread(D, INNER) * mine[0]
    new_inner = w_inner - LR_MAT * spread(D, INNER) * mine[1]
    new_out = w_out - LR_MAT * spread(INNER, D) * mine[2].T
    new_step = w_step - LR_MAT * spread(D, HEADS) * mine[3][:, : w_step.shape[1]]
    state_slice = lax.dynamic_slice_in_dim(w_state, col_first, col_width, 1)
    new_state = state_slice - LR_MAT * spread(D, 2 * STATE) * mine[4][:, :col_width]
    m_norm = MU_VEC * moment_norm_gain + grad_norm
    m_conv_inner = MU_VEC * moment_conv_inner + grad_conv_inner
    m_conv_state = MU_VEC * moment_conv_state + grad_conv_state
    m_head = MU_VEC * moment_head_params + grad_head
    m_gate_gain = MU_VEC * moment_gate_gain + grad_gate_gain
    return (
        output,
        d_stream,
        grad_norm,
        grad_gate_w,
        grad_inner_w,
        grad_state_w,
        grad_step_w,
        grad_conv_inner,
        grad_conv_state,
        grad_head,
        grad_gate_gain,
        grad_out_w,
        norm_gain - LR_VEC * m_norm,
        new_gate,
        new_inner,
        new_state,
        new_step,
        conv_inner - LR_VEC * m_conv_inner,
        conv_state - LR_VEC * m_conv_state,
        head_params - LR_VEC * m_head,
        gate_gain - LR_VEC * m_gate_gain,
        new_out,
        m_norm,
        m_gate,
        m_inner,
        m_state,
        m_step,
        m_conv_inner,
        m_conv_state,
        m_head,
        m_gate_gain,
        m_out,
    )


MESH_ID = pl.DeviceIdType.MESH
SHARD = 48
PLAN = (("out", 768), ("gate", 768), ("inner", 768), ("small", 256))
PLANE_OF = {"small": 0, "inner": 1, "gate": 2, "out": 3}


def place():
    index = lax.axis_index("dp")
    z = lax.div(index, 4)
    y = lax.rem(lax.div(index, 2), 2)
    x = lax.rem(index, 2)
    at_x = {"dp": z * 4 + y * 2 + (1 - x)}
    at_y = {"dp": z * 4 + (1 - y) * 2 + x}
    at_z = [{"dp": lax.rem(z + step, 4) * 4 + y * 2 + x} for step in range(1, 4)]
    return x, y, z, at_x, at_y, at_z


def greet(peers):
    barrier = pltpu.get_barrier_semaphore()
    for peer in peers:
        pl.semaphore_signal(barrier, inc=1, device_id=peer, device_id_type=MESH_ID)
    pl.semaphore_wait(barrier, len(peers))


def remote(src, dst, send, recv, peer):
    return pltpu.make_async_remote_copy(
        src_ref=src, dst_ref=dst, send_sem=send, recv_sem=recv, device_id=peer, device_id_type=MESH_ID
    )

EARLY = 2
COUNT = 8


def half_steps(parts, at_x, at_y, x, y, arrived, summed, arrived_two, one_send, one_recv, two_send, two_recv):
    def span(task, route):
        half = parts[task].shape[-1] // 2
        return pl.ds(route * half, half), pl.ds(0, half)

    def one(task, route):
        cols, mine = span(task, route)
        other = parts[task].at[:, 1 - y, :, :, cols] if route else parts[task].at[:, :, 1 - x, :, cols]
        return remote(
            other, arrived.at[task, route, :, :, :, mine], one_send.at[task, route],
            one_recv.at[task, route], at_y if route else at_x,
        )

    def two(task, route):
        mine = span(task, route)[1]
        return remote(
            summed.at[task, route, :, 1 - x if route else 1 - y, :, mine],
            arrived_two.at[task, route, :, :, mine], two_send.at[task, route],
            two_recv.at[task, route], at_x if route else at_y,
        )

    def add(task, route, own):
        mine = span(task, route)[1]
        got = arrived[task, route, :, :, :, mine]
        summed[task, route, :, :, :, mine] = (own.astype(jnp.float32) + got.astype(jnp.float32)).astype(jnp.bfloat16)

    def settle(task, route, held):
        cols, mine = span(task, route)
        own = summed[task, route, :, x if route else y, :, mine]
        got = arrived_two[task, route, :, :, mine]
        held[:, :, cols] = (own.astype(jnp.float32) + got.astype(jnp.float32)).astype(jnp.bfloat16)

    return span, one, two, add, settle


def early_reduce(parts, held, own, arrived, summed, arrived_two, own_sem, one_send, one_recv, two_send, two_recv):
    step = pl.program_id(0)
    x, y, z, at_x, at_y, _ = place()
    span, one, two, add, settle = half_steps(
        parts, at_x, at_y, x, y, arrived, summed, arrived_two, one_send, one_recv, two_send, two_recv
    )
    pairs = [(task, route) for task in range(EARLY) for route in range(2)]

    def load(task, route):
        cols = span(task, route)[0]
        src = parts[task].at[:, y, :, :, cols] if route else parts[task].at[:, :, x, :, cols]
        return pltpu.make_async_copy(src, own.at[task, route], own_sem.at[task, route])

    @pl.when(step == 0)
    def _():
        greet([at_x, at_y, {"tensor": 1 - lax.axis_index("tensor")}])
        for route in range(2):
            one(0, route).start()
        for task, route in pairs:
            load(task, route).start()
        for route in range(2):
            one(1, route).start()

    for task, at in ((0, 3), (1, 5)):

        @pl.when(step == at)
        def _():
            for route in range(2):
                load(task, route).wait()
                one(task, route).wait()
                add(task, route, own[task, route])
                two(task, route).start()

    for task, at in ((0, 6), (1, 7)):

        @pl.when(step == at)
        def _():
            for route in range(2):
                two(task, route).wait()
                settle(task, route, held[task])


CHUNK = 128
PACK = 16


def sigmoid(value):
    return 0.5 * jnp.tanh(0.5 * value) + 0.5


def expand_matrix():
    row = jnp.arange(128)[:, None]
    col = jnp.arange(768)[None, :] // 64
    return ((row == col) | (row == col + PACK)).astype(jnp.bfloat16)


def two_term(value):
    lane = lax.broadcasted_iota(jnp.int32, value.shape, 1)
    high = value.astype(jnp.bfloat16).astype(jnp.float32)
    return jnp.where(lane < PACK, high, value - high).astype(jnp.bfloat16)


def split_terms(value, terms):
    out = []
    for _ in range(terms):
        piece = value.astype(jnp.bfloat16)
        out.append(piece)
        value = value - piece.astype(jnp.float32)
    return out


def dot(left, right, dims=((1,), (0,))):
    return lax.dot_general(left, right, (dims, ((), ())), preferred_element_type=jnp.float32)


def head_terms(step_ref, head_ref, pos):
    shifted = step_ref[...] + head_ref[0:1, :]
    small = jnp.exp(-jnp.abs(shifted))
    step = jnp.maximum(shifted, 0.0) + jnp.log1p(small)
    log_decay = -step * jnp.exp(head_ref[1:2, :])
    row = lax.broadcasted_iota(jnp.int32, (CHUNK, 128), 0)
    col = lax.broadcasted_iota(jnp.int32, (CHUNK, 128), 1)
    lower = (row >= col).astype(jnp.bfloat16)
    cumulative = sum(dot(lower, piece) for piece in split_terms(log_decay, 3))
    last = cumulative[CHUNK - 1 : CHUNK, :]
    back = (row - col).astype(jnp.float32)
    linked = (row >= col) & (back <= jnp.maximum(pos, 0.0))
    row = row.astype(jnp.float32)
    carry_in = jnp.where(pos > row, jnp.exp(cumulative), 0.0)
    pos_last = pos[CHUNK - 1 : CHUNK, :]
    tail_linked = (CHUNK - 1.0 - row) <= jnp.maximum(pos_last, 0.0)
    tail = jnp.where(tail_linked, jnp.exp(jnp.minimum(last - cumulative, 0.0)), 0.0)
    carry = jnp.where(pos_last > CHUNK - 1.0, jnp.exp(last), 0.0)
    return shifted, step, log_decay, cumulative, linked, carry_in, tail, carry


def pair_decay(cumulative, across, pair):
    parts = []
    for head in (2 * pair, 2 * pair + 1):
        spacing = cumulative[:, head : head + 1] - across[head : head + 1, :]
        parts.append(jnp.exp(jnp.minimum(spacing, 0.0)))
    return parts


def forward_kernel(
    inner_ref, step_ref, gate_ref, state_ref, dno_ref, pos_ref, taps_ref, taps_s_ref, head_ref,
    skip_ref, gain_ref, wide_ref,
    scanned_ref, zi_ref, zs_ref, enter_ref, sums_ref,
    halo_i, halo_s, hold,
):
    @pl.when(pl.program_id(0) == 0)
    def _():
        halo_i[...] = jnp.zeros_like(halo_i)
        halo_s[...] = jnp.zeros_like(halo_s)
        hold[...] = jnp.zeros_like(hold)

    low = jnp.bfloat16
    pos = pos_ref[...]
    marks = [(pos >= lag).astype(jnp.float32) for lag in range(4)]

    def conv(ref, halo, taps, out_ref, first):
        value = ref[:, first : first + 128]
        ext = jnp.concatenate([halo[:, first : first + 128], value], axis=0)
        total = taps[4:5, first : first + 128] + marks[0] * (value * taps[0:1, first : first + 128])
        for lag in range(1, 4):
            moved = pltpu.roll(ext, lag, 0)[8:]
            total = total + marks[lag] * (moved * taps[lag : lag + 1, first : first + 128])
        out_ref[:, first : first + 128] = total
        return total * sigmoid(total)

    shifted, step, log_decay, cumulative, linked, carry_in, tail, carry = head_terms(
        step_ref, head_ref, pos
    )
    across = cumulative.T
    wide = dot(
        jnp.concatenate(
            [
                two_term(step),
                two_term(carry_in),
                two_term(tail * step),
                two_term(jnp.broadcast_to(carry, (16, 128))),
            ],
            axis=0,
        ),
        wide_ref[...],
    )
    input_map = conv(state_ref, halo_s, taps_s_ref, zs_ref, 0).astype(low)
    output_map = conv(state_ref, halo_s, taps_s_ref, zs_ref, 128).astype(low)
    scores = jnp.where(linked, dot(output_map, input_map, ((1,), (1,))), 0.0)
    state = hold[...]
    state_low = state.astype(low)
    enter_ref[...] = state_low
    entered = dot(output_map, state_low)
    lane = lax.broadcasted_iota(jnp.int32, (CHUNK, 128), 1)
    squares = jnp.zeros((CHUNK, 128), jnp.float32)
    crosses = jnp.zeros((CHUNK, 128), jnp.float32)
    fed = []
    for pair in range(6):
        cols = slice(pair * 128, pair * 128 + 128)
        act = conv(inner_ref, halo_i, taps_ref, zi_ref, pair * 128)
        stepped = (wide[:CHUNK, cols] * act).astype(low)
        first, second = pair_decay(cumulative, across, pair)
        mixing = jnp.concatenate([(scores * first).astype(low), (scores * second).astype(low)], axis=0)
        both = dot(mixing, stepped)
        within = jnp.where(lane < 64, both[:CHUNK], both[CHUNK:])
        scanned = (
            within + entered[:, cols] * wide[CHUNK : 2 * CHUNK, cols] + skip_ref[0:1, cols] * act
        )
        scanned_ref[:, cols] = scanned
        fed.append((wide[2 * CHUNK : 3 * CHUNK, cols] * act).astype(low))
        gate = gate_ref[:, cols]
        gated = scanned * (gate * sigmoid(gate))
        squares = squares + gated * gated
        crosses = crosses + dno_ref[:, cols] * gain_ref[0:1, cols] * gated
    fresh = dot(input_map, jnp.concatenate(fed, axis=1), ((0,), (0,)))
    hold[...] = wide[3 * CHUNK : 3 * CHUNK + 1, :] * state + fresh
    halo_i[...] = inner_ref[CHUNK - 8 :, :]
    halo_s[...] = state_ref[CHUNK - 8 :, :]
    square = jnp.sum(squares, axis=1, keepdims=True)
    cross = jnp.sum(crosses * marks[0], axis=1, keepdims=True)
    sums_ref[...] = jnp.where(lane == 0, square, cross)


def gate_kernel(
    gate_ref, scanned_ref, dno_ref, sums_ref, twin_ref, gain_ref, pos_ref,
    normed_ref, d_gate_ref, d_scan_ref, g_gain_ref,
):
    @pl.when(pl.program_id(0) == 0)
    def _():
        g_gain_ref[...] = jnp.zeros_like(g_gain_ref)

    low = jnp.bfloat16
    alive = (pos_ref[...] >= 0).astype(jnp.float32)
    sums = sums_ref[...] + twin_ref[...]
    inv = jnp.broadcast_to(lax.rsqrt(sums[:, 0:1] / INNER + EPS), alive.shape)
    pull = inv * inv * inv * jnp.broadcast_to(sums[:, 1:2] / INNER, alive.shape)
    live = inv * alive
    for pair in range(6):
        cols = slice(pair * 128, pair * 128 + 128)
        gain = gain_ref[0:1, cols]
        gate, scanned, d_normed_out = gate_ref[:, cols], scanned_ref[:, cols], dno_ref[:, cols]
        sig = sigmoid(gate)
        gate_act = gate * sig
        gated = scanned * gate_act
        normed_ref[:, cols] = (gated * live * gain).astype(low)
        product = d_normed_out * gated * live
        g_gain_ref[:, cols] += jnp.sum(product.reshape(CHUNK // 8, 8, 128), axis=0)
        d_gated = live * gain * d_normed_out - gated * pull
        d_scan_ref[:, cols] = (d_gated * gate_act).astype(low)
        d_gate_ref[:, cols] = (d_gated * scanned * (sig * (1.0 + gate * (1.0 - sig)))).astype(low)


def gate_stage(first_pre, scanned, d_normed_out, sums, twin_sums, gain, pos):
    rows = first_pre.shape[0]
    at = lambda width: pl.BlockSpec((CHUNK, width), lambda c: (c, 0))
    f32, low = jnp.float32, jnp.bfloat16
    wide = jax.ShapeDtypeStruct((rows, 768), low)
    return pl.pallas_call(
        gate_kernel,
        grid=(rows // CHUNK,),
        in_specs=[
            at(768), at(768), at(768), at(128), at(128), pl.BlockSpec((1, 768), lambda c: (0, 0)), at(128),
        ],
        out_specs=[at(768), at(768), at(768), pl.BlockSpec((8, 768), lambda c: (0, 0))],
        out_shape=[wide, wide, wide, jax.ShapeDtypeStruct((8, 768), f32)],
        compiler_params=pltpu.CompilerParams(vmem_limit_bytes=40 * 2**20),
        cost_estimate=pl.CostEstimate(flops=10**8, bytes_accessed=15 * 10**6, transcendentals=10**6),
        name="gate_stage",
    )(first_pre, scanned, d_normed_out, sums, twin_sums, gain, pos)


def backward_kernel(
    inner_ref, step_ref, state_ref, zi_ref, zs_ref, scanned_ref, dscan_ref, enter_ref, pos_ref,
    taps_ref, taps_s_ref, head_ref, skip_ref, wide_ref, out_part, gate_part,
    d_inner_ref, d_state_ref, d_step_ref, g_taps_ref, g_taps_s_ref, g_skip_ref, g_head_ref, held_out, held_gate,
    halo_i, halo_s, halo_p, hold, state_out, state_in, state_send, state_recv, *reducing,
):
    low = jnp.bfloat16
    step_at = pl.program_id(0)
    last_step = pl.num_programs(0) - 1
    core = lax.axis_index("tensor")
    early_reduce((out_part, gate_part), (held_out, held_gate), *reducing)
    chunk = last_step - step_at
    twin = {"tensor": 1 - core}
    here = pl.ds(pl.multiple_of(chunk * CHUNK, CHUNK), CHUNK)

    @pl.when(pl.program_id(0) == 0)
    def _():
        for ref in (halo_i, halo_s, halo_p, hold, g_taps_ref, g_taps_s_ref, g_skip_ref, g_head_ref):
            ref[...] = jnp.zeros_like(ref)

    pos = pos_ref[...]
    pos_ext = jnp.concatenate([pos, halo_p[...]], axis=0)
    marks = [(pos_ext >= lag).astype(jnp.float32) for lag in range(4)]
    lane = lax.broadcasted_iota(jnp.int32, (CHUNK, 128), 1)
    row = lax.broadcasted_iota(jnp.int32, (CHUNK, 128), 0)
    col = lane

    def slope(total):
        sig = sigmoid(total)
        return sig * (1.0 + total * (1.0 - sig)), total * sig

    def fold(value):
        return jnp.sum(value.reshape(CHUNK // 8, 8, 128), axis=0)

    def conv_back(grad, ref, halo, taps, out_ref, g_ref, first):
        cols = slice(first, first + 128)
        ext = jnp.concatenate([grad, halo[:, cols]], axis=0)
        value = ref[:, cols]
        halo[:, cols] = grad[:8]
        g_ref[4, :, cols] += fold(grad)
        total = jnp.zeros((CHUNK, 128), jnp.float32)
        for lag in range(4):
            masked = ext * marks[lag]
            if lag:
                masked = pltpu.roll(masked, CHUNK + 8 - lag, 0)
            masked = masked[:CHUNK]
            g_ref[lag, :, cols] += fold(masked * value)
            total = total + masked * taps[lag : lag + 1, cols]
        if out_ref is not None:
            out_ref[:, cols] = total.astype(low)
        return total

    shifted, step, log_decay, cumulative, linked, carry_in, tail, carry = head_terms(
        step_ref, head_ref, pos
    )
    across = cumulative.T
    wide = dot(
        jnp.concatenate(
            [
                two_term(step),
                two_term(carry_in),
                two_term(tail),
                two_term(jnp.broadcast_to(carry, (16, 128))),
            ],
            axis=0,
        ),
        wide_ref[...],
    )
    slope_b, input_map = slope(zs_ref[:, :128])
    slope_c, output_map = slope(zs_ref[:, 128:])
    input_low, output_low = input_map.astype(low), output_map.astype(low)
    scores = jnp.where(linked, dot(output_low, input_low, ((1,), (1,))), 0.0)
    entering = enter_ref[...]
    d_next = hold[...]
    d_next_low = d_next.astype(low)
    pulled = dot(input_low, d_next_low)
    d_scores = jnp.zeros((CHUNK, 128), jnp.float32)
    d_entered, fed, balance, direct, extra = [], [], [], [], []
    carry_wide = wide[3 * CHUNK : 3 * CHUNK + 1, :]
    carry_grad = jnp.sum(d_next * entering.astype(jnp.float32), axis=0, keepdims=True) * carry_wide
    for pair in range(6):
        cols = slice(pair * 128, pair * 128 + 128)
        slope_x, act = slope(zi_ref[:, cols])
        d_low = dscan_ref[:, cols]
        skip = skip_ref[0:1, cols]
        stepped = (wide[:CHUNK, cols] * act).astype(low)
        stepped_wide = stepped.astype(jnp.float32)
        d_exact = d_low.astype(jnp.float32)
        d_both = jnp.concatenate(
            [jnp.where(lane < 64, d_exact, 0.0).astype(low), jnp.where(lane < 64, 0.0, d_exact).astype(low)],
            axis=0,
        )
        first, second = pair_decay(cumulative, across, pair)
        mixing = jnp.concatenate([(scores * first).astype(low), (scores * second).astype(low)], axis=0)
        d_mixing = dot(d_both, stepped, ((1,), (1,)))
        d_scores = d_scores + d_mixing[:CHUNK] * first + d_mixing[CHUNK:] * second
        tail_cols = wide[2 * CHUNK : 3 * CHUNK, cols]
        tailed = tail_cols * pulled[:, cols]
        d_stepped = dot(mixing, d_both, ((0,), (0,))) + tailed
        extra.append(jnp.sum(stepped_wide * tailed, axis=0, keepdims=True) + carry_grad[:, cols])
        fed.append((tail_cols * stepped_wide).astype(low))
        d_entered.append((wide[CHUNK : 2 * CHUNK, cols] * d_exact).astype(low))
        balance.append(d_exact * (scanned_ref[:, cols] - skip * act) - stepped_wide * d_stepped)
        direct.append(act * d_stepped)
        g_skip_ref[:, cols] += fold(d_exact * act)
        d_act = skip * d_exact + wide[:CHUNK, cols] * d_stepped
        conv_back(d_act * slope_x, inner_ref, halo_i, taps_ref, d_inner_ref, g_taps_ref, pair * 128)
    d_entered = jnp.concatenate(d_entered, axis=1)
    fed = jnp.concatenate(fed, axis=1)
    d_scores = jnp.where(linked, d_scores, 0.0).astype(low)
    d_output = dot(d_scores, input_low) + dot(d_entered, entering, ((1,), (1,)))
    d_input = dot(d_scores, output_low, ((0,), (0,))) + dot(fed, d_next_low, ((1,), (1,)))
    hold[...] = carry_wide * d_next + dot(output_low, d_entered, ((0,), (0,)))
    for_first = conv_back(d_input * slope_b, state_ref, halo_s, taps_s_ref, None, g_taps_s_ref, 0)
    for_second = conv_back(d_output * slope_c, state_ref, halo_s, taps_s_ref, None, g_taps_s_ref, 128)
    state_out[step_at] = jnp.where(core == 0, for_second, for_first).astype(low)
    d_state_ref[here, :] = jnp.where(core == 0, for_first, for_second).astype(low)

    def lend(at):
        return remote(state_out.at[at], state_in.at[at], state_send.at[at], state_recv.at[at], twin)

    lend(step_at).start()
    halo_p[...] = pos[:8]
    spread_back = wide_ref[...]
    extra = jnp.broadcast_to(jnp.concatenate(extra, axis=1), (16, 768))
    stacked = jnp.concatenate(
        split_terms(jnp.concatenate(balance, axis=1), 2)
        + split_terms(jnp.concatenate(direct, axis=1), 2)
        + split_terms(extra, 2),
        axis=0,
    )
    summed = dot(stacked, spread_back, ((1,), (1,)))
    d_sum = summed[:CHUNK] + summed[CHUNK : 2 * CHUNK]
    d_direct = summed[2 * CHUNK : 3 * CHUNK] + summed[3 * CHUNK : 4 * CHUNK]
    d_last = summed[4 * CHUNK : 4 * CHUNK + 1] + summed[4 * CHUNK + 16 : 4 * CHUNK + 17]
    upper = (row <= col).astype(low)
    d_decay = sum(dot(upper, piece) for piece in split_terms(d_sum, 3)) + d_last
    d_step = (d_direct - d_decay * jnp.exp(head_ref[1:2, :])) * sigmoid(shifted)
    d_step = jnp.where(lane < PACK, d_step, 0.0)
    d_step_ref[...] = d_step.astype(low)
    g_head_ref[0] += fold(d_step)
    g_head_ref[1] += fold(d_decay * log_decay)

    @pl.when(step_at == last_step)
    def _():
        for at in range(COUNT):
            lend(at).wait()
            rows = pl.ds((COUNT - 1 - at) * CHUNK, CHUNK)
            d_state_ref[rows, :] = (
                d_state_ref[rows, :].astype(jnp.float32) + state_in[at].astype(jnp.float32)
            ).astype(low)


def forward_core(first_pre, second_pre, d_normed_out, pos, taps, taps_s, heads_lanes, skip, gain, wide):
    rows = first_pre.shape[0]
    at = lambda width, col: pl.BlockSpec((CHUNK, width), lambda c: (c, col))
    whole = lambda arr: pl.BlockSpec(arr.shape, lambda c: (0,) * arr.ndim)
    f32 = jnp.float32
    return pl.pallas_call(
        forward_kernel,
        grid=(rows // CHUNK,),
        in_specs=[
            at(768, 0), at(128, 6), at(768, 0), at(256, 3), at(768, 0), at(128, 0),
            whole(taps), whole(taps_s), whole(heads_lanes), whole(skip), whole(gain), whole(wide),
        ],
        out_specs=[at(768, 0), at(768, 0), at(256, 0), at(768, 0), at(128, 0)],
        out_shape=[
            jax.ShapeDtypeStruct((rows, 768), f32),
            jax.ShapeDtypeStruct((rows, 768), f32),
            jax.ShapeDtypeStruct((rows, 256), f32),
            jax.ShapeDtypeStruct((rows, 768), jnp.bfloat16),
            jax.ShapeDtypeStruct((rows, 128), f32),
        ],
        scratch_shapes=[
            pltpu.VMEM((8, 768), f32), pltpu.VMEM((8, 256), f32), pltpu.VMEM((128, 768), f32),
        ],
        compiler_params=pltpu.CompilerParams(vmem_limit_bytes=40 * 2**20),
        cost_estimate=pl.CostEstimate(flops=8 * 10**9, bytes_accessed=24 * 10**6, transcendentals=4 * 10**6),
        name="mixer_forward",
    )(second_pre, second_pre, first_pre, first_pre, d_normed_out, pos, taps, taps_s, heads_lanes, skip, gain, wide)


def backward_core(
    first_pre, second_pre, zi, zs, scanned, d_scan, enter, pos, taps, taps_s, heads_lanes, skip, wide, out_part, gate_part
):
    rows = first_pre.shape[0]
    count = rows // CHUNK
    at = lambda width, col: pl.BlockSpec((CHUNK, width), lambda c: (count - 1 - c, col))
    whole = lambda shape: pl.BlockSpec(shape, lambda c: (0,) * len(shape))
    f32, low = jnp.float32, jnp.bfloat16
    return pl.pallas_call(
        backward_kernel,
        grid=(count,),
        in_specs=[
            at(768, 0), at(128, 6), at(256, 3), at(768, 0), at(256, 0), at(768, 0), at(768, 0),
            at(768, 0), at(128, 0),
            whole(taps.shape), whole(taps_s.shape), whole(heads_lanes.shape), whole(skip.shape), whole(wide.shape),
            pl.BlockSpec(memory_space=pl.ANY), pl.BlockSpec(memory_space=pl.ANY),
        ],
        out_specs=[
            at(768, 0), whole((rows, 128)), at(128, 0),
            whole((5, 8, 768)), whole((5, 8, 256)), whole((8, 768)), whole((2, 8, 128)),
            whole((4, SHARD, 768)), whole((4, SHARD, 768)),
        ],
        out_shape=[
            jax.ShapeDtypeStruct((rows, 768), low),
            jax.ShapeDtypeStruct((rows, 128), low),
            jax.ShapeDtypeStruct((rows, 128), low),
            jax.ShapeDtypeStruct((5, 8, 768), f32),
            jax.ShapeDtypeStruct((5, 8, 256), f32),
            jax.ShapeDtypeStruct((8, 768), f32),
            jax.ShapeDtypeStruct((2, 8, 128), f32),
            jax.ShapeDtypeStruct((4, SHARD, 768), low),
            jax.ShapeDtypeStruct((4, SHARD, 768), low),
        ],
        scratch_shapes=[
            pltpu.VMEM((8, 768), f32), pltpu.VMEM((8, 256), f32), pltpu.VMEM((8, 128), f32),
            pltpu.VMEM((128, 768), f32),
            pltpu.VMEM((COUNT, CHUNK, 128), low), pltpu.VMEM((COUNT, CHUNK, 128), low),
            pltpu.SemaphoreType.DMA((COUNT,)), pltpu.SemaphoreType.DMA((COUNT,)),
            pltpu.VMEM((EARLY, 2, 4, 2, SHARD, 384), low),
            pltpu.VMEM((EARLY, 2, 4, 2, SHARD, 384), low),
            pltpu.VMEM((EARLY, 2, 4, 2, SHARD, 384), low),
            pltpu.VMEM((EARLY, 2, 4, SHARD, 384), low),
        ]
        + [pltpu.SemaphoreType.DMA((EARLY, 2))] * 5,
        compiler_params=pltpu.CompilerParams(
            collective_id=3, has_side_effects=True, vmem_limit_bytes=48 * 2**20
        ),
        cost_estimate=pl.CostEstimate(flops=16 * 10**9, bytes_accessed=24 * 10**6, transcendentals=6 * 10**6),
        name="mixer_backward",
    )(
        second_pre, second_pre, first_pre, zi, zs, scanned, d_scan, enter, pos, taps, taps_s, heads_lanes, skip, wide,
        out_part.reshape(4, 2, 2, SHARD, 768), gate_part.reshape(4, 2, 2, SHARD, 768),
    )


def swap(value):
    return lax.ppermute(value, "tensor", [(0, 1), (1, 0)])


def pad_cols(value, width):
    return jnp.pad(value, ((0, 0), (0, width - value.shape[1])))


GATHER_PIECES = (
    (1, 0, 384, 0), (1, 384, 512, 1), (0, 0, 512, 0), (0, 512, 512, 1), (2, 0, 384, 0), (2, 384, 384, 1),
)


def gather_kernel(
    first_ref, second_ref, out_ref, stream_ref, cot_ref, gain_ref,
    full_first, full_second, full_out, rows_ref, cots_ref, pre_first, pre_second, pre_out,
    held_first, held_second, held_out,
    pre_sem, row_sem, z_send, z_recv, one_send, one_recv, two_send, two_recv,
):
    x, y, z, at_x, at_y, at_z = place()
    core = lax.axis_index("tensor")
    twin = {"tensor": 1 - core}
    greet([at_x, at_y, twin] + at_z)
    shards = (first_ref, second_ref, out_ref)
    fulls = (full_first, full_second, full_out)
    results = ((held_first, pre_first), (held_second, pre_second), (held_out, pre_out))
    z_copies, ones, twos, copies = {}, {}, {}, []

    def step_zero(piece):
        which, start, width, _ = GATHER_PIECES[piece]
        cols = pl.ds(start, width)
        z_copies[piece] = []
        for step, peer in enumerate(at_z):
            copy = remote(
                shards[which].at[:, cols], fulls[which].at[z, y, x, :, cols],
                z_send.at[piece, step], z_recv.at[piece, step], peer,
            )
            copy.start()
            z_copies[piece].append(copy)

    def step_one(piece):
        which, start, width, route = GATHER_PIECES[piece]
        for copy in z_copies[piece]:
            copy.wait()
        part = fulls[which].at[:, y, x, :, pl.ds(start, width)]
        ones[piece] = remote(part, part, one_send.at[piece], one_recv.at[piece], at_x if route else at_y)
        ones[piece].start()

    def step_two(piece):
        which, start, width, route = GATHER_PIECES[piece]
        cols = pl.ds(start, width)
        ones[piece].wait()
        part = fulls[which].at[:, y, :, :, cols] if route else fulls[which].at[:, :, x, :, cols]
        twos[piece] = remote(part, part, two_send.at[piece], two_recv.at[piece], at_y if route else at_x)
        twos[piece].start()

    def finish(piece):
        which, start, width, _ = GATHER_PIECES[piece]
        cols = pl.ds(start, width)
        twos[piece].wait()
        left = cots_ref if which == 2 else rows_ref
        held, pre = results[which]
        weights = fulls[which]

        def tile(at, carry):
            here = pl.ds(pl.multiple_of(lax.rem(at, 2) * 256, 256), 256)
            there = pl.ds(pl.multiple_of(at * 256, 256), 256)
            held[there, cols] = dot(
                left[lax.div(at, 2), here, :], weights[:, :, :, :, cols].reshape(768, width)
            )
            return carry

        lax.fori_loop(0, 4, tile, 0)
        copy = pltpu.make_async_copy(held.at[:, cols], pre.at[:, cols], pre_sem.at[piece])
        copy.start()
        copies.append(copy)

    step_zero(0)
    for shard, full in zip(shards, fulls):
        full[z, y, x] = shard[...]
    step_zero(1)
    for part in range(4):
        here = pl.ds(part * 128, 128)
        value = stream_ref[here, :]
        inv = lax.rsqrt(jnp.sum(value * value, axis=1, keepdims=True) / D + EPS)
        rows_ref[core, here, :] = (value * inv * gain_ref[...]).astype(jnp.bfloat16)
        cots_ref[core, here, :] = cot_ref[here, :].astype(jnp.bfloat16)
    swaps = []
    for at, ref in enumerate((rows_ref, cots_ref)):
        swaps.append(remote(ref.at[core], ref.at[core], row_sem.at[at], row_sem.at[2 + at], twin))
        swaps[-1].start()
    count = len(GATHER_PIECES)
    for piece in range(count + 1):
        if piece < count:
            step_one(piece)
        if piece + 2 < count:
            step_zero(piece + 2)
        if piece >= 1:
            step_two(piece - 1)
        if piece == 3:
            for copy in swaps:
                copy.wait()
        if piece >= 4:
            finish(piece - 4)
    for piece in range(count - 3, count):
        finish(piece)
    for copy in copies:
        copy.wait()


def gather_all(first, second, out, stream, cotangent, gain):
    f32, low = jnp.float32, jnp.bfloat16
    vmem = pl.BlockSpec(memory_space=pltpu.VMEM)
    count = len(GATHER_PIECES)
    dma = pltpu.SemaphoreType.DMA
    tokens = 2 * stream.shape[0]
    full = lambda arr: jax.ShapeDtypeStruct((4, 2, 2) + arr.shape, low)
    rows = jax.ShapeDtypeStruct((2,) + stream.shape, low)
    pre = lambda arr: jax.ShapeDtypeStruct((tokens, arr.shape[1]), f32)
    got = pl.pallas_call(
        gather_kernel,
        in_specs=[vmem] * 6,
        out_specs=[vmem] * 5 + [pl.BlockSpec(memory_space=pl.ANY)] * 3,
        out_shape=[full(first), full(second), full(out), rows, rows, pre(first), pre(second), pre(out)],
        scratch_shapes=[
            pltpu.VMEM((tokens, first.shape[1]), f32),
            pltpu.VMEM((tokens, second.shape[1]), f32),
            pltpu.VMEM((tokens, out.shape[1]), f32),
            dma((count,)), dma((4,)), dma((count, 3)), dma((count, 3)),
            dma((count,)), dma((count,)), dma((count,)), dma((count,)),
        ],
        compiler_params=pltpu.CompilerParams(
            collective_id=0, has_side_effects=True, vmem_limit_bytes=48 * 2**20
        ),
        cost_estimate=pl.CostEstimate(flops=4 * 10**9, bytes_accessed=120 * 10**6, transcendentals=0),
        name="gather_weights",
    )(first, second, out, stream, cotangent, gain)
    return [item.reshape(-1, item.shape[-1]) for item in got]


SHARED_ROW = 9
NORM_ROW = 14


def reduce_kernel(
    held_out, held_gate, inner_ref, small_ref, vec_ref, moment_ref, gain_ref, *rest,
):
    sources, rest = rest[:10], rest[10:]
    whole_ref, other_ref, grads_ref, total_ref, output_ref, d_stream_ref = rest[:6]
    local, rest = rest[6:16], rest[16:]
    reduce_body(
        held_out, held_gate, inner_ref, small_ref, vec_ref, moment_ref, gain_ref, sources,
        whole_ref, other_ref, grads_ref, total_ref, output_ref, d_stream_ref, local, *rest,
    )


def reduce_body(
    held_out, held_gate, inner_ref, small_ref, vec_ref, moment_ref, gain_ref, sources,
    whole_ref, other_ref, grads_ref, total_ref, output_ref, d_stream_ref, local,
    load_sem, mine_f, lent_b, got_b, vec_own, vec_twin, w_send, w_recv,
    arrived, summed, arrived_two, held_inner, held_small, slots, moments,
    block, back, vec_in, vec_mid, vec_slots,
    m_send, m_recv, one_send, one_recv, two_send, two_recv, z_send, z_recv, g_send, g_recv,
    p_send, p_recv, t_send, t_recv, v_send, v_recv,
):
    f32, low = jnp.float32, jnp.bfloat16
    x, y, z, at_x, at_y, at_z = place()
    core = lax.axis_index("tensor")
    twin = {"tensor": 1 - core}
    greet([at_x, at_y, twin] + at_z)
    parts = (inner_ref, small_ref)
    held = (held_out, held_gate, held_inner, held_small)
    steps_z = [lax.rem(z + step, 4) for step in range(1, 4)]
    span, one, two, add, settle = half_steps(
        parts, at_x, at_y, x, y, arrived, summed, arrived_two, one_send, one_recv, two_send, two_recv
    )

    def to_plane(task):
        plane, width = PLANE_OF[PLAN[task][0]], PLAN[task][1]

        @pl.when(z != plane)
        def _():
            remote(
                held[task], slots.at[z, :, :, pl.ds(0, width)], z_send.at[task], z_recv.at[z],
                {"dp": plane * 4 + y * 2 + x},
            ).start()

    for task in range(2):
        for route in range(2):
            one(task, route).start()
    to_plane(0)
    to_plane(1)
    moment_copies = []
    for step, (peer, plane) in enumerate(zip(at_z, steps_z)):
        copy = remote(moment_ref.at[plane], moments.at[z], m_send.at[step], m_recv.at[step], peer)
        copy.start()
        moment_copies.append(copy)
    loads = [pltpu.make_async_copy(src, dst, load_sem.at[at]) for at, (src, dst) in enumerate(zip(sources, local))]
    for copy in loads:
        copy.start()
    d_gate, d_inner, d_state, d_step, normed, w_first, w_second, w_out, stream_ref, cot_ref = local
    half_rows = stream_ref.shape[0]
    turned = ((1,), (1,))
    state_cols = pl.ds(pl.multiple_of(768 + core * 128, 128), 128)

    def product(which, rows):
        if which == 1:
            return dot(normed[rows, :], w_out[...], turned)
        first = dot(d_gate[rows, :], w_first[:, pl.ds(0, 768)], turned)
        second = dot(d_inner[rows, :], w_second[:, pl.ds(0, 768)], turned)
        third = dot(d_state[rows, :], w_first[:, state_cols], turned)
        return first + second + third + dot(d_step[rows, :], w_second[:, pl.ds(768, 128)], turned)

    for copy in loads:
        copy.wait()

    def products(who, store):
        for which in range(2):

            def tile(at, carry):
                rows = pl.ds(pl.multiple_of(who * half_rows + at * 128, 128), 128)
                store(which, pl.ds(pl.multiple_of(at * 128, 128), 128), product(which, rows))
                return carry

            lax.fori_loop(0, half_rows // 128, tile, 0)

    def store_lent(which, rows, value):
        lent_b[which, rows, :] = value.astype(low)

    def store_mine(which, rows, value):
        mine_f[which, rows, :] = value

    products(1 - core, store_lent)
    lends = []
    for which in range(2):
        lends.append(remote(lent_b.at[which], got_b.at[which], w_send.at[which], w_recv.at[which], twin))
        lends[-1].start()
    products(core, store_mine)
    for task in range(2):
        for route in range(2):
            cols = span(task, route)[0]
            one(task, route).wait()
            add(task, route, parts[task][:, y, :, :, cols] if route else parts[task][:, :, x, :, cols])
            two(task, route).start()
    for copy in lends:
        copy.wait()
    grad_norm = jnp.zeros((1, 768), f32)
    gain = gain_ref[...]
    for part in range(half_rows // 128):
        rows = pl.ds(part * 128, 128)
        value = stream_ref[rows, :]
        output_ref[rows, :] = value + (mine_f[1, rows, :] + got_b[1, rows, :].astype(f32))
        inv = lax.rsqrt(jnp.sum(value * value, axis=1, keepdims=True) / D + EPS)
        d_normed = mine_f[0, rows, :] + got_b[0, rows, :].astype(f32)
        scaled = value * inv
        grad_norm = grad_norm + jnp.sum(d_normed * scaled, axis=0, keepdims=True)
        weighted = d_normed * gain
        inner = jnp.sum(weighted * scaled, axis=1, keepdims=True) / D
        d_stream_ref[rows, :] = cot_ref[rows, :] + inv * (weighted - scaled * inner)
    vec_rows = lax.broadcasted_iota(jnp.int32, vec_ref.shape, 0)
    vec_own[...] = jnp.where(vec_rows == NORM_ROW, grad_norm, vec_ref[...])
    vec_x = remote(vec_own, vec_in.at[0], v_send.at[0], v_recv.at[0], at_x)
    vec_x.start()
    for task in range(2):
        for route in range(2):
            two(task, route).wait()
            settle(task, route, held[2 + task])
        to_plane(2 + task)
    vec_x.wait()
    vec_mid[0] = vec_own[...] + vec_in[0]
    vec_y = remote(vec_mid.at[0], vec_in.at[1], v_send.at[1], v_recv.at[1], at_y)
    vec_y.start()
    for copy in moment_copies:
        copy.wait()
    moments[z] = moment_ref[z]
    vec_y.wait()
    vec_mid[1] = vec_mid[0] + vec_in[1]
    vec_slots[z] = vec_mid[1]
    vec_z = []
    for step, peer in enumerate(at_z):
        copy = remote(vec_mid.at[1], vec_slots.at[z], v_send.at[2 + step], v_recv.at[2 + step], peer)
        copy.start()
        vec_z.append(copy)

    for task, (name, width) in enumerate(PLAN):
        plane = PLANE_OF[name]
        cols = pl.ds(0, width)

        @pl.when(z == plane)
        def _():
            for source in range(4):
                if source != plane:
                    remote(
                        held[task], slots.at[source, :, :, cols], z_send.at[task], z_recv.at[source], at_x
                    ).wait_recv()
            total = held[task][...].astype(f32)
            for source in range(4):
                if source != plane:
                    total = total + slots[source, :, :, cols].astype(f32)
            if width < 768:
                back[...] = jnp.zeros_like(back)
                block[...] = jnp.zeros_like(block)
            back[:, :, cols] = total.astype(low)
            block[:, :, cols] = (MU_MAT * moments[:, :, cols].astype(f32) + total).astype(low)

    half = 384
    routes = (pl.ds(0, half), pl.ds(half, half))
    for row in range(4):
        whole_ref[row, y, x] = block[row]
    plane_one = []
    for route, peer in enumerate((at_x, at_y)):
        copy = remote(
            block.at[:, :, routes[route]], whole_ref.at[:, y, x, :, routes[route]],
            p_send.at[0, route], p_recv.at[0, route], peer,
        )
        copy.start()
        plane_one.append(copy)
    twin_own = remote(block, other_ref.at[:, y, x], t_send.at[0], t_recv.at[0], twin)
    twin_own.start()
    grads_ref[z] = back[z]
    returns = []
    for step, (peer, plane) in enumerate(zip(at_z, steps_z)):
        copy = remote(back.at[plane], grads_ref.at[z], g_send.at[step], g_recv.at[step], peer)
        copy.start()
        returns.append(copy)
    plane_two = []
    for route, peer in enumerate((at_y, at_x)):
        plane_one[route].wait()
        part = (
            whole_ref.at[:, :, x, :, routes[1]] if route else whole_ref.at[:, y, :, :, routes[0]]
        )
        copy = remote(part, part, p_send.at[1, route], p_recv.at[1, route], peer)
        copy.start()
        plane_two.append(copy)
    twins = [twin_own]
    for route in range(2):
        src = whole_ref.at[:, 1 - y, x, :, routes[1]] if route else whole_ref.at[:, y, 1 - x, :, routes[0]]
        dst = other_ref.at[:, 1 - y, x, :, routes[1]] if route else other_ref.at[:, y, 1 - x, :, routes[0]]
        copy = remote(src, dst, t_send.at[1 + route], t_recv.at[1 + route], twin)
        copy.start()
        twins.append(copy)
    for route in range(2):
        plane_two[route].wait()
        src = whole_ref.at[:, :, 1 - x, :, routes[1]] if route else whole_ref.at[:, 1 - y, :, :, routes[0]]
        dst = other_ref.at[:, :, 1 - x, :, routes[1]] if route else other_ref.at[:, 1 - y, :, :, routes[0]]
        copy = remote(src, dst, t_send.at[3 + route], t_recv.at[3 + route], twin)
        copy.start()
        twins.append(copy)
    for copy in vec_z:
        copy.wait()
    vec_mid[0] = (vec_slots[0] + vec_slots[1]) + (vec_slots[2] + vec_slots[3])
    vec_swap = remote(vec_mid.at[0], vec_twin, w_send.at[2], w_recv.at[2], twin)
    vec_swap.start()
    for copy in twins + returns:
        copy.wait()
    vec_swap.wait()
    total_ref[...] = vec_mid[0] + jnp.where(vec_rows >= SHARED_ROW, vec_twin[...], 0.0)
    for task, (name, width) in enumerate(PLAN):
        plane = PLANE_OF[name]

        @pl.when(z != plane)
        def _():
            remote(
                held[task], slots.at[z, :, :, pl.ds(0, width)], z_send.at[task], z_recv.at[z],
                {"dp": plane * 4 + y * 2 + x},
            ).wait_send()


def reduce_all(held, parts, vectors, moments, gain, sources):
    f32, low = jnp.float32, jnp.bfloat16
    vmem = pl.BlockSpec(memory_space=pltpu.VMEM)
    dma = pltpu.SemaphoreType.DMA
    parts = [part.reshape(4, 2, 2, SHARD, part.shape[1]) for part in parts]
    buf = pltpu.VMEM
    tokens = sources[-1].shape
    whole, other, grads, total, output, d_stream = pl.pallas_call(
        reduce_kernel,
        in_specs=[vmem] * 7 + [pl.BlockSpec(memory_space=pl.ANY)] * len(sources),
        out_specs=[vmem] * 6,
        out_shape=[
            jax.ShapeDtypeStruct((4, 2, 2, SHARD, 768), low),
            jax.ShapeDtypeStruct((4, 2, 2, SHARD, 768), low),
            jax.ShapeDtypeStruct((4, SHARD, 768), low),
            jax.ShapeDtypeStruct(vectors.shape, f32),
            jax.ShapeDtypeStruct(tokens, f32),
            jax.ShapeDtypeStruct(tokens, f32),
        ],
        scratch_shapes=[buf(item.shape, item.dtype) for item in sources]
        + [
            dma((len(sources),)), buf((2,) + tokens, f32), buf((2,) + tokens, low), buf((2,) + tokens, low),
            buf(vectors.shape, f32), buf(vectors.shape, f32), dma((3,)), dma((3,)),
            buf((2, 2, 4, 2, SHARD, 384), low), buf((2, 2, 4, 2, SHARD, 384), low),
            buf((2, 2, 4, SHARD, 384), low),
            buf((4, SHARD, 768), low), buf((4, SHARD, 256), low),
            buf((4, 4, SHARD, 768), low), buf((4, SHARD, 768), low),
            buf((4, SHARD, 768), low), buf((4, SHARD, 768), low),
            buf((2,) + vectors.shape, f32), buf((2,) + vectors.shape, f32), buf((4,) + vectors.shape, f32),
            dma((3,)), dma((3,)), dma((2, 2)), dma((2, 2)), dma((2, 2)), dma((2, 2)),
            dma((4,)), dma((4,)), dma((3,)), dma((3,)), dma((2, 2)), dma((2, 2)),
            dma((5,)), dma((5,)), dma((5,)), dma((5,)),
        ],
        compiler_params=pltpu.CompilerParams(
            collective_id=1, has_side_effects=True, vmem_limit_bytes=56 * 2**20
        ),
        cost_estimate=pl.CostEstimate(flops=0, bytes_accessed=150 * 10**6, transcendentals=0),
        name="reduce_grads",
    )(*held, *parts, vectors, moments, gain, *sources)
    return whole.reshape(768, 768), other.reshape(768, 768), grads, total, output, d_stream


def newton_kernel(full_ref, out_ref, current, gram, mix):
    f32, low = jnp.float32, jnp.bfloat16
    rows, cols = current.shape
    tile = 256
    count = rows // tile
    row_ids = lax.broadcasted_iota(jnp.int32, (tile, tile), 0)
    col_ids = lax.broadcasted_iota(jnp.int32, (tile, tile), 1)
    blocks = [pl.ds(at * tile, tile) for at in range(count)]

    def symmetric(source, store):
        for first in range(count):
            for second in range(first, count):
                store(first, second, dot(source[blocks[first], :], source[blocks[second], :], ((1,), (1,))))

    def put(ref, first, second, value):
        ref[blocks[first], blocks[second]] = value.astype(low)
        if first != second:
            ref[blocks[second], blocks[first]] = value.T.astype(low)

    firsts = {}
    symmetric(full_ref, lambda first, second, value: firsts.update({(first, second): value}))
    trace = sum(
        jnp.sum(jnp.where(row_ids == col_ids, firsts[at, at], 0.0), keepdims=True) for at in range(count)
    )
    scale = jnp.sqrt(trace) + 1e-07
    inverse, inverse_square = 1.0 / scale, 1.0 / (scale * scale)
    for (first, second), value in firsts.items():
        put(gram, first, second, value * inverse_square)
    for at in range(count):
        current[blocks[at], :] = (full_ref[blocks[at], :].astype(f32) * inverse).astype(low)

    def mixed():
        def store(first, second, value):
            piece = gram[blocks[first], blocks[second]].astype(f32)
            put(mix, first, second, NS_B * piece + NS_C * value)

        symmetric(gram, store)

    def turn(_, carry):
        mixed()

        def update(at, carry):
            here = pl.ds(pl.multiple_of(at * tile, tile), tile)
            held = current[:, here]
            current[:, here] = (NS_A * held.astype(f32) + dot(mix[...], held)).astype(low)
            return carry

        lax.fori_loop(0, cols // tile, update, 0)
        symmetric(current, lambda first, second, value: put(gram, first, second, value))
        return carry

    lax.fori_loop(0, NS_STEPS - 1, turn, 0)
    mixed()
    for at in range(out_ref.shape[1] // tile):
        here = pl.ds(at * tile, tile)
        held = current[:, here]
        out_ref[:, here] = (NS_A * held.astype(f32) + dot(mix[...], held)).astype(low)


def newton(full, width):
    low = jnp.bfloat16
    rows = full.shape[0]
    return pl.pallas_call(
        newton_kernel,
        in_specs=[pl.BlockSpec(memory_space=pltpu.VMEM)],
        out_specs=pl.BlockSpec(memory_space=pltpu.VMEM),
        out_shape=jax.ShapeDtypeStruct((rows, width), low),
        scratch_shapes=[
            pltpu.VMEM(full.shape, low), pltpu.VMEM((rows, rows), low), pltpu.VMEM((rows, rows), low),
        ],
        compiler_params=pltpu.CompilerParams(vmem_limit_bytes=48 * 2**20),
        cost_estimate=pl.CostEstimate(flops=20 * 10**9, bytes_accessed=4 * 10**6, transcendentals=0),
        name="newton_schulz",
    )(full)


def return_kernel(done_ref, back_ref, send, recv):
    x, y, z, _, _, at_z = place()
    greet(at_z)
    copies = []
    for step, peer in enumerate(at_z):
        plane = lax.rem(z + step + 1, 4)
        copies.append(
            remote(done_ref.at[plane, y, x], back_ref.at[z], send.at[step], recv.at[step], peer)
        )
        copies[-1].start()
    back_ref[z] = done_ref[z, y, x]
    for copy in copies:
        copy.wait()


def return_rows(done):
    vmem = pl.BlockSpec(memory_space=pltpu.VMEM)
    dma = pltpu.SemaphoreType.DMA
    return pl.pallas_call(
        return_kernel,
        in_specs=[vmem],
        out_specs=vmem,
        out_shape=jax.ShapeDtypeStruct((4, SHARD, 768), done.dtype),
        scratch_shapes=[dma((3,)), dma((3,))],
        compiler_params=pltpu.CompilerParams(collective_id=2, has_side_effects=True, vmem_limit_bytes=16 * 2**20),
        cost_estimate=pl.CostEstimate(flops=0, bytes_accessed=20 * 10**6, transcendentals=0),
        name="return_rows",
    )(done.reshape(4, 2, 2, SHARD, 768))


def orthogonal_owned(own, other, state_width):
    width = own.shape[1]
    small = lax.axis_index("dp") // 4 == PLANE_OF["small"]
    full = jnp.concatenate([own, other], axis=1)
    col = jnp.arange(2 * width)[None, :] % width
    keep = (col < state_width) == (lax.axis_index("tensor") == 0)
    full = jnp.where(small & ~keep, jnp.zeros_like(full), full)
    done = newton(full, width + 2 * state_width)
    half, lent = done[:, :width], done[:, width:]
    edge = half[:, : 2 * state_width]
    edge = edge + jnp.where(small, swap(lent), jnp.zeros_like(lent))
    return jnp.concatenate([edge, half[:, 2 * state_width :]], axis=1)


def paired_shards(
    stream,
    cotangent,
    positions,
    norm_gain,
    w_gate,
    w_inner,
    w_state,
    w_step,
    conv_inner,
    conv_state,
    head_params,
    gate_gain,
    w_out,
    moment_norm_gain,
    moment_w_gate,
    moment_w_inner,
    moment_w_state,
    moment_w_step,
    moment_conv_inner,
    moment_conv_state,
    moment_head_params,
    moment_gate_gain,
    moment_w_out,
):
    low = jnp.bfloat16
    core = lax.axis_index("tensor")
    room = w_gate.shape[1]
    wide = w_state.shape[1]
    col_width = wide // 2
    heads = w_step.shape[1]
    first_pack = jnp.concatenate([w_gate.astype(low), w_state.astype(low)], axis=1)
    step_low = w_step.astype(low)
    step_lanes = jnp.concatenate([pad_cols(step_low, PACK), pad_cols(step_low, 128 - PACK)], axis=1)
    second_pack = jnp.concatenate([w_inner.astype(low), step_lanes], axis=1)
    full_first, full_second, full_out, token_rows, cotangent_rows, first_pre, second_pre, d_normed_out = gather_all(
        first_pack, second_pack, w_out.astype(low).T, stream, cotangent, norm_gain[None, :]
    )
    pos = jnp.broadcast_to(positions.astype(jnp.float32)[:, None], (positions.shape[0], 128))
    taps = jnp.pad(conv_inner, ((0, 3), (0, 0)))
    taps_s = jnp.pad(conv_state, ((0, 3), (0, 0)))
    lanes = jnp.concatenate([pad_cols(head_params, PACK), pad_cols(head_params, 128 - PACK)], axis=1)
    lanes = jnp.pad(lanes, ((0, 5), (0, 0)))
    skip = jnp.repeat(head_params[2], room // heads)[None, :]
    wide_map = expand_matrix()
    scanned, zi, zs, enter, sums = forward_core(
        first_pre, second_pre, d_normed_out, pos, taps, taps_s, lanes, skip, gate_gain[None, :], wide_map
    )
    normed_out, d_gate_pre, d_scan, gain_part = gate_stage(
        first_pre, scanned, d_normed_out, sums, swap(sums), gate_gain[None, :], pos
    )
    grad_gate_part = jnp.sum(gain_part, axis=0)
    out_part = contract_rows(cotangent_rows, normed_out).astype(low)
    gate_part = contract_rows(token_rows, d_gate_pre).astype(low)
    d_inner, d_state_low, d_step, taps_part, taps_s_part, skip_part, head_part, held_out, held_gate = backward_core(
        first_pre, second_pre, zi, zs, scanned, d_scan, enter, pos, taps, taps_s, lanes, skip, wide_map, out_part, gate_part
    )
    grad_conv_inner_part = jnp.sum(taps_part, axis=1)
    grad_conv_state_part = jnp.sum(taps_s_part, axis=1)
    head_rows = jnp.sum(head_part, axis=1)[:, :heads]
    skip_row = jnp.sum(jnp.sum(skip_part, axis=0).reshape(heads, -1), axis=1)
    grad_head_part = jnp.concatenate([head_rows, skip_row[None, :]], axis=0)
    col_first = core * col_width
    inner_part = contract_rows(token_rows, d_inner).astype(low)
    small_part = contract_rows(token_rows, jnp.concatenate([d_state_low, d_step], axis=1)).astype(low)
    vectors = jnp.concatenate(
        [
            grad_conv_inner_part,
            grad_gate_part[None, :],
            pad_cols(grad_head_part, room),
            pad_cols(grad_conv_state_part, room),
        ],
        axis=0,
    )
    vectors = jnp.pad(vectors, ((0, 16 - vectors.shape[0]), (0, 0)))
    small_moment = pad_cols(jnp.concatenate([moment_w_state, moment_w_step], axis=1), room)
    moment_rows = jnp.stack([small_moment, moment_w_inner, moment_w_gate, moment_w_out.T]).astype(low)
    own, other, grads, vectors, output, d_stream = reduce_all(
        (held_out, held_gate), (inner_part, small_part), vectors, moment_rows, norm_gain[None, :],
        (
            d_gate_pre, d_inner, d_state_low, d_step, normed_out, full_first, full_second, full_out,
            stream, cotangent,
        ),
    )
    grads = grads.astype(jnp.float32)
    grad_gate_w = grads[2]
    grad_inner_w = grads[1]
    grad_out_w = grads[3].T
    grad_state_w = grads[0][:, :col_width]
    grad_step_w = grads[0][:, col_width : col_width + heads]
    grad_conv_inner = vectors[:5]
    grad_gate_gain = vectors[5]
    grad_head = vectors[6:9, :heads]
    grad_conv_state = vectors[9:14, :wide]
    grad_norm = vectors[NORM_ROW]
    m_gate = MU_MAT * moment_w_gate + grad_gate_w
    m_inner = MU_MAT * moment_w_inner + grad_inner_w
    m_state = MU_MAT * moment_w_state + grad_state_w
    m_step = MU_MAT * moment_w_step + grad_step_w
    m_out = MU_MAT * moment_w_out + grad_out_w
    mine = return_rows(orthogonal_owned(own, other, col_width)).astype(jnp.float32)
    new_gate = w_gate - LR_MAT * spread(D, INNER) * mine[2]
    new_inner = w_inner - LR_MAT * spread(D, INNER) * mine[1]
    new_out = w_out - LR_MAT * spread(INNER, D) * mine[3].T
    new_step = w_step - LR_MAT * spread(D, HEADS) * mine[0][:, col_width : col_width + heads]
    state_slice = lax.dynamic_slice_in_dim(w_state, col_first, col_width, 1)
    new_state = state_slice - LR_MAT * spread(D, 2 * STATE) * mine[0][:, :col_width]
    m_norm = MU_VEC * moment_norm_gain + grad_norm
    m_conv_inner = MU_VEC * moment_conv_inner + grad_conv_inner
    m_conv_state = MU_VEC * moment_conv_state + grad_conv_state
    m_head = MU_VEC * moment_head_params + grad_head
    m_gate_gain = MU_VEC * moment_gate_gain + grad_gate_gain
    return (
        output,
        d_stream,
        grad_norm,
        grad_gate_w,
        grad_inner_w,
        grad_state_w,
        grad_step_w,
        grad_conv_inner,
        grad_conv_state,
        grad_head,
        grad_gate_gain,
        grad_out_w,
        norm_gain - LR_VEC * m_norm,
        new_gate,
        new_inner,
        new_state,
        new_step,
        conv_inner - LR_VEC * m_conv_inner,
        conv_state - LR_VEC * m_conv_state,
        head_params - LR_VEC * m_head,
        gate_gain - LR_VEC * m_gate_gain,
        new_out,
        m_norm,
        m_gate,
        m_inner,
        m_state,
        m_step,
        m_conv_inner,
        m_conv_state,
        m_head,
        m_gate_gain,
        m_out,
    )


def solution(mesh):
    paired = mesh.shape["dp"] == 16 and mesh.shape["tensor"] == 2
    return jax.shard_map(
        paired_shards if paired else shards,
        mesh=mesh,
        in_specs=(
            P(("dp", "tensor"), None),
            P(("dp", "tensor"), None),
            P("dp"),
            P(),
            P("dp", "tensor"),
            P("dp", "tensor"),
            P("dp", None),
            P("dp", "tensor"),
            P(None, "tensor"),
            P(),
            P(None, "tensor"),
            P("tensor"),
            P("tensor", "dp"),
            P(),
            P("dp", "tensor"),
            P("dp", "tensor"),
            P("dp", "tensor"),
            P("dp", "tensor"),
            P(None, "tensor"),
            P(),
            P(None, "tensor"),
            P("tensor"),
            P("tensor", "dp"),
        ),
        out_specs=(
            P(("dp", "tensor"), None),
            P(("dp", "tensor"), None),
            P(),
            P("dp", "tensor"),
            P("dp", "tensor"),
            P("dp", "tensor"),
            P("dp", "tensor"),
            P(None, "tensor"),
            P(),
            P(None, "tensor"),
            P("tensor"),
            P("tensor", "dp"),
            P(),
            P("dp", "tensor"),
            P("dp", "tensor"),
            P("dp", "tensor"),
            P("dp", "tensor"),
            P(None, "tensor"),
            P(),
            P(None, "tensor"),
            P("tensor"),
            P("tensor", "dp"),
            P(),
            P("dp", "tensor"),
            P("dp", "tensor"),
            P("dp", "tensor"),
            P("dp", "tensor"),
            P(None, "tensor"),
            P(),
            P(None, "tensor"),
            P("tensor"),
            P("tensor", "dp"),
        ),
        check_vma=False,
    )
```

```python
from functools import partial
import math

import jax
import jax.numpy as jnp
from jax import lax
from jax.experimental import pallas as pl
from jax.experimental.pallas import tpu as pltpu
from jax.sharding import PartitionSpec as P

D = 768
INNER = 1536
HEADS = 24
STATE = 128
BLOCK = 256
NS_STEPS = 5


EPS = 1e-05
NS_A = 3.4445
NS_B = -4.775
NS_C = 2.0315
MU_MAT = 0.95
MU_VEC = 0.9
LR_MAT = 0.3
LR_VEC = 0.001
HIGH = lax.Precision.HIGHEST
CORE = lax.Precision.DEFAULT


def silu_slope(value):
    sig = jax.nn.sigmoid(value)
    return sig * (1.0 + value * (1.0 - sig))


def contract_rows(left, right):
    return lax.dot_general(
        left, right, (((0,), (0,)), ((), ())), preferred_element_type=jnp.float32
    )


def times_transpose(left, right):
    return lax.dot_general(
        left, right, (((1,), (1,)), ((), ())), preferred_element_type=jnp.float32
    )


def causal_conv(signal, taps, positions):
    length = signal.shape[0]
    reach = taps.shape[0] - 1
    total = jnp.zeros_like(signal) + taps[reach]
    for lag_step in range(reach):
        moved = jnp.pad(signal, ((lag_step, 0), (0, 0)))[:length]
        total = total + jnp.where((positions >= lag_step)[:, None], moved * taps[lag_step], 0.0)
    return jax.nn.silu(total)


def mixer_core(inner_pre, state_pre, step_pre, conv_inner, conv_state, head_params, positions, precision=HIGH):
    length = inner_pre.shape[0]
    heads = step_pre.shape[1]
    head_size = inner_pre.shape[1] // heads
    states = state_pre.shape[1] // 2
    blocks = length // BLOCK
    inner_act = causal_conv(inner_pre, conv_inner, positions).reshape(
        blocks, BLOCK, heads, head_size
    )
    state_act = causal_conv(state_pre, conv_state, positions)
    input_map = state_act[:, :states].reshape(blocks, BLOCK, states)
    output_map = state_act[:, states:].reshape(blocks, BLOCK, states)
    step_size = jax.nn.softplus(step_pre + head_params[0])
    log_decay = (step_size * -jnp.exp(head_params[1])).reshape(blocks, BLOCK, heads)
    step_size = step_size.reshape(blocks, BLOCK, heads)
    resets = (positions <= 0).astype(jnp.float32).reshape(blocks, BLOCK)
    order = jnp.arange(BLOCK)
    lower = (order[:, None] >= order[None, :]).astype(jnp.float32)
    cumulative = jnp.einsum("ij,cjh->cih", lower, log_decay, precision=HIGH)
    seen = jnp.einsum("ij,cj->ci", lower, resets, precision=HIGH)
    linked = (seen[:, :, None] == seen[:, None, :]) & (order[:, None] >= order[None, :])[None]
    linked_heads = linked[..., None]
    spacing = cumulative[:, :, None, :] - cumulative[:, None, :, :]
    decay = jnp.where(linked_heads, jnp.exp(jnp.where(linked_heads, spacing, 0.0)), 0.0)
    scores = jnp.einsum("cin,cjn->cij", output_map, input_map, precision=precision)
    mixing = scores[..., None] * decay * step_size[:, None, :, :]
    within = jnp.einsum("cijh,cjhp->cihp", mixing, inner_act, precision=precision)
    tail_linked = (seen[:, -1:] == seen)[..., None]
    tail = (
        jnp.where(
            tail_linked,
            jnp.exp(jnp.where(tail_linked, cumulative[:, -1:, :] - cumulative, 0.0)),
            0.0,
        )
        * step_size
    )
    own_state = jnp.einsum("cjh,cjhp,cjn->chpn", tail, inner_act, input_map, precision=precision)
    carry_rate = jnp.exp(cumulative[:, -1, :]) * (seen[:, -1] == 0).astype(jnp.float32)[:, None]

    state = jnp.zeros((heads, head_size, states), jnp.float32)
    entering = []
    for block in range(blocks):
        entering.append(state)
        state = carry_rate[block][:, None, None] * state + own_state[block]
    entering = jnp.stack(entering)
    fresh = (seen == 0)[..., None]
    carry_in = jnp.where(fresh, jnp.exp(cumulative), 0.0)
    across = (
        jnp.einsum("cin,chpn->cihp", output_map, entering, precision=precision) * carry_in[..., None]
    )
    result = within + across + head_params[2][None, None, :, None] * inner_act
    return result.reshape(length, heads * head_size)


def gram_total(low):
    return lax.psum(
        jnp.dot(low, low.T, preferred_element_type=jnp.float32).astype(jnp.bfloat16), "tensor"
    ).astype(jnp.float32)


def orthogonalize(matrix):
    first = gram_total(matrix.astype(jnp.bfloat16))
    scale = jnp.sqrt(jnp.trace(first)) + 1e-07
    current = (matrix / scale).astype(jnp.bfloat16)
    gram = (first / (scale * scale)).astype(jnp.bfloat16)
    for turn in range(NS_STEPS):
        if turn > 0:
            gram = gram_total(current).astype(jnp.bfloat16)
        applied = jnp.dot(gram, current, preferred_element_type=jnp.float32)
        twice = jnp.dot(gram, applied.astype(jnp.bfloat16), preferred_element_type=jnp.float32)
        current = (NS_A * current.astype(jnp.float32) + NS_B * applied + NS_C * twice).astype(
            jnp.bfloat16
        )
    return current.astype(jnp.float32)


def spread(rows, cols):
    return math.sqrt(max(1.0, rows / cols))


def shards(
    stream,
    cotangent,
    positions,
    norm_gain,
    w_gate,
    w_inner,
    w_state,
    w_step,
    conv_inner,
    conv_state,
    head_params,
    gate_gain,
    w_out,
    moment_norm_gain,
    moment_w_gate,
    moment_w_inner,
    moment_w_state,
    moment_w_step,
    moment_conv_inner,
    moment_conv_state,
    moment_head_params,
    moment_gate_gain,
    moment_w_out,
):
    dp_count = lax.axis_size("dp")
    inv_first = lax.rsqrt(jnp.mean(stream * stream, axis=1, keepdims=True) + EPS)
    normed = (stream * inv_first * norm_gain).astype(jnp.bfloat16)
    token_rows, cotangent_rows = (
        lax.all_gather(normed, "tensor", axis=0, tiled=True),
        lax.all_gather(cotangent.astype(jnp.bfloat16), "tensor", axis=0, tiled=True),
    )
    local_weights = (
        w_gate.astype(jnp.bfloat16),
        w_inner.astype(jnp.bfloat16),
        w_step.astype(jnp.bfloat16),
        w_state.astype(jnp.bfloat16),
        w_out.astype(jnp.bfloat16),
    )
    full_gate, full_inner, full_step, full_state, full_out = (
        lax.all_gather(local_weights[0], "dp", axis=0, tiled=True),
        lax.all_gather(local_weights[1], "dp", axis=0, tiled=True),
        lax.all_gather(local_weights[2], "dp", axis=0, tiled=True),
        lax.all_gather(local_weights[3], "dp", axis=0, tiled=True),
        lax.all_gather(local_weights[4], "dp", axis=1, tiled=True),
    )
    gate_pre = jnp.dot(token_rows, full_gate, preferred_element_type=jnp.float32)
    inner_pre = jnp.dot(token_rows, full_inner, preferred_element_type=jnp.float32)
    state_pre = jnp.dot(token_rows, full_state, preferred_element_type=jnp.float32)
    step_pre = jnp.dot(token_rows, full_step, preferred_element_type=jnp.float32)
    alive = (positions >= 0).astype(jnp.float32)[:, None]
    scanned, core_back = jax.vjp(
        partial(mixer_core, positions=positions),
        inner_pre,
        state_pre,
        step_pre,
        conv_inner,
        conv_state,
        head_params,
    )
    gate_act = jax.nn.silu(gate_pre)
    gated = scanned * gate_act
    square_sum = lax.psum(jnp.sum(gated * gated, axis=1), "tensor")
    inv_second = lax.rsqrt(square_sum / INNER + EPS)[:, None]
    normed_out = (gated * inv_second * gate_gain * alive).astype(jnp.bfloat16)
    mixed = lax.psum_scatter(
        jnp.dot(normed_out, full_out, preferred_element_type=jnp.float32).astype(jnp.bfloat16),
        "tensor",
        scatter_dimension=0,
        tiled=True,
    ).astype(jnp.float32)
    output = stream + mixed
    d_normed_out = times_transpose(cotangent_rows, full_out)
    grad_out_part = contract_rows(normed_out, cotangent_rows)
    scaled = d_normed_out * gate_gain * alive
    grad_gate_part = jnp.sum(d_normed_out * gated * inv_second * alive, axis=0)
    cross_sum = lax.psum(jnp.sum(scaled * gated, axis=1), "tensor")
    d_gated = inv_second * scaled - gated * inv_second**3 * (cross_sum / INNER)[:, None]
    d_gate_pre = (d_gated * scanned * silu_slope(gate_pre)).astype(jnp.bfloat16)
    d_inner, d_state_part, d_step, grad_conv_inner_part, grad_conv_state_part, grad_head_part = (
        core_back(d_gated * gate_act)
    )
    d_state_cols = lax.psum_scatter(
        d_state_part.astype(jnp.bfloat16), "tensor", scatter_dimension=1, tiled=True
    ).astype(jnp.float32)
    d_inner_low = d_inner.astype(jnp.bfloat16)
    d_state_low = d_state_cols.astype(jnp.bfloat16)
    d_step_low = d_step.astype(jnp.bfloat16)
    col_width = d_state_cols.shape[1]
    col_first = lax.axis_index("tensor") * col_width
    state_cols = lax.dynamic_slice_in_dim(full_state, col_first, col_width, 1)
    total = times_transpose(d_gate_pre, full_gate)
    total = total + times_transpose(d_inner_low, full_inner)
    total = total + times_transpose(d_state_low, state_cols)
    d_normed = lax.psum_scatter(
        (total + times_transpose(d_step_low, full_step)).astype(jnp.bfloat16),
        "tensor",
        scatter_dimension=0,
        tiled=True,
    ).astype(jnp.float32)
    grad_gate_w, grad_inner_w, grad_state_w, grad_step_w, grad_out_w = (
        lax.psum_scatter(
            contract_rows(token_rows, d_gate_pre).astype(jnp.bfloat16),
            "dp",
            scatter_dimension=0,
            tiled=True,
        ).astype(jnp.float32),
        lax.psum_scatter(
            contract_rows(token_rows, d_inner_low).astype(jnp.bfloat16),
            "dp",
            scatter_dimension=0,
            tiled=True,
        ).astype(jnp.float32),
        lax.psum_scatter(
            contract_rows(token_rows, d_state_low).astype(jnp.bfloat16),
            "dp",
            scatter_dimension=0,
            tiled=True,
        ).astype(jnp.float32),
        lax.psum_scatter(
            contract_rows(token_rows, d_step_low).astype(jnp.bfloat16),
            "dp",
            scatter_dimension=0,
            tiled=True,
        ).astype(jnp.float32),
        lax.psum_scatter(
            grad_out_part.astype(jnp.bfloat16), "dp", scatter_dimension=1, tiled=True
        ).astype(jnp.float32),
    )
    grad_norm_part = jnp.sum(d_normed * stream * inv_first, axis=0)
    weighted = d_normed * norm_gain
    d_stream = (
        cotangent
        + inv_first * weighted
        - stream * inv_first**3 * jnp.mean(weighted * stream, axis=1, keepdims=True)
    )
    grad_conv_inner, grad_gate_gain, grad_head = lax.psum(
        (grad_conv_inner_part, grad_gate_part, grad_head_part), "dp"
    )
    grad_conv_state, grad_norm = lax.psum((grad_conv_state_part, grad_norm_part), ("dp", "tensor"))
    m_gate = MU_MAT * moment_w_gate + grad_gate_w
    m_inner = MU_MAT * moment_w_inner + grad_inner_w
    m_state = MU_MAT * moment_w_state + grad_state_w
    m_step = MU_MAT * moment_w_step + grad_step_w
    m_out = MU_MAT * moment_w_out + grad_out_w
    room = w_gate.shape[1]
    shard_rows = w_gate.shape[0]
    stacked = jnp.stack(
        [
            m_gate,
            m_inner,
            m_out.T,
            jnp.pad(m_step, ((0, 0), (0, room - m_step.shape[1]))),
            jnp.pad(m_state, ((0, 0), (0, room - m_state.shape[1]))),
        ]
    )
    matrix_count = stacked.shape[0]
    owner_index = jnp.arange(matrix_count, dtype=jnp.int32) * dp_count // matrix_count
    select = (owner_index[None, :] == jnp.arange(dp_count, dtype=jnp.int32)[:, None]).astype(
        jnp.float32
    )
    outgoing = jnp.einsum("jk,krc->jrc", select, stacked, precision=HIGH)
    owned = (
        lax.all_to_all(outgoing.astype(jnp.bfloat16), "dp", split_axis=0, concat_axis=0, tiled=True)
        .astype(outgoing.dtype)
        .reshape(dp_count * shard_rows, room)
    )
    ortho = orthogonalize(owned)
    returned = lax.all_to_all(
        ortho.reshape(dp_count, shard_rows, room).astype(jnp.bfloat16),
        "dp",
        split_axis=0,
        concat_axis=0,
        tiled=True,
    ).astype(jnp.float32)
    mine = jnp.einsum("jk,jrc->krc", select, returned, precision=HIGH)
    new_gate = w_gate - LR_MAT * spread(D, INNER) * mine[0]
    new_inner = w_inner - LR_MAT * spread(D, INNER) * mine[1]
    new_out = w_out - LR_MAT * spread(INNER, D) * mine[2].T
    new_step = w_step - LR_MAT * spread(D, HEADS) * mine[3][:, : w_step.shape[1]]
    state_slice = lax.dynamic_slice_in_dim(w_state, col_first, col_width, 1)
    new_state = state_slice - LR_MAT * spread(D, 2 * STATE) * mine[4][:, :col_width]
    m_norm = MU_VEC * moment_norm_gain + grad_norm
    m_conv_inner = MU_VEC * moment_conv_inner + grad_conv_inner
    m_conv_state = MU_VEC * moment_conv_state + grad_conv_state
    m_head = MU_VEC * moment_head_params + grad_head
    m_gate_gain = MU_VEC * moment_gate_gain + grad_gate_gain
    return (
        output,
        d_stream,
        grad_norm,
        grad_gate_w,
        grad_inner_w,
        grad_state_w,
        grad_step_w,
        grad_conv_inner,
        grad_conv_state,
        grad_head,
        grad_gate_gain,
        grad_out_w,
        norm_gain - LR_VEC * m_norm,
        new_gate,
        new_inner,
        new_state,
        new_step,
        conv_inner - LR_VEC * m_conv_inner,
        conv_state - LR_VEC * m_conv_state,
        head_params - LR_VEC * m_head,
        gate_gain - LR_VEC * m_gate_gain,
        new_out,
        m_norm,
        m_gate,
        m_inner,
        m_state,
        m_step,
        m_conv_inner,
        m_conv_state,
        m_head,
        m_gate_gain,
        m_out,
    )


MESH_ID = pl.DeviceIdType.MESH
SHARD = 48
PLAN = (("out", 768), ("gate", 768), ("inner", 768), ("small", 256))
PLANE_OF = {"out": 0, "inner": 1, "gate": 2, "small": 3}


def place():
    index = lax.axis_index("dp")
    z = lax.div(index, 4)
    y = lax.rem(lax.div(index, 2), 2)
    x = lax.rem(index, 2)
    at_x = {"dp": z * 4 + y * 2 + (1 - x)}
    at_y = {"dp": z * 4 + (1 - y) * 2 + x}
    at_z = [{"dp": lax.rem(z + step, 4) * 4 + y * 2 + x} for step in range(1, 4)]
    return x, y, z, at_x, at_y, at_z


def greet(peers):
    barrier = pltpu.get_barrier_semaphore()
    for peer in peers:
        pl.semaphore_signal(barrier, inc=1, device_id=peer, device_id_type=MESH_ID)
    pl.semaphore_wait(barrier, len(peers))


def remote(src, dst, send, recv, peer):
    return pltpu.make_async_remote_copy(
        src_ref=src, dst_ref=dst, send_sem=send, recv_sem=recv, device_id=peer, device_id_type=MESH_ID
    )

EARLY = 2
COUNT = 8


def half_steps(parts, at_x, at_y, x, y, arrived, summed, arrived_two, one_send, one_recv, two_send, two_recv):
    def span(task, route):
        half = parts[task].shape[-1] // 2
        return pl.ds(route * half, half), pl.ds(0, half)

    def one(task, route):
        cols, mine = span(task, route)
        other = parts[task].at[:, 1 - y, :, :, cols] if route else parts[task].at[:, :, 1 - x, :, cols]
        return remote(
            other, arrived.at[task, route, :, :, :, mine], one_send.at[task, route],
            one_recv.at[task, route], at_y if route else at_x,
        )

    def two(task, route):
        mine = span(task, route)[1]
        return remote(
            summed.at[task, route, :, 1 - x if route else 1 - y, :, mine],
            arrived_two.at[task, route, :, :, mine], two_send.at[task, route],
            two_recv.at[task, route], at_x if route else at_y,
        )

    def add(task, route, own):
        mine = span(task, route)[1]
        got = arrived[task, route, :, :, :, mine]
        summed[task, route, :, :, :, mine] = (own.astype(jnp.float32) + got.astype(jnp.float32)).astype(jnp.bfloat16)

    def settle(task, route, held):
        cols, mine = span(task, route)
        own = summed[task, route, :, x if route else y, :, mine]
        got = arrived_two[task, route, :, :, mine]
        held[:, :, cols] = (own.astype(jnp.float32) + got.astype(jnp.float32)).astype(jnp.bfloat16)

    return span, one, two, add, settle


def early_reduce(parts, held, own, arrived, summed, arrived_two, own_sem, one_send, one_recv, two_send, two_recv):
    step = pl.program_id(0)
    x, y, z, at_x, at_y, _ = place()
    span, one, two, add, settle = half_steps(
        parts, at_x, at_y, x, y, arrived, summed, arrived_two, one_send, one_recv, two_send, two_recv
    )
    pairs = [(task, route) for task in range(EARLY) for route in range(2)]

    def load(task, route):
        cols = span(task, route)[0]
        src = parts[task].at[:, y, :, :, cols] if route else parts[task].at[:, :, x, :, cols]
        return pltpu.make_async_copy(src, own.at[task, route], own_sem.at[task, route])

    @pl.when(step == 0)
    def _():
        greet([at_x, at_y, {"tensor": 1 - lax.axis_index("tensor")}])
        for route in range(2):
            one(0, route).start()
        for task, route in pairs:
            load(task, route).start()
        for route in range(2):
            one(1, route).start()

    for task, at in ((0, 3), (1, 5)):

        @pl.when(step == at)
        def _():
            for route in range(2):
                load(task, route).wait()
                one(task, route).wait()
                add(task, route, own[task, route])
                two(task, route).start()

    for task, at in ((0, 6), (1, 7)):

        @pl.when(step == at)
        def _():
            for route in range(2):
                two(task, route).wait()
                settle(task, route, held[task])


CHUNK = 128
PACK = 16


def sigmoid(value):
    return 0.5 * jnp.tanh(0.5 * value) + 0.5


def expand_matrix():
    row = jnp.arange(128)[:, None]
    col = jnp.arange(768)[None, :] // 64
    return ((row == col) | (row == col + PACK)).astype(jnp.bfloat16)


def two_term(value):
    lane = lax.broadcasted_iota(jnp.int32, value.shape, 1)
    high = value.astype(jnp.bfloat16).astype(jnp.float32)
    return jnp.where(lane < PACK, high, value - high).astype(jnp.bfloat16)


def split_terms(value, terms):
    out = []
    for _ in range(terms):
        piece = value.astype(jnp.bfloat16)
        out.append(piece)
        value = value - piece.astype(jnp.float32)
    return out


def dot(left, right, dims=((1,), (0,))):
    return lax.dot_general(left, right, (dims, ((), ())), preferred_element_type=jnp.float32)


def head_terms(step_ref, head_ref, pos):
    shifted = step_ref[...] + head_ref[0:1, :]
    small = jnp.exp(-jnp.abs(shifted))
    step = jnp.maximum(shifted, 0.0) + jnp.log1p(small)
    log_decay = -step * jnp.exp(head_ref[1:2, :])
    row = lax.broadcasted_iota(jnp.int32, (CHUNK, 128), 0)
    col = lax.broadcasted_iota(jnp.int32, (CHUNK, 128), 1)
    lower = (row >= col).astype(jnp.bfloat16)
    cumulative = sum(dot(lower, piece) for piece in split_terms(log_decay, 3))
    last = cumulative[CHUNK - 1 : CHUNK, :]
    back = (row - col).astype(jnp.float32)
    linked = (row >= col) & (back <= jnp.maximum(pos, 0.0))
    row = row.astype(jnp.float32)
    carry_in = jnp.where(pos > row, jnp.exp(cumulative), 0.0)
    pos_last = pos[CHUNK - 1 : CHUNK, :]
    tail_linked = (CHUNK - 1.0 - row) <= jnp.maximum(pos_last, 0.0)
    tail = jnp.where(tail_linked, jnp.exp(jnp.minimum(last - cumulative, 0.0)), 0.0)
    carry = jnp.where(pos_last > CHUNK - 1.0, jnp.exp(last), 0.0)
    return shifted, step, log_decay, cumulative, linked, carry_in, tail, carry


def pair_decay(cumulative, across, pair):
    parts = []
    for head in (2 * pair, 2 * pair + 1):
        spacing = cumulative[:, head : head + 1] - across[head : head + 1, :]
        parts.append(jnp.exp(jnp.minimum(spacing, 0.0)))
    return parts


def forward_kernel(
    inner_ref, step_ref, gate_ref, state_ref, dno_ref, pos_ref, taps_ref, taps_s_ref, head_ref,
    skip_ref, gain_ref, wide_ref,
    scanned_ref, zi_ref, zs_ref, enter_ref, sums_ref,
    halo_i, halo_s, hold,
):
    @pl.when(pl.program_id(0) == 0)
    def _():
        halo_i[...] = jnp.zeros_like(halo_i)
        halo_s[...] = jnp.zeros_like(halo_s)
        hold[...] = jnp.zeros_like(hold)

    low = jnp.bfloat16
    pos = pos_ref[...]
    marks = [(pos >= lag).astype(jnp.float32) for lag in range(4)]

    def conv(ref, halo, taps, out_ref, first):
        value = ref[:, first : first + 128]
        ext = jnp.concatenate([halo[:, first : first + 128], value], axis=0)
        total = taps[4:5, first : first + 128] + marks[0] * (value * taps[0:1, first : first + 128])
        for lag in range(1, 4):
            moved = pltpu.roll(ext, lag, 0)[8:]
            total = total + marks[lag] * (moved * taps[lag : lag + 1, first : first + 128])
        out_ref[:, first : first + 128] = total
        return total * sigmoid(total)

    shifted, step, log_decay, cumulative, linked, carry_in, tail, carry = head_terms(
        step_ref, head_ref, pos
    )
    across = cumulative.T
    wide = dot(
        jnp.concatenate(
            [
                two_term(step),
                two_term(carry_in),
                two_term(tail * step),
                two_term(jnp.broadcast_to(carry, (16, 128))),
            ],
            axis=0,
        ),
        wide_ref[...],
    )
    input_map = conv(state_ref, halo_s, taps_s_ref, zs_ref, 0).astype(low)
    output_map = conv(state_ref, halo_s, taps_s_ref, zs_ref, 128).astype(low)
    scores = jnp.where(linked, dot(output_map, input_map, ((1,), (1,))), 0.0)
    state = hold[...]
    state_low = state.astype(low)
    enter_ref[...] = state_low
    entered = dot(output_map, state_low)
    lane = lax.broadcasted_iota(jnp.int32, (CHUNK, 128), 1)
    squares = jnp.zeros((CHUNK, 128), jnp.float32)
    crosses = jnp.zeros((CHUNK, 128), jnp.float32)
    fed = []
    for pair in range(6):
        cols = slice(pair * 128, pair * 128 + 128)
        act = conv(inner_ref, halo_i, taps_ref, zi_ref, pair * 128)
        stepped = (wide[:CHUNK, cols] * act).astype(low)
        first, second = pair_decay(cumulative, across, pair)
        mixing = jnp.concatenate([(scores * first).astype(low), (scores * second).astype(low)], axis=0)
        both = dot(mixing, stepped)
        within = jnp.where(lane < 64, both[:CHUNK], both[CHUNK:])
        scanned = (
            within + entered[:, cols] * wide[CHUNK : 2 * CHUNK, cols] + skip_ref[0:1, cols] * act
        )
        scanned_ref[:, cols] = scanned
        fed.append((wide[2 * CHUNK : 3 * CHUNK, cols] * act).astype(low))
        gate = gate_ref[:, cols]
        gated = scanned * (gate * sigmoid(gate))
        squares = squares + gated * gated
        crosses = crosses + dno_ref[:, cols] * gain_ref[0:1, cols] * gated
    fresh = dot(input_map, jnp.concatenate(fed, axis=1), ((0,), (0,)))
    hold[...] = wide[3 * CHUNK : 3 * CHUNK + 1, :] * state + fresh
    halo_i[...] = inner_ref[CHUNK - 8 :, :]
    halo_s[...] = state_ref[CHUNK - 8 :, :]
    square = jnp.sum(squares, axis=1, keepdims=True)
    cross = jnp.sum(crosses * marks[0], axis=1, keepdims=True)
    sums_ref[...] = jnp.where(lane == 0, square, cross)


def gate_kernel(
    gate_ref, scanned_ref, dno_ref, sums_ref, twin_ref, gain_ref, pos_ref,
    normed_ref, d_gate_ref, d_scan_ref, g_gain_ref,
):
    @pl.when(pl.program_id(0) == 0)
    def _():
        g_gain_ref[...] = jnp.zeros_like(g_gain_ref)

    low = jnp.bfloat16
    alive = (pos_ref[...] >= 0).astype(jnp.float32)
    sums = sums_ref[...] + twin_ref[...]
    inv = jnp.broadcast_to(lax.rsqrt(sums[:, 0:1] / INNER + EPS), alive.shape)
    pull = inv * inv * inv * jnp.broadcast_to(sums[:, 1:2] / INNER, alive.shape)
    live = inv * alive
    for pair in range(6):
        cols = slice(pair * 128, pair * 128 + 128)
        gain = gain_ref[0:1, cols]
        gate, scanned, d_normed_out = gate_ref[:, cols], scanned_ref[:, cols], dno_ref[:, cols]
        sig = sigmoid(gate)
        gate_act = gate * sig
        gated = scanned * gate_act
        normed_ref[:, cols] = (gated * live * gain).astype(low)
        product = d_normed_out * gated * live
        g_gain_ref[:, cols] += jnp.sum(product.reshape(CHUNK // 8, 8, 128), axis=0)
        d_gated = live * gain * d_normed_out - gated * pull
        d_scan_ref[:, cols] = (d_gated * gate_act).astype(low)
        d_gate_ref[:, cols] = (d_gated * scanned * (sig * (1.0 + gate * (1.0 - sig)))).astype(low)


def gate_stage(first_pre, scanned, d_normed_out, sums, twin_sums, gain, pos):
    rows = first_pre.shape[0]
    at = lambda width: pl.BlockSpec((CHUNK, width), lambda c: (c, 0))
    f32, low = jnp.float32, jnp.bfloat16
    wide = jax.ShapeDtypeStruct((rows, 768), low)
    return pl.pallas_call(
        gate_kernel,
        grid=(rows // CHUNK,),
        in_specs=[
            at(768), at(768), at(768), at(128), at(128), pl.BlockSpec((1, 768), lambda c: (0, 0)), at(128),
        ],
        out_specs=[at(768), at(768), at(768), pl.BlockSpec((8, 768), lambda c: (0, 0))],
        out_shape=[wide, wide, wide, jax.ShapeDtypeStruct((8, 768), f32)],
        compiler_params=pltpu.CompilerParams(vmem_limit_bytes=60 * 2**20),
        cost_estimate=pl.CostEstimate(flops=10**8, bytes_accessed=15 * 10**6, transcendentals=10**6),
        name="gate_stage",
    )(first_pre, scanned, d_normed_out, sums, twin_sums, gain, pos)


def backward_kernel(
    inner_ref, step_ref, state_ref, zi_ref, zs_ref, scanned_ref, dscan_ref, enter_ref, pos_ref,
    taps_ref, taps_s_ref, head_ref, skip_ref, wide_ref, out_part, gate_part,
    d_inner_ref, d_state_ref, d_step_ref, g_taps_ref, g_taps_s_ref, g_skip_ref, g_head_ref, held_out, held_gate,
    halo_i, halo_s, halo_p, hold, state_out, state_in, state_send, state_recv, *reducing,
):
    low = jnp.bfloat16
    step_at = pl.program_id(0)
    last_step = pl.num_programs(0) - 1
    core = lax.axis_index("tensor")
    early_reduce((out_part, gate_part), (held_out, held_gate), *reducing)
    chunk = last_step - step_at
    twin = {"tensor": 1 - core}
    here = pl.ds(pl.multiple_of(chunk * CHUNK, CHUNK), CHUNK)

    @pl.when(pl.program_id(0) == 0)
    def _():
        for ref in (halo_i, halo_s, halo_p, hold, g_taps_ref, g_taps_s_ref, g_skip_ref, g_head_ref):
            ref[...] = jnp.zeros_like(ref)

    pos = pos_ref[...]
    pos_ext = jnp.concatenate([pos, halo_p[...]], axis=0)
    marks = [(pos_ext >= lag).astype(jnp.float32) for lag in range(4)]
    lane = lax.broadcasted_iota(jnp.int32, (CHUNK, 128), 1)
    row = lax.broadcasted_iota(jnp.int32, (CHUNK, 128), 0)
    col = lane

    def slope(total):
        sig = sigmoid(total)
        return sig * (1.0 + total * (1.0 - sig)), total * sig

    def fold(value):
        return jnp.sum(value.reshape(CHUNK // 8, 8, 128), axis=0)

    def conv_back(grad, ref, halo, taps, out_ref, g_ref, first):
        cols = slice(first, first + 128)
        ext = jnp.concatenate([grad, halo[:, cols]], axis=0)
        value = ref[:, cols]
        halo[:, cols] = grad[:8]
        g_ref[4, :, cols] += fold(grad)
        total = jnp.zeros((CHUNK, 128), jnp.float32)
        for lag in range(4):
            masked = ext * marks[lag]
            if lag:
                masked = pltpu.roll(masked, CHUNK + 8 - lag, 0)
            masked = masked[:CHUNK]
            g_ref[lag, :, cols] += fold(masked * value)
            total = total + masked * taps[lag : lag + 1, cols]
        if out_ref is not None:
            out_ref[:, cols] = total.astype(low)
        return total

    shifted, step, log_decay, cumulative, linked, carry_in, tail, carry = head_terms(
        step_ref, head_ref, pos
    )
    across = cumulative.T
    wide = dot(
        jnp.concatenate(
            [
                two_term(step),
                two_term(carry_in),
                two_term(tail),
                two_term(jnp.broadcast_to(carry, (16, 128))),
            ],
            axis=0,
        ),
        wide_ref[...],
    )
    slope_b, input_map = slope(zs_ref[:, :128])
    slope_c, output_map = slope(zs_ref[:, 128:])
    input_low, output_low = input_map.astype(low), output_map.astype(low)
    scores = jnp.where(linked, dot(output_low, input_low, ((1,), (1,))), 0.0)
    entering = enter_ref[...]
    d_next = hold[...]
    d_next_low = d_next.astype(low)
    pulled = dot(input_low, d_next_low)
    d_scores = jnp.zeros((CHUNK, 128), jnp.float32)
    d_entered, fed, balance, direct, extra = [], [], [], [], []
    carry_wide = wide[3 * CHUNK : 3 * CHUNK + 1, :]
    carry_grad = jnp.sum(d_next * entering.astype(jnp.float32), axis=0, keepdims=True) * carry_wide
    for pair in range(6):
        cols = slice(pair * 128, pair * 128 + 128)
        slope_x, act = slope(zi_ref[:, cols])
        d_low = dscan_ref[:, cols]
        skip = skip_ref[0:1, cols]
        stepped = (wide[:CHUNK, cols] * act).astype(low)
        stepped_wide = stepped.astype(jnp.float32)
        d_exact = d_low.astype(jnp.float32)
        d_both = jnp.concatenate(
            [jnp.where(lane < 64, d_exact, 0.0).astype(low), jnp.where(lane < 64, 0.0, d_exact).astype(low)],
            axis=0,
        )
        first, second = pair_decay(cumulative, across, pair)
        mixing = jnp.concatenate([(scores * first).astype(low), (scores * second).astype(low)], axis=0)
        d_mixing = dot(d_both, stepped, ((1,), (1,)))
        d_scores = d_scores + d_mixing[:CHUNK] * first + d_mixing[CHUNK:] * second
        tail_cols = wide[2 * CHUNK : 3 * CHUNK, cols]
        tailed = tail_cols * pulled[:, cols]
        d_stepped = dot(mixing, d_both, ((0,), (0,))) + tailed
        extra.append(jnp.sum(stepped_wide * tailed, axis=0, keepdims=True) + carry_grad[:, cols])
        fed.append((tail_cols * stepped_wide).astype(low))
        d_entered.append((wide[CHUNK : 2 * CHUNK, cols] * d_exact).astype(low))
        balance.append(d_exact * (scanned_ref[:, cols] - skip * act) - stepped_wide * d_stepped)
        direct.append(act * d_stepped)
        g_skip_ref[:, cols] += fold(d_exact * act)
        d_act = skip * d_exact + wide[:CHUNK, cols] * d_stepped
        conv_back(d_act * slope_x, inner_ref, halo_i, taps_ref, d_inner_ref, g_taps_ref, pair * 128)
    d_entered = jnp.concatenate(d_entered, axis=1)
    fed = jnp.concatenate(fed, axis=1)
    d_scores = jnp.where(linked, d_scores, 0.0).astype(low)
    d_output = dot(d_scores, input_low) + dot(d_entered, entering, ((1,), (1,)))
    d_input = dot(d_scores, output_low, ((0,), (0,))) + dot(fed, d_next_low, ((1,), (1,)))
    hold[...] = carry_wide * d_next + dot(output_low, d_entered, ((0,), (0,)))
    for_first = conv_back(d_input * slope_b, state_ref, halo_s, taps_s_ref, None, g_taps_s_ref, 0)
    for_second = conv_back(d_output * slope_c, state_ref, halo_s, taps_s_ref, None, g_taps_s_ref, 128)
    state_out[step_at] = jnp.where(core == 0, for_second, for_first).astype(low)
    d_state_ref[here, :] = jnp.where(core == 0, for_first, for_second).astype(low)

    def lend(at):
        return remote(state_out.at[at], state_in.at[at], state_send.at[at], state_recv.at[at], twin)

    lend(step_at).start()
    halo_p[...] = pos[:8]
    spread_back = wide_ref[...]
    extra = jnp.broadcast_to(jnp.concatenate(extra, axis=1), (16, 768))
    stacked = jnp.concatenate(
        split_terms(jnp.concatenate(balance, axis=1), 2)
        + split_terms(jnp.concatenate(direct, axis=1), 2)
        + split_terms(extra, 2),
        axis=0,
    )
    summed = dot(stacked, spread_back, ((1,), (1,)))
    d_sum = summed[:CHUNK] + summed[CHUNK : 2 * CHUNK]
    d_direct = summed[2 * CHUNK : 3 * CHUNK] + summed[3 * CHUNK : 4 * CHUNK]
    d_last = summed[4 * CHUNK : 4 * CHUNK + 1] + summed[4 * CHUNK + 16 : 4 * CHUNK + 17]
    upper = (row <= col).astype(low)
    d_decay = sum(dot(upper, piece) for piece in split_terms(d_sum, 3)) + d_last
    d_step = (d_direct - d_decay * jnp.exp(head_ref[1:2, :])) * sigmoid(shifted)
    d_step = jnp.where(lane < PACK, d_step, 0.0)
    d_step_ref[...] = d_step.astype(low)
    g_head_ref[0] += fold(d_step)
    g_head_ref[1] += fold(d_decay * log_decay)

    @pl.when(step_at == last_step)
    def _():
        for at in range(COUNT):
            lend(at).wait()
            rows = pl.ds((COUNT - 1 - at) * CHUNK, CHUNK)
            d_state_ref[rows, :] = (
                d_state_ref[rows, :].astype(jnp.float32) + state_in[at].astype(jnp.float32)
            ).astype(low)


def forward_core(first_pre, second_pre, d_normed_out, pos, taps, taps_s, heads_lanes, skip, gain, wide):
    rows = first_pre.shape[0]
    at = lambda width, col: pl.BlockSpec((CHUNK, width), lambda c: (c, col))
    whole = lambda arr: pl.BlockSpec(arr.shape, lambda c: (0,) * arr.ndim)
    f32 = jnp.float32
    return pl.pallas_call(
        forward_kernel,
        grid=(rows // CHUNK,),
        in_specs=[
            at(768, 0), at(128, 6), at(768, 0), at(256, 3), at(768, 0), at(128, 0),
            whole(taps), whole(taps_s), whole(heads_lanes), whole(skip), whole(gain), whole(wide),
        ],
        out_specs=[at(768, 0), at(768, 0), at(256, 0), at(768, 0), at(128, 0)],
        out_shape=[
            jax.ShapeDtypeStruct((rows, 768), f32),
            jax.ShapeDtypeStruct((rows, 768), f32),
            jax.ShapeDtypeStruct((rows, 256), f32),
            jax.ShapeDtypeStruct((rows, 768), jnp.bfloat16),
            jax.ShapeDtypeStruct((rows, 128), f32),
        ],
        scratch_shapes=[
            pltpu.VMEM((8, 768), f32), pltpu.VMEM((8, 256), f32), pltpu.VMEM((128, 768), f32),
        ],
        compiler_params=pltpu.CompilerParams(vmem_limit_bytes=60 * 2**20),
        cost_estimate=pl.CostEstimate(flops=8 * 10**9, bytes_accessed=24 * 10**6, transcendentals=4 * 10**6),
        name="mixer_forward",
    )(second_pre, second_pre, first_pre, first_pre, d_normed_out, pos, taps, taps_s, heads_lanes, skip, gain, wide)


def backward_core(
    first_pre, second_pre, zi, zs, scanned, d_scan, enter, pos, taps, taps_s, heads_lanes, skip, wide, out_part, gate_part
):
    rows = first_pre.shape[0]
    count = rows // CHUNK
    at = lambda width, col: pl.BlockSpec((CHUNK, width), lambda c: (count - 1 - c, col))
    whole = lambda shape: pl.BlockSpec(shape, lambda c: (0,) * len(shape))
    f32, low = jnp.float32, jnp.bfloat16
    return pl.pallas_call(
        backward_kernel,
        grid=(count,),
        in_specs=[
            at(768, 0), at(128, 6), at(256, 3), at(768, 0), at(256, 0), at(768, 0), at(768, 0),
            at(768, 0), at(128, 0),
            whole(taps.shape), whole(taps_s.shape), whole(heads_lanes.shape), whole(skip.shape), whole(wide.shape),
            pl.BlockSpec(memory_space=pl.ANY), pl.BlockSpec(memory_space=pl.ANY),
        ],
        out_specs=[
            at(768, 0), whole((rows, 128)), at(128, 0),
            whole((5, 8, 768)), whole((5, 8, 256)), whole((8, 768)), whole((2, 8, 128)),
            whole((4, SHARD, 768)), whole((4, SHARD, 768)),
        ],
        out_shape=[
            jax.ShapeDtypeStruct((rows, 768), low),
            jax.ShapeDtypeStruct((rows, 128), low),
            jax.ShapeDtypeStruct((rows, 128), low),
            jax.ShapeDtypeStruct((5, 8, 768), f32),
            jax.ShapeDtypeStruct((5, 8, 256), f32),
            jax.ShapeDtypeStruct((8, 768), f32),
            jax.ShapeDtypeStruct((2, 8, 128), f32),
            jax.ShapeDtypeStruct((4, SHARD, 768), low),
            jax.ShapeDtypeStruct((4, SHARD, 768), low),
        ],
        scratch_shapes=[
            pltpu.VMEM((8, 768), f32), pltpu.VMEM((8, 256), f32), pltpu.VMEM((8, 128), f32),
            pltpu.VMEM((128, 768), f32),
            pltpu.VMEM((COUNT, CHUNK, 128), low), pltpu.VMEM((COUNT, CHUNK, 128), low),
            pltpu.SemaphoreType.DMA((COUNT,)), pltpu.SemaphoreType.DMA((COUNT,)),
            pltpu.VMEM((EARLY, 2, 4, 2, SHARD, 384), low),
            pltpu.VMEM((EARLY, 2, 4, 2, SHARD, 384), low),
            pltpu.VMEM((EARLY, 2, 4, 2, SHARD, 384), low),
            pltpu.VMEM((EARLY, 2, 4, SHARD, 384), low),
        ]
        + [pltpu.SemaphoreType.DMA((EARLY, 2))] * 5,
        compiler_params=pltpu.CompilerParams(
            collective_id=3, has_side_effects=True, vmem_limit_bytes=60 * 2**20
        ),
        cost_estimate=pl.CostEstimate(flops=16 * 10**9, bytes_accessed=24 * 10**6, transcendentals=6 * 10**6),
        name="mixer_backward",
    )(
        second_pre, second_pre, first_pre, zi, zs, scanned, d_scan, enter, pos, taps, taps_s, heads_lanes, skip, wide,
        out_part.reshape(4, 2, 2, SHARD, 768), gate_part.reshape(4, 2, 2, SHARD, 768),
    )


def swap(value):
    return lax.ppermute(value, "tensor", [(0, 1), (1, 0)])


def pad_cols(value, width):
    return jnp.pad(value, ((0, 0), (0, width - value.shape[1])))


GATHER_PIECES = (
    (1, 0, 384, 0), (1, 384, 512, 1), (0, 0, 512, 0), (0, 512, 512, 1), (2, 0, 384, 0), (2, 384, 384, 1),
)


def gather_kernel(
    gate_ref, state_ref, inner_ref, step_ref, out_ref, stream_ref, cot_ref, gain_ref,
    full_first, full_second, full_out, rows_ref, cots_ref, pre_first, pre_second, pre_out,
    first_ref, second_ref, lanes_ref, held_first, held_second, held_out,
    pre_sem, row_sem, z_send, z_recv, one_send, one_recv, two_send, two_recv,
):
    x, y, z, at_x, at_y, at_z = place()
    core = lax.axis_index("tensor")
    twin = {"tensor": 1 - core}
    low = jnp.bfloat16
    first_ref[:, pl.ds(0, 768)] = gate_ref[...].astype(low)
    first_ref[:, pl.ds(768, 256)] = state_ref[...].astype(low)
    second_ref[:, pl.ds(0, 768)] = inner_ref[...].astype(low)
    lanes_ref[...] = jnp.zeros_like(lanes_ref)
    lanes_ref[:, : step_ref.shape[1]] = step_ref[...]
    lanes = lanes_ref[...]
    second_ref[:, pl.ds(768, 128)] = (lanes + pltpu.roll(lanes, PACK, 1)).astype(low)
    greet([at_x, at_y, twin] + at_z)
    shards = (first_ref, second_ref, out_ref)
    fulls = (full_first, full_second, full_out)
    results = ((held_first, pre_first), (held_second, pre_second), (held_out, pre_out))
    z_copies, ones, twos, copies = {}, {}, {}, []

    def step_zero(piece):
        which, start, width, _ = GATHER_PIECES[piece]
        cols = pl.ds(start, width)
        z_copies[piece] = []
        for step, peer in enumerate(at_z):
            copy = remote(
                shards[which].at[:, cols], fulls[which].at[z, y, x, :, cols],
                z_send.at[piece, step], z_recv.at[piece, step], peer,
            )
            copy.start()
            z_copies[piece].append(copy)

    def step_one(piece):
        which, start, width, route = GATHER_PIECES[piece]
        for copy in z_copies[piece]:
            copy.wait()
        part = fulls[which].at[:, y, x, :, pl.ds(start, width)]
        ones[piece] = remote(part, part, one_send.at[piece], one_recv.at[piece], at_x if route else at_y)
        ones[piece].start()

    def step_two(piece):
        which, start, width, route = GATHER_PIECES[piece]
        cols = pl.ds(start, width)
        ones[piece].wait()
        part = fulls[which].at[:, y, :, :, cols] if route else fulls[which].at[:, :, x, :, cols]
        twos[piece] = remote(part, part, two_send.at[piece], two_recv.at[piece], at_y if route else at_x)
        twos[piece].start()

    def finish(piece):
        which, start, width, _ = GATHER_PIECES[piece]
        cols = pl.ds(start, width)
        twos[piece].wait()
        left = cots_ref if which == 2 else rows_ref
        held, pre = results[which]
        weights = fulls[which]

        def tile(at, carry):
            here = pl.ds(pl.multiple_of(lax.rem(at, 2) * 256, 256), 256)
            there = pl.ds(pl.multiple_of(at * 256, 256), 256)
            held[there, cols] = dot(
                left[lax.div(at, 2), here, :], weights[:, :, :, :, cols].reshape(768, width)
            )
            return carry

        lax.fori_loop(0, 4, tile, 0)
        copy = pltpu.make_async_copy(held.at[:, cols], pre.at[:, cols], pre_sem.at[piece])
        copy.start()
        copies.append(copy)

    step_zero(0)
    for shard, full in zip(shards, fulls):
        full[z, y, x] = shard[...]
    step_zero(1)
    for part in range(4):
        here = pl.ds(part * 128, 128)
        value = stream_ref[here, :]
        inv = lax.rsqrt(jnp.sum(value * value, axis=1, keepdims=True) / D + EPS)
        rows_ref[core, here, :] = (value * inv * gain_ref[...]).astype(jnp.bfloat16)
        cots_ref[core, here, :] = cot_ref[here, :].astype(jnp.bfloat16)
    swaps = []
    for at, ref in enumerate((rows_ref, cots_ref)):
        swaps.append(remote(ref.at[core], ref.at[core], row_sem.at[at], row_sem.at[2 + at], twin))
        swaps[-1].start()
    count = len(GATHER_PIECES)
    for piece in range(count + 1):
        if piece < count:
            step_one(piece)
        if piece + 2 < count:
            step_zero(piece + 2)
        if piece >= 1:
            step_two(piece - 1)
        if piece == 3:
            for copy in swaps:
                copy.wait()
        if piece >= 4:
            finish(piece - 4)
    for piece in range(count - 3, count):
        finish(piece)
    for copy in copies:
        copy.wait()


def gather_all(gate, state, inner, step, out, stream, cotangent, gain):
    f32, low = jnp.float32, jnp.bfloat16
    vmem = pl.BlockSpec(memory_space=pltpu.VMEM)
    count = len(GATHER_PIECES)
    dma = pltpu.SemaphoreType.DMA
    tokens = 2 * stream.shape[0]
    first = jax.ShapeDtypeStruct((SHARD, 1024), low)
    second = jax.ShapeDtypeStruct((SHARD, 896), low)
    full = lambda arr: jax.ShapeDtypeStruct((4, 2, 2) + arr.shape, low)
    rows = jax.ShapeDtypeStruct((2,) + stream.shape, low)
    pre = lambda arr: jax.ShapeDtypeStruct((tokens, arr.shape[1]), f32)
    got = pl.pallas_call(
        gather_kernel,
        in_specs=[vmem] * 8,
        out_specs=[vmem] * 5 + [pl.BlockSpec(memory_space=pl.ANY)] * 3,
        out_shape=[full(first), full(second), full(out), rows, rows, pre(first), pre(second), pre(out)],
        scratch_shapes=[
            pltpu.VMEM(first.shape, low), pltpu.VMEM(second.shape, low), pltpu.VMEM((SHARD, 128), f32),
            pltpu.VMEM((tokens, first.shape[1]), f32),
            pltpu.VMEM((tokens, second.shape[1]), f32),
            pltpu.VMEM((tokens, out.shape[1]), f32),
            dma((count,)), dma((4,)), dma((count, 3)), dma((count, 3)),
            dma((count,)), dma((count,)), dma((count,)), dma((count,)),
        ],
        compiler_params=pltpu.CompilerParams(
            collective_id=0, has_side_effects=True, vmem_limit_bytes=60 * 2**20
        ),
        cost_estimate=pl.CostEstimate(flops=4 * 10**9, bytes_accessed=120 * 10**6, transcendentals=0),
        name="gather_weights",
    )(gate, state, inner, step, out, stream, cotangent, gain)
    return [item.reshape(-1, item.shape[-1]) for item in got]


SHARED_ROW = 9
NORM_ROW = 14


def reduce_kernel(
    held_out, held_gate, inner_ref, small_ref, vec_ref, moment_ref, gain_ref, *rest,
):
    sources, rest = rest[:10], rest[10:]
    whole_ref, other_ref, grads_ref, total_ref, output_ref, d_stream_ref = rest[:6]
    local, rest = rest[6:16], rest[16:]
    reduce_body(
        held_out, held_gate, inner_ref, small_ref, vec_ref, moment_ref, gain_ref, sources,
        whole_ref, other_ref, grads_ref, total_ref, output_ref, d_stream_ref, local, *rest,
    )


def reduce_body(
    held_out, held_gate, inner_ref, small_ref, vec_ref, moment_ref, gain_ref, sources,
    whole_ref, other_ref, grads_ref, total_ref, output_ref, d_stream_ref, local,
    load_sem, mine_f, lent_b, got_b, vec_own, vec_twin, w_send, w_recv,
    arrived, summed, arrived_two, held_inner, held_small, slots, moments,
    block, back, vec_in, vec_mid, vec_slots,
    m_send, m_recv, one_send, one_recv, two_send, two_recv, z_send, z_recv, g_send, g_recv,
    p_send, p_recv, t_send, t_recv, v_send, v_recv,
):
    f32, low = jnp.float32, jnp.bfloat16
    x, y, z, at_x, at_y, at_z = place()
    core = lax.axis_index("tensor")
    twin = {"tensor": 1 - core}
    greet([at_x, at_y, twin] + at_z)
    parts = (inner_ref, small_ref)
    held = (held_out, held_gate, held_inner, held_small)
    steps_z = [lax.rem(z + step, 4) for step in range(1, 4)]
    span, one, two, add, settle = half_steps(
        parts, at_x, at_y, x, y, arrived, summed, arrived_two, one_send, one_recv, two_send, two_recv
    )

    def to_plane(task):
        plane, width = PLANE_OF[PLAN[task][0]], PLAN[task][1]

        @pl.when(z != plane)
        def _():
            remote(
                held[task], slots.at[z, :, :, pl.ds(0, width)], z_send.at[task], z_recv.at[z],
                {"dp": plane * 4 + y * 2 + x},
            ).start()

    for task in range(2):
        for route in range(2):
            one(task, route).start()
    to_plane(0)
    to_plane(1)
    moment_copies = []
    for step, (peer, plane) in enumerate(zip(at_z, steps_z)):
        copy = remote(moment_ref.at[plane], moments.at[z], m_send.at[step], m_recv.at[step], peer)
        copy.start()
        moment_copies.append(copy)
    loads = [pltpu.make_async_copy(src, dst, load_sem.at[at]) for at, (src, dst) in enumerate(zip(sources, local))]
    for copy in loads:
        copy.start()
    d_gate, d_inner, d_state, d_step, normed, w_first, w_second, w_out, stream_ref, cot_ref = local
    half_rows = stream_ref.shape[0]
    turned = ((1,), (1,))
    state_cols = pl.ds(pl.multiple_of(768 + core * 128, 128), 128)

    def product(which, rows):
        if which == 1:
            return dot(normed[rows, :], w_out[...], turned)
        first = dot(d_gate[rows, :], w_first[:, pl.ds(0, 768)], turned)
        second = dot(d_inner[rows, :], w_second[:, pl.ds(0, 768)], turned)
        third = dot(d_state[rows, :], w_first[:, state_cols], turned)
        return first + second + third + dot(d_step[rows, :], w_second[:, pl.ds(768, 128)], turned)

    for copy in loads:
        copy.wait()

    def products(who, store):
        for which in range(2):

            def tile(at, carry):
                rows = pl.ds(pl.multiple_of(who * half_rows + at * 128, 128), 128)
                store(which, pl.ds(pl.multiple_of(at * 128, 128), 128), product(which, rows))
                return carry

            lax.fori_loop(0, half_rows // 128, tile, 0)

    def store_lent(which, rows, value):
        lent_b[which, rows, :] = value.astype(low)

    def store_mine(which, rows, value):
        mine_f[which, rows, :] = value

    products(1 - core, store_lent)
    lends = []
    for which in range(2):
        lends.append(remote(lent_b.at[which], got_b.at[which], w_send.at[which], w_recv.at[which], twin))
        lends[-1].start()
    for task in range(2):
        for route in range(2):
            cols = span(task, route)[0]
            one(task, route).wait()
            add(task, route, parts[task][:, y, :, :, cols] if route else parts[task][:, :, x, :, cols])
            two(task, route).start()
    products(core, store_mine)
    for task in range(2):
        for route in range(2):
            two(task, route).wait()
            settle(task, route, held[2 + task])
        to_plane(2 + task)
    for copy in lends:
        copy.wait()
    grad_norm = jnp.zeros((1, 768), f32)
    gain = gain_ref[...]
    for part in range(half_rows // 128):
        rows = pl.ds(part * 128, 128)
        value = stream_ref[rows, :]
        output_ref[rows, :] = value + (mine_f[1, rows, :] + got_b[1, rows, :].astype(f32))
        inv = lax.rsqrt(jnp.sum(value * value, axis=1, keepdims=True) / D + EPS)
        d_normed = mine_f[0, rows, :] + got_b[0, rows, :].astype(f32)
        scaled = value * inv
        grad_norm = grad_norm + jnp.sum(d_normed * scaled, axis=0, keepdims=True)
        weighted = d_normed * gain
        inner = jnp.sum(weighted * scaled, axis=1, keepdims=True) / D
        d_stream_ref[rows, :] = cot_ref[rows, :] + inv * (weighted - scaled * inner)
    vec_rows = lax.broadcasted_iota(jnp.int32, vec_ref.shape, 0)
    vec_own[...] = jnp.where(vec_rows == NORM_ROW, grad_norm, vec_ref[...])
    vec_x = remote(vec_own, vec_in.at[0], v_send.at[0], v_recv.at[0], at_x)
    vec_x.start()
    vec_x.wait()
    vec_mid[0] = vec_own[...] + vec_in[0]
    vec_y = remote(vec_mid.at[0], vec_in.at[1], v_send.at[1], v_recv.at[1], at_y)
    vec_y.start()
    for copy in moment_copies:
        copy.wait()
    moments[z] = moment_ref[z]
    vec_y.wait()
    vec_mid[1] = vec_mid[0] + vec_in[1]
    vec_slots[z] = vec_mid[1]
    vec_z = []
    for step, peer in enumerate(at_z):
        copy = remote(vec_mid.at[1], vec_slots.at[z], v_send.at[2 + step], v_recv.at[2 + step], peer)
        copy.start()
        vec_z.append(copy)

    for task, (name, width) in enumerate(PLAN):
        plane = PLANE_OF[name]
        cols = pl.ds(0, width)

        @pl.when(z == plane)
        def _():
            for source in range(4):
                if source != plane:
                    remote(
                        held[task], slots.at[source, :, :, cols], z_send.at[task], z_recv.at[source], at_x
                    ).wait_recv()
            total = held[task][...].astype(f32)
            for source in range(4):
                if source != plane:
                    total = total + slots[source, :, :, cols].astype(f32)
            if width < 768:
                back[...] = jnp.zeros_like(back)
                block[...] = jnp.zeros_like(block)
            back[:, :, cols] = total.astype(low)
            block[:, :, cols] = (MU_MAT * moments[:, :, cols].astype(f32) + total).astype(low)

    half = 384
    routes = (pl.ds(0, half), pl.ds(half, half))
    for row in range(4):
        whole_ref[row, y, x] = block[row]
    plane_one = []
    for route, peer in enumerate((at_x, at_y)):
        copy = remote(
            block.at[:, :, routes[route]], whole_ref.at[:, y, x, :, routes[route]],
            p_send.at[0, route], p_recv.at[0, route], peer,
        )
        copy.start()
        plane_one.append(copy)
    twin_own = remote(block, other_ref.at[:, y, x], t_send.at[0], t_recv.at[0], twin)
    twin_own.start()
    grads_ref[z] = back[z]
    returns = []
    for step, (peer, plane) in enumerate(zip(at_z, steps_z)):
        copy = remote(back.at[plane], grads_ref.at[z], g_send.at[step], g_recv.at[step], peer)
        copy.start()
        returns.append(copy)
    plane_two = []
    for route, peer in enumerate((at_y, at_x)):
        plane_one[route].wait()
        part = (
            whole_ref.at[:, :, x, :, routes[1]] if route else whole_ref.at[:, y, :, :, routes[0]]
        )
        copy = remote(part, part, p_send.at[1, route], p_recv.at[1, route], peer)
        copy.start()
        plane_two.append(copy)
    twins = [twin_own]
    for route in range(2):
        src = whole_ref.at[:, 1 - y, x, :, routes[1]] if route else whole_ref.at[:, y, 1 - x, :, routes[0]]
        dst = other_ref.at[:, 1 - y, x, :, routes[1]] if route else other_ref.at[:, y, 1 - x, :, routes[0]]
        copy = remote(src, dst, t_send.at[1 + route], t_recv.at[1 + route], twin)
        copy.start()
        twins.append(copy)
    for route in range(2):
        plane_two[route].wait()
        src = whole_ref.at[:, :, 1 - x, :, routes[1]] if route else whole_ref.at[:, 1 - y, :, :, routes[0]]
        dst = other_ref.at[:, :, 1 - x, :, routes[1]] if route else other_ref.at[:, 1 - y, :, :, routes[0]]
        copy = remote(src, dst, t_send.at[3 + route], t_recv.at[3 + route], twin)
        copy.start()
        twins.append(copy)
    for copy in vec_z:
        copy.wait()
    vec_mid[0] = (vec_slots[0] + vec_slots[1]) + (vec_slots[2] + vec_slots[3])
    vec_swap = remote(vec_mid.at[0], vec_twin, w_send.at[2], w_recv.at[2], twin)
    vec_swap.start()
    for copy in twins + returns:
        copy.wait()
    vec_swap.wait()
    total_ref[...] = vec_mid[0] + jnp.where(vec_rows >= SHARED_ROW, vec_twin[...], 0.0)
    for task, (name, width) in enumerate(PLAN):
        plane = PLANE_OF[name]

        @pl.when(z != plane)
        def _():
            remote(
                held[task], slots.at[z, :, :, pl.ds(0, width)], z_send.at[task], z_recv.at[z],
                {"dp": plane * 4 + y * 2 + x},
            ).wait_send()


def reduce_all(held, parts, vectors, moments, gain, sources):
    f32, low = jnp.float32, jnp.bfloat16
    vmem = pl.BlockSpec(memory_space=pltpu.VMEM)
    dma = pltpu.SemaphoreType.DMA
    parts = [part.reshape(4, 2, 2, SHARD, part.shape[1]) for part in parts]
    buf = pltpu.VMEM
    tokens = sources[-1].shape
    whole, other, grads, total, output, d_stream = pl.pallas_call(
        reduce_kernel,
        in_specs=[vmem] * 7 + [pl.BlockSpec(memory_space=pl.ANY)] * len(sources),
        out_specs=[vmem] * 6,
        out_shape=[
            jax.ShapeDtypeStruct((4, 2, 2, SHARD, 768), low),
            jax.ShapeDtypeStruct((4, 2, 2, SHARD, 768), low),
            jax.ShapeDtypeStruct((4, SHARD, 768), low),
            jax.ShapeDtypeStruct(vectors.shape, f32),
            jax.ShapeDtypeStruct(tokens, f32),
            jax.ShapeDtypeStruct(tokens, f32),
        ],
        scratch_shapes=[buf(item.shape, item.dtype) for item in sources]
        + [
            dma((len(sources),)), buf((2,) + tokens, f32), buf((2,) + tokens, low), buf((2,) + tokens, low),
            buf(vectors.shape, f32), buf(vectors.shape, f32), dma((3,)), dma((3,)),
            buf((2, 2, 4, 2, SHARD, 384), low), buf((2, 2, 4, 2, SHARD, 384), low),
            buf((2, 2, 4, SHARD, 384), low),
            buf((4, SHARD, 768), low), buf((4, SHARD, 256), low),
            buf((4, 4, SHARD, 768), low), buf((4, SHARD, 768), low),
            buf((4, SHARD, 768), low), buf((4, SHARD, 768), low),
            buf((2,) + vectors.shape, f32), buf((2,) + vectors.shape, f32), buf((4,) + vectors.shape, f32),
            dma((3,)), dma((3,)), dma((2, 2)), dma((2, 2)), dma((2, 2)), dma((2, 2)),
            dma((4,)), dma((4,)), dma((3,)), dma((3,)), dma((2, 2)), dma((2, 2)),
            dma((5,)), dma((5,)), dma((5,)), dma((5,)),
        ],
        compiler_params=pltpu.CompilerParams(
            collective_id=1, has_side_effects=True, vmem_limit_bytes=60 * 2**20
        ),
        cost_estimate=pl.CostEstimate(flops=0, bytes_accessed=150 * 10**6, transcendentals=0),
        name="reduce_grads",
    )(*held, *parts, vectors, moments, gain, *sources)
    return whole.reshape(768, 768), other.reshape(768, 768), grads, total, output, d_stream


def newton_kernel(full_ref, out_ref, current, gram, mix):
    f32, low = jnp.float32, jnp.bfloat16
    rows, cols = current.shape
    tile = 256
    count = rows // tile
    row_ids = lax.broadcasted_iota(jnp.int32, (tile, tile), 0)
    col_ids = lax.broadcasted_iota(jnp.int32, (tile, tile), 1)
    blocks = [pl.ds(at * tile, tile) for at in range(count)]

    def symmetric(source, store):
        for first in range(count):
            for second in range(first, count):
                store(first, second, dot(source[blocks[first], :], source[blocks[second], :], ((1,), (1,))))

    def put(ref, first, second, value):
        ref[blocks[first], blocks[second]] = value.astype(low)
        if first != second:
            ref[blocks[second], blocks[first]] = value.T.astype(low)

    firsts = {}
    symmetric(full_ref, lambda first, second, value: firsts.update({(first, second): value}))
    trace = sum(
        jnp.sum(jnp.where(row_ids == col_ids, firsts[at, at], 0.0), keepdims=True) for at in range(count)
    )
    scale = jnp.sqrt(trace) + 1e-07
    inverse, inverse_square = 1.0 / scale, 1.0 / (scale * scale)
    for (first, second), value in firsts.items():
        put(gram, first, second, value * inverse_square)
    for at in range(count):
        current[blocks[at], :] = (full_ref[blocks[at], :].astype(f32) * inverse).astype(low)

    def mixed():
        def store(first, second, value):
            piece = gram[blocks[first], blocks[second]].astype(f32)
            put(mix, first, second, NS_B * piece + NS_C * value)

        symmetric(gram, store)

    def turn(_, carry):
        mixed()

        def update(at, carry):
            here = pl.ds(pl.multiple_of(at * tile, tile), tile)
            held = current[:, here]
            current[:, here] = (NS_A * held.astype(f32) + dot(mix[...], held)).astype(low)
            return carry

        lax.fori_loop(0, cols // tile, update, 0)
        symmetric(current, lambda first, second, value: put(gram, first, second, value))
        return carry

    lax.fori_loop(0, NS_STEPS - 1, turn, 0)
    mixed()
    for at in range(out_ref.shape[1] // tile):
        here = pl.ds(at * tile, tile)
        held = current[:, here]
        out_ref[:, here] = (NS_A * held.astype(f32) + dot(mix[...], held)).astype(low)


def newton(full, width):
    low = jnp.bfloat16
    rows = full.shape[0]
    return pl.pallas_call(
        newton_kernel,
        in_specs=[pl.BlockSpec(memory_space=pltpu.VMEM)],
        out_specs=pl.BlockSpec(memory_space=pltpu.VMEM),
        out_shape=jax.ShapeDtypeStruct((rows, width), low),
        scratch_shapes=[
            pltpu.VMEM(full.shape, low), pltpu.VMEM((rows, rows), low), pltpu.VMEM((rows, rows), low),
        ],
        compiler_params=pltpu.CompilerParams(vmem_limit_bytes=60 * 2**20),
        cost_estimate=pl.CostEstimate(flops=20 * 10**9, bytes_accessed=4 * 10**6, transcendentals=0),
        name="newton_schulz",
    )(full)


def return_kernel(done_ref, back_ref, send, recv):
    x, y, z, _, _, at_z = place()
    greet(at_z)
    copies = []
    for step, peer in enumerate(at_z):
        plane = lax.rem(z + step + 1, 4)
        copies.append(
            remote(done_ref.at[plane, y, x], back_ref.at[z], send.at[step], recv.at[step], peer)
        )
        copies[-1].start()
    back_ref[z] = done_ref[z, y, x]
    for copy in copies:
        copy.wait()


def return_rows(done):
    vmem = pl.BlockSpec(memory_space=pltpu.VMEM)
    dma = pltpu.SemaphoreType.DMA
    return pl.pallas_call(
        return_kernel,
        in_specs=[vmem],
        out_specs=vmem,
        out_shape=jax.ShapeDtypeStruct((4, SHARD, 768), done.dtype),
        scratch_shapes=[dma((3,)), dma((3,))],
        compiler_params=pltpu.CompilerParams(collective_id=2, has_side_effects=True, vmem_limit_bytes=16 * 2**20),
        cost_estimate=pl.CostEstimate(flops=0, bytes_accessed=20 * 10**6, transcendentals=0),
        name="return_rows",
    )(done.reshape(4, 2, 2, SHARD, 768))


def orthogonal_owned(own, other, state_width):
    width = own.shape[1]
    small = lax.axis_index("dp") // 4 == PLANE_OF["small"]
    full = jnp.concatenate([own, other], axis=1)
    col = jnp.arange(2 * width)[None, :] % width
    keep = (col < state_width) == (lax.axis_index("tensor") == 0)
    full = jnp.where(small & ~keep, jnp.zeros_like(full), full)
    done = newton(full, width + 2 * state_width)
    half, lent = done[:, :width], done[:, width:]
    edge = half[:, : 2 * state_width]
    edge = edge + jnp.where(small, swap(lent), jnp.zeros_like(lent))
    return jnp.concatenate([edge, half[:, 2 * state_width :]], axis=1)


def paired_shards(
    stream,
    cotangent,
    positions,
    norm_gain,
    w_gate,
    w_inner,
    w_state,
    w_step,
    conv_inner,
    conv_state,
    head_params,
    gate_gain,
    w_out,
    moment_norm_gain,
    moment_w_gate,
    moment_w_inner,
    moment_w_state,
    moment_w_step,
    moment_conv_inner,
    moment_conv_state,
    moment_head_params,
    moment_gate_gain,
    moment_w_out,
):
    low = jnp.bfloat16
    core = lax.axis_index("tensor")
    room = w_gate.shape[1]
    wide = w_state.shape[1]
    col_width = wide // 2
    heads = w_step.shape[1]
    full_first, full_second, full_out, token_rows, cotangent_rows, first_pre, second_pre, d_normed_out = gather_all(
        w_gate, w_state, w_inner, w_step, w_out.astype(low).T, stream, cotangent, norm_gain[None, :]
    )
    pos = jnp.broadcast_to(positions.astype(jnp.float32)[:, None], (positions.shape[0], 128))
    taps = jnp.pad(conv_inner, ((0, 3), (0, 0)))
    taps_s = jnp.pad(conv_state, ((0, 3), (0, 0)))
    lanes = jnp.concatenate([pad_cols(head_params, PACK), pad_cols(head_params, 128 - PACK)], axis=1)
    lanes = jnp.pad(lanes, ((0, 5), (0, 0)))
    skip = jnp.repeat(head_params[2], room // heads)[None, :]
    wide_map = expand_matrix()
    scanned, zi, zs, enter, sums = forward_core(
        first_pre, second_pre, d_normed_out, pos, taps, taps_s, lanes, skip, gate_gain[None, :], wide_map
    )
    normed_out, d_gate_pre, d_scan, gain_part = gate_stage(
        first_pre, scanned, d_normed_out, sums, swap(sums), gate_gain[None, :], pos
    )
    grad_gate_part = jnp.sum(gain_part, axis=0)
    out_part = contract_rows(cotangent_rows, normed_out).astype(low)
    gate_part = contract_rows(token_rows, d_gate_pre).astype(low)
    d_inner, d_state_low, d_step, taps_part, taps_s_part, skip_part, head_part, held_out, held_gate = backward_core(
        first_pre, second_pre, zi, zs, scanned, d_scan, enter, pos, taps, taps_s, lanes, skip, wide_map, out_part, gate_part
    )
    grad_conv_inner_part = jnp.sum(taps_part, axis=1)
    grad_conv_state_part = jnp.sum(taps_s_part, axis=1)
    head_rows = jnp.sum(head_part, axis=1)[:, :heads]
    skip_row = jnp.sum(jnp.sum(skip_part, axis=0).reshape(heads, -1), axis=1)
    grad_head_part = jnp.concatenate([head_rows, skip_row[None, :]], axis=0)
    col_first = core * col_width
    inner_part = contract_rows(token_rows, d_inner).astype(low)
    small_part = contract_rows(token_rows, jnp.concatenate([d_state_low, d_step], axis=1)).astype(low)
    vectors = jnp.concatenate(
        [
            grad_conv_inner_part,
            grad_gate_part[None, :],
            pad_cols(grad_head_part, room),
            pad_cols(grad_conv_state_part, room),
        ],
        axis=0,
    )
    vectors = jnp.pad(vectors, ((0, 16 - vectors.shape[0]), (0, 0)))
    small_moment = pad_cols(jnp.concatenate([moment_w_state, moment_w_step], axis=1), room)
    moment_rows = jnp.stack([moment_w_out.T, moment_w_inner, moment_w_gate, small_moment]).astype(low)
    own, other, grads, vectors, output, d_stream = reduce_all(
        (held_out, held_gate), (inner_part, small_part), vectors, moment_rows, norm_gain[None, :],
        (
            d_gate_pre, d_inner, d_state_low, d_step, normed_out, full_first, full_second, full_out,
            stream, cotangent,
        ),
    )
    grads = grads.astype(jnp.float32)
    grad_gate_w = grads[2]
    grad_inner_w = grads[1]
    grad_out_w = grads[0].T
    grad_state_w = grads[3][:, :col_width]
    grad_step_w = grads[3][:, col_width : col_width + heads]
    grad_conv_inner = vectors[:5]
    grad_gate_gain = vectors[5]
    grad_head = vectors[6:9, :heads]
    grad_conv_state = vectors[9:14, :wide]
    grad_norm = vectors[NORM_ROW]
    m_gate = MU_MAT * moment_w_gate + grad_gate_w
    m_inner = MU_MAT * moment_w_inner + grad_inner_w
    m_state = MU_MAT * moment_w_state + grad_state_w
    m_step = MU_MAT * moment_w_step + grad_step_w
    m_out = MU_MAT * moment_w_out + grad_out_w
    mine = return_rows(orthogonal_owned(own, other, col_width)).astype(jnp.float32)
    new_gate = w_gate - LR_MAT * spread(D, INNER) * mine[2]
    new_inner = w_inner - LR_MAT * spread(D, INNER) * mine[1]
    new_out = w_out - LR_MAT * spread(INNER, D) * mine[0].T
    new_step = w_step - LR_MAT * spread(D, HEADS) * mine[3][:, col_width : col_width + heads]
    state_slice = lax.dynamic_slice_in_dim(w_state, col_first, col_width, 1)
    new_state = state_slice - LR_MAT * spread(D, 2 * STATE) * mine[3][:, :col_width]
    m_norm = MU_VEC * moment_norm_gain + grad_norm
    m_conv_inner = MU_VEC * moment_conv_inner + grad_conv_inner
    m_conv_state = MU_VEC * moment_conv_state + grad_conv_state
    m_head = MU_VEC * moment_head_params + grad_head
    m_gate_gain = MU_VEC * moment_gate_gain + grad_gate_gain
    return (
        output,
        d_stream,
        grad_norm,
        grad_gate_w,
        grad_inner_w,
        grad_state_w,
        grad_step_w,
        grad_conv_inner,
        grad_conv_state,
        grad_head,
        grad_gate_gain,
        grad_out_w,
        norm_gain - LR_VEC * m_norm,
        new_gate,
        new_inner,
        new_state,
        new_step,
        conv_inner - LR_VEC * m_conv_inner,
        conv_state - LR_VEC * m_conv_state,
        head_params - LR_VEC * m_head,
        gate_gain - LR_VEC * m_gate_gain,
        new_out,
        m_norm,
        m_gate,
        m_inner,
        m_state,
        m_step,
        m_conv_inner,
        m_conv_state,
        m_head,
        m_gate_gain,
        m_out,
    )


def solution(mesh):
    paired = mesh.shape["dp"] == 16 and mesh.shape["tensor"] == 2
    return jax.shard_map(
        paired_shards if paired else shards,
        mesh=mesh,
        in_specs=(
            P(("dp", "tensor"), None),
            P(("dp", "tensor"), None),
            P("dp"),
            P(),
            P("dp", "tensor"),
            P("dp", "tensor"),
            P("dp", None),
            P("dp", "tensor"),
            P(None, "tensor"),
            P(),
            P(None, "tensor"),
            P("tensor"),
            P("tensor", "dp"),
            P(),
            P("dp", "tensor"),
            P("dp", "tensor"),
            P("dp", "tensor"),
            P("dp", "tensor"),
            P(None, "tensor"),
            P(),
            P(None, "tensor"),
            P("tensor"),
            P("tensor", "dp"),
        ),
        out_specs=(
            P(("dp", "tensor"), None),
            P(("dp", "tensor"), None),
            P(),
            P("dp", "tensor"),
            P("dp", "tensor"),
            P("dp", "tensor"),
            P("dp", "tensor"),
            P(None, "tensor"),
            P(),
            P(None, "tensor"),
            P("tensor"),
            P("tensor", "dp"),
            P(),
            P("dp", "tensor"),
            P("dp", "tensor"),
            P("dp", "tensor"),
            P("dp", "tensor"),
            P(None, "tensor"),
            P(),
            P(None, "tensor"),
            P("tensor"),
            P("tensor", "dp"),
            P(),
            P("dp", "tensor"),
            P("dp", "tensor"),
            P("dp", "tensor"),
            P("dp", "tensor"),
            P(None, "tensor"),
            P(),
            P(None, "tensor"),
            P("tensor"),
            P("tensor", "dp"),
        ),
        check_vma=False,
    )
```

```python
from functools import partial
import math

import jax
import jax.numpy as jnp
from jax import lax
from jax.experimental import pallas as pl
from jax.experimental.pallas import tpu as pltpu
from jax.sharding import PartitionSpec as P

D = 768
INNER = 1536
HEADS = 24
STATE = 128
BLOCK = 256
NS_STEPS = 5


EPS = 1e-05
NS_A = 3.4445
NS_B = -4.775
NS_C = 2.0315
MU_MAT = 0.95
MU_VEC = 0.9
LR_MAT = 0.3
LR_VEC = 0.001
HIGH = lax.Precision.HIGHEST
CORE = lax.Precision.DEFAULT


def silu_slope(value):
    sig = jax.nn.sigmoid(value)
    return sig * (1.0 + value * (1.0 - sig))


def contract_rows(left, right):
    return lax.dot_general(
        left, right, (((0,), (0,)), ((), ())), preferred_element_type=jnp.float32
    )


def times_transpose(left, right):
    return lax.dot_general(
        left, right, (((1,), (1,)), ((), ())), preferred_element_type=jnp.float32
    )


def causal_conv(signal, taps, positions):
    length = signal.shape[0]
    reach = taps.shape[0] - 1
    total = jnp.zeros_like(signal) + taps[reach]
    for lag_step in range(reach):
        moved = jnp.pad(signal, ((lag_step, 0), (0, 0)))[:length]
        total = total + jnp.where((positions >= lag_step)[:, None], moved * taps[lag_step], 0.0)
    return jax.nn.silu(total)


def mixer_core(inner_pre, state_pre, step_pre, conv_inner, conv_state, head_params, positions, precision=HIGH):
    length = inner_pre.shape[0]
    heads = step_pre.shape[1]
    head_size = inner_pre.shape[1] // heads
    states = state_pre.shape[1] // 2
    blocks = length // BLOCK
    inner_act = causal_conv(inner_pre, conv_inner, positions).reshape(
        blocks, BLOCK, heads, head_size
    )
    state_act = causal_conv(state_pre, conv_state, positions)
    input_map = state_act[:, :states].reshape(blocks, BLOCK, states)
    output_map = state_act[:, states:].reshape(blocks, BLOCK, states)
    step_size = jax.nn.softplus(step_pre + head_params[0])
    log_decay = (step_size * -jnp.exp(head_params[1])).reshape(blocks, BLOCK, heads)
    step_size = step_size.reshape(blocks, BLOCK, heads)
    resets = (positions <= 0).astype(jnp.float32).reshape(blocks, BLOCK)
    order = jnp.arange(BLOCK)
    lower = (order[:, None] >= order[None, :]).astype(jnp.float32)
    cumulative = jnp.einsum("ij,cjh->cih", lower, log_decay, precision=HIGH)
    seen = jnp.einsum("ij,cj->ci", lower, resets, precision=HIGH)
    linked = (seen[:, :, None] == seen[:, None, :]) & (order[:, None] >= order[None, :])[None]
    linked_heads = linked[..., None]
    spacing = cumulative[:, :, None, :] - cumulative[:, None, :, :]
    decay = jnp.where(linked_heads, jnp.exp(jnp.where(linked_heads, spacing, 0.0)), 0.0)
    scores = jnp.einsum("cin,cjn->cij", output_map, input_map, precision=precision)
    mixing = scores[..., None] * decay * step_size[:, None, :, :]
    within = jnp.einsum("cijh,cjhp->cihp", mixing, inner_act, precision=precision)
    tail_linked = (seen[:, -1:] == seen)[..., None]
    tail = (
        jnp.where(
            tail_linked,
            jnp.exp(jnp.where(tail_linked, cumulative[:, -1:, :] - cumulative, 0.0)),
            0.0,
        )
        * step_size
    )
    own_state = jnp.einsum("cjh,cjhp,cjn->chpn", tail, inner_act, input_map, precision=precision)
    carry_rate = jnp.exp(cumulative[:, -1, :]) * (seen[:, -1] == 0).astype(jnp.float32)[:, None]

    state = jnp.zeros((heads, head_size, states), jnp.float32)
    entering = []
    for block in range(blocks):
        entering.append(state)
        state = carry_rate[block][:, None, None] * state + own_state[block]
    entering = jnp.stack(entering)
    fresh = (seen == 0)[..., None]
    carry_in = jnp.where(fresh, jnp.exp(cumulative), 0.0)
    across = (
        jnp.einsum("cin,chpn->cihp", output_map, entering, precision=precision) * carry_in[..., None]
    )
    result = within + across + head_params[2][None, None, :, None] * inner_act
    return result.reshape(length, heads * head_size)


def gram_total(low):
    return lax.psum(
        jnp.dot(low, low.T, preferred_element_type=jnp.float32).astype(jnp.bfloat16), "tensor"
    ).astype(jnp.float32)


def orthogonalize(matrix):
    first = gram_total(matrix.astype(jnp.bfloat16))
    scale = jnp.sqrt(jnp.trace(first)) + 1e-07
    current = (matrix / scale).astype(jnp.bfloat16)
    gram = (first / (scale * scale)).astype(jnp.bfloat16)
    for turn in range(NS_STEPS):
        if turn > 0:
            gram = gram_total(current).astype(jnp.bfloat16)
        applied = jnp.dot(gram, current, preferred_element_type=jnp.float32)
        twice = jnp.dot(gram, applied.astype(jnp.bfloat16), preferred_element_type=jnp.float32)
        current = (NS_A * current.astype(jnp.float32) + NS_B * applied + NS_C * twice).astype(
            jnp.bfloat16
        )
    return current.astype(jnp.float32)


def spread(rows, cols):
    return math.sqrt(max(1.0, rows / cols))


def shards(
    stream,
    cotangent,
    positions,
    norm_gain,
    w_gate,
    w_inner,
    w_state,
    w_step,
    conv_inner,
    conv_state,
    head_params,
    gate_gain,
    w_out,
    moment_norm_gain,
    moment_w_gate,
    moment_w_inner,
    moment_w_state,
    moment_w_step,
    moment_conv_inner,
    moment_conv_state,
    moment_head_params,
    moment_gate_gain,
    moment_w_out,
):
    dp_count = lax.axis_size("dp")
    inv_first = lax.rsqrt(jnp.mean(stream * stream, axis=1, keepdims=True) + EPS)
    normed = (stream * inv_first * norm_gain).astype(jnp.bfloat16)
    token_rows, cotangent_rows = (
        lax.all_gather(normed, "tensor", axis=0, tiled=True),
        lax.all_gather(cotangent.astype(jnp.bfloat16), "tensor", axis=0, tiled=True),
    )
    local_weights = (
        w_gate.astype(jnp.bfloat16),
        w_inner.astype(jnp.bfloat16),
        w_step.astype(jnp.bfloat16),
        w_state.astype(jnp.bfloat16),
        w_out.astype(jnp.bfloat16),
    )
    full_gate, full_inner, full_step, full_state, full_out = (
        lax.all_gather(local_weights[0], "dp", axis=0, tiled=True),
        lax.all_gather(local_weights[1], "dp", axis=0, tiled=True),
        lax.all_gather(local_weights[2], "dp", axis=0, tiled=True),
        lax.all_gather(local_weights[3], "dp", axis=0, tiled=True),
        lax.all_gather(local_weights[4], "dp", axis=1, tiled=True),
    )
    gate_pre = jnp.dot(token_rows, full_gate, preferred_element_type=jnp.float32)
    inner_pre = jnp.dot(token_rows, full_inner, preferred_element_type=jnp.float32)
    state_pre = jnp.dot(token_rows, full_state, preferred_element_type=jnp.float32)
    step_pre = jnp.dot(token_rows, full_step, preferred_element_type=jnp.float32)
    alive = (positions >= 0).astype(jnp.float32)[:, None]
    scanned, core_back = jax.vjp(
        partial(mixer_core, positions=positions),
        inner_pre,
        state_pre,
        step_pre,
        conv_inner,
        conv_state,
        head_params,
    )
    gate_act = jax.nn.silu(gate_pre)
    gated = scanned * gate_act
    square_sum = lax.psum(jnp.sum(gated * gated, axis=1), "tensor")
    inv_second = lax.rsqrt(square_sum / INNER + EPS)[:, None]
    normed_out = (gated * inv_second * gate_gain * alive).astype(jnp.bfloat16)
    mixed = lax.psum_scatter(
        jnp.dot(normed_out, full_out, preferred_element_type=jnp.float32).astype(jnp.bfloat16),
        "tensor",
        scatter_dimension=0,
        tiled=True,
    ).astype(jnp.float32)
    output = stream + mixed
    d_normed_out = times_transpose(cotangent_rows, full_out)
    grad_out_part = contract_rows(normed_out, cotangent_rows)
    scaled = d_normed_out * gate_gain * alive
    grad_gate_part = jnp.sum(d_normed_out * gated * inv_second * alive, axis=0)
    cross_sum = lax.psum(jnp.sum(scaled * gated, axis=1), "tensor")
    d_gated = inv_second * scaled - gated * inv_second**3 * (cross_sum / INNER)[:, None]
    d_gate_pre = (d_gated * scanned * silu_slope(gate_pre)).astype(jnp.bfloat16)
    d_inner, d_state_part, d_step, grad_conv_inner_part, grad_conv_state_part, grad_head_part = (
        core_back(d_gated * gate_act)
    )
    d_state_cols = lax.psum_scatter(
        d_state_part.astype(jnp.bfloat16), "tensor", scatter_dimension=1, tiled=True
    ).astype(jnp.float32)
    d_inner_low = d_inner.astype(jnp.bfloat16)
    d_state_low = d_state_cols.astype(jnp.bfloat16)
    d_step_low = d_step.astype(jnp.bfloat16)
    col_width = d_state_cols.shape[1]
    col_first = lax.axis_index("tensor") * col_width
    state_cols = lax.dynamic_slice_in_dim(full_state, col_first, col_width, 1)
    total = times_transpose(d_gate_pre, full_gate)
    total = total + times_transpose(d_inner_low, full_inner)
    total = total + times_transpose(d_state_low, state_cols)
    d_normed = lax.psum_scatter(
        (total + times_transpose(d_step_low, full_step)).astype(jnp.bfloat16),
        "tensor",
        scatter_dimension=0,
        tiled=True,
    ).astype(jnp.float32)
    grad_gate_w, grad_inner_w, grad_state_w, grad_step_w, grad_out_w = (
        lax.psum_scatter(
            contract_rows(token_rows, d_gate_pre).astype(jnp.bfloat16),
            "dp",
            scatter_dimension=0,
            tiled=True,
        ).astype(jnp.float32),
        lax.psum_scatter(
            contract_rows(token_rows, d_inner_low).astype(jnp.bfloat16),
            "dp",
            scatter_dimension=0,
            tiled=True,
        ).astype(jnp.float32),
        lax.psum_scatter(
            contract_rows(token_rows, d_state_low).astype(jnp.bfloat16),
            "dp",
            scatter_dimension=0,
            tiled=True,
        ).astype(jnp.float32),
        lax.psum_scatter(
            contract_rows(token_rows, d_step_low).astype(jnp.bfloat16),
            "dp",
            scatter_dimension=0,
            tiled=True,
        ).astype(jnp.float32),
        lax.psum_scatter(
            grad_out_part.astype(jnp.bfloat16), "dp", scatter_dimension=1, tiled=True
        ).astype(jnp.float32),
    )
    grad_norm_part = jnp.sum(d_normed * stream * inv_first, axis=0)
    weighted = d_normed * norm_gain
    d_stream = (
        cotangent
        + inv_first * weighted
        - stream * inv_first**3 * jnp.mean(weighted * stream, axis=1, keepdims=True)
    )
    grad_conv_inner, grad_gate_gain, grad_head = lax.psum(
        (grad_conv_inner_part, grad_gate_part, grad_head_part), "dp"
    )
    grad_conv_state, grad_norm = lax.psum((grad_conv_state_part, grad_norm_part), ("dp", "tensor"))
    m_gate = MU_MAT * moment_w_gate + grad_gate_w
    m_inner = MU_MAT * moment_w_inner + grad_inner_w
    m_state = MU_MAT * moment_w_state + grad_state_w
    m_step = MU_MAT * moment_w_step + grad_step_w
    m_out = MU_MAT * moment_w_out + grad_out_w
    room = w_gate.shape[1]
    shard_rows = w_gate.shape[0]
    stacked = jnp.stack(
        [
            m_gate,
            m_inner,
            m_out.T,
            jnp.pad(m_step, ((0, 0), (0, room - m_step.shape[1]))),
            jnp.pad(m_state, ((0, 0), (0, room - m_state.shape[1]))),
        ]
    )
    matrix_count = stacked.shape[0]
    owner_index = jnp.arange(matrix_count, dtype=jnp.int32) * dp_count // matrix_count
    select = (owner_index[None, :] == jnp.arange(dp_count, dtype=jnp.int32)[:, None]).astype(
        jnp.float32
    )
    outgoing = jnp.einsum("jk,krc->jrc", select, stacked, precision=HIGH)
    owned = (
        lax.all_to_all(outgoing.astype(jnp.bfloat16), "dp", split_axis=0, concat_axis=0, tiled=True)
        .astype(outgoing.dtype)
        .reshape(dp_count * shard_rows, room)
    )
    ortho = orthogonalize(owned)
    returned = lax.all_to_all(
        ortho.reshape(dp_count, shard_rows, room).astype(jnp.bfloat16),
        "dp",
        split_axis=0,
        concat_axis=0,
        tiled=True,
    ).astype(jnp.float32)
    mine = jnp.einsum("jk,jrc->krc", select, returned, precision=HIGH)
    new_gate = w_gate - LR_MAT * spread(D, INNER) * mine[0]
    new_inner = w_inner - LR_MAT * spread(D, INNER) * mine[1]
    new_out = w_out - LR_MAT * spread(INNER, D) * mine[2].T
    new_step = w_step - LR_MAT * spread(D, HEADS) * mine[3][:, : w_step.shape[1]]
    state_slice = lax.dynamic_slice_in_dim(w_state, col_first, col_width, 1)
    new_state = state_slice - LR_MAT * spread(D, 2 * STATE) * mine[4][:, :col_width]
    m_norm = MU_VEC * moment_norm_gain + grad_norm
    m_conv_inner = MU_VEC * moment_conv_inner + grad_conv_inner
    m_conv_state = MU_VEC * moment_conv_state + grad_conv_state
    m_head = MU_VEC * moment_head_params + grad_head
    m_gate_gain = MU_VEC * moment_gate_gain + grad_gate_gain
    return (
        output,
        d_stream,
        grad_norm,
        grad_gate_w,
        grad_inner_w,
        grad_state_w,
        grad_step_w,
        grad_conv_inner,
        grad_conv_state,
        grad_head,
        grad_gate_gain,
        grad_out_w,
        norm_gain - LR_VEC * m_norm,
        new_gate,
        new_inner,
        new_state,
        new_step,
        conv_inner - LR_VEC * m_conv_inner,
        conv_state - LR_VEC * m_conv_state,
        head_params - LR_VEC * m_head,
        gate_gain - LR_VEC * m_gate_gain,
        new_out,
        m_norm,
        m_gate,
        m_inner,
        m_state,
        m_step,
        m_conv_inner,
        m_conv_state,
        m_head,
        m_gate_gain,
        m_out,
    )


MESH_ID = pl.DeviceIdType.MESH
SHARD = 48
PLAN = (("out", 768), ("gate", 768), ("inner", 768), ("small", 256))
PLANE_OF = {"out": 0, "inner": 1, "gate": 2, "small": 3}


def place():
    index = lax.axis_index("dp")
    z = lax.div(index, 4)
    y = lax.rem(lax.div(index, 2), 2)
    x = lax.rem(index, 2)
    at_x = {"dp": z * 4 + y * 2 + (1 - x)}
    at_y = {"dp": z * 4 + (1 - y) * 2 + x}
    at_z = [{"dp": lax.rem(z + step, 4) * 4 + y * 2 + x} for step in range(1, 4)]
    return x, y, z, at_x, at_y, at_z


def greet(peers):
    barrier = pltpu.get_barrier_semaphore()
    for peer in peers:
        pl.semaphore_signal(barrier, inc=1, device_id=peer, device_id_type=MESH_ID)
    pl.semaphore_wait(barrier, len(peers))


def remote(src, dst, send, recv, peer):
    return pltpu.make_async_remote_copy(
        src_ref=src, dst_ref=dst, send_sem=send, recv_sem=recv, device_id=peer, device_id_type=MESH_ID
    )

EARLY = 2
COUNT = 8
SHARED_ROW = 9
NORM_ROW = 14


def half_steps(parts, at_x, at_y, x, y, arrived, summed, arrived_two, one_send, one_recv, two_send, two_recv):
    def span(task, route):
        half = parts[task].shape[-1] // 2
        return pl.ds(route * half, half), pl.ds(0, half)

    def one(task, route):
        cols, mine = span(task, route)
        other = parts[task].at[:, 1 - y, :, :, cols] if route else parts[task].at[:, :, 1 - x, :, cols]
        return remote(
            other, arrived.at[task, route, :, :, :, mine], one_send.at[task, route],
            one_recv.at[task, route], at_y if route else at_x,
        )

    def two(task, route):
        mine = span(task, route)[1]
        return remote(
            summed.at[task, route, :, 1 - x if route else 1 - y, :, mine],
            arrived_two.at[task, route, :, :, mine], two_send.at[task, route],
            two_recv.at[task, route], at_x if route else at_y,
        )

    def add(task, route, own):
        mine = span(task, route)[1]
        got = arrived[task, route, :, :, :, mine]
        summed[task, route, :, :, :, mine] = (own.astype(jnp.float32) + got.astype(jnp.float32)).astype(jnp.bfloat16)

    def settle(task, route, held):
        cols, mine = span(task, route)
        own = summed[task, route, :, x if route else y, :, mine]
        got = arrived_two[task, route, :, :, mine]
        held[:, :, cols] = (own.astype(jnp.float32) + got.astype(jnp.float32)).astype(jnp.bfloat16)

    return span, one, two, add, settle


def early_reduce(parts, held, own, arrived, summed, arrived_two, own_sem, one_send, one_recv, two_send, two_recv):
    step = pl.program_id(0)
    x, y, z, at_x, at_y, _ = place()
    span, one, two, add, settle = half_steps(
        parts, at_x, at_y, x, y, arrived, summed, arrived_two, one_send, one_recv, two_send, two_recv
    )
    pairs = [(task, route) for task in range(EARLY) for route in range(2)]

    def load(task, route):
        cols = span(task, route)[0]
        src = parts[task].at[:, y, :, :, cols] if route else parts[task].at[:, :, x, :, cols]
        return pltpu.make_async_copy(src, own.at[task, route], own_sem.at[task, route])

    @pl.when(step == 0)
    def _():
        greet([at_x, at_y, {"tensor": 1 - lax.axis_index("tensor")}])
        for route in range(2):
            one(0, route).start()
        for task, route in pairs:
            load(task, route).start()
        for route in range(2):
            one(1, route).start()

    for task, at in ((0, 3), (1, 5)):

        @pl.when(step == at)
        def _():
            for route in range(2):
                load(task, route).wait()
                one(task, route).wait()
                add(task, route, own[task, route])
                two(task, route).start()

    for task, at in ((0, 6), (1, 7)):

        @pl.when(step == at)
        def _():
            for route in range(2):
                two(task, route).wait()
                settle(task, route, held[task])


CHUNK = 128
PACK = 16


def sigmoid(value):
    return 0.5 * jnp.tanh(0.5 * value) + 0.5


def expand_matrix():
    row = jnp.arange(128)[:, None]
    col = jnp.arange(768)[None, :] // 64
    return ((row == col) | (row == col + PACK)).astype(jnp.bfloat16)


def two_term(value):
    lane = lax.broadcasted_iota(jnp.int32, value.shape, 1)
    high = value.astype(jnp.bfloat16).astype(jnp.float32)
    return jnp.where(lane < PACK, high, value - high).astype(jnp.bfloat16)


def split_terms(value, terms):
    out = []
    for _ in range(terms):
        piece = value.astype(jnp.bfloat16)
        out.append(piece)
        value = value - piece.astype(jnp.float32)
    return out


def dot(left, right, dims=((1,), (0,))):
    return lax.dot_general(left, right, (dims, ((), ())), preferred_element_type=jnp.float32)


def head_terms(step_ref, head_ref, pos):
    shifted = step_ref[...] + head_ref[0:1, :]
    small = jnp.exp(-jnp.abs(shifted))
    step = jnp.maximum(shifted, 0.0) + jnp.log1p(small)
    log_decay = -step * jnp.exp(head_ref[1:2, :])
    row = lax.broadcasted_iota(jnp.int32, (CHUNK, 128), 0)
    col = lax.broadcasted_iota(jnp.int32, (CHUNK, 128), 1)
    lower = (row >= col).astype(jnp.bfloat16)
    cumulative = sum(dot(lower, piece) for piece in split_terms(log_decay, 3))
    last = cumulative[CHUNK - 1 : CHUNK, :]
    back = (row - col).astype(jnp.float32)
    linked = (row >= col) & (back <= jnp.maximum(pos, 0.0))
    row = row.astype(jnp.float32)
    carry_in = jnp.where(pos > row, jnp.exp(cumulative), 0.0)
    pos_last = pos[CHUNK - 1 : CHUNK, :]
    tail_linked = (CHUNK - 1.0 - row) <= jnp.maximum(pos_last, 0.0)
    tail = jnp.where(tail_linked, jnp.exp(jnp.minimum(last - cumulative, 0.0)), 0.0)
    carry = jnp.where(pos_last > CHUNK - 1.0, jnp.exp(last), 0.0)
    return shifted, step, log_decay, cumulative, linked, carry_in, tail, carry


def pair_decay(cumulative, across, pair):
    parts = []
    for head in (2 * pair, 2 * pair + 1):
        spacing = cumulative[:, head : head + 1] - across[head : head + 1, :]
        parts.append(jnp.exp(jnp.minimum(spacing, 0.0)))
    return parts


def forward_kernel(
    inner_ref, step_ref, gate_ref, state_ref, dno_ref, pos_ref, taps_ref, taps_s_ref, head_ref,
    skip_ref, gain_ref, wide_ref,
    scanned_ref, zi_ref, zs_ref, enter_ref, sums_ref,
    halo_i, halo_s, hold,
):
    @pl.when(pl.program_id(0) == 0)
    def _():
        halo_i[...] = jnp.zeros_like(halo_i)
        halo_s[...] = jnp.zeros_like(halo_s)
        hold[...] = jnp.zeros_like(hold)

    low = jnp.bfloat16
    pos = pos_ref[...]
    marks = [(pos >= lag).astype(jnp.float32) for lag in range(4)]

    def conv(ref, halo, taps, out_ref, first):
        value = ref[:, first : first + 128]
        ext = jnp.concatenate([halo[:, first : first + 128], value], axis=0)
        total = taps[4:5, first : first + 128] + marks[0] * (value * taps[0:1, first : first + 128])
        for lag in range(1, 4):
            moved = pltpu.roll(ext, lag, 0)[8:]
            total = total + marks[lag] * (moved * taps[lag : lag + 1, first : first + 128])
        out_ref[:, first : first + 128] = total
        return total * sigmoid(total)

    shifted, step, log_decay, cumulative, linked, carry_in, tail, carry = head_terms(
        step_ref, head_ref, pos
    )
    across = cumulative.T
    wide = dot(
        jnp.concatenate(
            [
                two_term(step),
                two_term(carry_in),
                two_term(tail * step),
                two_term(jnp.broadcast_to(carry, (16, 128))),
            ],
            axis=0,
        ),
        wide_ref[...],
    )
    input_map = conv(state_ref, halo_s, taps_s_ref, zs_ref, 0).astype(low)
    output_map = conv(state_ref, halo_s, taps_s_ref, zs_ref, 128).astype(low)
    scores = jnp.where(linked, dot(output_map, input_map, ((1,), (1,))), 0.0)
    state = hold[...]
    state_low = state.astype(low)
    enter_ref[...] = state_low
    entered = dot(output_map, state_low)
    lane = lax.broadcasted_iota(jnp.int32, (CHUNK, 128), 1)
    squares = jnp.zeros((CHUNK, 128), jnp.float32)
    crosses = jnp.zeros((CHUNK, 128), jnp.float32)
    fed = []
    for pair in range(6):
        cols = slice(pair * 128, pair * 128 + 128)
        act = conv(inner_ref, halo_i, taps_ref, zi_ref, pair * 128)
        stepped = (wide[:CHUNK, cols] * act).astype(low)
        first, second = pair_decay(cumulative, across, pair)
        mixing = jnp.concatenate([(scores * first).astype(low), (scores * second).astype(low)], axis=0)
        both = dot(mixing, stepped)
        within = jnp.where(lane < 64, both[:CHUNK], both[CHUNK:])
        scanned = (
            within + entered[:, cols] * wide[CHUNK : 2 * CHUNK, cols] + skip_ref[0:1, cols] * act
        )
        scanned_ref[:, cols] = scanned
        fed.append((wide[2 * CHUNK : 3 * CHUNK, cols] * act).astype(low))
        gate = gate_ref[:, cols]
        gated = scanned * (gate * sigmoid(gate))
        squares = squares + gated * gated
        crosses = crosses + dno_ref[:, cols] * gain_ref[0:1, cols] * gated
    fresh = dot(input_map, jnp.concatenate(fed, axis=1), ((0,), (0,)))
    hold[...] = wide[3 * CHUNK : 3 * CHUNK + 1, :] * state + fresh
    halo_i[...] = inner_ref[CHUNK - 8 :, :]
    halo_s[...] = state_ref[CHUNK - 8 :, :]
    square = jnp.sum(squares, axis=1, keepdims=True)
    cross = jnp.sum(crosses * marks[0], axis=1, keepdims=True)
    sums_ref[...] = jnp.where(lane == 0, square, cross)


def gate_kernel(
    gate_ref, scanned_ref, dno_ref, sums_ref, twin_ref, gain_ref, pos_ref,
    normed_ref, d_gate_ref, d_scan_ref, g_gain_ref,
):
    @pl.when(pl.program_id(0) == 0)
    def _():
        g_gain_ref[...] = jnp.zeros_like(g_gain_ref)

    low = jnp.bfloat16
    alive = (pos_ref[...] >= 0).astype(jnp.float32)
    sums = sums_ref[...] + twin_ref[...]
    inv = jnp.broadcast_to(lax.rsqrt(sums[:, 0:1] / INNER + EPS), alive.shape)
    pull = inv * inv * inv * jnp.broadcast_to(sums[:, 1:2] / INNER, alive.shape)
    live = inv * alive
    for pair in range(6):
        cols = slice(pair * 128, pair * 128 + 128)
        gain = gain_ref[0:1, cols]
        gate, scanned, d_normed_out = gate_ref[:, cols], scanned_ref[:, cols], dno_ref[:, cols]
        sig = sigmoid(gate)
        gate_act = gate * sig
        gated = scanned * gate_act
        normed_ref[:, cols] = (gated * live * gain).astype(low)
        product = d_normed_out * gated * live
        g_gain_ref[:, cols] += jnp.sum(product.reshape(CHUNK // 8, 8, 128), axis=0)
        d_gated = live * gain * d_normed_out - gated * pull
        d_scan_ref[:, cols] = (d_gated * gate_act).astype(low)
        d_gate_ref[:, cols] = (d_gated * scanned * (sig * (1.0 + gate * (1.0 - sig)))).astype(low)


def gate_stage(first_pre, scanned, d_normed_out, sums, twin_sums, gain, pos):
    rows = first_pre.shape[0]
    at = lambda width: pl.BlockSpec((CHUNK, width), lambda c: (c, 0))
    f32, low = jnp.float32, jnp.bfloat16
    wide = jax.ShapeDtypeStruct((rows, 768), low)
    return pl.pallas_call(
        gate_kernel,
        grid=(rows // CHUNK,),
        in_specs=[
            at(768), at(768), at(768), at(128), at(128), pl.BlockSpec((1, 768), lambda c: (0, 0)), at(128),
        ],
        out_specs=[at(768), at(768), at(768), pl.BlockSpec((8, 768), lambda c: (0, 0))],
        out_shape=[wide, wide, wide, jax.ShapeDtypeStruct((8, 768), f32)],
        compiler_params=pltpu.CompilerParams(vmem_limit_bytes=40 * 2**20),
        cost_estimate=pl.CostEstimate(flops=10**8, bytes_accessed=15 * 10**6, transcendentals=10**6),
        name="gate_stage",
    )(first_pre, scanned, d_normed_out, sums, twin_sums, gain, pos)


def backward_kernel(
    inner_ref, step_ref, state_ref, zi_ref, zs_ref, scanned_ref, dscan_ref, enter_ref, pos_ref,
    taps_ref, taps_s_ref, head_ref, skip_ref, wide_ref, gain_ref, out_part, gate_part,
    d_inner_ref, d_state_ref, d_step_ref, vec_ref, held_out, held_gate,
    g_taps_ref, g_taps_s_ref, g_skip_ref, g_head_ref,
    halo_i, halo_s, halo_p, hold, state_out, state_in, state_send, state_recv, *reducing,
):
    low = jnp.bfloat16
    step_at = pl.program_id(0)
    last_step = pl.num_programs(0) - 1
    core = lax.axis_index("tensor")
    early_reduce((out_part, gate_part), (held_out, held_gate), *reducing)
    chunk = last_step - step_at
    twin = {"tensor": 1 - core}
    here = pl.ds(pl.multiple_of(chunk * CHUNK, CHUNK), CHUNK)

    @pl.when(pl.program_id(0) == 0)
    def _():
        for ref in (halo_i, halo_s, halo_p, hold, g_taps_ref, g_taps_s_ref, g_skip_ref, g_head_ref):
            ref[...] = jnp.zeros_like(ref)

    pos = pos_ref[...]
    pos_ext = jnp.concatenate([pos, halo_p[...]], axis=0)
    marks = [(pos_ext >= lag).astype(jnp.float32) for lag in range(4)]
    lane = lax.broadcasted_iota(jnp.int32, (CHUNK, 128), 1)
    row = lax.broadcasted_iota(jnp.int32, (CHUNK, 128), 0)
    col = lane

    def slope(total):
        sig = sigmoid(total)
        return sig * (1.0 + total * (1.0 - sig)), total * sig

    def fold(value):
        return jnp.sum(value.reshape(CHUNK // 8, 8, 128), axis=0)

    def conv_back(grad, ref, halo, taps, out_ref, g_ref, first):
        cols = slice(first, first + 128)
        ext = jnp.concatenate([grad, halo[:, cols]], axis=0)
        value = ref[:, cols]
        halo[:, cols] = grad[:8]
        g_ref[4, :, cols] += fold(grad)
        total = jnp.zeros((CHUNK, 128), jnp.float32)
        for lag in range(4):
            masked = ext * marks[lag]
            if lag:
                masked = pltpu.roll(masked, CHUNK + 8 - lag, 0)
            masked = masked[:CHUNK]
            g_ref[lag, :, cols] += fold(masked * value)
            total = total + masked * taps[lag : lag + 1, cols]
        if out_ref is not None:
            out_ref[:, cols] = total.astype(low)
        return total

    shifted, step, log_decay, cumulative, linked, carry_in, tail, carry = head_terms(
        step_ref, head_ref, pos
    )
    across = cumulative.T
    wide = dot(
        jnp.concatenate(
            [
                two_term(step),
                two_term(carry_in),
                two_term(tail),
                two_term(jnp.broadcast_to(carry, (16, 128))),
            ],
            axis=0,
        ),
        wide_ref[...],
    )
    slope_b, input_map = slope(zs_ref[:, :128])
    slope_c, output_map = slope(zs_ref[:, 128:])
    input_low, output_low = input_map.astype(low), output_map.astype(low)
    scores = jnp.where(linked, dot(output_low, input_low, ((1,), (1,))), 0.0)
    entering = enter_ref[...]
    d_next = hold[...]
    d_next_low = d_next.astype(low)
    pulled = dot(input_low, d_next_low)
    d_scores = jnp.zeros((CHUNK, 128), jnp.float32)
    d_entered, fed, balance, direct, extra = [], [], [], [], []
    carry_wide = wide[3 * CHUNK : 3 * CHUNK + 1, :]
    carry_grad = jnp.sum(d_next * entering.astype(jnp.float32), axis=0, keepdims=True) * carry_wide
    for pair in range(6):
        cols = slice(pair * 128, pair * 128 + 128)
        slope_x, act = slope(zi_ref[:, cols])
        d_low = dscan_ref[:, cols]
        skip = skip_ref[0:1, cols]
        stepped = (wide[:CHUNK, cols] * act).astype(low)
        stepped_wide = stepped.astype(jnp.float32)
        d_exact = d_low.astype(jnp.float32)
        d_both = jnp.concatenate(
            [jnp.where(lane < 64, d_exact, 0.0).astype(low), jnp.where(lane < 64, 0.0, d_exact).astype(low)],
            axis=0,
        )
        first, second = pair_decay(cumulative, across, pair)
        mixing = jnp.concatenate([(scores * first).astype(low), (scores * second).astype(low)], axis=0)
        d_mixing = dot(d_both, stepped, ((1,), (1,)))
        d_scores = d_scores + d_mixing[:CHUNK] * first + d_mixing[CHUNK:] * second
        tail_cols = wide[2 * CHUNK : 3 * CHUNK, cols]
        tailed = tail_cols * pulled[:, cols]
        d_stepped = dot(mixing, d_both, ((0,), (0,))) + tailed
        extra.append(jnp.sum(stepped_wide * tailed, axis=0, keepdims=True) + carry_grad[:, cols])
        fed.append((tail_cols * stepped_wide).astype(low))
        d_entered.append((wide[CHUNK : 2 * CHUNK, cols] * d_exact).astype(low))
        balance.append(d_exact * (scanned_ref[:, cols] - skip * act) - stepped_wide * d_stepped)
        direct.append(act * d_stepped)
        g_skip_ref[:, cols] += fold(d_exact * act)
        d_act = skip * d_exact + wide[:CHUNK, cols] * d_stepped
        conv_back(d_act * slope_x, inner_ref, halo_i, taps_ref, d_inner_ref, g_taps_ref, pair * 128)
    d_entered = jnp.concatenate(d_entered, axis=1)
    fed = jnp.concatenate(fed, axis=1)
    d_scores = jnp.where(linked, d_scores, 0.0).astype(low)
    d_output = dot(d_scores, input_low) + dot(d_entered, entering, ((1,), (1,)))
    d_input = dot(d_scores, output_low, ((0,), (0,))) + dot(fed, d_next_low, ((1,), (1,)))
    hold[...] = carry_wide * d_next + dot(output_low, d_entered, ((0,), (0,)))
    for_first = conv_back(d_input * slope_b, state_ref, halo_s, taps_s_ref, None, g_taps_s_ref, 0)
    for_second = conv_back(d_output * slope_c, state_ref, halo_s, taps_s_ref, None, g_taps_s_ref, 128)
    state_out[step_at] = jnp.where(core == 0, for_second, for_first).astype(low)
    d_state_ref[here, :] = jnp.where(core == 0, for_first, for_second).astype(low)

    def lend(at):
        return remote(state_out.at[at], state_in.at[at], state_send.at[at], state_recv.at[at], twin)

    lend(step_at).start()
    halo_p[...] = pos[:8]
    spread_back = wide_ref[...]
    extra = jnp.broadcast_to(jnp.concatenate(extra, axis=1), (16, 768))
    stacked = jnp.concatenate(
        split_terms(jnp.concatenate(balance, axis=1), 2)
        + split_terms(jnp.concatenate(direct, axis=1), 2)
        + split_terms(extra, 2),
        axis=0,
    )
    summed = dot(stacked, spread_back, ((1,), (1,)))
    d_sum = summed[:CHUNK] + summed[CHUNK : 2 * CHUNK]
    d_direct = summed[2 * CHUNK : 3 * CHUNK] + summed[3 * CHUNK : 4 * CHUNK]
    d_last = summed[4 * CHUNK : 4 * CHUNK + 1] + summed[4 * CHUNK + 16 : 4 * CHUNK + 17]
    upper = (row <= col).astype(low)
    d_decay = sum(dot(upper, piece) for piece in split_terms(d_sum, 3)) + d_last
    d_step = (d_direct - d_decay * jnp.exp(head_ref[1:2, :])) * sigmoid(shifted)
    d_step = jnp.where(lane < PACK, d_step, 0.0)
    d_step_ref[...] = d_step.astype(low)
    g_head_ref[0] += fold(d_step)
    g_head_ref[1] += fold(d_decay * log_decay)

    @pl.when(step_at == last_step)
    def _():
        vec_ref[...] = jnp.zeros_like(vec_ref)
        total = lambda value: jnp.sum(value, axis=0, keepdims=True)
        for lag in range(5):
            vec_ref[lag : lag + 1, :] = total(g_taps_ref[lag])
            vec_ref[SHARED_ROW + lag : SHARED_ROW + lag + 1, :256] = total(g_taps_s_ref[lag])
        vec_ref[5:6, :] = total(gain_ref[...])
        for at in range(2):
            vec_ref[6 + at : 7 + at, :128] = total(g_head_ref[at])
        skip_row = jnp.broadcast_to(total(g_skip_ref[...]), (16, 768))
        vec_ref[8:9, :128] = sum(
            dot(piece, spread_back, ((1,), (1,))) for piece in split_terms(skip_row, 3)
        )[0:1]
        for at in range(COUNT):
            lend(at).wait()
            rows = pl.ds((COUNT - 1 - at) * CHUNK, CHUNK)
            d_state_ref[rows, :] = (
                d_state_ref[rows, :].astype(jnp.float32) + state_in[at].astype(jnp.float32)
            ).astype(low)


def forward_core(first_pre, second_pre, d_normed_out, pos, taps, taps_s, heads_lanes, skip, gain, wide):
    rows = first_pre.shape[0]
    at = lambda width, col: pl.BlockSpec((CHUNK, width), lambda c: (c, col))
    whole = lambda arr: pl.BlockSpec(arr.shape, lambda c: (0,) * arr.ndim)
    f32 = jnp.float32
    return pl.pallas_call(
        forward_kernel,
        grid=(rows // CHUNK,),
        in_specs=[
            at(768, 0), at(128, 6), at(768, 0), at(256, 3), at(768, 0), at(128, 0),
            whole(taps), whole(taps_s), whole(heads_lanes), whole(skip), whole(gain), whole(wide),
        ],
        out_specs=[at(768, 0), at(768, 0), at(256, 0), at(768, 0), at(128, 0)],
        out_shape=[
            jax.ShapeDtypeStruct((rows, 768), f32),
            jax.ShapeDtypeStruct((rows, 768), f32),
            jax.ShapeDtypeStruct((rows, 256), f32),
            jax.ShapeDtypeStruct((rows, 768), jnp.bfloat16),
            jax.ShapeDtypeStruct((rows, 128), f32),
        ],
        scratch_shapes=[
            pltpu.VMEM((8, 768), f32), pltpu.VMEM((8, 256), f32), pltpu.VMEM((128, 768), f32),
        ],
        compiler_params=pltpu.CompilerParams(vmem_limit_bytes=60 * 2**20),
        cost_estimate=pl.CostEstimate(flops=8 * 10**9, bytes_accessed=24 * 10**6, transcendentals=4 * 10**6),
        name="mixer_forward",
    )(second_pre, second_pre, first_pre, first_pre, d_normed_out, pos, taps, taps_s, heads_lanes, skip, gain, wide)


def backward_core(
    first_pre, second_pre, zi, zs, scanned, d_scan, enter, pos, taps, taps_s, heads_lanes, skip, wide, gain_part, out_part, gate_part
):
    rows = first_pre.shape[0]
    count = rows // CHUNK
    at = lambda width, col: pl.BlockSpec((CHUNK, width), lambda c: (count - 1 - c, col))
    whole = lambda shape: pl.BlockSpec(shape, lambda c: (0,) * len(shape))
    f32, low = jnp.float32, jnp.bfloat16
    return pl.pallas_call(
        backward_kernel,
        grid=(count,),
        in_specs=[
            at(768, 0), at(128, 6), at(256, 3), at(768, 0), at(256, 0), at(768, 0), at(768, 0),
            at(768, 0), at(128, 0),
            whole(taps.shape), whole(taps_s.shape), whole(heads_lanes.shape), whole(skip.shape), whole(wide.shape),
            whole(gain_part.shape), pl.BlockSpec(memory_space=pl.ANY), pl.BlockSpec(memory_space=pl.ANY),
        ],
        out_specs=[
            at(768, 0), whole((rows, 128)), at(128, 0),
            whole((16, 768)),
            whole((4, SHARD, 768)), whole((4, SHARD, 768)),
        ],
        out_shape=[
            jax.ShapeDtypeStruct((rows, 768), low),
            jax.ShapeDtypeStruct((rows, 128), low),
            jax.ShapeDtypeStruct((rows, 128), low),
            jax.ShapeDtypeStruct((16, 768), f32),
            jax.ShapeDtypeStruct((4, SHARD, 768), low),
            jax.ShapeDtypeStruct((4, SHARD, 768), low),
        ],
        scratch_shapes=[
            pltpu.VMEM((5, 8, 768), f32), pltpu.VMEM((5, 8, 256), f32), pltpu.VMEM((8, 768), f32),
            pltpu.VMEM((2, 8, 128), f32),
            pltpu.VMEM((8, 768), f32), pltpu.VMEM((8, 256), f32), pltpu.VMEM((8, 128), f32),
            pltpu.VMEM((128, 768), f32),
            pltpu.VMEM((COUNT, CHUNK, 128), low), pltpu.VMEM((COUNT, CHUNK, 128), low),
            pltpu.SemaphoreType.DMA((COUNT,)), pltpu.SemaphoreType.DMA((COUNT,)),
            pltpu.VMEM((EARLY, 2, 4, 2, SHARD, 384), low),
            pltpu.VMEM((EARLY, 2, 4, 2, SHARD, 384), low),
            pltpu.VMEM((EARLY, 2, 4, 2, SHARD, 384), low),
            pltpu.VMEM((EARLY, 2, 4, SHARD, 384), low),
        ]
        + [pltpu.SemaphoreType.DMA((EARLY, 2))] * 5,
        compiler_params=pltpu.CompilerParams(
            collective_id=3, has_side_effects=True, vmem_limit_bytes=60 * 2**20
        ),
        cost_estimate=pl.CostEstimate(flops=16 * 10**9, bytes_accessed=24 * 10**6, transcendentals=6 * 10**6),
        name="mixer_backward",
    )(
        second_pre, second_pre, first_pre, zi, zs, scanned, d_scan, enter, pos, taps, taps_s, heads_lanes, skip, wide,
        gain_part, out_part.reshape(4, 2, 2, SHARD, 768), gate_part.reshape(4, 2, 2, SHARD, 768),
    )


def swap(value):
    return lax.ppermute(value, "tensor", [(0, 1), (1, 0)])


def pad_cols(value, width):
    return jnp.pad(value, ((0, 0), (0, width - value.shape[1])))


GATHER_PIECES = (
    (1, 0, 384, 0), (1, 384, 512, 1), (0, 0, 512, 0), (0, 512, 512, 1), (2, 0, 384, 0), (2, 384, 384, 1),
)


def gather_kernel(
    gate_ref, state_ref, inner_ref, step_ref, out_ref, stream_ref, cot_ref, gain_ref,
    full_first, full_second, full_out, rows_ref, cots_ref, pre_first, pre_second, pre_out,
    first_ref, second_ref, lanes_ref, held_first, held_second, held_out,
    pre_sem, row_sem, z_send, z_recv, one_send, one_recv, two_send, two_recv,
):
    x, y, z, at_x, at_y, at_z = place()
    core = lax.axis_index("tensor")
    twin = {"tensor": 1 - core}
    low = jnp.bfloat16
    first_ref[:, pl.ds(0, 768)] = gate_ref[...].astype(low)
    first_ref[:, pl.ds(768, 256)] = state_ref[...].astype(low)
    second_ref[:, pl.ds(0, 768)] = inner_ref[...].astype(low)
    lanes_ref[...] = jnp.zeros_like(lanes_ref)
    lanes_ref[:, : step_ref.shape[1]] = step_ref[...]
    lanes = lanes_ref[...]
    second_ref[:, pl.ds(768, 128)] = (lanes + pltpu.roll(lanes, PACK, 1)).astype(low)
    greet([at_x, at_y, twin] + at_z)
    shards = (first_ref, second_ref, out_ref)
    fulls = (full_first, full_second, full_out)
    results = ((held_first, pre_first), (held_second, pre_second), (held_out, pre_out))
    z_copies, ones, twos, copies = {}, {}, {}, []

    def step_zero(piece):
        which, start, width, _ = GATHER_PIECES[piece]
        cols = pl.ds(start, width)
        z_copies[piece] = []
        for step, peer in enumerate(at_z):
            copy = remote(
                shards[which].at[:, cols], fulls[which].at[z, y, x, :, cols],
                z_send.at[piece, step], z_recv.at[piece, step], peer,
            )
            copy.start()
            z_copies[piece].append(copy)

    def step_one(piece):
        which, start, width, route = GATHER_PIECES[piece]
        for copy in z_copies[piece]:
            copy.wait()
        part = fulls[which].at[:, y, x, :, pl.ds(start, width)]
        ones[piece] = remote(part, part, one_send.at[piece], one_recv.at[piece], at_x if route else at_y)
        ones[piece].start()

    def step_two(piece):
        which, start, width, route = GATHER_PIECES[piece]
        cols = pl.ds(start, width)
        ones[piece].wait()
        part = fulls[which].at[:, y, :, :, cols] if route else fulls[which].at[:, :, x, :, cols]
        twos[piece] = remote(part, part, two_send.at[piece], two_recv.at[piece], at_y if route else at_x)
        twos[piece].start()

    def finish(piece):
        which, start, width, _ = GATHER_PIECES[piece]
        cols = pl.ds(start, width)
        twos[piece].wait()
        left = cots_ref if which == 2 else rows_ref
        held, pre = results[which]
        weights = fulls[which]

        def tile(at, carry):
            here = pl.ds(pl.multiple_of(lax.rem(at, 2) * 256, 256), 256)
            there = pl.ds(pl.multiple_of(at * 256, 256), 256)
            held[there, cols] = dot(
                left[lax.div(at, 2), here, :], weights[:, :, :, :, cols].reshape(768, width)
            )
            return carry

        lax.fori_loop(0, 4, tile, 0)
        copy = pltpu.make_async_copy(held.at[:, cols], pre.at[:, cols], pre_sem.at[piece])
        copy.start()
        copies.append(copy)

    step_zero(0)
    for shard, full in zip(shards, fulls):
        full[z, y, x] = shard[...]
    step_zero(1)
    for part in range(4):
        here = pl.ds(part * 128, 128)
        value = stream_ref[here, :]
        inv = lax.rsqrt(jnp.sum(value * value, axis=1, keepdims=True) / D + EPS)
        rows_ref[core, here, :] = (value * inv * gain_ref[...]).astype(jnp.bfloat16)
        cots_ref[core, here, :] = cot_ref[here, :].astype(jnp.bfloat16)
    swaps = []
    for at, ref in enumerate((rows_ref, cots_ref)):
        swaps.append(remote(ref.at[core], ref.at[core], row_sem.at[at], row_sem.at[2 + at], twin))
        swaps[-1].start()
    count = len(GATHER_PIECES)
    for piece in range(count + 1):
        if piece < count:
            step_one(piece)
        if piece + 2 < count:
            step_zero(piece + 2)
        if piece >= 1:
            step_two(piece - 1)
        if piece == 3:
            for copy in swaps:
                copy.wait()
        if piece >= 4:
            finish(piece - 4)
    for piece in range(count - 3, count):
        finish(piece)
    for copy in copies:
        copy.wait()


def gather_all(gate, state, inner, step, out, stream, cotangent, gain):
    f32, low = jnp.float32, jnp.bfloat16
    vmem = pl.BlockSpec(memory_space=pltpu.VMEM)
    count = len(GATHER_PIECES)
    dma = pltpu.SemaphoreType.DMA
    tokens = 2 * stream.shape[0]
    first = jax.ShapeDtypeStruct((SHARD, 1024), low)
    second = jax.ShapeDtypeStruct((SHARD, 896), low)
    full = lambda arr: jax.ShapeDtypeStruct((4, 2, 2) + arr.shape, low)
    rows = jax.ShapeDtypeStruct((2,) + stream.shape, low)
    pre = lambda arr: jax.ShapeDtypeStruct((tokens, arr.shape[1]), f32)
    got = pl.pallas_call(
        gather_kernel,
        in_specs=[vmem] * 8,
        out_specs=[vmem] * 5 + [pl.BlockSpec(memory_space=pl.ANY)] * 3,
        out_shape=[full(first), full(second), full(out), rows, rows, pre(first), pre(second), pre(out)],
        scratch_shapes=[
            pltpu.VMEM(first.shape, low), pltpu.VMEM(second.shape, low), pltpu.VMEM((SHARD, 128), f32),
            pltpu.VMEM((tokens, first.shape[1]), f32),
            pltpu.VMEM((tokens, second.shape[1]), f32),
            pltpu.VMEM((tokens, out.shape[1]), f32),
            dma((count,)), dma((4,)), dma((count, 3)), dma((count, 3)),
            dma((count,)), dma((count,)), dma((count,)), dma((count,)),
        ],
        compiler_params=pltpu.CompilerParams(
            collective_id=0, has_side_effects=True, vmem_limit_bytes=48 * 2**20
        ),
        cost_estimate=pl.CostEstimate(flops=4 * 10**9, bytes_accessed=120 * 10**6, transcendentals=0),
        name="gather_weights",
    )(gate, state, inner, step, out, stream, cotangent, gain)
    return [item.reshape(-1, item.shape[-1]) for item in got]


def reduce_kernel(
    held_out, held_gate, inner_ref, small_ref, vec_ref, moment_ref, gain_ref, *rest,
):
    sources, rest = rest[:10], rest[10:]
    whole_ref, other_ref, grads_ref, total_ref, output_ref, d_stream_ref = rest[:6]
    local, rest = rest[6:16], rest[16:]
    reduce_body(
        held_out, held_gate, inner_ref, small_ref, vec_ref, moment_ref, gain_ref, sources,
        whole_ref, other_ref, grads_ref, total_ref, output_ref, d_stream_ref, local, *rest,
    )


def reduce_body(
    held_out, held_gate, inner_ref, small_ref, vec_ref, moment_ref, gain_ref, sources,
    whole_ref, other_ref, grads_ref, total_ref, output_ref, d_stream_ref, local,
    load_sem, mine_f, lent_b, got_b, vec_own, vec_twin, w_send, w_recv,
    arrived, summed, arrived_two, held_inner, held_small, slots, moments,
    block, back, vec_in, vec_mid, vec_slots,
    m_send, m_recv, one_send, one_recv, two_send, two_recv, z_send, z_recv, g_send, g_recv,
    p_send, p_recv, t_send, t_recv, v_send, v_recv,
):
    f32, low = jnp.float32, jnp.bfloat16
    x, y, z, at_x, at_y, at_z = place()
    core = lax.axis_index("tensor")
    twin = {"tensor": 1 - core}
    greet([at_x, at_y, twin] + at_z)
    parts = (inner_ref, small_ref)
    held = (held_out, held_gate, held_inner, held_small)
    steps_z = [lax.rem(z + step, 4) for step in range(1, 4)]
    span, one, two, add, settle = half_steps(
        parts, at_x, at_y, x, y, arrived, summed, arrived_two, one_send, one_recv, two_send, two_recv
    )

    def to_plane(task):
        plane, width = PLANE_OF[PLAN[task][0]], PLAN[task][1]

        @pl.when(z != plane)
        def _():
            remote(
                held[task], slots.at[z, :, :, pl.ds(0, width)], z_send.at[task], z_recv.at[z],
                {"dp": plane * 4 + y * 2 + x},
            ).start()

    for task in range(2):
        for route in range(2):
            one(task, route).start()
    to_plane(0)
    to_plane(1)
    moment_copies = []
    for step, (peer, plane) in enumerate(zip(at_z, steps_z)):
        copy = remote(moment_ref.at[plane], moments.at[z], m_send.at[step], m_recv.at[step], peer)
        copy.start()
        moment_copies.append(copy)
    loads = [pltpu.make_async_copy(src, dst, load_sem.at[at]) for at, (src, dst) in enumerate(zip(sources, local))]
    for copy in loads:
        copy.start()
    d_gate, d_inner, d_state, d_step, normed, w_first, w_second, w_out, stream_ref, cot_ref = local
    half_rows = stream_ref.shape[0]
    turned = ((1,), (1,))
    state_cols = pl.ds(pl.multiple_of(768 + core * 128, 128), 128)

    def product(which, rows):
        if which == 1:
            return dot(normed[rows, :], w_out[...], turned)
        first = dot(d_gate[rows, :], w_first[:, pl.ds(0, 768)], turned)
        second = dot(d_inner[rows, :], w_second[:, pl.ds(0, 768)], turned)
        third = dot(d_state[rows, :], w_first[:, state_cols], turned)
        return first + second + third + dot(d_step[rows, :], w_second[:, pl.ds(768, 128)], turned)

    for copy in loads:
        copy.wait()

    def products(who, store):
        for which in range(2):

            def tile(at, carry):
                rows = pl.ds(pl.multiple_of(who * half_rows + at * 256, 256), 256)
                store(which, pl.ds(pl.multiple_of(at * 256, 256), 256), product(which, rows))
                return carry

            lax.fori_loop(0, half_rows // 256, tile, 0)

    def store_lent(which, rows, value):
        lent_b[which, rows, :] = value.astype(low)

    def store_mine(which, rows, value):
        mine_f[which, rows, :] = value

    products(1 - core, store_lent)
    lends = []
    for which in range(2):
        lends.append(remote(lent_b.at[which], got_b.at[which], w_send.at[which], w_recv.at[which], twin))
        lends[-1].start()
    for task in range(2):
        for route in range(2):
            cols = span(task, route)[0]
            one(task, route).wait()
            add(task, route, parts[task][:, y, :, :, cols] if route else parts[task][:, :, x, :, cols])
            two(task, route).start()
    products(core, store_mine)
    for task in range(2):
        for route in range(2):
            two(task, route).wait()
            settle(task, route, held[2 + task])
        to_plane(2 + task)
    for copy in lends:
        copy.wait()
    grad_norm = jnp.zeros((1, 768), f32)
    gain = gain_ref[...]
    for part in range(half_rows // 128):
        rows = pl.ds(part * 128, 128)
        value = stream_ref[rows, :]
        output_ref[rows, :] = value + (mine_f[1, rows, :] + got_b[1, rows, :].astype(f32))
        inv = lax.rsqrt(jnp.sum(value * value, axis=1, keepdims=True) / D + EPS)
        d_normed = mine_f[0, rows, :] + got_b[0, rows, :].astype(f32)
        scaled = value * inv
        grad_norm = grad_norm + jnp.sum(d_normed * scaled, axis=0, keepdims=True)
        weighted = d_normed * gain
        inner = jnp.sum(weighted * scaled, axis=1, keepdims=True) / D
        d_stream_ref[rows, :] = cot_ref[rows, :] + inv * (weighted - scaled * inner)
    vec_rows = lax.broadcasted_iota(jnp.int32, vec_ref.shape, 0)
    vec_own[...] = jnp.where(vec_rows == NORM_ROW, grad_norm, vec_ref[...])
    vec_x = remote(vec_own, vec_in.at[0], v_send.at[0], v_recv.at[0], at_x)
    vec_x.start()
    vec_x.wait()
    vec_mid[0] = vec_own[...] + vec_in[0]
    vec_y = remote(vec_mid.at[0], vec_in.at[1], v_send.at[1], v_recv.at[1], at_y)
    vec_y.start()
    for copy in moment_copies:
        copy.wait()
    moments[z] = moment_ref[z]
    vec_y.wait()
    vec_mid[1] = vec_mid[0] + vec_in[1]
    vec_slots[z] = vec_mid[1]
    vec_z = []
    for step, peer in enumerate(at_z):
        copy = remote(vec_mid.at[1], vec_slots.at[z], v_send.at[2 + step], v_recv.at[2 + step], peer)
        copy.start()
        vec_z.append(copy)

    for task, (name, width) in enumerate(PLAN):
        plane = PLANE_OF[name]
        cols = pl.ds(0, width)

        @pl.when(z == plane)
        def _():
            for source in range(4):
                if source != plane:
                    remote(
                        held[task], slots.at[source, :, :, cols], z_send.at[task], z_recv.at[source], at_x
                    ).wait_recv()
            total = held[task][...].astype(f32)
            for source in range(4):
                if source != plane:
                    total = total + slots[source, :, :, cols].astype(f32)
            if width < 768:
                back[...] = jnp.zeros_like(back)
                block[...] = jnp.zeros_like(block)
            back[:, :, cols] = total.astype(low)
            block[:, :, cols] = (MU_MAT * moments[:, :, cols].astype(f32) + total).astype(low)

    half = 384
    routes = (pl.ds(0, half), pl.ds(half, half))
    for row in range(4):
        whole_ref[row, y, x] = block[row]
    plane_one = []
    for route, peer in enumerate((at_x, at_y)):
        copy = remote(
            block.at[:, :, routes[route]], whole_ref.at[:, y, x, :, routes[route]],
            p_send.at[0, route], p_recv.at[0, route], peer,
        )
        copy.start()
        plane_one.append(copy)
    twin_own = remote(block, other_ref.at[:, y, x], t_send.at[0], t_recv.at[0], twin)
    twin_own.start()
    grads_ref[z] = back[z]
    returns = []
    for step, (peer, plane) in enumerate(zip(at_z, steps_z)):
        copy = remote(back.at[plane], grads_ref.at[z], g_send.at[step], g_recv.at[step], peer)
        copy.start()
        returns.append(copy)
    plane_two = []
    for route, peer in enumerate((at_y, at_x)):
        plane_one[route].wait()
        part = (
            whole_ref.at[:, :, x, :, routes[1]] if route else whole_ref.at[:, y, :, :, routes[0]]
        )
        copy = remote(part, part, p_send.at[1, route], p_recv.at[1, route], peer)
        copy.start()
        plane_two.append(copy)
    twins = [twin_own]
    for route in range(2):
        src = whole_ref.at[:, 1 - y, x, :, routes[1]] if route else whole_ref.at[:, y, 1 - x, :, routes[0]]
        dst = other_ref.at[:, 1 - y, x, :, routes[1]] if route else other_ref.at[:, y, 1 - x, :, routes[0]]
        copy = remote(src, dst, t_send.at[1 + route], t_recv.at[1 + route], twin)
        copy.start()
        twins.append(copy)
    for route in range(2):
        plane_two[route].wait()
        src = whole_ref.at[:, :, 1 - x, :, routes[1]] if route else whole_ref.at[:, 1 - y, :, :, routes[0]]
        dst = other_ref.at[:, :, 1 - x, :, routes[1]] if route else other_ref.at[:, 1 - y, :, :, routes[0]]
        copy = remote(src, dst, t_send.at[3 + route], t_recv.at[3 + route], twin)
        copy.start()
        twins.append(copy)
    for copy in vec_z:
        copy.wait()
    vec_mid[0] = (vec_slots[0] + vec_slots[1]) + (vec_slots[2] + vec_slots[3])
    vec_swap = remote(vec_mid.at[0], vec_twin, w_send.at[2], w_recv.at[2], twin)
    vec_swap.start()
    for copy in twins + returns:
        copy.wait()
    vec_swap.wait()
    total_ref[...] = vec_mid[0] + jnp.where(vec_rows >= SHARED_ROW, vec_twin[...], 0.0)
    for task, (name, width) in enumerate(PLAN):
        plane = PLANE_OF[name]

        @pl.when(z != plane)
        def _():
            remote(
                held[task], slots.at[z, :, :, pl.ds(0, width)], z_send.at[task], z_recv.at[z],
                {"dp": plane * 4 + y * 2 + x},
            ).wait_send()


def reduce_all(held, parts, vectors, moments, gain, sources):
    f32, low = jnp.float32, jnp.bfloat16
    vmem = pl.BlockSpec(memory_space=pltpu.VMEM)
    dma = pltpu.SemaphoreType.DMA
    parts = [part.reshape(4, 2, 2, SHARD, part.shape[1]) for part in parts]
    buf = pltpu.VMEM
    tokens = sources[-1].shape
    whole, other, grads, total, output, d_stream = pl.pallas_call(
        reduce_kernel,
        in_specs=[vmem] * 7 + [pl.BlockSpec(memory_space=pl.ANY)] * len(sources),
        out_specs=[vmem] * 6,
        out_shape=[
            jax.ShapeDtypeStruct((4, 2, 2, SHARD, 768), low),
            jax.ShapeDtypeStruct((4, 2, 2, SHARD, 768), low),
            jax.ShapeDtypeStruct((4, SHARD, 768), low),
            jax.ShapeDtypeStruct(vectors.shape, f32),
            jax.ShapeDtypeStruct(tokens, f32),
            jax.ShapeDtypeStruct(tokens, f32),
        ],
        scratch_shapes=[buf(item.shape, item.dtype) for item in sources]
        + [
            dma((len(sources),)), buf((2,) + tokens, f32), buf((2,) + tokens, low), buf((2,) + tokens, low),
            buf(vectors.shape, f32), buf(vectors.shape, f32), dma((3,)), dma((3,)),
            buf((2, 2, 4, 2, SHARD, 384), low), buf((2, 2, 4, 2, SHARD, 384), low),
            buf((2, 2, 4, SHARD, 384), low),
            buf((4, SHARD, 768), low), buf((4, SHARD, 256), low),
            buf((4, 4, SHARD, 768), low), buf((4, SHARD, 768), low),
            buf((4, SHARD, 768), low), buf((4, SHARD, 768), low),
            buf((2,) + vectors.shape, f32), buf((2,) + vectors.shape, f32), buf((4,) + vectors.shape, f32),
            dma((3,)), dma((3,)), dma((2, 2)), dma((2, 2)), dma((2, 2)), dma((2, 2)),
            dma((4,)), dma((4,)), dma((3,)), dma((3,)), dma((2, 2)), dma((2, 2)),
            dma((5,)), dma((5,)), dma((5,)), dma((5,)),
        ],
        compiler_params=pltpu.CompilerParams(
            collective_id=1, has_side_effects=True, vmem_limit_bytes=60 * 2**20
        ),
        cost_estimate=pl.CostEstimate(flops=0, bytes_accessed=150 * 10**6, transcendentals=0),
        name="reduce_grads",
    )(*held, *parts, vectors, moments, gain, *sources)
    return whole.reshape(768, 768), other.reshape(768, 768), grads, total, output, d_stream


def newton_kernel(own_ref, other_ref, mask_ref, half_ref, lent_ref, full_ref, current, gram, mix):
    f32, low = jnp.float32, jnp.bfloat16
    rows, cols = current.shape
    tile = 256
    count = rows // tile
    row_ids = lax.broadcasted_iota(jnp.int32, (tile, tile), 0)
    col_ids = lax.broadcasted_iota(jnp.int32, (tile, tile), 1)
    blocks = [pl.ds(at * tile, tile) for at in range(count)]

    wide = own_ref.shape[1]
    for at in range(count):
        for ref, start in ((own_ref, 0), (other_ref, wide)):
            cut = pl.ds(start, wide)
            full_ref[blocks[at], cut] = (ref[blocks[at], :].astype(f32) * mask_ref[:, cut]).astype(low)

    def symmetric(source, store):
        for second in range(count):
            column = dot(source[pl.ds(0, (second + 1) * tile), :], source[blocks[second], :], ((1,), (1,)))
            for first in range(second + 1):
                store(first, second, column[first * tile : (first + 1) * tile])

    def put(ref, first, second, value):
        ref[blocks[first], blocks[second]] = value.astype(low)
        if first != second:
            ref[blocks[second], blocks[first]] = value.T.astype(low)

    firsts = {}
    symmetric(full_ref, lambda first, second, value: firsts.update({(first, second): value}))
    trace = sum(
        jnp.sum(jnp.where(row_ids == col_ids, firsts[at, at], 0.0), keepdims=True) for at in range(count)
    )
    scale = jnp.sqrt(trace) + 1e-07
    inverse, inverse_square = 1.0 / scale, 1.0 / (scale * scale)
    for (first, second), value in firsts.items():
        put(gram, first, second, value * inverse_square)
    for at in range(count):
        current[blocks[at], :] = (full_ref[blocks[at], :].astype(f32) * inverse).astype(low)

    def mixed():
        def store(first, second, value):
            piece = gram[blocks[first], blocks[second]].astype(f32)
            put(mix, first, second, NS_B * piece + NS_C * value)

        symmetric(gram, store)

    def turn(_, carry):
        mixed()

        def update(at, carry):
            here = pl.ds(pl.multiple_of(at * tile, tile), tile)
            held = current[:, here]
            current[:, here] = (NS_A * held.astype(f32) + dot(mix[...], held)).astype(low)
            return carry

        lax.fori_loop(0, cols // tile, update, 0)
        symmetric(current, lambda first, second, value: put(gram, first, second, value))
        return carry

    lax.fori_loop(0, NS_STEPS - 1, turn, 0)
    mixed()
    for at in range(wide // tile + 1):
        here = pl.ds(at * tile, tile)
        held = current[:, here]
        value = (NS_A * held.astype(f32) + dot(mix[...], held)).astype(low)
        if at < wide // tile:
            half_ref[:, here] = value
        else:
            lent_ref[...] = value


def newton(own, other, mask):
    low = jnp.bfloat16
    rows, width = own.shape
    vmem = pl.BlockSpec(memory_space=pltpu.VMEM)
    whole = pltpu.VMEM((rows, 2 * width), low)
    return pl.pallas_call(
        newton_kernel,
        in_specs=[vmem] * 3,
        out_specs=[vmem] * 2,
        out_shape=[jax.ShapeDtypeStruct((rows, width), low), jax.ShapeDtypeStruct((rows, 256), low)],
        scratch_shapes=[whole, whole, pltpu.VMEM((rows, rows), low), pltpu.VMEM((rows, rows), low)],
        compiler_params=pltpu.CompilerParams(vmem_limit_bytes=40 * 2**20),
        cost_estimate=pl.CostEstimate(flops=20 * 10**9, bytes_accessed=4 * 10**6, transcendentals=0),
        name="newton_schulz",
    )(own, other, mask)


def return_kernel(done_ref, lent_ref, back_ref, ready, send, recv):
    x, y, z, _, _, at_z = place()
    greet(at_z)
    small = (z == PLANE_OF["small"]).astype(jnp.float32)
    edge = lent_ref.shape[-1]
    for plane in range(4):
        ready[plane] = done_ref[plane, y, x]
        lent = lent_ref[plane, y, x].astype(jnp.float32) * small
        ready[plane, :, pl.ds(0, edge)] = (
            done_ref[plane, y, x, :, pl.ds(0, edge)].astype(jnp.float32) + lent
        ).astype(ready.dtype)
    copies = []
    for step, peer in enumerate(at_z):
        plane = lax.rem(z + step + 1, 4)
        copies.append(
            remote(ready.at[plane], back_ref.at[z], send.at[step], recv.at[step], peer)
        )
        copies[-1].start()
    back_ref[z] = ready[z]
    for copy in copies:
        copy.wait()


def return_rows(done, lent):
    vmem = pl.BlockSpec(memory_space=pltpu.VMEM)
    dma = pltpu.SemaphoreType.DMA
    return pl.pallas_call(
        return_kernel,
        in_specs=[vmem] * 2,
        out_specs=vmem,
        out_shape=jax.ShapeDtypeStruct((4, SHARD, 768), done.dtype),
        scratch_shapes=[pltpu.VMEM((4, SHARD, 768), done.dtype), dma((3,)), dma((3,))],
        compiler_params=pltpu.CompilerParams(collective_id=2, has_side_effects=True, vmem_limit_bytes=16 * 2**20),
        cost_estimate=pl.CostEstimate(flops=0, bytes_accessed=20 * 10**6, transcendentals=0),
        name="return_rows",
    )(done.reshape(4, 2, 2, SHARD, 768), lent.reshape(4, 2, 2, SHARD, lent.shape[1]))


def orthogonal_owned(own, other, state_width):
    width = own.shape[1]
    small = lax.axis_index("dp") // 4 == PLANE_OF["small"]
    col = jnp.arange(2 * width)[None, :] % width
    keep = (col < state_width) == (lax.axis_index("tensor") == 0)
    half, lent = newton(own, other, (keep | ~small).astype(jnp.float32))
    return half, swap(lent)


def paired_shards(
    stream,
    cotangent,
    positions,
    norm_gain,
    w_gate,
    w_inner,
    w_state,
    w_step,
    conv_inner,
    conv_state,
    head_params,
    gate_gain,
    w_out,
    moment_norm_gain,
    moment_w_gate,
    moment_w_inner,
    moment_w_state,
    moment_w_step,
    moment_conv_inner,
    moment_conv_state,
    moment_head_params,
    moment_gate_gain,
    moment_w_out,
):
    low = jnp.bfloat16
    core = lax.axis_index("tensor")
    room = w_gate.shape[1]
    wide = w_state.shape[1]
    col_width = wide // 2
    heads = w_step.shape[1]
    full_first, full_second, full_out, token_rows, cotangent_rows, first_pre, second_pre, d_normed_out = gather_all(
        w_gate, w_state, w_inner, w_step, w_out.astype(low).T, stream, cotangent, norm_gain[None, :]
    )
    pos = jnp.broadcast_to(positions.astype(jnp.float32)[:, None], (positions.shape[0], 128))
    taps = jnp.pad(conv_inner, ((0, 3), (0, 0)))
    taps_s = jnp.pad(conv_state, ((0, 3), (0, 0)))
    lanes = jnp.concatenate([pad_cols(head_params, PACK), pad_cols(head_params, 128 - PACK)], axis=1)
    lanes = jnp.pad(lanes, ((0, 5), (0, 0)))
    skip = jnp.repeat(head_params[2], room // heads)[None, :]
    wide_map = expand_matrix()
    scanned, zi, zs, enter, sums = forward_core(
        first_pre, second_pre, d_normed_out, pos, taps, taps_s, lanes, skip, gate_gain[None, :], wide_map
    )
    normed_out, d_gate_pre, d_scan, gain_part = gate_stage(
        first_pre, scanned, d_normed_out, sums, swap(sums), gate_gain[None, :], pos
    )
    out_part = contract_rows(cotangent_rows, normed_out).astype(low)
    gate_part = contract_rows(token_rows, d_gate_pre).astype(low)
    d_inner, d_state_low, d_step, vectors, held_out, held_gate = backward_core(
        first_pre, second_pre, zi, zs, scanned, d_scan, enter, pos, taps, taps_s, lanes, skip, wide_map, gain_part, out_part, gate_part
    )
    col_first = core * col_width
    inner_part = contract_rows(token_rows, d_inner).astype(low)
    small_part = contract_rows(token_rows, jnp.concatenate([d_state_low, d_step], axis=1)).astype(low)
    small_moment = pad_cols(jnp.concatenate([moment_w_state, moment_w_step], axis=1), room)
    moment_rows = jnp.stack([moment_w_out.T, moment_w_inner, moment_w_gate, small_moment]).astype(low)
    own, other, grads, vectors, output, d_stream = reduce_all(
        (held_out, held_gate), (inner_part, small_part), vectors, moment_rows, norm_gain[None, :],
        (
            d_gate_pre, d_inner, d_state_low, d_step, normed_out, full_first, full_second, full_out,
            stream, cotangent,
        ),
    )
    grads = grads.astype(jnp.float32)
    grad_gate_w = grads[2]
    grad_inner_w = grads[1]
    grad_out_w = grads[0].T
    grad_state_w = grads[3][:, :col_width]
    grad_step_w = grads[3][:, col_width : col_width + heads]
    grad_conv_inner = vectors[:5]
    grad_gate_gain = vectors[5]
    grad_head = vectors[6:9, :heads]
    grad_conv_state = vectors[9:14, :wide]
    grad_norm = vectors[NORM_ROW]
    m_gate = MU_MAT * moment_w_gate + grad_gate_w
    m_inner = MU_MAT * moment_w_inner + grad_inner_w
    m_state = MU_MAT * moment_w_state + grad_state_w
    m_step = MU_MAT * moment_w_step + grad_step_w
    m_out = MU_MAT * moment_w_out + grad_out_w
    mine = return_rows(*orthogonal_owned(own, other, col_width)).astype(jnp.float32)
    new_gate = w_gate - LR_MAT * spread(D, INNER) * mine[2]
    new_inner = w_inner - LR_MAT * spread(D, INNER) * mine[1]
    new_out = w_out - LR_MAT * spread(INNER, D) * mine[0].T
    new_step = w_step - LR_MAT * spread(D, HEADS) * mine[3][:, col_width : col_width + heads]
    state_slice = lax.dynamic_slice_in_dim(w_state, col_first, col_width, 1)
    new_state = state_slice - LR_MAT * spread(D, 2 * STATE) * mine[3][:, :col_width]
    m_norm = MU_VEC * moment_norm_gain + grad_norm
    m_conv_inner = MU_VEC * moment_conv_inner + grad_conv_inner
    m_conv_state = MU_VEC * moment_conv_state + grad_conv_state
    m_head = MU_VEC * moment_head_params + grad_head
    m_gate_gain = MU_VEC * moment_gate_gain + grad_gate_gain
    return (
        output,
        d_stream,
        grad_norm,
        grad_gate_w,
        grad_inner_w,
        grad_state_w,
        grad_step_w,
        grad_conv_inner,
        grad_conv_state,
        grad_head,
        grad_gate_gain,
        grad_out_w,
        norm_gain - LR_VEC * m_norm,
        new_gate,
        new_inner,
        new_state,
        new_step,
        conv_inner - LR_VEC * m_conv_inner,
        conv_state - LR_VEC * m_conv_state,
        head_params - LR_VEC * m_head,
        gate_gain - LR_VEC * m_gate_gain,
        new_out,
        m_norm,
        m_gate,
        m_inner,
        m_state,
        m_step,
        m_conv_inner,
        m_conv_state,
        m_head,
        m_gate_gain,
        m_out,
    )


def solution(mesh):
    paired = mesh.shape["dp"] == 16 and mesh.shape["tensor"] == 2
    return jax.shard_map(
        paired_shards if paired else shards,
        mesh=mesh,
        in_specs=(
            P(("dp", "tensor"), None),
            P(("dp", "tensor"), None),
            P("dp"),
            P(),
            P("dp", "tensor"),
            P("dp", "tensor"),
            P("dp", None),
            P("dp", "tensor"),
            P(None, "tensor"),
            P(),
            P(None, "tensor"),
            P("tensor"),
            P("tensor", "dp"),
            P(),
            P("dp", "tensor"),
            P("dp", "tensor"),
            P("dp", "tensor"),
            P("dp", "tensor"),
            P(None, "tensor"),
            P(),
            P(None, "tensor"),
            P("tensor"),
            P("tensor", "dp"),
        ),
        out_specs=(
            P(("dp", "tensor"), None),
            P(("dp", "tensor"), None),
            P(),
            P("dp", "tensor"),
            P("dp", "tensor"),
            P("dp", "tensor"),
            P("dp", "tensor"),
            P(None, "tensor"),
            P(),
            P(None, "tensor"),
            P("tensor"),
            P("tensor", "dp"),
            P(),
            P("dp", "tensor"),
            P("dp", "tensor"),
            P("dp", "tensor"),
            P("dp", "tensor"),
            P(None, "tensor"),
            P(),
            P(None, "tensor"),
            P("tensor"),
            P("tensor", "dp"),
            P(),
            P("dp", "tensor"),
            P("dp", "tensor"),
            P("dp", "tensor"),
            P("dp", "tensor"),
            P(None, "tensor"),
            P(),
            P(None, "tensor"),
            P("tensor"),
            P("tensor", "dp"),
        ),
        check_vma=False,
    )
```

```python
from functools import partial
import math

import jax
import jax.numpy as jnp
from jax import lax
from jax.experimental import pallas as pl
from jax.experimental.pallas import tpu as pltpu
from jax.sharding import PartitionSpec as P

D = 768
INNER = 1536
HEADS = 24
STATE = 128
BLOCK = 256
NS_STEPS = 5


EPS = 1e-05
NS_A = 3.4445
NS_B = -4.775
NS_C = 2.0315
MU_MAT = 0.95
MU_VEC = 0.9
LR_MAT = 0.3
LR_VEC = 0.001
HIGH = lax.Precision.HIGHEST
CORE = lax.Precision.DEFAULT


def silu_slope(value):
    sig = jax.nn.sigmoid(value)
    return sig * (1.0 + value * (1.0 - sig))


def contract_rows(left, right):
    return lax.dot_general(
        left, right, (((0,), (0,)), ((), ())), preferred_element_type=jnp.float32
    )


def times_transpose(left, right):
    return lax.dot_general(
        left, right, (((1,), (1,)), ((), ())), preferred_element_type=jnp.float32
    )


def causal_conv(signal, taps, positions):
    length = signal.shape[0]
    reach = taps.shape[0] - 1
    total = jnp.zeros_like(signal) + taps[reach]
    for lag_step in range(reach):
        moved = jnp.pad(signal, ((lag_step, 0), (0, 0)))[:length]
        total = total + jnp.where((positions >= lag_step)[:, None], moved * taps[lag_step], 0.0)
    return jax.nn.silu(total)


def mixer_core(inner_pre, state_pre, step_pre, conv_inner, conv_state, head_params, positions, precision=HIGH):
    length = inner_pre.shape[0]
    heads = step_pre.shape[1]
    head_size = inner_pre.shape[1] // heads
    states = state_pre.shape[1] // 2
    blocks = length // BLOCK
    inner_act = causal_conv(inner_pre, conv_inner, positions).reshape(
        blocks, BLOCK, heads, head_size
    )
    state_act = causal_conv(state_pre, conv_state, positions)
    input_map = state_act[:, :states].reshape(blocks, BLOCK, states)
    output_map = state_act[:, states:].reshape(blocks, BLOCK, states)
    step_size = jax.nn.softplus(step_pre + head_params[0])
    log_decay = (step_size * -jnp.exp(head_params[1])).reshape(blocks, BLOCK, heads)
    step_size = step_size.reshape(blocks, BLOCK, heads)
    resets = (positions <= 0).astype(jnp.float32).reshape(blocks, BLOCK)
    order = jnp.arange(BLOCK)
    lower = (order[:, None] >= order[None, :]).astype(jnp.float32)
    cumulative = jnp.einsum("ij,cjh->cih", lower, log_decay, precision=HIGH)
    seen = jnp.einsum("ij,cj->ci", lower, resets, precision=HIGH)
    linked = (seen[:, :, None] == seen[:, None, :]) & (order[:, None] >= order[None, :])[None]
    linked_heads = linked[..., None]
    spacing = cumulative[:, :, None, :] - cumulative[:, None, :, :]
    decay = jnp.where(linked_heads, jnp.exp(jnp.where(linked_heads, spacing, 0.0)), 0.0)
    scores = jnp.einsum("cin,cjn->cij", output_map, input_map, precision=precision)
    mixing = scores[..., None] * decay * step_size[:, None, :, :]
    within = jnp.einsum("cijh,cjhp->cihp", mixing, inner_act, precision=precision)
    tail_linked = (seen[:, -1:] == seen)[..., None]
    tail = (
        jnp.where(
            tail_linked,
            jnp.exp(jnp.where(tail_linked, cumulative[:, -1:, :] - cumulative, 0.0)),
            0.0,
        )
        * step_size
    )
    own_state = jnp.einsum("cjh,cjhp,cjn->chpn", tail, inner_act, input_map, precision=precision)
    carry_rate = jnp.exp(cumulative[:, -1, :]) * (seen[:, -1] == 0).astype(jnp.float32)[:, None]

    state = jnp.zeros((heads, head_size, states), jnp.float32)
    entering = []
    for block in range(blocks):
        entering.append(state)
        state = carry_rate[block][:, None, None] * state + own_state[block]
    entering = jnp.stack(entering)
    fresh = (seen == 0)[..., None]
    carry_in = jnp.where(fresh, jnp.exp(cumulative), 0.0)
    across = (
        jnp.einsum("cin,chpn->cihp", output_map, entering, precision=precision) * carry_in[..., None]
    )
    result = within + across + head_params[2][None, None, :, None] * inner_act
    return result.reshape(length, heads * head_size)


def gram_total(low):
    return lax.psum(
        jnp.dot(low, low.T, preferred_element_type=jnp.float32).astype(jnp.bfloat16), "tensor"
    ).astype(jnp.float32)


def orthogonalize(matrix):
    first = gram_total(matrix.astype(jnp.bfloat16))
    scale = jnp.sqrt(jnp.trace(first)) + 1e-07
    current = (matrix / scale).astype(jnp.bfloat16)
    gram = (first / (scale * scale)).astype(jnp.bfloat16)
    for turn in range(NS_STEPS):
        if turn > 0:
            gram = gram_total(current).astype(jnp.bfloat16)
        applied = jnp.dot(gram, current, preferred_element_type=jnp.float32)
        twice = jnp.dot(gram, applied.astype(jnp.bfloat16), preferred_element_type=jnp.float32)
        current = (NS_A * current.astype(jnp.float32) + NS_B * applied + NS_C * twice).astype(
            jnp.bfloat16
        )
    return current.astype(jnp.float32)


def spread(rows, cols):
    return math.sqrt(max(1.0, rows / cols))


def shards(
    stream,
    cotangent,
    positions,
    norm_gain,
    w_gate,
    w_inner,
    w_state,
    w_step,
    conv_inner,
    conv_state,
    head_params,
    gate_gain,
    w_out,
    moment_norm_gain,
    moment_w_gate,
    moment_w_inner,
    moment_w_state,
    moment_w_step,
    moment_conv_inner,
    moment_conv_state,
    moment_head_params,
    moment_gate_gain,
    moment_w_out,
):
    dp_count = lax.axis_size("dp")
    inv_first = lax.rsqrt(jnp.mean(stream * stream, axis=1, keepdims=True) + EPS)
    normed = (stream * inv_first * norm_gain).astype(jnp.bfloat16)
    token_rows, cotangent_rows = (
        lax.all_gather(normed, "tensor", axis=0, tiled=True),
        lax.all_gather(cotangent.astype(jnp.bfloat16), "tensor", axis=0, tiled=True),
    )
    local_weights = (
        w_gate.astype(jnp.bfloat16),
        w_inner.astype(jnp.bfloat16),
        w_step.astype(jnp.bfloat16),
        w_state.astype(jnp.bfloat16),
        w_out.astype(jnp.bfloat16),
    )
    full_gate, full_inner, full_step, full_state, full_out = (
        lax.all_gather(local_weights[0], "dp", axis=0, tiled=True),
        lax.all_gather(local_weights[1], "dp", axis=0, tiled=True),
        lax.all_gather(local_weights[2], "dp", axis=0, tiled=True),
        lax.all_gather(local_weights[3], "dp", axis=0, tiled=True),
        lax.all_gather(local_weights[4], "dp", axis=1, tiled=True),
    )
    gate_pre = jnp.dot(token_rows, full_gate, preferred_element_type=jnp.float32)
    inner_pre = jnp.dot(token_rows, full_inner, preferred_element_type=jnp.float32)
    state_pre = jnp.dot(token_rows, full_state, preferred_element_type=jnp.float32)
    step_pre = jnp.dot(token_rows, full_step, preferred_element_type=jnp.float32)
    alive = (positions >= 0).astype(jnp.float32)[:, None]
    scanned, core_back = jax.vjp(
        partial(mixer_core, positions=positions),
        inner_pre,
        state_pre,
        step_pre,
        conv_inner,
        conv_state,
        head_params,
    )
    gate_act = jax.nn.silu(gate_pre)
    gated = scanned * gate_act
    square_sum = lax.psum(jnp.sum(gated * gated, axis=1), "tensor")
    inv_second = lax.rsqrt(square_sum / INNER + EPS)[:, None]
    normed_out = (gated * inv_second * gate_gain * alive).astype(jnp.bfloat16)
    mixed = lax.psum_scatter(
        jnp.dot(normed_out, full_out, preferred_element_type=jnp.float32).astype(jnp.bfloat16),
        "tensor",
        scatter_dimension=0,
        tiled=True,
    ).astype(jnp.float32)
    output = stream + mixed
    d_normed_out = times_transpose(cotangent_rows, full_out)
    grad_out_part = contract_rows(normed_out, cotangent_rows)
    scaled = d_normed_out * gate_gain * alive
    grad_gate_part = jnp.sum(d_normed_out * gated * inv_second * alive, axis=0)
    cross_sum = lax.psum(jnp.sum(scaled * gated, axis=1), "tensor")
    d_gated = inv_second * scaled - gated * inv_second**3 * (cross_sum / INNER)[:, None]
    d_gate_pre = (d_gated * scanned * silu_slope(gate_pre)).astype(jnp.bfloat16)
    d_inner, d_state_part, d_step, grad_conv_inner_part, grad_conv_state_part, grad_head_part = (
        core_back(d_gated * gate_act)
    )
    d_state_cols = lax.psum_scatter(
        d_state_part.astype(jnp.bfloat16), "tensor", scatter_dimension=1, tiled=True
    ).astype(jnp.float32)
    d_inner_low = d_inner.astype(jnp.bfloat16)
    d_state_low = d_state_cols.astype(jnp.bfloat16)
    d_step_low = d_step.astype(jnp.bfloat16)
    col_width = d_state_cols.shape[1]
    col_first = lax.axis_index("tensor") * col_width
    state_cols = lax.dynamic_slice_in_dim(full_state, col_first, col_width, 1)
    total = times_transpose(d_gate_pre, full_gate)
    total = total + times_transpose(d_inner_low, full_inner)
    total = total + times_transpose(d_state_low, state_cols)
    d_normed = lax.psum_scatter(
        (total + times_transpose(d_step_low, full_step)).astype(jnp.bfloat16),
        "tensor",
        scatter_dimension=0,
        tiled=True,
    ).astype(jnp.float32)
    grad_gate_w, grad_inner_w, grad_state_w, grad_step_w, grad_out_w = (
        lax.psum_scatter(
            contract_rows(token_rows, d_gate_pre).astype(jnp.bfloat16),
            "dp",
            scatter_dimension=0,
            tiled=True,
        ).astype(jnp.float32),
        lax.psum_scatter(
            contract_rows(token_rows, d_inner_low).astype(jnp.bfloat16),
            "dp",
            scatter_dimension=0,
            tiled=True,
        ).astype(jnp.float32),
        lax.psum_scatter(
            contract_rows(token_rows, d_state_low).astype(jnp.bfloat16),
            "dp",
            scatter_dimension=0,
            tiled=True,
        ).astype(jnp.float32),
        lax.psum_scatter(
            contract_rows(token_rows, d_step_low).astype(jnp.bfloat16),
            "dp",
            scatter_dimension=0,
            tiled=True,
        ).astype(jnp.float32),
        lax.psum_scatter(
            grad_out_part.astype(jnp.bfloat16), "dp", scatter_dimension=1, tiled=True
        ).astype(jnp.float32),
    )
    grad_norm_part = jnp.sum(d_normed * stream * inv_first, axis=0)
    weighted = d_normed * norm_gain
    d_stream = (
        cotangent
        + inv_first * weighted
        - stream * inv_first**3 * jnp.mean(weighted * stream, axis=1, keepdims=True)
    )
    grad_conv_inner, grad_gate_gain, grad_head = lax.psum(
        (grad_conv_inner_part, grad_gate_part, grad_head_part), "dp"
    )
    grad_conv_state, grad_norm = lax.psum((grad_conv_state_part, grad_norm_part), ("dp", "tensor"))
    m_gate = MU_MAT * moment_w_gate + grad_gate_w
    m_inner = MU_MAT * moment_w_inner + grad_inner_w
    m_state = MU_MAT * moment_w_state + grad_state_w
    m_step = MU_MAT * moment_w_step + grad_step_w
    m_out = MU_MAT * moment_w_out + grad_out_w
    room = w_gate.shape[1]
    shard_rows = w_gate.shape[0]
    stacked = jnp.stack(
        [
            m_gate,
            m_inner,
            m_out.T,
            jnp.pad(m_step, ((0, 0), (0, room - m_step.shape[1]))),
            jnp.pad(m_state, ((0, 0), (0, room - m_state.shape[1]))),
        ]
    )
    matrix_count = stacked.shape[0]
    owner_index = jnp.arange(matrix_count, dtype=jnp.int32) * dp_count // matrix_count
    select = (owner_index[None, :] == jnp.arange(dp_count, dtype=jnp.int32)[:, None]).astype(
        jnp.float32
    )
    outgoing = jnp.einsum("jk,krc->jrc", select, stacked, precision=HIGH)
    owned = (
        lax.all_to_all(outgoing.astype(jnp.bfloat16), "dp", split_axis=0, concat_axis=0, tiled=True)
        .astype(outgoing.dtype)
        .reshape(dp_count * shard_rows, room)
    )
    ortho = orthogonalize(owned)
    returned = lax.all_to_all(
        ortho.reshape(dp_count, shard_rows, room).astype(jnp.bfloat16),
        "dp",
        split_axis=0,
        concat_axis=0,
        tiled=True,
    ).astype(jnp.float32)
    mine = jnp.einsum("jk,jrc->krc", select, returned, precision=HIGH)
    new_gate = w_gate - LR_MAT * spread(D, INNER) * mine[0]
    new_inner = w_inner - LR_MAT * spread(D, INNER) * mine[1]
    new_out = w_out - LR_MAT * spread(INNER, D) * mine[2].T
    new_step = w_step - LR_MAT * spread(D, HEADS) * mine[3][:, : w_step.shape[1]]
    state_slice = lax.dynamic_slice_in_dim(w_state, col_first, col_width, 1)
    new_state = state_slice - LR_MAT * spread(D, 2 * STATE) * mine[4][:, :col_width]
    m_norm = MU_VEC * moment_norm_gain + grad_norm
    m_conv_inner = MU_VEC * moment_conv_inner + grad_conv_inner
    m_conv_state = MU_VEC * moment_conv_state + grad_conv_state
    m_head = MU_VEC * moment_head_params + grad_head
    m_gate_gain = MU_VEC * moment_gate_gain + grad_gate_gain
    return (
        output,
        d_stream,
        grad_norm,
        grad_gate_w,
        grad_inner_w,
        grad_state_w,
        grad_step_w,
        grad_conv_inner,
        grad_conv_state,
        grad_head,
        grad_gate_gain,
        grad_out_w,
        norm_gain - LR_VEC * m_norm,
        new_gate,
        new_inner,
        new_state,
        new_step,
        conv_inner - LR_VEC * m_conv_inner,
        conv_state - LR_VEC * m_conv_state,
        head_params - LR_VEC * m_head,
        gate_gain - LR_VEC * m_gate_gain,
        new_out,
        m_norm,
        m_gate,
        m_inner,
        m_state,
        m_step,
        m_conv_inner,
        m_conv_state,
        m_head,
        m_gate_gain,
        m_out,
    )


MESH_ID = pl.DeviceIdType.MESH
SHARD = 48
PLAN = (("out", 768), ("gate", 768), ("inner", 768), ("small", 256))
PLANE_OF = {"out": 0, "inner": 1, "gate": 2, "small": 3}


def place():
    index = lax.axis_index("dp")
    z = lax.div(index, 4)
    y = lax.rem(lax.div(index, 2), 2)
    x = lax.rem(index, 2)
    at_x = {"dp": z * 4 + y * 2 + (1 - x)}
    at_y = {"dp": z * 4 + (1 - y) * 2 + x}
    at_z = [{"dp": lax.rem(z + step, 4) * 4 + y * 2 + x} for step in range(1, 4)]
    return x, y, z, at_x, at_y, at_z


def greet(peers):
    barrier = pltpu.get_barrier_semaphore()
    for peer in peers:
        pl.semaphore_signal(barrier, inc=1, device_id=peer, device_id_type=MESH_ID)
    pl.semaphore_wait(barrier, len(peers))


def remote(src, dst, send, recv, peer):
    return pltpu.make_async_remote_copy(
        src_ref=src, dst_ref=dst, send_sem=send, recv_sem=recv, device_id=peer, device_id_type=MESH_ID
    )

EARLY = 2
COUNT = 8
SHARED_ROW = 9
NORM_ROW = 14


def half_steps(parts, at_x, at_y, x, y, arrived, summed, arrived_two, one_send, one_recv, two_send, two_recv):
    def span(task, route):
        half = parts[task].shape[-1] // 2
        return pl.ds(route * half, half), pl.ds(0, half)

    def one(task, route):
        cols, mine = span(task, route)
        other = parts[task].at[:, 1 - y, :, :, cols] if route else parts[task].at[:, :, 1 - x, :, cols]
        return remote(
            other, arrived.at[task, route, :, :, :, mine], one_send.at[task, route],
            one_recv.at[task, route], at_y if route else at_x,
        )

    def two(task, route):
        mine = span(task, route)[1]
        return remote(
            summed.at[task, route, :, 1 - x if route else 1 - y, :, mine],
            arrived_two.at[task, route, :, :, mine], two_send.at[task, route],
            two_recv.at[task, route], at_x if route else at_y,
        )

    def add(task, route, own):
        mine = span(task, route)[1]
        got = arrived[task, route, :, :, :, mine]
        summed[task, route, :, :, :, mine] = (own.astype(jnp.float32) + got.astype(jnp.float32)).astype(jnp.bfloat16)

    def settle(task, route, held):
        cols, mine = span(task, route)
        own = summed[task, route, :, x if route else y, :, mine]
        got = arrived_two[task, route, :, :, mine]
        held[:, :, cols] = (own.astype(jnp.float32) + got.astype(jnp.float32)).astype(jnp.bfloat16)

    return span, one, two, add, settle


def send_moments(source, target, own_sem, send, recv):
    _, _, z, _, _, at_z = place()

    def copies():
        yield pltpu.make_async_copy(source.at[z], target.at[z], own_sem.at[0])
        for step, peer in enumerate(at_z):
            plane = lax.rem(z + step + 1, 4)
            yield remote(source.at[plane], target.at[z], send.at[step], recv.at[step], peer)

    @pl.when(pl.program_id(0) == 0)
    def _():
        for copy in copies():
            copy.start()

    @pl.when(pl.program_id(0) == COUNT - 1)
    def _():
        for copy in copies():
            copy.wait()


def early_reduce(parts, held, own, arrived, summed, arrived_two, own_sem, one_send, one_recv, two_send, two_recv):
    step = pl.program_id(0)
    x, y, z, at_x, at_y, at_z = place()
    span, one, two, add, settle = half_steps(
        parts, at_x, at_y, x, y, arrived, summed, arrived_two, one_send, one_recv, two_send, two_recv
    )
    pairs = [(task, route) for task in range(EARLY) for route in range(2)]

    def load(task, route):
        cols = span(task, route)[0]
        src = parts[task].at[:, y, :, :, cols] if route else parts[task].at[:, :, x, :, cols]
        return pltpu.make_async_copy(src, own.at[task, route], own_sem.at[task, route])

    @pl.when(step == 0)
    def _():
        greet([at_x, at_y, {"tensor": 1 - lax.axis_index("tensor")}] + at_z)
        for route in range(2):
            one(0, route).start()
        for task, route in pairs:
            load(task, route).start()
        for route in range(2):
            one(1, route).start()

    for task, at in ((0, 3), (1, 5)):

        @pl.when(step == at)
        def _():
            for route in range(2):
                load(task, route).wait()
                one(task, route).wait()
                add(task, route, own[task, route])
                two(task, route).start()

    for task, at in ((0, 6), (1, 7)):

        @pl.when(step == at)
        def _():
            for route in range(2):
                two(task, route).wait()
                settle(task, route, held[task])


CHUNK = 128
PACK = 16


def sigmoid(value):
    return 0.5 * jnp.tanh(0.5 * value) + 0.5


def expand_matrix():
    row = jnp.arange(128)[:, None]
    col = jnp.arange(768)[None, :] // 64
    return ((row == col) | (row == col + PACK)).astype(jnp.bfloat16)


def two_term(value):
    lane = lax.broadcasted_iota(jnp.int32, value.shape, 1)
    high = value.astype(jnp.bfloat16).astype(jnp.float32)
    return jnp.where(lane < PACK, high, value - high).astype(jnp.bfloat16)


def split_terms(value, terms):
    out = []
    for _ in range(terms):
        piece = value.astype(jnp.bfloat16)
        out.append(piece)
        value = value - piece.astype(jnp.float32)
    return out


def dot(left, right, dims=((1,), (0,))):
    return lax.dot_general(left, right, (dims, ((), ())), preferred_element_type=jnp.float32)


def head_terms(step_ref, head_ref, pos):
    shifted = step_ref[...] + head_ref[0:1, :]
    small = jnp.exp(-jnp.abs(shifted))
    step = jnp.maximum(shifted, 0.0) + jnp.log1p(small)
    log_decay = -step * jnp.exp(head_ref[1:2, :])
    row = lax.broadcasted_iota(jnp.int32, (CHUNK, 128), 0)
    col = lax.broadcasted_iota(jnp.int32, (CHUNK, 128), 1)
    lower = (row >= col).astype(jnp.bfloat16)
    cumulative = sum(dot(lower, piece) for piece in split_terms(log_decay, 3))
    last = cumulative[CHUNK - 1 : CHUNK, :]
    back = (row - col).astype(jnp.float32)
    linked = (row >= col) & (back <= jnp.maximum(pos, 0.0))
    row = row.astype(jnp.float32)
    carry_in = jnp.where(pos > row, jnp.exp(cumulative), 0.0)
    pos_last = pos[CHUNK - 1 : CHUNK, :]
    tail_linked = (CHUNK - 1.0 - row) <= jnp.maximum(pos_last, 0.0)
    tail = jnp.where(tail_linked, jnp.exp(jnp.minimum(last - cumulative, 0.0)), 0.0)
    carry = jnp.where(pos_last > CHUNK - 1.0, jnp.exp(last), 0.0)
    return shifted, step, log_decay, cumulative, linked, carry_in, tail, carry


def pair_decay(cumulative, across, pair):
    parts = []
    for head in (2 * pair, 2 * pair + 1):
        spacing = cumulative[:, head : head + 1] - across[head : head + 1, :]
        parts.append(jnp.exp(jnp.minimum(spacing, 0.0)))
    return parts


def forward_kernel(
    inner_ref, step_ref, gate_ref, state_ref, dno_ref, pos_ref, taps_ref, taps_s_ref, head_ref,
    skip_ref, gain_ref, wide_ref,
    scanned_ref, zi_ref, zs_ref, enter_ref, sums_ref,
    halo_i, halo_s, hold,
):
    @pl.when(pl.program_id(0) == 0)
    def _():
        halo_i[...] = jnp.zeros_like(halo_i)
        halo_s[...] = jnp.zeros_like(halo_s)
        hold[...] = jnp.zeros_like(hold)

    low = jnp.bfloat16
    pos = pos_ref[...]
    marks = [(pos >= lag).astype(jnp.float32) for lag in range(4)]

    def conv(ref, halo, taps, out_ref, first):
        value = ref[:, first : first + 128]
        ext = jnp.concatenate([halo[:, first : first + 128], value], axis=0)
        total = taps[4:5, first : first + 128] + marks[0] * (value * taps[0:1, first : first + 128])
        for lag in range(1, 4):
            moved = pltpu.roll(ext, lag, 0)[8:]
            total = total + marks[lag] * (moved * taps[lag : lag + 1, first : first + 128])
        out_ref[:, first : first + 128] = total
        return total * sigmoid(total)

    shifted, step, log_decay, cumulative, linked, carry_in, tail, carry = head_terms(
        step_ref, head_ref, pos
    )
    across = cumulative.T
    wide = dot(
        jnp.concatenate(
            [
                two_term(step),
                two_term(carry_in),
                two_term(tail * step),
                two_term(jnp.broadcast_to(carry, (16, 128))),
            ],
            axis=0,
        ),
        wide_ref[...],
    )
    input_map = conv(state_ref, halo_s, taps_s_ref, zs_ref, 0).astype(low)
    output_map = conv(state_ref, halo_s, taps_s_ref, zs_ref, 128).astype(low)
    scores = jnp.where(linked, dot(output_map, input_map, ((1,), (1,))), 0.0)
    state = hold[...]
    state_low = state.astype(low)
    enter_ref[...] = state_low
    entered = dot(output_map, state_low)
    lane = lax.broadcasted_iota(jnp.int32, (CHUNK, 128), 1)
    squares = jnp.zeros((CHUNK, 128), jnp.float32)
    crosses = jnp.zeros((CHUNK, 128), jnp.float32)
    fed = []
    for pair in range(6):
        cols = slice(pair * 128, pair * 128 + 128)
        act = conv(inner_ref, halo_i, taps_ref, zi_ref, pair * 128)
        stepped = (wide[:CHUNK, cols] * act).astype(low)
        first, second = pair_decay(cumulative, across, pair)
        mixing = jnp.concatenate([(scores * first).astype(low), (scores * second).astype(low)], axis=0)
        both = dot(mixing, stepped)
        within = jnp.where(lane < 64, both[:CHUNK], both[CHUNK:])
        scanned = (
            within + entered[:, cols] * wide[CHUNK : 2 * CHUNK, cols] + skip_ref[0:1, cols] * act
        )
        scanned_ref[:, cols] = scanned
        fed.append((wide[2 * CHUNK : 3 * CHUNK, cols] * act).astype(low))
        gate = gate_ref[:, cols]
        gated = scanned * (gate * sigmoid(gate))
        squares = squares + gated * gated
        crosses = crosses + dno_ref[:, cols] * gain_ref[0:1, cols] * gated
    fresh = dot(input_map, jnp.concatenate(fed, axis=1), ((0,), (0,)))
    hold[...] = wide[3 * CHUNK : 3 * CHUNK + 1, :] * state + fresh
    halo_i[...] = inner_ref[CHUNK - 8 :, :]
    halo_s[...] = state_ref[CHUNK - 8 :, :]
    square = jnp.sum(squares, axis=1, keepdims=True)
    cross = jnp.sum(crosses * marks[0], axis=1, keepdims=True)
    sums_ref[...] = jnp.where(lane == 0, square, cross)


def gate_kernel(
    gate_ref, scanned_ref, dno_ref, sums_ref, twin_ref, gain_ref, pos_ref,
    normed_ref, d_gate_ref, d_scan_ref, g_gain_ref,
):
    @pl.when(pl.program_id(0) == 0)
    def _():
        g_gain_ref[...] = jnp.zeros_like(g_gain_ref)

    low = jnp.bfloat16
    alive = (pos_ref[...] >= 0).astype(jnp.float32)
    sums = sums_ref[...] + twin_ref[...]
    inv = jnp.broadcast_to(lax.rsqrt(sums[:, 0:1] / INNER + EPS), alive.shape)
    pull = inv * inv * inv * jnp.broadcast_to(sums[:, 1:2] / INNER, alive.shape)
    live = inv * alive
    for pair in range(6):
        cols = slice(pair * 128, pair * 128 + 128)
        gain = gain_ref[0:1, cols]
        gate, scanned, d_normed_out = gate_ref[:, cols], scanned_ref[:, cols], dno_ref[:, cols]
        sig = sigmoid(gate)
        gate_act = gate * sig
        gated = scanned * gate_act
        normed_ref[:, cols] = (gated * live * gain).astype(low)
        product = d_normed_out * gated * live
        g_gain_ref[:, cols] += jnp.sum(product.reshape(CHUNK // 8, 8, 128), axis=0)
        d_gated = live * gain * d_normed_out - gated * pull
        d_scan_ref[:, cols] = (d_gated * gate_act).astype(low)
        d_gate_ref[:, cols] = (d_gated * scanned * (sig * (1.0 + gate * (1.0 - sig)))).astype(low)


def gate_stage(first_pre, scanned, d_normed_out, sums, twin_sums, gain, pos):
    rows = first_pre.shape[0]
    at = lambda width: pl.BlockSpec((CHUNK, width), lambda c: (c, 0))
    f32, low = jnp.float32, jnp.bfloat16
    wide = jax.ShapeDtypeStruct((rows, 768), low)
    return pl.pallas_call(
        gate_kernel,
        grid=(rows // CHUNK,),
        in_specs=[
            at(768), at(768), at(768), at(128), at(128), pl.BlockSpec((1, 768), lambda c: (0, 0)), at(128),
        ],
        out_specs=[at(768), at(768), at(768), pl.BlockSpec((8, 768), lambda c: (0, 0))],
        out_shape=[wide, wide, wide, jax.ShapeDtypeStruct((8, 768), f32)],
        compiler_params=pltpu.CompilerParams(vmem_limit_bytes=60 * 2**20),
        cost_estimate=pl.CostEstimate(flops=10**8, bytes_accessed=15 * 10**6, transcendentals=10**6),
        name="gate_stage",
    )(first_pre, scanned, d_normed_out, sums, twin_sums, gain, pos)


def backward_kernel(
    inner_ref, step_ref, state_ref, zi_ref, zs_ref, scanned_ref, dscan_ref, enter_ref, pos_ref,
    taps_ref, taps_s_ref, head_ref, skip_ref, wide_ref, gain_ref, out_part, gate_part, moment_ref,
    d_inner_ref, d_state_ref, d_step_ref, vec_ref, held_out, held_gate, moments_ref,
    g_taps_ref, g_taps_s_ref, g_skip_ref, g_head_ref,
    halo_i, halo_s, halo_p, hold, state_out, state_in, state_send, state_recv, own_sem, m_send, m_recv, *reducing,
):
    low = jnp.bfloat16
    step_at = pl.program_id(0)
    last_step = pl.num_programs(0) - 1
    core = lax.axis_index("tensor")
    early_reduce((out_part, gate_part), (held_out, held_gate), *reducing)
    send_moments(moment_ref, moments_ref, own_sem, m_send, m_recv)
    chunk = last_step - step_at
    twin = {"tensor": 1 - core}
    here = pl.ds(pl.multiple_of(chunk * CHUNK, CHUNK), CHUNK)

    @pl.when(pl.program_id(0) == 0)
    def _():
        for ref in (halo_i, halo_s, halo_p, hold, g_taps_ref, g_taps_s_ref, g_skip_ref, g_head_ref):
            ref[...] = jnp.zeros_like(ref)

    pos = pos_ref[...]
    pos_ext = jnp.concatenate([pos, halo_p[...]], axis=0)
    marks = [(pos_ext >= lag).astype(jnp.float32) for lag in range(4)]
    lane = lax.broadcasted_iota(jnp.int32, (CHUNK, 128), 1)
    row = lax.broadcasted_iota(jnp.int32, (CHUNK, 128), 0)
    col = lane

    def slope(total):
        sig = sigmoid(total)
        return sig * (1.0 + total * (1.0 - sig)), total * sig

    def fold(value):
        return jnp.sum(value.reshape(CHUNK // 8, 8, 128), axis=0)

    def conv_back(grad, ref, halo, taps, out_ref, g_ref, first):
        cols = slice(first, first + 128)
        ext = jnp.concatenate([grad, halo[:, cols]], axis=0)
        value = ref[:, cols]
        halo[:, cols] = grad[:8]
        g_ref[4, :, cols] += fold(grad)
        total = jnp.zeros((CHUNK, 128), jnp.float32)
        for lag in range(4):
            masked = ext * marks[lag]
            if lag:
                masked = pltpu.roll(masked, CHUNK + 8 - lag, 0)
            masked = masked[:CHUNK]
            g_ref[lag, :, cols] += fold(masked * value)
            total = total + masked * taps[lag : lag + 1, cols]
        if out_ref is not None:
            out_ref[:, cols] = total.astype(low)
        return total

    shifted, step, log_decay, cumulative, linked, carry_in, tail, carry = head_terms(
        step_ref, head_ref, pos
    )
    across = cumulative.T
    wide = dot(
        jnp.concatenate(
            [
                two_term(step),
                two_term(carry_in),
                two_term(tail),
                two_term(jnp.broadcast_to(carry, (16, 128))),
            ],
            axis=0,
        ),
        wide_ref[...],
    )
    slope_b, input_map = slope(zs_ref[:, :128])
    slope_c, output_map = slope(zs_ref[:, 128:])
    input_low, output_low = input_map.astype(low), output_map.astype(low)
    scores = jnp.where(linked, dot(output_low, input_low, ((1,), (1,))), 0.0)
    entering = enter_ref[...]
    d_next = hold[...]
    d_next_low = d_next.astype(low)
    pulled = dot(input_low, d_next_low)
    d_scores = jnp.zeros((CHUNK, 128), jnp.float32)
    d_entered, fed, balance, direct, extra = [], [], [], [], []
    carry_wide = wide[3 * CHUNK : 3 * CHUNK + 1, :]
    carry_grad = jnp.sum(d_next * entering.astype(jnp.float32), axis=0, keepdims=True) * carry_wide
    for pair in range(6):
        cols = slice(pair * 128, pair * 128 + 128)
        slope_x, act = slope(zi_ref[:, cols])
        d_low = dscan_ref[:, cols]
        skip = skip_ref[0:1, cols]
        stepped = (wide[:CHUNK, cols] * act).astype(low)
        stepped_wide = stepped.astype(jnp.float32)
        d_exact = d_low.astype(jnp.float32)
        d_both = jnp.concatenate(
            [jnp.where(lane < 64, d_exact, 0.0).astype(low), jnp.where(lane < 64, 0.0, d_exact).astype(low)],
            axis=0,
        )
        first, second = pair_decay(cumulative, across, pair)
        mixing = jnp.concatenate([(scores * first).astype(low), (scores * second).astype(low)], axis=0)
        d_mixing = dot(d_both, stepped, ((1,), (1,)))
        d_scores = d_scores + d_mixing[:CHUNK] * first + d_mixing[CHUNK:] * second
        tail_cols = wide[2 * CHUNK : 3 * CHUNK, cols]
        tailed = tail_cols * pulled[:, cols]
        d_stepped = dot(mixing, d_both, ((0,), (0,))) + tailed
        extra.append(jnp.sum(stepped_wide * tailed, axis=0, keepdims=True) + carry_grad[:, cols])
        fed.append((tail_cols * stepped_wide).astype(low))
        d_entered.append((wide[CHUNK : 2 * CHUNK, cols] * d_exact).astype(low))
        balance.append(d_exact * (scanned_ref[:, cols] - skip * act) - stepped_wide * d_stepped)
        direct.append(act * d_stepped)
        g_skip_ref[:, cols] += fold(d_exact * act)
        d_act = skip * d_exact + wide[:CHUNK, cols] * d_stepped
        conv_back(d_act * slope_x, inner_ref, halo_i, taps_ref, d_inner_ref, g_taps_ref, pair * 128)
    d_entered = jnp.concatenate(d_entered, axis=1)
    fed = jnp.concatenate(fed, axis=1)
    d_scores = jnp.where(linked, d_scores, 0.0).astype(low)
    d_output = dot(d_scores, input_low) + dot(d_entered, entering, ((1,), (1,)))
    d_input = dot(d_scores, output_low, ((0,), (0,))) + dot(fed, d_next_low, ((1,), (1,)))
    hold[...] = carry_wide * d_next + dot(output_low, d_entered, ((0,), (0,)))
    for_first = conv_back(d_input * slope_b, state_ref, halo_s, taps_s_ref, None, g_taps_s_ref, 0)
    for_second = conv_back(d_output * slope_c, state_ref, halo_s, taps_s_ref, None, g_taps_s_ref, 128)
    state_out[step_at] = jnp.where(core == 0, for_second, for_first).astype(low)
    d_state_ref[here, :] = jnp.where(core == 0, for_first, for_second).astype(low)

    def lend(at):
        return remote(state_out.at[at], state_in.at[at], state_send.at[at], state_recv.at[at], twin)

    lend(step_at).start()
    halo_p[...] = pos[:8]
    spread_back = wide_ref[...]
    extra = jnp.broadcast_to(jnp.concatenate(extra, axis=1), (16, 768))
    stacked = jnp.concatenate(
        split_terms(jnp.concatenate(balance, axis=1), 2)
        + split_terms(jnp.concatenate(direct, axis=1), 2)
        + split_terms(extra, 2),
        axis=0,
    )
    summed = dot(stacked, spread_back, ((1,), (1,)))
    d_sum = summed[:CHUNK] + summed[CHUNK : 2 * CHUNK]
    d_direct = summed[2 * CHUNK : 3 * CHUNK] + summed[3 * CHUNK : 4 * CHUNK]
    d_last = summed[4 * CHUNK : 4 * CHUNK + 1] + summed[4 * CHUNK + 16 : 4 * CHUNK + 17]
    upper = (row <= col).astype(low)
    d_decay = sum(dot(upper, piece) for piece in split_terms(d_sum, 3)) + d_last
    d_step = (d_direct - d_decay * jnp.exp(head_ref[1:2, :])) * sigmoid(shifted)
    d_step = jnp.where(lane < PACK, d_step, 0.0)
    d_step_ref[...] = d_step.astype(low)
    g_head_ref[0] += fold(d_step)
    g_head_ref[1] += fold(d_decay * log_decay)

    @pl.when(step_at == last_step)
    def _():
        vec_ref[...] = jnp.zeros_like(vec_ref)
        total = lambda value: jnp.sum(value, axis=0, keepdims=True)
        for lag in range(5):
            vec_ref[lag : lag + 1, :] = total(g_taps_ref[lag])
            vec_ref[SHARED_ROW + lag : SHARED_ROW + lag + 1, :256] = total(g_taps_s_ref[lag])
        vec_ref[5:6, :] = total(gain_ref[...])
        for at in range(2):
            vec_ref[6 + at : 7 + at, :128] = total(g_head_ref[at])
        skip_row = jnp.broadcast_to(total(g_skip_ref[...]), (16, 768))
        vec_ref[8:9, :128] = sum(
            dot(piece, spread_back, ((1,), (1,))) for piece in split_terms(skip_row, 3)
        )[0:1]
        for at in range(COUNT):
            lend(at).wait()
            rows = pl.ds((COUNT - 1 - at) * CHUNK, CHUNK)
            d_state_ref[rows, :] = (
                d_state_ref[rows, :].astype(jnp.float32) + state_in[at].astype(jnp.float32)
            ).astype(low)


def forward_core(first_pre, second_pre, d_normed_out, pos, taps, taps_s, heads_lanes, skip, gain, wide):
    rows = first_pre.shape[0]
    at = lambda width, col: pl.BlockSpec((CHUNK, width), lambda c: (c, col))
    whole = lambda arr: pl.BlockSpec(arr.shape, lambda c: (0,) * arr.ndim)
    f32 = jnp.float32
    return pl.pallas_call(
        forward_kernel,
        grid=(rows // CHUNK,),
        in_specs=[
            at(768, 0), at(128, 6), at(768, 0), at(256, 3), at(768, 0), at(128, 0),
            whole(taps), whole(taps_s), whole(heads_lanes), whole(skip), whole(gain), whole(wide),
        ],
        out_specs=[at(768, 0), at(768, 0), at(256, 0), at(768, 0), at(128, 0)],
        out_shape=[
            jax.ShapeDtypeStruct((rows, 768), f32),
            jax.ShapeDtypeStruct((rows, 768), f32),
            jax.ShapeDtypeStruct((rows, 256), f32),
            jax.ShapeDtypeStruct((rows, 768), jnp.bfloat16),
            jax.ShapeDtypeStruct((rows, 128), f32),
        ],
        scratch_shapes=[
            pltpu.VMEM((8, 768), f32), pltpu.VMEM((8, 256), f32), pltpu.VMEM((128, 768), f32),
        ],
        compiler_params=pltpu.CompilerParams(vmem_limit_bytes=60 * 2**20),
        cost_estimate=pl.CostEstimate(flops=8 * 10**9, bytes_accessed=24 * 10**6, transcendentals=4 * 10**6),
        name="mixer_forward",
    )(second_pre, second_pre, first_pre, first_pre, d_normed_out, pos, taps, taps_s, heads_lanes, skip, gain, wide)


def backward_core(
    first_pre, second_pre, zi, zs, scanned, d_scan, enter, pos, taps, taps_s, heads_lanes, skip, wide, gain_part, out_part, gate_part, moment_rows
):
    rows = first_pre.shape[0]
    count = rows // CHUNK
    at = lambda width, col: pl.BlockSpec((CHUNK, width), lambda c: (count - 1 - c, col))
    whole = lambda shape: pl.BlockSpec(shape, lambda c: (0,) * len(shape))
    f32, low = jnp.float32, jnp.bfloat16
    return pl.pallas_call(
        backward_kernel,
        grid=(count,),
        in_specs=[
            at(768, 0), at(128, 6), at(256, 3), at(768, 0), at(256, 0), at(768, 0), at(768, 0),
            at(768, 0), at(128, 0),
            whole(taps.shape), whole(taps_s.shape), whole(heads_lanes.shape), whole(skip.shape), whole(wide.shape),
            whole(gain_part.shape), pl.BlockSpec(memory_space=pl.ANY), pl.BlockSpec(memory_space=pl.ANY), pl.BlockSpec(memory_space=pl.ANY),
        ],
        out_specs=[
            at(768, 0), whole((rows, 128)), at(128, 0),
            whole((16, 768)),
            whole((4, SHARD, 768)), whole((4, SHARD, 768)), pl.BlockSpec(memory_space=pl.ANY),
        ],
        out_shape=[
            jax.ShapeDtypeStruct((rows, 768), low),
            jax.ShapeDtypeStruct((rows, 128), low),
            jax.ShapeDtypeStruct((rows, 128), low),
            jax.ShapeDtypeStruct((16, 768), f32),
            jax.ShapeDtypeStruct((4, SHARD, 768), low),
            jax.ShapeDtypeStruct((4, SHARD, 768), low),
            jax.ShapeDtypeStruct((4, SHARD, 768), low),
        ],
        scratch_shapes=[
            pltpu.VMEM((5, 8, 768), f32), pltpu.VMEM((5, 8, 256), f32), pltpu.VMEM((8, 768), f32),
            pltpu.VMEM((2, 8, 128), f32),
            pltpu.VMEM((8, 768), f32), pltpu.VMEM((8, 256), f32), pltpu.VMEM((8, 128), f32),
            pltpu.VMEM((128, 768), f32),
            pltpu.VMEM((COUNT, CHUNK, 128), low), pltpu.VMEM((COUNT, CHUNK, 128), low),
            pltpu.SemaphoreType.DMA((COUNT,)), pltpu.SemaphoreType.DMA((COUNT,)),
            pltpu.SemaphoreType.DMA((1,)), pltpu.SemaphoreType.DMA((3,)), pltpu.SemaphoreType.DMA((3,)),
            pltpu.VMEM((EARLY, 2, 4, 2, SHARD, 384), low),
            pltpu.VMEM((EARLY, 2, 4, 2, SHARD, 384), low),
            pltpu.VMEM((EARLY, 2, 4, 2, SHARD, 384), low),
            pltpu.VMEM((EARLY, 2, 4, SHARD, 384), low),
        ]
        + [pltpu.SemaphoreType.DMA((EARLY, 2))] * 5,
        compiler_params=pltpu.CompilerParams(
            collective_id=3, has_side_effects=True, vmem_limit_bytes=60 * 2**20
        ),
        cost_estimate=pl.CostEstimate(flops=16 * 10**9, bytes_accessed=24 * 10**6, transcendentals=6 * 10**6),
        name="mixer_backward",
    )(
        second_pre, second_pre, first_pre, zi, zs, scanned, d_scan, enter, pos, taps, taps_s, heads_lanes, skip, wide,
        gain_part, out_part.reshape(4, 2, 2, SHARD, 768), gate_part.reshape(4, 2, 2, SHARD, 768),
        moment_rows,
    )


def swap(value):
    return lax.ppermute(value, "tensor", [(0, 1), (1, 0)])


def pad_cols(value, width):
    return jnp.pad(value, ((0, 0), (0, width - value.shape[1])))


GATHER_PIECES = (
    (1, 0, 384, 0), (1, 384, 512, 1), (0, 0, 512, 0), (0, 512, 512, 1), (2, 0, 384, 0), (2, 384, 384, 1),
)


def gather_kernel(
    gate_ref, state_ref, inner_ref, step_ref, out_ref, stream_ref, cot_ref, gain_ref,
    full_first, full_second, full_out, rows_ref, cots_ref, pre_first, pre_second, pre_out,
    first_ref, second_ref, lanes_ref, held_first, held_second, held_out,
    pre_sem, row_sem, z_send, z_recv, one_send, one_recv, two_send, two_recv,
):
    x, y, z, at_x, at_y, at_z = place()
    core = lax.axis_index("tensor")
    twin = {"tensor": 1 - core}
    low = jnp.bfloat16
    first_ref[:, pl.ds(0, 768)] = gate_ref[...].astype(low)
    first_ref[:, pl.ds(768, 256)] = state_ref[...].astype(low)
    second_ref[:, pl.ds(0, 768)] = inner_ref[...].astype(low)
    lanes_ref[...] = jnp.zeros_like(lanes_ref)
    lanes_ref[:, : step_ref.shape[1]] = step_ref[...]
    lanes = lanes_ref[...]
    second_ref[:, pl.ds(768, 128)] = (lanes + pltpu.roll(lanes, PACK, 1)).astype(low)
    greet([at_x, at_y, twin] + at_z)
    shards = (first_ref, second_ref, out_ref)
    fulls = (full_first, full_second, full_out)
    results = ((held_first, pre_first), (held_second, pre_second), (held_out, pre_out))
    z_copies, ones, twos, copies = {}, {}, {}, []

    def step_zero(piece):
        which, start, width, _ = GATHER_PIECES[piece]
        cols = pl.ds(start, width)
        z_copies[piece] = []
        for step, peer in enumerate(at_z):
            copy = remote(
                shards[which].at[:, cols], fulls[which].at[z, y, x, :, cols],
                z_send.at[piece, step], z_recv.at[piece, step], peer,
            )
            copy.start()
            z_copies[piece].append(copy)

    def step_one(piece):
        which, start, width, route = GATHER_PIECES[piece]
        for copy in z_copies[piece]:
            copy.wait()
        part = fulls[which].at[:, y, x, :, pl.ds(start, width)]
        ones[piece] = remote(part, part, one_send.at[piece], one_recv.at[piece], at_x if route else at_y)
        ones[piece].start()

    def step_two(piece):
        which, start, width, route = GATHER_PIECES[piece]
        cols = pl.ds(start, width)
        ones[piece].wait()
        part = fulls[which].at[:, y, :, :, cols] if route else fulls[which].at[:, :, x, :, cols]
        twos[piece] = remote(part, part, two_send.at[piece], two_recv.at[piece], at_y if route else at_x)
        twos[piece].start()

    def finish(piece):
        which, start, width, _ = GATHER_PIECES[piece]
        cols = pl.ds(start, width)
        twos[piece].wait()
        left = cots_ref if which == 2 else rows_ref
        held, pre = results[which]
        weights = fulls[which]

        def tile(at, carry):
            here = pl.ds(pl.multiple_of(lax.rem(at, 2) * 256, 256), 256)
            there = pl.ds(pl.multiple_of(at * 256, 256), 256)
            held[there, cols] = dot(
                left[lax.div(at, 2), here, :], weights[:, :, :, :, cols].reshape(768, width)
            )
            return carry

        lax.fori_loop(0, 4, tile, 0)
        copy = pltpu.make_async_copy(held.at[:, cols], pre.at[:, cols], pre_sem.at[piece])
        copy.start()
        copies.append(copy)

    step_zero(0)
    for shard, full in zip(shards, fulls):
        full[z, y, x] = shard[...]
    step_zero(1)
    for part in range(4):
        here = pl.ds(part * 128, 128)
        value = stream_ref[here, :]
        inv = lax.rsqrt(jnp.sum(value * value, axis=1, keepdims=True) / D + EPS)
        rows_ref[core, here, :] = (value * inv * gain_ref[...]).astype(jnp.bfloat16)
        cots_ref[core, here, :] = cot_ref[here, :].astype(jnp.bfloat16)
    swaps = []
    for at, ref in enumerate((rows_ref, cots_ref)):
        swaps.append(remote(ref.at[core], ref.at[core], row_sem.at[at], row_sem.at[2 + at], twin))
        swaps[-1].start()
    count = len(GATHER_PIECES)
    for piece in range(count + 1):
        if piece < count:
            step_one(piece)
        if piece + 2 < count:
            step_zero(piece + 2)
        if piece >= 1:
            step_two(piece - 1)
        if piece == 3:
            for copy in swaps:
                copy.wait()
        if piece >= 4:
            finish(piece - 4)
    for piece in range(count - 3, count):
        finish(piece)
    for copy in copies:
        copy.wait()


def gather_all(gate, state, inner, step, out, stream, cotangent, gain):
    f32, low = jnp.float32, jnp.bfloat16
    vmem = pl.BlockSpec(memory_space=pltpu.VMEM)
    count = len(GATHER_PIECES)
    dma = pltpu.SemaphoreType.DMA
    tokens = 2 * stream.shape[0]
    first = jax.ShapeDtypeStruct((SHARD, 1024), low)
    second = jax.ShapeDtypeStruct((SHARD, 896), low)
    full = lambda arr: jax.ShapeDtypeStruct((4, 2, 2) + arr.shape, low)
    rows = jax.ShapeDtypeStruct((2,) + stream.shape, low)
    pre = lambda arr: jax.ShapeDtypeStruct((tokens, arr.shape[1]), f32)
    got = pl.pallas_call(
        gather_kernel,
        in_specs=[vmem] * 8,
        out_specs=[vmem] * 5 + [pl.BlockSpec(memory_space=pl.ANY)] * 3,
        out_shape=[full(first), full(second), full(out), rows, rows, pre(first), pre(second), pre(out)],
        scratch_shapes=[
            pltpu.VMEM(first.shape, low), pltpu.VMEM(second.shape, low), pltpu.VMEM((SHARD, 128), f32),
            pltpu.VMEM((tokens, first.shape[1]), f32),
            pltpu.VMEM((tokens, second.shape[1]), f32),
            pltpu.VMEM((tokens, out.shape[1]), f32),
            dma((count,)), dma((4,)), dma((count, 3)), dma((count, 3)),
            dma((count,)), dma((count,)), dma((count,)), dma((count,)),
        ],
        compiler_params=pltpu.CompilerParams(
            collective_id=0, has_side_effects=True, vmem_limit_bytes=60 * 2**20
        ),
        cost_estimate=pl.CostEstimate(flops=4 * 10**9, bytes_accessed=120 * 10**6, transcendentals=0),
        name="gather_weights",
    )(gate, state, inner, step, out, stream, cotangent, gain)
    return [item.reshape(-1, item.shape[-1]) for item in got]


def reduce_kernel(
    held_out, held_gate, inner_ref, small_ref, vec_ref, moments, gain_ref, *rest,
):
    sources, rest = rest[:10], rest[10:]
    whole_ref, other_ref, grads_ref, total_ref, output_ref, d_stream_ref = rest[:6]
    local, rest = rest[6:16], rest[16:]
    reduce_body(
        held_out, held_gate, inner_ref, small_ref, vec_ref, moments, gain_ref, sources,
        whole_ref, other_ref, grads_ref, total_ref, output_ref, d_stream_ref, local, *rest,
    )


def reduce_body(
    held_out, held_gate, inner_ref, small_ref, vec_ref, moments, gain_ref, sources,
    whole_ref, other_ref, grads_ref, total_ref, output_ref, d_stream_ref, local,
    load_sem, mine_f, lent_b, got_b, vec_own, vec_twin, w_send, w_recv,
    arrived, summed, arrived_two, held_inner, held_small, slots,
    block, back, vec_in, vec_mid, vec_slots,
    one_send, one_recv, two_send, two_recv, z_send, z_recv, g_send, g_recv,
    p_send, p_recv, t_send, t_recv, v_send, v_recv,
):
    f32, low = jnp.float32, jnp.bfloat16
    x, y, z, at_x, at_y, at_z = place()
    core = lax.axis_index("tensor")
    twin = {"tensor": 1 - core}
    greet([at_x, at_y, twin] + at_z)
    parts = (inner_ref, small_ref)
    held = (held_out, held_gate, held_inner, held_small)
    steps_z = [lax.rem(z + step, 4) for step in range(1, 4)]
    span, one, two, add, settle = half_steps(
        parts, at_x, at_y, x, y, arrived, summed, arrived_two, one_send, one_recv, two_send, two_recv
    )

    def to_plane(task):
        plane, width = PLANE_OF[PLAN[task][0]], PLAN[task][1]

        @pl.when(z != plane)
        def _():
            remote(
                held[task], slots.at[z, :, :, pl.ds(0, width)], z_send.at[task], z_recv.at[z],
                {"dp": plane * 4 + y * 2 + x},
            ).start()

    for task in range(2):
        for route in range(2):
            one(task, route).start()
    to_plane(0)
    to_plane(1)
    loads = [pltpu.make_async_copy(src, dst, load_sem.at[at]) for at, (src, dst) in enumerate(zip(sources, local))]
    for copy in loads:
        copy.start()
    d_gate, d_inner, d_state, d_step, normed, w_first, w_second, w_out, stream_ref, cot_ref = local
    half_rows = stream_ref.shape[0]
    turned = ((1,), (1,))
    state_cols = pl.ds(pl.multiple_of(768 + core * 128, 128), 128)

    def product(which, rows):
        if which == 1:
            return dot(normed[rows, :], w_out[...], turned)
        first = dot(d_gate[rows, :], w_first[:, pl.ds(0, 768)], turned)
        second = dot(d_inner[rows, :], w_second[:, pl.ds(0, 768)], turned)
        third = dot(d_state[rows, :], w_first[:, state_cols], turned)
        return first + second + third + dot(d_step[rows, :], w_second[:, pl.ds(768, 128)], turned)

    for copy in loads:
        copy.wait()

    def products(who, store):
        for which in range(2):

            def tile(at, carry):
                rows = pl.ds(pl.multiple_of(who * half_rows + at * 256, 256), 256)
                store(which, pl.ds(pl.multiple_of(at * 256, 256), 256), product(which, rows))
                return carry

            lax.fori_loop(0, half_rows // 256, tile, 0)

    def store_lent(which, rows, value):
        lent_b[which, rows, :] = value.astype(low)

    def store_mine(which, rows, value):
        mine_f[which, rows, :] = value

    products(1 - core, store_lent)
    lends = []
    for which in range(2):
        lends.append(remote(lent_b.at[which], got_b.at[which], w_send.at[which], w_recv.at[which], twin))
        lends[-1].start()
    for task in range(2):
        for route in range(2):
            cols = span(task, route)[0]
            one(task, route).wait()
            add(task, route, parts[task][:, y, :, :, cols] if route else parts[task][:, :, x, :, cols])
            two(task, route).start()
    products(core, store_mine)
    for task in range(2):
        for route in range(2):
            two(task, route).wait()
            settle(task, route, held[2 + task])
        to_plane(2 + task)
    for copy in lends:
        copy.wait()
    grad_norm = jnp.zeros((1, 768), f32)
    gain = gain_ref[...]
    for part in range(half_rows // 128):
        rows = pl.ds(part * 128, 128)
        value = stream_ref[rows, :]
        output_ref[rows, :] = value + (mine_f[1, rows, :] + got_b[1, rows, :].astype(f32))
        inv = lax.rsqrt(jnp.sum(value * value, axis=1, keepdims=True) / D + EPS)
        d_normed = mine_f[0, rows, :] + got_b[0, rows, :].astype(f32)
        scaled = value * inv
        grad_norm = grad_norm + jnp.sum(d_normed * scaled, axis=0, keepdims=True)
        weighted = d_normed * gain
        inner = jnp.sum(weighted * scaled, axis=1, keepdims=True) / D
        d_stream_ref[rows, :] = cot_ref[rows, :] + inv * (weighted - scaled * inner)
    vec_rows = lax.broadcasted_iota(jnp.int32, vec_ref.shape, 0)
    vec_own[...] = jnp.where(vec_rows == NORM_ROW, grad_norm, vec_ref[...])
    vec_x = remote(vec_own, vec_in.at[0], v_send.at[0], v_recv.at[0], at_x)
    vec_x.start()
    vec_x.wait()
    vec_mid[0] = vec_own[...] + vec_in[0]
    vec_y = remote(vec_mid.at[0], vec_in.at[1], v_send.at[1], v_recv.at[1], at_y)
    vec_y.start()
    vec_y.wait()
    vec_mid[1] = vec_mid[0] + vec_in[1]
    vec_slots[z] = vec_mid[1]
    vec_z = []
    for step, peer in enumerate(at_z):
        copy = remote(vec_mid.at[1], vec_slots.at[z], v_send.at[2 + step], v_recv.at[2 + step], peer)
        copy.start()
        vec_z.append(copy)

    for task, (name, width) in enumerate(PLAN):
        plane = PLANE_OF[name]
        cols = pl.ds(0, width)

        @pl.when(z == plane)
        def _():
            for source in range(4):
                if source != plane:
                    remote(
                        held[task], slots.at[source, :, :, cols], z_send.at[task], z_recv.at[source], at_x
                    ).wait_recv()
            total = held[task][...].astype(f32)
            for source in range(4):
                if source != plane:
                    total = total + slots[source, :, :, cols].astype(f32)
            if width < 768:
                back[...] = jnp.zeros_like(back)
                block[...] = jnp.zeros_like(block)
            back[:, :, cols] = total.astype(low)
            block[:, :, cols] = (MU_MAT * moments[:, :, cols].astype(f32) + total).astype(low)

    half = 384
    routes = (pl.ds(0, half), pl.ds(half, half))
    for row in range(4):
        whole_ref[row, y, x] = block[row]
    plane_one = []
    for route, peer in enumerate((at_x, at_y)):
        copy = remote(
            block.at[:, :, routes[route]], whole_ref.at[:, y, x, :, routes[route]],
            p_send.at[0, route], p_recv.at[0, route], peer,
        )
        copy.start()
        plane_one.append(copy)
    twin_own = remote(block, other_ref.at[:, y, x], t_send.at[0], t_recv.at[0], twin)
    twin_own.start()
    grads_ref[z] = back[z]
    returns = []
    for step, (peer, plane) in enumerate(zip(at_z, steps_z)):
        copy = remote(back.at[plane], grads_ref.at[z], g_send.at[step], g_recv.at[step], peer)
        copy.start()
        returns.append(copy)
    plane_two = []
    for route, peer in enumerate((at_y, at_x)):
        plane_one[route].wait()
        part = (
            whole_ref.at[:, :, x, :, routes[1]] if route else whole_ref.at[:, y, :, :, routes[0]]
        )
        copy = remote(part, part, p_send.at[1, route], p_recv.at[1, route], peer)
        copy.start()
        plane_two.append(copy)
    twins = [twin_own]
    for route in range(2):
        src = whole_ref.at[:, 1 - y, x, :, routes[1]] if route else whole_ref.at[:, y, 1 - x, :, routes[0]]
        dst = other_ref.at[:, 1 - y, x, :, routes[1]] if route else other_ref.at[:, y, 1 - x, :, routes[0]]
        copy = remote(src, dst, t_send.at[1 + route], t_recv.at[1 + route], twin)
        copy.start()
        twins.append(copy)
    for route in range(2):
        plane_two[route].wait()
        src = whole_ref.at[:, :, 1 - x, :, routes[1]] if route else whole_ref.at[:, 1 - y, :, :, routes[0]]
        dst = other_ref.at[:, :, 1 - x, :, routes[1]] if route else other_ref.at[:, 1 - y, :, :, routes[0]]
        copy = remote(src, dst, t_send.at[3 + route], t_recv.at[3 + route], twin)
        copy.start()
        twins.append(copy)
    for copy in vec_z:
        copy.wait()
    vec_mid[0] = (vec_slots[0] + vec_slots[1]) + (vec_slots[2] + vec_slots[3])
    vec_swap = remote(vec_mid.at[0], vec_twin, w_send.at[2], w_recv.at[2], twin)
    vec_swap.start()
    for copy in twins + returns:
        copy.wait()
    vec_swap.wait()
    total_ref[...] = vec_mid[0] + jnp.where(vec_rows >= SHARED_ROW, vec_twin[...], 0.0)
    for task, (name, width) in enumerate(PLAN):
        plane = PLANE_OF[name]

        @pl.when(z != plane)
        def _():
            remote(
                held[task], slots.at[z, :, :, pl.ds(0, width)], z_send.at[task], z_recv.at[z],
                {"dp": plane * 4 + y * 2 + x},
            ).wait_send()


def reduce_all(held, parts, vectors, moments, gain, sources):
    f32, low = jnp.float32, jnp.bfloat16
    vmem = pl.BlockSpec(memory_space=pltpu.VMEM)
    dma = pltpu.SemaphoreType.DMA
    parts = [part.reshape(4, 2, 2, SHARD, part.shape[1]) for part in parts]
    buf = pltpu.VMEM
    tokens = sources[-1].shape
    whole, other, grads, total, output, d_stream = pl.pallas_call(
        reduce_kernel,
        in_specs=[vmem] * 7 + [pl.BlockSpec(memory_space=pl.ANY)] * len(sources),
        out_specs=[vmem] * 6,
        out_shape=[
            jax.ShapeDtypeStruct((4, 2, 2, SHARD, 768), low),
            jax.ShapeDtypeStruct((4, 2, 2, SHARD, 768), low),
            jax.ShapeDtypeStruct((4, SHARD, 768), low),
            jax.ShapeDtypeStruct(vectors.shape, f32),
            jax.ShapeDtypeStruct(tokens, f32),
            jax.ShapeDtypeStruct(tokens, f32),
        ],
        scratch_shapes=[buf(item.shape, item.dtype) for item in sources]
        + [
            dma((len(sources),)), buf((2,) + tokens, f32), buf((2,) + tokens, low), buf((2,) + tokens, low),
            buf(vectors.shape, f32), buf(vectors.shape, f32), dma((3,)), dma((3,)),
            buf((2, 2, 4, 2, SHARD, 384), low), buf((2, 2, 4, 2, SHARD, 384), low),
            buf((2, 2, 4, SHARD, 384), low),
            buf((4, SHARD, 768), low), buf((4, SHARD, 256), low),
            buf((4, 4, SHARD, 768), low),
            buf((4, SHARD, 768), low), buf((4, SHARD, 768), low),
            buf((2,) + vectors.shape, f32), buf((2,) + vectors.shape, f32), buf((4,) + vectors.shape, f32),
            dma((2, 2)), dma((2, 2)), dma((2, 2)), dma((2, 2)),
            dma((4,)), dma((4,)), dma((3,)), dma((3,)), dma((2, 2)), dma((2, 2)),
            dma((5,)), dma((5,)), dma((5,)), dma((5,)),
        ],
        compiler_params=pltpu.CompilerParams(
            collective_id=1, has_side_effects=True, vmem_limit_bytes=60 * 2**20
        ),
        cost_estimate=pl.CostEstimate(flops=0, bytes_accessed=150 * 10**6, transcendentals=0),
        name="reduce_grads",
    )(*held, *parts, vectors, moments, gain, *sources)
    return whole.reshape(768, 768), other.reshape(768, 768), grads, total, output, d_stream


def newton_kernel(own_ref, other_ref, mask_ref, half_ref, lent_ref, full_ref, current, gram, mix):
    f32, low = jnp.float32, jnp.bfloat16
    rows, cols = current.shape
    tile = 256
    count = rows // tile
    row_ids = lax.broadcasted_iota(jnp.int32, (tile, tile), 0)
    col_ids = lax.broadcasted_iota(jnp.int32, (tile, tile), 1)
    blocks = [pl.ds(at * tile, tile) for at in range(count)]

    wide = own_ref.shape[1]
    for at in range(count):
        for ref, start in ((own_ref, 0), (other_ref, wide)):
            cut = pl.ds(start, wide)
            full_ref[blocks[at], cut] = (ref[blocks[at], :].astype(f32) * mask_ref[:, cut]).astype(low)

    def symmetric(source, store):
        for second in range(count):
            column = dot(source[pl.ds(0, (second + 1) * tile), :], source[blocks[second], :], ((1,), (1,)))
            for first in range(second + 1):
                store(first, second, column[first * tile : (first + 1) * tile])

    def put(ref, first, second, value):
        ref[blocks[first], blocks[second]] = value.astype(low)
        if first != second:
            ref[blocks[second], blocks[first]] = value.T.astype(low)

    firsts = {}
    symmetric(full_ref, lambda first, second, value: firsts.update({(first, second): value}))
    trace = sum(
        jnp.sum(jnp.where(row_ids == col_ids, firsts[at, at], 0.0), keepdims=True) for at in range(count)
    )
    scale = jnp.sqrt(trace) + 1e-07
    inverse, inverse_square = 1.0 / scale, 1.0 / (scale * scale)
    for (first, second), value in firsts.items():
        put(gram, first, second, value * inverse_square)
    for at in range(count):
        current[blocks[at], :] = (full_ref[blocks[at], :].astype(f32) * inverse).astype(low)

    def mixed():
        def store(first, second, value):
            piece = gram[blocks[first], blocks[second]].astype(f32)
            put(mix, first, second, NS_B * piece + NS_C * value)

        symmetric(gram, store)

    def turn(_, carry):
        mixed()

        def update(at, carry):
            here = pl.ds(pl.multiple_of(at * tile, tile), tile)
            held = current[:, here]
            current[:, here] = (NS_A * held.astype(f32) + dot(mix[...], held)).astype(low)
            return carry

        lax.fori_loop(0, cols // tile, update, 0)
        symmetric(current, lambda first, second, value: put(gram, first, second, value))
        return carry

    lax.fori_loop(0, NS_STEPS - 1, turn, 0)
    mixed()
    for at in range(wide // tile + 1):
        here = pl.ds(at * tile, tile)
        held = current[:, here]
        value = (NS_A * held.astype(f32) + dot(mix[...], held)).astype(low)
        if at < wide // tile:
            half_ref[:, here] = value
        else:
            lent_ref[...] = value


def newton(own, other, mask):
    low = jnp.bfloat16
    rows, width = own.shape
    vmem = pl.BlockSpec(memory_space=pltpu.VMEM)
    whole = pltpu.VMEM((rows, 2 * width), low)
    return pl.pallas_call(
        newton_kernel,
        in_specs=[vmem] * 3,
        out_specs=[vmem] * 2,
        out_shape=[jax.ShapeDtypeStruct((rows, width), low), jax.ShapeDtypeStruct((rows, 256), low)],
        scratch_shapes=[whole, whole, pltpu.VMEM((rows, rows), low), pltpu.VMEM((rows, rows), low)],
        compiler_params=pltpu.CompilerParams(vmem_limit_bytes=40 * 2**20),
        cost_estimate=pl.CostEstimate(flops=20 * 10**9, bytes_accessed=4 * 10**6, transcendentals=0),
        name="newton_schulz",
    )(own, other, mask)


def return_kernel(done_ref, lent_ref, back_ref, ready, send, recv):
    x, y, z, _, _, at_z = place()
    greet(at_z)
    small = (z == PLANE_OF["small"]).astype(jnp.float32)
    edge = lent_ref.shape[-1]
    for plane in range(4):
        ready[plane] = done_ref[plane, y, x]
        lent = lent_ref[plane, y, x].astype(jnp.float32) * small
        ready[plane, :, pl.ds(0, edge)] = (
            done_ref[plane, y, x, :, pl.ds(0, edge)].astype(jnp.float32) + lent
        ).astype(ready.dtype)
    copies = []
    for step, peer in enumerate(at_z):
        plane = lax.rem(z + step + 1, 4)
        copies.append(
            remote(ready.at[plane], back_ref.at[z], send.at[step], recv.at[step], peer)
        )
        copies[-1].start()
    back_ref[z] = ready[z]
    for copy in copies:
        copy.wait()


def return_rows(done, lent):
    vmem = pl.BlockSpec(memory_space=pltpu.VMEM)
    dma = pltpu.SemaphoreType.DMA
    return pl.pallas_call(
        return_kernel,
        in_specs=[vmem] * 2,
        out_specs=vmem,
        out_shape=jax.ShapeDtypeStruct((4, SHARD, 768), done.dtype),
        scratch_shapes=[pltpu.VMEM((4, SHARD, 768), done.dtype), dma((3,)), dma((3,))],
        compiler_params=pltpu.CompilerParams(collective_id=2, has_side_effects=True, vmem_limit_bytes=16 * 2**20),
        cost_estimate=pl.CostEstimate(flops=0, bytes_accessed=20 * 10**6, transcendentals=0),
        name="return_rows",
    )(done.reshape(4, 2, 2, SHARD, 768), lent.reshape(4, 2, 2, SHARD, lent.shape[1]))


def orthogonal_owned(own, other, state_width):
    width = own.shape[1]
    small = lax.axis_index("dp") // 4 == PLANE_OF["small"]
    col = jnp.arange(2 * width)[None, :] % width
    keep = (col < state_width) == (lax.axis_index("tensor") == 0)
    half, lent = newton(own, other, (keep | ~small).astype(jnp.float32))
    return half, swap(lent)


def paired_shards(
    stream,
    cotangent,
    positions,
    norm_gain,
    w_gate,
    w_inner,
    w_state,
    w_step,
    conv_inner,
    conv_state,
    head_params,
    gate_gain,
    w_out,
    moment_norm_gain,
    moment_w_gate,
    moment_w_inner,
    moment_w_state,
    moment_w_step,
    moment_conv_inner,
    moment_conv_state,
    moment_head_params,
    moment_gate_gain,
    moment_w_out,
):
    low = jnp.bfloat16
    core = lax.axis_index("tensor")
    room = w_gate.shape[1]
    wide = w_state.shape[1]
    col_width = wide // 2
    heads = w_step.shape[1]
    full_first, full_second, full_out, token_rows, cotangent_rows, first_pre, second_pre, d_normed_out = gather_all(
        w_gate, w_state, w_inner, w_step, w_out.astype(low).T, stream, cotangent, norm_gain[None, :]
    )
    pos = jnp.broadcast_to(positions.astype(jnp.float32)[:, None], (positions.shape[0], 128))
    taps = jnp.pad(conv_inner, ((0, 3), (0, 0)))
    taps_s = jnp.pad(conv_state, ((0, 3), (0, 0)))
    lanes = jnp.concatenate([pad_cols(head_params, PACK), pad_cols(head_params, 128 - PACK)], axis=1)
    lanes = jnp.pad(lanes, ((0, 5), (0, 0)))
    skip = jnp.repeat(head_params[2], room // heads)[None, :]
    wide_map = expand_matrix()
    scanned, zi, zs, enter, sums = forward_core(
        first_pre, second_pre, d_normed_out, pos, taps, taps_s, lanes, skip, gate_gain[None, :], wide_map
    )
    normed_out, d_gate_pre, d_scan, gain_part = gate_stage(
        first_pre, scanned, d_normed_out, sums, swap(sums), gate_gain[None, :], pos
    )
    out_part = contract_rows(cotangent_rows, normed_out).astype(low)
    gate_part = contract_rows(token_rows, d_gate_pre).astype(low)
    small_moment = pad_cols(jnp.concatenate([moment_w_state, moment_w_step], axis=1), room)
    moment_rows = jnp.stack([moment_w_out.T, moment_w_inner, moment_w_gate, small_moment]).astype(low)
    d_inner, d_state_low, d_step, vectors, held_out, held_gate, moments = backward_core(
        first_pre, second_pre, zi, zs, scanned, d_scan, enter, pos, taps, taps_s, lanes, skip, wide_map, gain_part, out_part, gate_part,
        moment_rows
    )
    col_first = core * col_width
    inner_part = contract_rows(token_rows, d_inner).astype(low)
    small_part = contract_rows(token_rows, jnp.concatenate([d_state_low, d_step], axis=1)).astype(low)
    own, other, grads, vectors, output, d_stream = reduce_all(
        (held_out, held_gate), (inner_part, small_part), vectors, moments, norm_gain[None, :],
        (
            d_gate_pre, d_inner, d_state_low, d_step, normed_out, full_first, full_second, full_out,
            stream, cotangent,
        ),
    )
    grads = grads.astype(jnp.float32)
    grad_gate_w = grads[2]
    grad_inner_w = grads[1]
    grad_out_w = grads[0].T
    grad_state_w = grads[3][:, :col_width]
    grad_step_w = grads[3][:, col_width : col_width + heads]
    grad_conv_inner = vectors[:5]
    grad_gate_gain = vectors[5]
    grad_head = vectors[6:9, :heads]
    grad_conv_state = vectors[9:14, :wide]
    grad_norm = vectors[NORM_ROW]
    m_gate = MU_MAT * moment_w_gate + grad_gate_w
    m_inner = MU_MAT * moment_w_inner + grad_inner_w
    m_state = MU_MAT * moment_w_state + grad_state_w
    m_step = MU_MAT * moment_w_step + grad_step_w
    m_out = MU_MAT * moment_w_out + grad_out_w
    mine = return_rows(*orthogonal_owned(own, other, col_width)).astype(jnp.float32)
    new_gate = w_gate - LR_MAT * spread(D, INNER) * mine[2]
    new_inner = w_inner - LR_MAT * spread(D, INNER) * mine[1]
    new_out = w_out - LR_MAT * spread(INNER, D) * mine[0].T
    new_step = w_step - LR_MAT * spread(D, HEADS) * mine[3][:, col_width : col_width + heads]
    state_slice = lax.dynamic_slice_in_dim(w_state, col_first, col_width, 1)
    new_state = state_slice - LR_MAT * spread(D, 2 * STATE) * mine[3][:, :col_width]
    m_norm = MU_VEC * moment_norm_gain + grad_norm
    m_conv_inner = MU_VEC * moment_conv_inner + grad_conv_inner
    m_conv_state = MU_VEC * moment_conv_state + grad_conv_state
    m_head = MU_VEC * moment_head_params + grad_head
    m_gate_gain = MU_VEC * moment_gate_gain + grad_gate_gain
    return (
        output,
        d_stream,
        grad_norm,
        grad_gate_w,
        grad_inner_w,
        grad_state_w,
        grad_step_w,
        grad_conv_inner,
        grad_conv_state,
        grad_head,
        grad_gate_gain,
        grad_out_w,
        norm_gain - LR_VEC * m_norm,
        new_gate,
        new_inner,
        new_state,
        new_step,
        conv_inner - LR_VEC * m_conv_inner,
        conv_state - LR_VEC * m_conv_state,
        head_params - LR_VEC * m_head,
        gate_gain - LR_VEC * m_gate_gain,
        new_out,
        m_norm,
        m_gate,
        m_inner,
        m_state,
        m_step,
        m_conv_inner,
        m_conv_state,
        m_head,
        m_gate_gain,
        m_out,
    )


def solution(mesh):
    paired = mesh.shape["dp"] == 16 and mesh.shape["tensor"] == 2
    return jax.shard_map(
        paired_shards if paired else shards,
        mesh=mesh,
        in_specs=(
            P(("dp", "tensor"), None),
            P(("dp", "tensor"), None),
            P("dp"),
            P(),
            P("dp", "tensor"),
            P("dp", "tensor"),
            P("dp", None),
            P("dp", "tensor"),
            P(None, "tensor"),
            P(),
            P(None, "tensor"),
            P("tensor"),
            P("tensor", "dp"),
            P(),
            P("dp", "tensor"),
            P("dp", "tensor"),
            P("dp", "tensor"),
            P("dp", "tensor"),
            P(None, "tensor"),
            P(),
            P(None, "tensor"),
            P("tensor"),
            P("tensor", "dp"),
        ),
        out_specs=(
            P(("dp", "tensor"), None),
            P(("dp", "tensor"), None),
            P(),
            P("dp", "tensor"),
            P("dp", "tensor"),
            P("dp", "tensor"),
            P("dp", "tensor"),
            P(None, "tensor"),
            P(),
            P(None, "tensor"),
            P("tensor"),
            P("tensor", "dp"),
            P(),
            P("dp", "tensor"),
            P("dp", "tensor"),
            P("dp", "tensor"),
            P("dp", "tensor"),
            P(None, "tensor"),
            P(),
            P(None, "tensor"),
            P("tensor"),
            P("tensor", "dp"),
            P(),
            P("dp", "tensor"),
            P("dp", "tensor"),
            P("dp", "tensor"),
            P("dp", "tensor"),
            P(None, "tensor"),
            P(),
            P(None, "tensor"),
            P("tensor"),
            P("tensor", "dp"),
        ),
        check_vma=False,
    )
```

```python
from functools import partial
import math

import jax
import jax.numpy as jnp
from jax import lax
from jax.experimental import pallas as pl
from jax.experimental.pallas import tpu as pltpu
from jax.sharding import PartitionSpec as P

D = 768
INNER = 1536
HEADS = 24
STATE = 128
BLOCK = 256
NS_STEPS = 5


EPS = 1e-05
NS_A = 3.4445
NS_B = -4.775
NS_C = 2.0315
MU_MAT = 0.95
MU_VEC = 0.9
LR_MAT = 0.3
LR_VEC = 0.001
HIGH = lax.Precision.HIGHEST
CORE = lax.Precision.DEFAULT


def silu_slope(value):
    sig = jax.nn.sigmoid(value)
    return sig * (1.0 + value * (1.0 - sig))


def contract_rows(left, right):
    return lax.dot_general(
        left, right, (((0,), (0,)), ((), ())), preferred_element_type=jnp.float32
    )


def times_transpose(left, right):
    return lax.dot_general(
        left, right, (((1,), (1,)), ((), ())), preferred_element_type=jnp.float32
    )


def causal_conv(signal, taps, positions):
    length = signal.shape[0]
    reach = taps.shape[0] - 1
    total = jnp.zeros_like(signal) + taps[reach]
    for lag_step in range(reach):
        moved = jnp.pad(signal, ((lag_step, 0), (0, 0)))[:length]
        total = total + jnp.where((positions >= lag_step)[:, None], moved * taps[lag_step], 0.0)
    return jax.nn.silu(total)


def mixer_core(inner_pre, state_pre, step_pre, conv_inner, conv_state, head_params, positions, precision=HIGH):
    length = inner_pre.shape[0]
    heads = step_pre.shape[1]
    head_size = inner_pre.shape[1] // heads
    states = state_pre.shape[1] // 2
    blocks = length // BLOCK
    inner_act = causal_conv(inner_pre, conv_inner, positions).reshape(
        blocks, BLOCK, heads, head_size
    )
    state_act = causal_conv(state_pre, conv_state, positions)
    input_map = state_act[:, :states].reshape(blocks, BLOCK, states)
    output_map = state_act[:, states:].reshape(blocks, BLOCK, states)
    step_size = jax.nn.softplus(step_pre + head_params[0])
    log_decay = (step_size * -jnp.exp(head_params[1])).reshape(blocks, BLOCK, heads)
    step_size = step_size.reshape(blocks, BLOCK, heads)
    resets = (positions <= 0).astype(jnp.float32).reshape(blocks, BLOCK)
    order = jnp.arange(BLOCK)
    lower = (order[:, None] >= order[None, :]).astype(jnp.float32)
    cumulative = jnp.einsum("ij,cjh->cih", lower, log_decay, precision=HIGH)
    seen = jnp.einsum("ij,cj->ci", lower, resets, precision=HIGH)
    linked = (seen[:, :, None] == seen[:, None, :]) & (order[:, None] >= order[None, :])[None]
    linked_heads = linked[..., None]
    spacing = cumulative[:, :, None, :] - cumulative[:, None, :, :]
    decay = jnp.where(linked_heads, jnp.exp(jnp.where(linked_heads, spacing, 0.0)), 0.0)
    scores = jnp.einsum("cin,cjn->cij", output_map, input_map, precision=precision)
    mixing = scores[..., None] * decay * step_size[:, None, :, :]
    within = jnp.einsum("cijh,cjhp->cihp", mixing, inner_act, precision=precision)
    tail_linked = (seen[:, -1:] == seen)[..., None]
    tail = (
        jnp.where(
            tail_linked,
            jnp.exp(jnp.where(tail_linked, cumulative[:, -1:, :] - cumulative, 0.0)),
            0.0,
        )
        * step_size
    )
    own_state = jnp.einsum("cjh,cjhp,cjn->chpn", tail, inner_act, input_map, precision=precision)
    carry_rate = jnp.exp(cumulative[:, -1, :]) * (seen[:, -1] == 0).astype(jnp.float32)[:, None]

    state = jnp.zeros((heads, head_size, states), jnp.float32)
    entering = []
    for block in range(blocks):
        entering.append(state)
        state = carry_rate[block][:, None, None] * state + own_state[block]
    entering = jnp.stack(entering)
    fresh = (seen == 0)[..., None]
    carry_in = jnp.where(fresh, jnp.exp(cumulative), 0.0)
    across = (
        jnp.einsum("cin,chpn->cihp", output_map, entering, precision=precision) * carry_in[..., None]
    )
    result = within + across + head_params[2][None, None, :, None] * inner_act
    return result.reshape(length, heads * head_size)


def gram_total(low):
    return lax.psum(
        jnp.dot(low, low.T, preferred_element_type=jnp.float32).astype(jnp.bfloat16), "tensor"
    ).astype(jnp.float32)


def orthogonalize(matrix):
    first = gram_total(matrix.astype(jnp.bfloat16))
    scale = jnp.sqrt(jnp.trace(first)) + 1e-07
    current = (matrix / scale).astype(jnp.bfloat16)
    gram = (first / (scale * scale)).astype(jnp.bfloat16)
    for turn in range(NS_STEPS):
        if turn > 0:
            gram = gram_total(current).astype(jnp.bfloat16)
        applied = jnp.dot(gram, current, preferred_element_type=jnp.float32)
        twice = jnp.dot(gram, applied.astype(jnp.bfloat16), preferred_element_type=jnp.float32)
        current = (NS_A * current.astype(jnp.float32) + NS_B * applied + NS_C * twice).astype(
            jnp.bfloat16
        )
    return current.astype(jnp.float32)


def spread(rows, cols):
    return math.sqrt(max(1.0, rows / cols))


def shards(
    stream,
    cotangent,
    positions,
    norm_gain,
    w_gate,
    w_inner,
    w_state,
    w_step,
    conv_inner,
    conv_state,
    head_params,
    gate_gain,
    w_out,
    moment_norm_gain,
    moment_w_gate,
    moment_w_inner,
    moment_w_state,
    moment_w_step,
    moment_conv_inner,
    moment_conv_state,
    moment_head_params,
    moment_gate_gain,
    moment_w_out,
):
    dp_count = lax.axis_size("dp")
    inv_first = lax.rsqrt(jnp.mean(stream * stream, axis=1, keepdims=True) + EPS)
    normed = (stream * inv_first * norm_gain).astype(jnp.bfloat16)
    token_rows, cotangent_rows = (
        lax.all_gather(normed, "tensor", axis=0, tiled=True),
        lax.all_gather(cotangent.astype(jnp.bfloat16), "tensor", axis=0, tiled=True),
    )
    local_weights = (
        w_gate.astype(jnp.bfloat16),
        w_inner.astype(jnp.bfloat16),
        w_step.astype(jnp.bfloat16),
        w_state.astype(jnp.bfloat16),
        w_out.astype(jnp.bfloat16),
    )
    full_gate, full_inner, full_step, full_state, full_out = (
        lax.all_gather(local_weights[0], "dp", axis=0, tiled=True),
        lax.all_gather(local_weights[1], "dp", axis=0, tiled=True),
        lax.all_gather(local_weights[2], "dp", axis=0, tiled=True),
        lax.all_gather(local_weights[3], "dp", axis=0, tiled=True),
        lax.all_gather(local_weights[4], "dp", axis=1, tiled=True),
    )
    gate_pre = jnp.dot(token_rows, full_gate, preferred_element_type=jnp.float32)
    inner_pre = jnp.dot(token_rows, full_inner, preferred_element_type=jnp.float32)
    state_pre = jnp.dot(token_rows, full_state, preferred_element_type=jnp.float32)
    step_pre = jnp.dot(token_rows, full_step, preferred_element_type=jnp.float32)
    alive = (positions >= 0).astype(jnp.float32)[:, None]
    scanned, core_back = jax.vjp(
        partial(mixer_core, positions=positions),
        inner_pre,
        state_pre,
        step_pre,
        conv_inner,
        conv_state,
        head_params,
    )
    gate_act = jax.nn.silu(gate_pre)
    gated = scanned * gate_act
    square_sum = lax.psum(jnp.sum(gated * gated, axis=1), "tensor")
    inv_second = lax.rsqrt(square_sum / INNER + EPS)[:, None]
    normed_out = (gated * inv_second * gate_gain * alive).astype(jnp.bfloat16)
    mixed = lax.psum_scatter(
        jnp.dot(normed_out, full_out, preferred_element_type=jnp.float32).astype(jnp.bfloat16),
        "tensor",
        scatter_dimension=0,
        tiled=True,
    ).astype(jnp.float32)
    output = stream + mixed
    d_normed_out = times_transpose(cotangent_rows, full_out)
    grad_out_part = contract_rows(normed_out, cotangent_rows)
    scaled = d_normed_out * gate_gain * alive
    grad_gate_part = jnp.sum(d_normed_out * gated * inv_second * alive, axis=0)
    cross_sum = lax.psum(jnp.sum(scaled * gated, axis=1), "tensor")
    d_gated = inv_second * scaled - gated * inv_second**3 * (cross_sum / INNER)[:, None]
    d_gate_pre = (d_gated * scanned * silu_slope(gate_pre)).astype(jnp.bfloat16)
    d_inner, d_state_part, d_step, grad_conv_inner_part, grad_conv_state_part, grad_head_part = (
        core_back(d_gated * gate_act)
    )
    d_state_cols = lax.psum_scatter(
        d_state_part.astype(jnp.bfloat16), "tensor", scatter_dimension=1, tiled=True
    ).astype(jnp.float32)
    d_inner_low = d_inner.astype(jnp.bfloat16)
    d_state_low = d_state_cols.astype(jnp.bfloat16)
    d_step_low = d_step.astype(jnp.bfloat16)
    col_width = d_state_cols.shape[1]
    col_first = lax.axis_index("tensor") * col_width
    state_cols = lax.dynamic_slice_in_dim(full_state, col_first, col_width, 1)
    total = times_transpose(d_gate_pre, full_gate)
    total = total + times_transpose(d_inner_low, full_inner)
    total = total + times_transpose(d_state_low, state_cols)
    d_normed = lax.psum_scatter(
        (total + times_transpose(d_step_low, full_step)).astype(jnp.bfloat16),
        "tensor",
        scatter_dimension=0,
        tiled=True,
    ).astype(jnp.float32)
    grad_gate_w, grad_inner_w, grad_state_w, grad_step_w, grad_out_w = (
        lax.psum_scatter(
            contract_rows(token_rows, d_gate_pre).astype(jnp.bfloat16),
            "dp",
            scatter_dimension=0,
            tiled=True,
        ).astype(jnp.float32),
        lax.psum_scatter(
            contract_rows(token_rows, d_inner_low).astype(jnp.bfloat16),
            "dp",
            scatter_dimension=0,
            tiled=True,
        ).astype(jnp.float32),
        lax.psum_scatter(
            contract_rows(token_rows, d_state_low).astype(jnp.bfloat16),
            "dp",
            scatter_dimension=0,
            tiled=True,
        ).astype(jnp.float32),
        lax.psum_scatter(
            contract_rows(token_rows, d_step_low).astype(jnp.bfloat16),
            "dp",
            scatter_dimension=0,
            tiled=True,
        ).astype(jnp.float32),
        lax.psum_scatter(
            grad_out_part.astype(jnp.bfloat16), "dp", scatter_dimension=1, tiled=True
        ).astype(jnp.float32),
    )
    grad_norm_part = jnp.sum(d_normed * stream * inv_first, axis=0)
    weighted = d_normed * norm_gain
    d_stream = (
        cotangent
        + inv_first * weighted
        - stream * inv_first**3 * jnp.mean(weighted * stream, axis=1, keepdims=True)
    )
    grad_conv_inner, grad_gate_gain, grad_head = lax.psum(
        (grad_conv_inner_part, grad_gate_part, grad_head_part), "dp"
    )
    grad_conv_state, grad_norm = lax.psum((grad_conv_state_part, grad_norm_part), ("dp", "tensor"))
    m_gate = MU_MAT * moment_w_gate + grad_gate_w
    m_inner = MU_MAT * moment_w_inner + grad_inner_w
    m_state = MU_MAT * moment_w_state + grad_state_w
    m_step = MU_MAT * moment_w_step + grad_step_w
    m_out = MU_MAT * moment_w_out + grad_out_w
    room = w_gate.shape[1]
    shard_rows = w_gate.shape[0]
    stacked = jnp.stack(
        [
            m_gate,
            m_inner,
            m_out.T,
            jnp.pad(m_step, ((0, 0), (0, room - m_step.shape[1]))),
            jnp.pad(m_state, ((0, 0), (0, room - m_state.shape[1]))),
        ]
    )
    matrix_count = stacked.shape[0]
    owner_index = jnp.arange(matrix_count, dtype=jnp.int32) * dp_count // matrix_count
    select = (owner_index[None, :] == jnp.arange(dp_count, dtype=jnp.int32)[:, None]).astype(
        jnp.float32
    )
    outgoing = jnp.einsum("jk,krc->jrc", select, stacked, precision=HIGH)
    owned = (
        lax.all_to_all(outgoing.astype(jnp.bfloat16), "dp", split_axis=0, concat_axis=0, tiled=True)
        .astype(outgoing.dtype)
        .reshape(dp_count * shard_rows, room)
    )
    ortho = orthogonalize(owned)
    returned = lax.all_to_all(
        ortho.reshape(dp_count, shard_rows, room).astype(jnp.bfloat16),
        "dp",
        split_axis=0,
        concat_axis=0,
        tiled=True,
    ).astype(jnp.float32)
    mine = jnp.einsum("jk,jrc->krc", select, returned, precision=HIGH)
    new_gate = w_gate - LR_MAT * spread(D, INNER) * mine[0]
    new_inner = w_inner - LR_MAT * spread(D, INNER) * mine[1]
    new_out = w_out - LR_MAT * spread(INNER, D) * mine[2].T
    new_step = w_step - LR_MAT * spread(D, HEADS) * mine[3][:, : w_step.shape[1]]
    state_slice = lax.dynamic_slice_in_dim(w_state, col_first, col_width, 1)
    new_state = state_slice - LR_MAT * spread(D, 2 * STATE) * mine[4][:, :col_width]
    m_norm = MU_VEC * moment_norm_gain + grad_norm
    m_conv_inner = MU_VEC * moment_conv_inner + grad_conv_inner
    m_conv_state = MU_VEC * moment_conv_state + grad_conv_state
    m_head = MU_VEC * moment_head_params + grad_head
    m_gate_gain = MU_VEC * moment_gate_gain + grad_gate_gain
    return (
        output,
        d_stream,
        grad_norm,
        grad_gate_w,
        grad_inner_w,
        grad_state_w,
        grad_step_w,
        grad_conv_inner,
        grad_conv_state,
        grad_head,
        grad_gate_gain,
        grad_out_w,
        norm_gain - LR_VEC * m_norm,
        new_gate,
        new_inner,
        new_state,
        new_step,
        conv_inner - LR_VEC * m_conv_inner,
        conv_state - LR_VEC * m_conv_state,
        head_params - LR_VEC * m_head,
        gate_gain - LR_VEC * m_gate_gain,
        new_out,
        m_norm,
        m_gate,
        m_inner,
        m_state,
        m_step,
        m_conv_inner,
        m_conv_state,
        m_head,
        m_gate_gain,
        m_out,
    )


MESH_ID = pl.DeviceIdType.MESH
SHARD = 48
PLAN = (("out", 768), ("gate", 768), ("inner", 768), ("small", 256))
PLANE_OF = {"out": 0, "inner": 1, "gate": 2, "small": 3}


def place():
    index = lax.axis_index("dp")
    z = lax.div(index, 4)
    y = lax.rem(lax.div(index, 2), 2)
    x = lax.rem(index, 2)
    at_x = {"dp": z * 4 + y * 2 + (1 - x)}
    at_y = {"dp": z * 4 + (1 - y) * 2 + x}
    at_z = [{"dp": lax.rem(z + step, 4) * 4 + y * 2 + x} for step in range(1, 4)]
    return x, y, z, at_x, at_y, at_z


def greet(peers):
    barrier = pltpu.get_barrier_semaphore()
    for peer in peers:
        pl.semaphore_signal(barrier, inc=1, device_id=peer, device_id_type=MESH_ID)
    pl.semaphore_wait(barrier, len(peers))


def remote(src, dst, send, recv, peer):
    return pltpu.make_async_remote_copy(
        src_ref=src, dst_ref=dst, send_sem=send, recv_sem=recv, device_id=peer, device_id_type=MESH_ID
    )

EARLY = 2
COUNT = 8
SHARED_ROW = 9
NORM_ROW = 14


def half_steps(parts, at_x, at_y, x, y, arrived, summed, arrived_two, one_send, one_recv, two_send, two_recv):
    def span(task, route):
        half = parts[task].shape[-1] // 2
        return pl.ds(route * half, half), pl.ds(0, half)

    def one(task, route):
        cols, mine = span(task, route)
        other = parts[task].at[:, 1 - y, :, :, cols] if route else parts[task].at[:, :, 1 - x, :, cols]
        return remote(
            other, arrived.at[task, route, :, :, :, mine], one_send.at[task, route],
            one_recv.at[task, route], at_y if route else at_x,
        )

    def two(task, route):
        mine = span(task, route)[1]
        return remote(
            summed.at[task, route, :, 1 - x if route else 1 - y, :, mine],
            arrived_two.at[task, route, :, :, mine], two_send.at[task, route],
            two_recv.at[task, route], at_x if route else at_y,
        )

    def add(task, route, own):
        mine = span(task, route)[1]
        got = arrived[task, route, :, :, :, mine]
        summed[task, route, :, :, :, mine] = (own.astype(jnp.float32) + got.astype(jnp.float32)).astype(jnp.bfloat16)

    def settle(task, route, held):
        cols, mine = span(task, route)
        own = summed[task, route, :, x if route else y, :, mine]
        got = arrived_two[task, route, :, :, mine]
        held[:, :, cols] = (own.astype(jnp.float32) + got.astype(jnp.float32)).astype(jnp.bfloat16)

    return span, one, two, add, settle


def send_moments(source, target, own_sem, send, recv):
    _, _, z, _, _, at_z = place()

    def copies():
        yield pltpu.make_async_copy(source.at[z], target.at[z], own_sem.at[0])
        for step, peer in enumerate(at_z):
            plane = lax.rem(z + step + 1, 4)
            yield remote(source.at[plane], target.at[z], send.at[step], recv.at[step], peer)

    @pl.when(pl.program_id(0) == 0)
    def _():
        for copy in copies():
            copy.start()

    @pl.when(pl.program_id(0) == COUNT - 1)
    def _():
        for copy in copies():
            copy.wait()


def early_reduce(parts, held, own, arrived, summed, arrived_two, own_sem, one_send, one_recv, two_send, two_recv):
    step = pl.program_id(0)
    x, y, z, at_x, at_y, at_z = place()
    span, one, two, add, settle = half_steps(
        parts, at_x, at_y, x, y, arrived, summed, arrived_two, one_send, one_recv, two_send, two_recv
    )
    pairs = [(task, route) for task in range(EARLY) for route in range(2)]

    def load(task, route):
        cols = span(task, route)[0]
        src = parts[task].at[:, y, :, :, cols] if route else parts[task].at[:, :, x, :, cols]
        return pltpu.make_async_copy(src, own.at[task, route], own_sem.at[task, route])

    @pl.when(step == 0)
    def _():
        greet([at_x, at_y, {"tensor": 1 - lax.axis_index("tensor")}] + at_z)
        for route in range(2):
            one(0, route).start()
        for task, route in pairs:
            load(task, route).start()
        for route in range(2):
            one(1, route).start()

    for task, at in ((0, 3), (1, 5)):

        @pl.when(step == at)
        def _():
            for route in range(2):
                load(task, route).wait()
                one(task, route).wait()
                add(task, route, own[task, route])
                two(task, route).start()

    for task, at in ((0, 6), (1, 7)):

        @pl.when(step == at)
        def _():
            for route in range(2):
                two(task, route).wait()
                settle(task, route, held[task])


CHUNK = 128
PACK = 16


def sigmoid(value):
    return 0.5 * jnp.tanh(0.5 * value) + 0.5


def expand_matrix():
    row = jnp.arange(128)[:, None]
    col = jnp.arange(768)[None, :] // 64
    return ((row == col) | (row == col + PACK)).astype(jnp.bfloat16)


def two_term(value):
    lane = lax.broadcasted_iota(jnp.int32, value.shape, 1)
    high = value.astype(jnp.bfloat16).astype(jnp.float32)
    return jnp.where(lane < PACK, high, value - high).astype(jnp.bfloat16)


def split_terms(value, terms):
    out = []
    for _ in range(terms):
        piece = value.astype(jnp.bfloat16)
        out.append(piece)
        value = value - piece.astype(jnp.float32)
    return out


def dot(left, right, dims=((1,), (0,))):
    return lax.dot_general(left, right, (dims, ((), ())), preferred_element_type=jnp.float32)


def head_terms(step_ref, head_ref, pos):
    shifted = step_ref[...] + head_ref[0:1, :]
    small = jnp.exp(-jnp.abs(shifted))
    step = jnp.maximum(shifted, 0.0) + jnp.log1p(small)
    log_decay = -step * jnp.exp(head_ref[1:2, :])
    row = lax.broadcasted_iota(jnp.int32, (CHUNK, 128), 0)
    col = lax.broadcasted_iota(jnp.int32, (CHUNK, 128), 1)
    lower = (row >= col).astype(jnp.bfloat16)
    cumulative = sum(dot(lower, piece) for piece in split_terms(log_decay, 3))
    last = cumulative[CHUNK - 1 : CHUNK, :]
    back = (row - col).astype(jnp.float32)
    linked = (row >= col) & (back <= jnp.maximum(pos, 0.0))
    row = row.astype(jnp.float32)
    carry_in = jnp.where(pos > row, jnp.exp(cumulative), 0.0)
    pos_last = pos[CHUNK - 1 : CHUNK, :]
    tail_linked = (CHUNK - 1.0 - row) <= jnp.maximum(pos_last, 0.0)
    tail = jnp.where(tail_linked, jnp.exp(jnp.minimum(last - cumulative, 0.0)), 0.0)
    carry = jnp.where(pos_last > CHUNK - 1.0, jnp.exp(last), 0.0)
    return shifted, step, log_decay, cumulative, linked, carry_in, tail, carry


def pair_decay(cumulative, across, pair):
    parts = []
    for head in (2 * pair, 2 * pair + 1):
        spacing = cumulative[:, head : head + 1] - across[head : head + 1, :]
        parts.append(jnp.exp(jnp.minimum(spacing, 0.0)))
    return parts


def forward_kernel(
    inner_ref, step_ref, gate_ref, state_ref, dno_ref, pos_ref, taps_ref, taps_s_ref, head_ref,
    skip_ref, gain_ref, wide_ref,
    scanned_ref, zi_ref, zs_ref, enter_ref, sums_ref,
    halo_i, halo_s, hold,
):
    @pl.when(pl.program_id(0) == 0)
    def _():
        halo_i[...] = jnp.zeros_like(halo_i)
        halo_s[...] = jnp.zeros_like(halo_s)
        hold[...] = jnp.zeros_like(hold)

    low = jnp.bfloat16
    pos = pos_ref[...]
    marks = [(pos >= lag).astype(jnp.float32) for lag in range(4)]

    def conv(ref, halo, taps, out_ref, first):
        value = ref[:, first : first + 128]
        ext = jnp.concatenate([halo[:, first : first + 128], value], axis=0)
        total = taps[4:5, first : first + 128] + marks[0] * (value * taps[0:1, first : first + 128])
        for lag in range(1, 4):
            moved = pltpu.roll(ext, lag, 0)[8:]
            total = total + marks[lag] * (moved * taps[lag : lag + 1, first : first + 128])
        out_ref[:, first : first + 128] = total
        return total * sigmoid(total)

    shifted, step, log_decay, cumulative, linked, carry_in, tail, carry = head_terms(
        step_ref, head_ref, pos
    )
    across = cumulative.T
    wide = dot(
        jnp.concatenate(
            [
                two_term(step),
                two_term(carry_in),
                two_term(tail * step),
                two_term(jnp.broadcast_to(carry, (16, 128))),
            ],
            axis=0,
        ),
        wide_ref[...],
    )
    input_map = conv(state_ref, halo_s, taps_s_ref, zs_ref, 0).astype(low)
    output_map = conv(state_ref, halo_s, taps_s_ref, zs_ref, 128).astype(low)
    scores = jnp.where(linked, dot(output_map, input_map, ((1,), (1,))), 0.0)
    state = hold[...]
    state_low = state.astype(low)
    enter_ref[...] = state_low
    entered = dot(output_map, state_low)
    lane = lax.broadcasted_iota(jnp.int32, (CHUNK, 128), 1)
    squares = jnp.zeros((CHUNK, 128), jnp.float32)
    crosses = jnp.zeros((CHUNK, 128), jnp.float32)
    fed = []
    for pair in range(6):
        cols = slice(pair * 128, pair * 128 + 128)
        act = conv(inner_ref, halo_i, taps_ref, zi_ref, pair * 128)
        stepped = (wide[:CHUNK, cols] * act).astype(low)
        first, second = pair_decay(cumulative, across, pair)
        mixing = jnp.concatenate([(scores * first).astype(low), (scores * second).astype(low)], axis=0)
        both = dot(mixing, stepped)
        within = jnp.where(lane < 64, both[:CHUNK], both[CHUNK:])
        scanned = (
            within + entered[:, cols] * wide[CHUNK : 2 * CHUNK, cols] + skip_ref[0:1, cols] * act
        )
        scanned_ref[:, cols] = scanned
        fed.append((wide[2 * CHUNK : 3 * CHUNK, cols] * act).astype(low))
        gate = gate_ref[:, cols]
        gated = scanned * (gate * sigmoid(gate))
        squares = squares + gated * gated
        crosses = crosses + dno_ref[:, cols] * gain_ref[0:1, cols] * gated
    fresh = dot(input_map, jnp.concatenate(fed, axis=1), ((0,), (0,)))
    hold[...] = wide[3 * CHUNK : 3 * CHUNK + 1, :] * state + fresh
    halo_i[...] = inner_ref[CHUNK - 8 :, :]
    halo_s[...] = state_ref[CHUNK - 8 :, :]
    square = jnp.sum(squares, axis=1, keepdims=True)
    cross = jnp.sum(crosses * marks[0], axis=1, keepdims=True)
    sums_ref[...] = jnp.where(lane == 0, square, cross)


def gate_kernel(
    gate_ref, scanned_ref, dno_ref, sums_ref, twin_ref, gain_ref, pos_ref,
    normed_ref, d_gate_ref, d_scan_ref, g_gain_ref,
):
    @pl.when(pl.program_id(0) == 0)
    def _():
        g_gain_ref[...] = jnp.zeros_like(g_gain_ref)

    low = jnp.bfloat16
    alive = (pos_ref[...] >= 0).astype(jnp.float32)
    sums = sums_ref[...] + twin_ref[...]
    inv = jnp.broadcast_to(lax.rsqrt(sums[:, 0:1] / INNER + EPS), alive.shape)
    pull = inv * inv * inv * jnp.broadcast_to(sums[:, 1:2] / INNER, alive.shape)
    live = inv * alive
    for pair in range(6):
        cols = slice(pair * 128, pair * 128 + 128)
        gain = gain_ref[0:1, cols]
        gate, scanned, d_normed_out = gate_ref[:, cols], scanned_ref[:, cols], dno_ref[:, cols]
        sig = sigmoid(gate)
        gate_act = gate * sig
        gated = scanned * gate_act
        normed_ref[:, cols] = (gated * live * gain).astype(low)
        product = d_normed_out * gated * live
        g_gain_ref[:, cols] += jnp.sum(product.reshape(CHUNK // 8, 8, 128), axis=0)
        d_gated = live * gain * d_normed_out - gated * pull
        d_scan_ref[:, cols] = (d_gated * gate_act).astype(low)
        d_gate_ref[:, cols] = (d_gated * scanned * (sig * (1.0 + gate * (1.0 - sig)))).astype(low)


def gate_stage(first_pre, scanned, d_normed_out, sums, twin_sums, gain, pos):
    rows = first_pre.shape[0]
    at = lambda width: pl.BlockSpec((CHUNK, width), lambda c: (c, 0))
    f32, low = jnp.float32, jnp.bfloat16
    wide = jax.ShapeDtypeStruct((rows, 768), low)
    return pl.pallas_call(
        gate_kernel,
        grid=(rows // CHUNK,),
        in_specs=[
            at(768), at(768), at(768), at(128), at(128), pl.BlockSpec((1, 768), lambda c: (0, 0)), at(128),
        ],
        out_specs=[at(768), at(768), at(768), pl.BlockSpec((8, 768), lambda c: (0, 0))],
        out_shape=[wide, wide, wide, jax.ShapeDtypeStruct((8, 768), f32)],
        compiler_params=pltpu.CompilerParams(vmem_limit_bytes=60 * 2**20),
        cost_estimate=pl.CostEstimate(flops=10**8, bytes_accessed=15 * 10**6, transcendentals=10**6),
        name="gate_stage",
    )(first_pre, scanned, d_normed_out, sums, twin_sums, gain, pos)


def backward_kernel(
    inner_ref, step_ref, state_ref, zi_ref, zs_ref, scanned_ref, dscan_ref, enter_ref, pos_ref,
    taps_ref, taps_s_ref, head_ref, skip_ref, wide_ref, gain_ref, out_part, gate_part, moment_ref,
    d_inner_ref, d_state_ref, d_step_ref, vec_ref, held_out, held_gate, moments_ref,
    g_taps_ref, g_taps_s_ref, g_skip_ref, g_head_ref,
    halo_i, halo_s, halo_p, hold, state_out, state_in, state_send, state_recv, own_sem, m_send, m_recv, *reducing,
):
    low = jnp.bfloat16
    step_at = pl.program_id(0)
    last_step = pl.num_programs(0) - 1
    core = lax.axis_index("tensor")
    early_reduce((out_part, gate_part), (held_out, held_gate), *reducing)
    send_moments(moment_ref, moments_ref, own_sem, m_send, m_recv)
    chunk = last_step - step_at
    twin = {"tensor": 1 - core}
    here = pl.ds(pl.multiple_of(chunk * CHUNK, CHUNK), CHUNK)

    @pl.when(pl.program_id(0) == 0)
    def _():
        for ref in (halo_i, halo_s, halo_p, hold, g_taps_ref, g_taps_s_ref, g_skip_ref, g_head_ref):
            ref[...] = jnp.zeros_like(ref)

    pos = pos_ref[...]
    pos_ext = jnp.concatenate([pos, halo_p[...]], axis=0)
    marks = [(pos_ext >= lag).astype(jnp.float32) for lag in range(4)]
    lane = lax.broadcasted_iota(jnp.int32, (CHUNK, 128), 1)
    row = lax.broadcasted_iota(jnp.int32, (CHUNK, 128), 0)
    col = lane

    def slope(total):
        sig = sigmoid(total)
        return sig * (1.0 + total * (1.0 - sig)), total * sig

    def fold(value):
        return jnp.sum(value.reshape(CHUNK // 8, 8, 128), axis=0)

    def conv_back(grad, ref, halo, taps, out_ref, g_ref, first):
        cols = slice(first, first + 128)
        ext = jnp.concatenate([grad, halo[:, cols]], axis=0)
        value = ref[:, cols]
        halo[:, cols] = grad[:8]
        g_ref[4, :, cols] += fold(grad)
        total = jnp.zeros((CHUNK, 128), jnp.float32)
        for lag in range(4):
            masked = ext * marks[lag]
            if lag:
                masked = pltpu.roll(masked, CHUNK + 8 - lag, 0)
            masked = masked[:CHUNK]
            g_ref[lag, :, cols] += fold(masked * value)
            total = total + masked * taps[lag : lag + 1, cols]
        if out_ref is not None:
            out_ref[:, cols] = total.astype(low)
        return total

    shifted, step, log_decay, cumulative, linked, carry_in, tail, carry = head_terms(
        step_ref, head_ref, pos
    )
    across = cumulative.T
    wide = dot(
        jnp.concatenate(
            [
                two_term(step),
                two_term(carry_in),
                two_term(tail),
                two_term(jnp.broadcast_to(carry, (16, 128))),
            ],
            axis=0,
        ),
        wide_ref[...],
    )
    slope_b, input_map = slope(zs_ref[:, :128])
    slope_c, output_map = slope(zs_ref[:, 128:])
    input_low, output_low = input_map.astype(low), output_map.astype(low)
    scores = jnp.where(linked, dot(output_low, input_low, ((1,), (1,))), 0.0)
    entering = enter_ref[...]
    d_next = hold[...]
    d_next_low = d_next.astype(low)
    pulled = dot(input_low, d_next_low)
    d_scores = jnp.zeros((CHUNK, 128), jnp.float32)
    d_entered, fed, balance, direct, extra = [], [], [], [], []
    carry_wide = wide[3 * CHUNK : 3 * CHUNK + 1, :]
    carry_grad = jnp.sum(d_next * entering.astype(jnp.float32), axis=0, keepdims=True) * carry_wide
    for pair in range(6):
        cols = slice(pair * 128, pair * 128 + 128)
        slope_x, act = slope(zi_ref[:, cols])
        d_low = dscan_ref[:, cols]
        skip = skip_ref[0:1, cols]
        stepped = (wide[:CHUNK, cols] * act).astype(low)
        stepped_wide = stepped.astype(jnp.float32)
        d_exact = d_low.astype(jnp.float32)
        d_both = jnp.concatenate(
            [jnp.where(lane < 64, d_exact, 0.0).astype(low), jnp.where(lane < 64, 0.0, d_exact).astype(low)],
            axis=0,
        )
        first, second = pair_decay(cumulative, across, pair)
        mixing = jnp.concatenate([(scores * first).astype(low), (scores * second).astype(low)], axis=0)
        d_mixing = dot(d_both, stepped, ((1,), (1,)))
        d_scores = d_scores + d_mixing[:CHUNK] * first + d_mixing[CHUNK:] * second
        tail_cols = wide[2 * CHUNK : 3 * CHUNK, cols]
        tailed = tail_cols * pulled[:, cols]
        d_stepped = dot(mixing, d_both, ((0,), (0,))) + tailed
        extra.append(jnp.sum(stepped_wide * tailed, axis=0, keepdims=True) + carry_grad[:, cols])
        fed.append((tail_cols * stepped_wide).astype(low))
        d_entered.append((wide[CHUNK : 2 * CHUNK, cols] * d_exact).astype(low))
        balance.append(d_exact * (scanned_ref[:, cols] - skip * act) - stepped_wide * d_stepped)
        direct.append(act * d_stepped)
        g_skip_ref[:, cols] += fold(d_exact * act)
        d_act = skip * d_exact + wide[:CHUNK, cols] * d_stepped
        conv_back(d_act * slope_x, inner_ref, halo_i, taps_ref, d_inner_ref, g_taps_ref, pair * 128)
    d_entered = jnp.concatenate(d_entered, axis=1)
    fed = jnp.concatenate(fed, axis=1)
    d_scores = jnp.where(linked, d_scores, 0.0).astype(low)
    d_output = dot(d_scores, input_low) + dot(d_entered, entering, ((1,), (1,)))
    d_input = dot(d_scores, output_low, ((0,), (0,))) + dot(fed, d_next_low, ((1,), (1,)))
    hold[...] = carry_wide * d_next + dot(output_low, d_entered, ((0,), (0,)))
    for_first = conv_back(d_input * slope_b, state_ref, halo_s, taps_s_ref, None, g_taps_s_ref, 0)
    for_second = conv_back(d_output * slope_c, state_ref, halo_s, taps_s_ref, None, g_taps_s_ref, 128)
    state_out[step_at] = jnp.where(core == 0, for_second, for_first).astype(low)
    d_state_ref[here, :] = jnp.where(core == 0, for_first, for_second).astype(low)

    def lend(at):
        return remote(state_out.at[at], state_in.at[at], state_send.at[at], state_recv.at[at], twin)

    lend(step_at).start()
    halo_p[...] = pos[:8]
    spread_back = wide_ref[...]
    extra = jnp.broadcast_to(jnp.concatenate(extra, axis=1), (16, 768))
    stacked = jnp.concatenate(
        split_terms(jnp.concatenate(balance, axis=1), 2)
        + split_terms(jnp.concatenate(direct, axis=1), 2)
        + split_terms(extra, 2),
        axis=0,
    )
    summed = dot(stacked, spread_back, ((1,), (1,)))
    d_sum = summed[:CHUNK] + summed[CHUNK : 2 * CHUNK]
    d_direct = summed[2 * CHUNK : 3 * CHUNK] + summed[3 * CHUNK : 4 * CHUNK]
    d_last = summed[4 * CHUNK : 4 * CHUNK + 1] + summed[4 * CHUNK + 16 : 4 * CHUNK + 17]
    upper = (row <= col).astype(low)
    d_decay = sum(dot(upper, piece) for piece in split_terms(d_sum, 3)) + d_last
    d_step = (d_direct - d_decay * jnp.exp(head_ref[1:2, :])) * sigmoid(shifted)
    d_step = jnp.where(lane < PACK, d_step, 0.0)
    d_step_ref[...] = d_step.astype(low)
    g_head_ref[0] += fold(d_step)
    g_head_ref[1] += fold(d_decay * log_decay)

    @pl.when(step_at == last_step)
    def _():
        vec_ref[...] = jnp.zeros_like(vec_ref)
        total = lambda value: jnp.sum(value, axis=0, keepdims=True)
        for lag in range(5):
            vec_ref[lag : lag + 1, :] = total(g_taps_ref[lag])
            vec_ref[SHARED_ROW + lag : SHARED_ROW + lag + 1, :256] = total(g_taps_s_ref[lag])
        vec_ref[5:6, :] = total(gain_ref[...])
        for at in range(2):
            vec_ref[6 + at : 7 + at, :128] = total(g_head_ref[at])
        skip_row = jnp.broadcast_to(total(g_skip_ref[...]), (16, 768))
        vec_ref[8:9, :128] = sum(
            dot(piece, spread_back, ((1,), (1,))) for piece in split_terms(skip_row, 3)
        )[0:1]
        for at in range(COUNT):
            lend(at).wait()
            rows = pl.ds((COUNT - 1 - at) * CHUNK, CHUNK)
            d_state_ref[rows, :] = (
                d_state_ref[rows, :].astype(jnp.float32) + state_in[at].astype(jnp.float32)
            ).astype(low)


def forward_core(first_pre, second_pre, d_normed_out, pos, taps, taps_s, heads_lanes, skip, gain, wide):
    rows = first_pre.shape[0]
    at = lambda width, col: pl.BlockSpec((CHUNK, width), lambda c: (c, col))
    whole = lambda arr: pl.BlockSpec(arr.shape, lambda c: (0,) * arr.ndim)
    f32 = jnp.float32
    return pl.pallas_call(
        forward_kernel,
        grid=(rows // CHUNK,),
        in_specs=[
            at(768, 0), at(128, 6), at(768, 0), at(256, 3), at(768, 0), at(128, 0),
            whole(taps), whole(taps_s), whole(heads_lanes), whole(skip), whole(gain), whole(wide),
        ],
        out_specs=[at(768, 0), at(768, 0), at(256, 0), at(768, 0), at(128, 0)],
        out_shape=[
            jax.ShapeDtypeStruct((rows, 768), f32),
            jax.ShapeDtypeStruct((rows, 768), f32),
            jax.ShapeDtypeStruct((rows, 256), f32),
            jax.ShapeDtypeStruct((rows, 768), jnp.bfloat16),
            jax.ShapeDtypeStruct((rows, 128), f32),
        ],
        scratch_shapes=[
            pltpu.VMEM((8, 768), f32), pltpu.VMEM((8, 256), f32), pltpu.VMEM((128, 768), f32),
        ],
        compiler_params=pltpu.CompilerParams(vmem_limit_bytes=60 * 2**20),
        cost_estimate=pl.CostEstimate(flops=8 * 10**9, bytes_accessed=24 * 10**6, transcendentals=4 * 10**6),
        name="mixer_forward",
    )(second_pre, second_pre, first_pre, first_pre, d_normed_out, pos, taps, taps_s, heads_lanes, skip, gain, wide)


def backward_core(
    first_pre, second_pre, zi, zs, scanned, d_scan, enter, pos, taps, taps_s, heads_lanes, skip, wide, gain_part, out_part, gate_part, moment_rows
):
    rows = first_pre.shape[0]
    count = rows // CHUNK
    at = lambda width, col: pl.BlockSpec((CHUNK, width), lambda c: (count - 1 - c, col))
    whole = lambda shape: pl.BlockSpec(shape, lambda c: (0,) * len(shape))
    f32, low = jnp.float32, jnp.bfloat16
    return pl.pallas_call(
        backward_kernel,
        grid=(count,),
        in_specs=[
            at(768, 0), at(128, 6), at(256, 3), at(768, 0), at(256, 0), at(768, 0), at(768, 0),
            at(768, 0), at(128, 0),
            whole(taps.shape), whole(taps_s.shape), whole(heads_lanes.shape), whole(skip.shape), whole(wide.shape),
            whole(gain_part.shape), pl.BlockSpec(memory_space=pl.ANY), pl.BlockSpec(memory_space=pl.ANY), pl.BlockSpec(memory_space=pl.ANY),
        ],
        out_specs=[
            at(768, 0), whole((rows, 128)), at(128, 0),
            whole((16, 768)),
            whole((4, SHARD, 768)), whole((4, SHARD, 768)), pl.BlockSpec(memory_space=pl.ANY),
        ],
        out_shape=[
            jax.ShapeDtypeStruct((rows, 768), low),
            jax.ShapeDtypeStruct((rows, 128), low),
            jax.ShapeDtypeStruct((rows, 128), low),
            jax.ShapeDtypeStruct((16, 768), f32),
            jax.ShapeDtypeStruct((4, SHARD, 768), low),
            jax.ShapeDtypeStruct((4, SHARD, 768), low),
            jax.ShapeDtypeStruct((4, SHARD, 768), low),
        ],
        scratch_shapes=[
            pltpu.VMEM((5, 8, 768), f32), pltpu.VMEM((5, 8, 256), f32), pltpu.VMEM((8, 768), f32),
            pltpu.VMEM((2, 8, 128), f32),
            pltpu.VMEM((8, 768), f32), pltpu.VMEM((8, 256), f32), pltpu.VMEM((8, 128), f32),
            pltpu.VMEM((128, 768), f32),
            pltpu.VMEM((COUNT, CHUNK, 128), low), pltpu.VMEM((COUNT, CHUNK, 128), low),
            pltpu.SemaphoreType.DMA((COUNT,)), pltpu.SemaphoreType.DMA((COUNT,)),
            pltpu.SemaphoreType.DMA((1,)), pltpu.SemaphoreType.DMA((3,)), pltpu.SemaphoreType.DMA((3,)),
            pltpu.VMEM((EARLY, 2, 4, 2, SHARD, 384), low),
            pltpu.VMEM((EARLY, 2, 4, 2, SHARD, 384), low),
            pltpu.VMEM((EARLY, 2, 4, 2, SHARD, 384), low),
            pltpu.VMEM((EARLY, 2, 4, SHARD, 384), low),
        ]
        + [pltpu.SemaphoreType.DMA((EARLY, 2))] * 5,
        compiler_params=pltpu.CompilerParams(
            collective_id=3, has_side_effects=True, vmem_limit_bytes=60 * 2**20
        ),
        cost_estimate=pl.CostEstimate(flops=16 * 10**9, bytes_accessed=24 * 10**6, transcendentals=6 * 10**6),
        name="mixer_backward",
    )(
        second_pre, second_pre, first_pre, zi, zs, scanned, d_scan, enter, pos, taps, taps_s, heads_lanes, skip, wide,
        gain_part, out_part.reshape(4, 2, 2, SHARD, 768), gate_part.reshape(4, 2, 2, SHARD, 768),
        moment_rows,
    )


def swap(value):
    return lax.ppermute(value, "tensor", [(0, 1), (1, 0)])


def pad_cols(value, width):
    return jnp.pad(value, ((0, 0), (0, width - value.shape[1])))


GATHER_PIECES = (
    (1, 0, 384, 0), (1, 384, 512, 1), (0, 0, 512, 0), (0, 512, 512, 1), (2, 0, 384, 0), (2, 384, 384, 1),
)


def gather_kernel(
    gate_ref, state_ref, inner_ref, step_ref, out_ref, stream_ref, cot_ref, gain_ref,
    full_first, full_second, full_out, rows_ref, cots_ref, pre_first, pre_second, pre_out,
    first_ref, second_ref, lanes_ref, held_first, held_second, held_out,
    pre_sem, row_sem, z_send, z_recv, one_send, one_recv, two_send, two_recv,
):
    x, y, z, at_x, at_y, at_z = place()
    core = lax.axis_index("tensor")
    twin = {"tensor": 1 - core}
    low = jnp.bfloat16
    first_ref[:, pl.ds(0, 768)] = gate_ref[...].astype(low)
    first_ref[:, pl.ds(768, 256)] = state_ref[...].astype(low)
    second_ref[:, pl.ds(0, 768)] = inner_ref[...].astype(low)
    lanes_ref[...] = jnp.zeros_like(lanes_ref)
    lanes_ref[:, : step_ref.shape[1]] = step_ref[...]
    lanes = lanes_ref[...]
    second_ref[:, pl.ds(768, 128)] = (lanes + pltpu.roll(lanes, PACK, 1)).astype(low)
    greet([at_x, at_y, twin] + at_z)
    shards = (first_ref, second_ref, out_ref)
    fulls = (full_first, full_second, full_out)
    results = ((held_first, pre_first), (held_second, pre_second), (held_out, pre_out))
    z_copies, ones, twos, copies = {}, {}, {}, []

    def step_zero(piece):
        which, start, width, _ = GATHER_PIECES[piece]
        cols = pl.ds(start, width)
        z_copies[piece] = []
        for step, peer in enumerate(at_z):
            copy = remote(
                shards[which].at[:, cols], fulls[which].at[z, y, x, :, cols],
                z_send.at[piece, step], z_recv.at[piece, step], peer,
            )
            copy.start()
            z_copies[piece].append(copy)

    def step_one(piece):
        which, start, width, route = GATHER_PIECES[piece]
        for copy in z_copies[piece]:
            copy.wait()
        part = fulls[which].at[:, y, x, :, pl.ds(start, width)]
        ones[piece] = remote(part, part, one_send.at[piece], one_recv.at[piece], at_x if route else at_y)
        ones[piece].start()

    def step_two(piece):
        which, start, width, route = GATHER_PIECES[piece]
        cols = pl.ds(start, width)
        ones[piece].wait()
        part = fulls[which].at[:, y, :, :, cols] if route else fulls[which].at[:, :, x, :, cols]
        twos[piece] = remote(part, part, two_send.at[piece], two_recv.at[piece], at_y if route else at_x)
        twos[piece].start()

    def finish(piece):
        which, start, width, _ = GATHER_PIECES[piece]
        cols = pl.ds(start, width)
        twos[piece].wait()
        left = cots_ref if which == 2 else rows_ref
        held, pre = results[which]
        weights = fulls[which]

        def tile(at, carry):
            here = pl.ds(pl.multiple_of(lax.rem(at, 2) * 256, 256), 256)
            there = pl.ds(pl.multiple_of(at * 256, 256), 256)
            held[there, cols] = dot(
                left[lax.div(at, 2), here, :], weights[:, :, :, :, cols].reshape(768, width)
            )
            return carry

        lax.fori_loop(0, 4, tile, 0)
        copy = pltpu.make_async_copy(held.at[:, cols], pre.at[:, cols], pre_sem.at[piece])
        copy.start()
        copies.append(copy)

    step_zero(0)
    for shard, full in zip(shards, fulls):
        full[z, y, x] = shard[...]
    step_zero(1)
    for part in range(4):
        here = pl.ds(part * 128, 128)
        value = stream_ref[here, :]
        inv = lax.rsqrt(jnp.sum(value * value, axis=1, keepdims=True) / D + EPS)
        rows_ref[core, here, :] = (value * inv * gain_ref[...]).astype(jnp.bfloat16)
        cots_ref[core, here, :] = cot_ref[here, :].astype(jnp.bfloat16)
    swaps = []
    for at, ref in enumerate((rows_ref, cots_ref)):
        swaps.append(remote(ref.at[core], ref.at[core], row_sem.at[at], row_sem.at[2 + at], twin))
        swaps[-1].start()
    count = len(GATHER_PIECES)
    for piece in range(count + 1):
        if piece < count:
            step_one(piece)
        if piece + 2 < count:
            step_zero(piece + 2)
        if piece >= 1:
            step_two(piece - 1)
        if piece == 3:
            for copy in swaps:
                copy.wait()
        if piece >= 4:
            finish(piece - 4)
    for piece in range(count - 3, count):
        finish(piece)
    for copy in copies:
        copy.wait()


def gather_all(gate, state, inner, step, out, stream, cotangent, gain):
    f32, low = jnp.float32, jnp.bfloat16
    vmem = pl.BlockSpec(memory_space=pltpu.VMEM)
    count = len(GATHER_PIECES)
    dma = pltpu.SemaphoreType.DMA
    tokens = 2 * stream.shape[0]
    first = jax.ShapeDtypeStruct((SHARD, 1024), low)
    second = jax.ShapeDtypeStruct((SHARD, 896), low)
    full = lambda arr: jax.ShapeDtypeStruct((4, 2, 2) + arr.shape, low)
    rows = jax.ShapeDtypeStruct((2,) + stream.shape, low)
    pre = lambda arr: jax.ShapeDtypeStruct((tokens, arr.shape[1]), f32)
    got = pl.pallas_call(
        gather_kernel,
        in_specs=[vmem] * 8,
        out_specs=[vmem] * 5 + [pl.BlockSpec(memory_space=pl.ANY)] * 3,
        out_shape=[full(first), full(second), full(out), rows, rows, pre(first), pre(second), pre(out)],
        scratch_shapes=[
            pltpu.VMEM(first.shape, low), pltpu.VMEM(second.shape, low), pltpu.VMEM((SHARD, 128), f32),
            pltpu.VMEM((tokens, first.shape[1]), f32),
            pltpu.VMEM((tokens, second.shape[1]), f32),
            pltpu.VMEM((tokens, out.shape[1]), f32),
            dma((count,)), dma((4,)), dma((count, 3)), dma((count, 3)),
            dma((count,)), dma((count,)), dma((count,)), dma((count,)),
        ],
        compiler_params=pltpu.CompilerParams(
            collective_id=0, has_side_effects=True, vmem_limit_bytes=60 * 2**20
        ),
        cost_estimate=pl.CostEstimate(flops=4 * 10**9, bytes_accessed=120 * 10**6, transcendentals=0),
        name="gather_weights",
    )(gate, state, inner, step, out, stream, cotangent, gain)
    return [item.reshape(-1, item.shape[-1]) for item in got]


def reduce_kernel(
    held_out, held_gate, inner_ref, small_ref, vec_ref, moments, gain_ref, *rest,
):
    sources, rest = rest[:10], rest[10:]
    whole_ref, other_ref, grads_ref, total_ref, output_ref, d_stream_ref = rest[:6]
    local, rest = rest[6:16], rest[16:]
    reduce_body(
        held_out, held_gate, inner_ref, small_ref, vec_ref, moments, gain_ref, sources,
        whole_ref, other_ref, grads_ref, total_ref, output_ref, d_stream_ref, local, *rest,
    )


def reduce_body(
    held_out, held_gate, inner_ref, small_ref, vec_ref, moments, gain_ref, sources,
    whole_ref, other_ref, grads_ref, total_ref, output_ref, d_stream_ref, local,
    load_sem, mine_f, lent_b, got_b, vec_own, vec_twin, w_send, w_recv,
    arrived, summed, arrived_two, held_inner, held_small, slots,
    block, back, vec_in, vec_mid, vec_slots,
    one_send, one_recv, two_send, two_recv, z_send, z_recv, g_send, g_recv,
    p_send, p_recv, t_send, t_recv, v_send, v_recv,
):
    f32, low = jnp.float32, jnp.bfloat16
    x, y, z, at_x, at_y, at_z = place()
    core = lax.axis_index("tensor")
    twin = {"tensor": 1 - core}
    greet([at_x, at_y, twin] + at_z)
    parts = (inner_ref, small_ref)
    held = (held_out, held_gate, held_inner, held_small)
    steps_z = [lax.rem(z + step, 4) for step in range(1, 4)]
    span, one, two, add, settle = half_steps(
        parts, at_x, at_y, x, y, arrived, summed, arrived_two, one_send, one_recv, two_send, two_recv
    )

    def to_plane(task):
        plane, width = PLANE_OF[PLAN[task][0]], PLAN[task][1]

        @pl.when(z != plane)
        def _():
            remote(
                held[task], slots.at[z, :, :, pl.ds(0, width)], z_send.at[task], z_recv.at[z],
                {"dp": plane * 4 + y * 2 + x},
            ).start()

    for task in range(2):
        for route in range(2):
            one(task, route).start()
    to_plane(0)
    to_plane(1)
    loads = [pltpu.make_async_copy(src, dst, load_sem.at[at]) for at, (src, dst) in enumerate(zip(sources, local))]
    for copy in loads:
        copy.start()
    d_gate, d_inner, d_state, d_step, normed, w_first, w_second, w_out, stream_ref, cot_ref = local
    half_rows = stream_ref.shape[0]
    turned = ((1,), (1,))
    state_cols = pl.ds(pl.multiple_of(768 + core * 128, 128), 128)

    def product(which, rows):
        if which == 1:
            return dot(normed[rows, :], w_out[...], turned)
        first = dot(d_gate[rows, :], w_first[:, pl.ds(0, 768)], turned)
        second = dot(d_inner[rows, :], w_second[:, pl.ds(0, 768)], turned)
        third = dot(d_state[rows, :], w_first[:, state_cols], turned)
        return first + second + third + dot(d_step[rows, :], w_second[:, pl.ds(768, 128)], turned)

    for copy in loads:
        copy.wait()

    def products(who, store):
        for which in range(2):

            def tile(at, carry):
                rows = pl.ds(pl.multiple_of(who * half_rows + at * 256, 256), 256)
                store(which, pl.ds(pl.multiple_of(at * 256, 256), 256), product(which, rows))
                return carry

            lax.fori_loop(0, half_rows // 256, tile, 0)

    def store_lent(which, rows, value):
        lent_b[which, rows, :] = value.astype(low)

    def store_mine(which, rows, value):
        mine_f[which, rows, :] = value

    products(1 - core, store_lent)
    lends = []
    for which in range(2):
        lends.append(remote(lent_b.at[which], got_b.at[which], w_send.at[which], w_recv.at[which], twin))
        lends[-1].start()
    for task in range(2):
        for route in range(2):
            cols = span(task, route)[0]
            one(task, route).wait()
            add(task, route, parts[task][:, y, :, :, cols] if route else parts[task][:, :, x, :, cols])
            two(task, route).start()
    products(core, store_mine)
    for task in range(2):
        for route in range(2):
            two(task, route).wait()
            settle(task, route, held[2 + task])
        to_plane(2 + task)
    for copy in lends:
        copy.wait()
    grad_norm = jnp.zeros((1, 768), f32)
    gain = gain_ref[...]
    for part in range(half_rows // 128):
        rows = pl.ds(part * 128, 128)
        value = stream_ref[rows, :]
        output_ref[rows, :] = value + (mine_f[1, rows, :] + got_b[1, rows, :].astype(f32))
        inv = lax.rsqrt(jnp.sum(value * value, axis=1, keepdims=True) / D + EPS)
        d_normed = mine_f[0, rows, :] + got_b[0, rows, :].astype(f32)
        scaled = value * inv
        grad_norm = grad_norm + jnp.sum(d_normed * scaled, axis=0, keepdims=True)
        weighted = d_normed * gain
        inner = jnp.sum(weighted * scaled, axis=1, keepdims=True) / D
        d_stream_ref[rows, :] = cot_ref[rows, :] + inv * (weighted - scaled * inner)
    vec_rows = lax.broadcasted_iota(jnp.int32, vec_ref.shape, 0)
    vec_own[...] = jnp.where(vec_rows == NORM_ROW, grad_norm, vec_ref[...])
    vec_x = remote(vec_own, vec_in.at[0], v_send.at[0], v_recv.at[0], at_x)
    vec_x.start()
    vec_x.wait()
    vec_mid[0] = vec_own[...] + vec_in[0]
    vec_y = remote(vec_mid.at[0], vec_in.at[1], v_send.at[1], v_recv.at[1], at_y)
    vec_y.start()
    vec_y.wait()
    vec_mid[1] = vec_mid[0] + vec_in[1]
    vec_slots[z] = vec_mid[1]
    vec_z = []
    for step, peer in enumerate(at_z):
        copy = remote(vec_mid.at[1], vec_slots.at[z], v_send.at[2 + step], v_recv.at[2 + step], peer)
        copy.start()
        vec_z.append(copy)

    for task, (name, width) in enumerate(PLAN):
        plane = PLANE_OF[name]
        cols = pl.ds(0, width)

        @pl.when(z == plane)
        def _():
            for source in range(4):
                if source != plane:
                    remote(
                        held[task], slots.at[source, :, :, cols], z_send.at[task], z_recv.at[source], at_x
                    ).wait_recv()
            total = held[task][...].astype(f32)
            for source in range(4):
                if source != plane:
                    total = total + slots[source, :, :, cols].astype(f32)
            if width < 768:
                back[...] = jnp.zeros_like(back)
                block[...] = jnp.zeros_like(block)
            back[:, :, cols] = total.astype(low)
            block[:, :, cols] = (MU_MAT * moments[:, :, cols].astype(f32) + total).astype(low)

    half = 384
    routes = (pl.ds(0, half), pl.ds(half, half))
    for row in range(4):
        whole_ref[row, y, x] = block[row]
    plane_one = []
    for route, peer in enumerate((at_x, at_y)):
        copy = remote(
            block.at[:, :, routes[route]], whole_ref.at[:, y, x, :, routes[route]],
            p_send.at[0, route], p_recv.at[0, route], peer,
        )
        copy.start()
        plane_one.append(copy)
    twin_own = remote(block, other_ref.at[:, y, x], t_send.at[0], t_recv.at[0], twin)
    twin_own.start()
    grads_ref[z] = back[z]
    returns = []
    for step, (peer, plane) in enumerate(zip(at_z, steps_z)):
        copy = remote(back.at[plane], grads_ref.at[z], g_send.at[step], g_recv.at[step], peer)
        copy.start()
        returns.append(copy)
    plane_two = []
    for route, peer in enumerate((at_y, at_x)):
        plane_one[route].wait()
        part = (
            whole_ref.at[:, :, x, :, routes[1]] if route else whole_ref.at[:, y, :, :, routes[0]]
        )
        copy = remote(part, part, p_send.at[1, route], p_recv.at[1, route], peer)
        copy.start()
        plane_two.append(copy)
    twins = [twin_own]
    for route in range(2):
        src = whole_ref.at[:, 1 - y, x, :, routes[1]] if route else whole_ref.at[:, y, 1 - x, :, routes[0]]
        dst = other_ref.at[:, 1 - y, x, :, routes[1]] if route else other_ref.at[:, y, 1 - x, :, routes[0]]
        copy = remote(src, dst, t_send.at[1 + route], t_recv.at[1 + route], twin)
        copy.start()
        twins.append(copy)
    for route in range(2):
        plane_two[route].wait()
        src = whole_ref.at[:, :, 1 - x, :, routes[1]] if route else whole_ref.at[:, 1 - y, :, :, routes[0]]
        dst = other_ref.at[:, :, 1 - x, :, routes[1]] if route else other_ref.at[:, 1 - y, :, :, routes[0]]
        copy = remote(src, dst, t_send.at[3 + route], t_recv.at[3 + route], twin)
        copy.start()
        twins.append(copy)
    for copy in vec_z:
        copy.wait()
    vec_mid[0] = (vec_slots[0] + vec_slots[1]) + (vec_slots[2] + vec_slots[3])
    vec_swap = remote(vec_mid.at[0], vec_twin, w_send.at[2], w_recv.at[2], twin)
    vec_swap.start()
    for copy in twins + returns:
        copy.wait()
    vec_swap.wait()
    total_ref[...] = vec_mid[0] + jnp.where(vec_rows >= SHARED_ROW, vec_twin[...], 0.0)
    for task, (name, width) in enumerate(PLAN):
        plane = PLANE_OF[name]

        @pl.when(z != plane)
        def _():
            remote(
                held[task], slots.at[z, :, :, pl.ds(0, width)], z_send.at[task], z_recv.at[z],
                {"dp": plane * 4 + y * 2 + x},
            ).wait_send()


def reduce_all(held, parts, vectors, moments, gain, sources):
    f32, low = jnp.float32, jnp.bfloat16
    vmem = pl.BlockSpec(memory_space=pltpu.VMEM)
    dma = pltpu.SemaphoreType.DMA
    parts = [part.reshape(4, 2, 2, SHARD, part.shape[1]) for part in parts]
    buf = pltpu.VMEM
    tokens = sources[-1].shape
    whole, other, grads, total, output, d_stream = pl.pallas_call(
        reduce_kernel,
        in_specs=[vmem] * 7 + [pl.BlockSpec(memory_space=pl.ANY)] * len(sources),
        out_specs=[vmem] * 6,
        out_shape=[
            jax.ShapeDtypeStruct((4, 2, 2, SHARD, 768), low),
            jax.ShapeDtypeStruct((4, 2, 2, SHARD, 768), low),
            jax.ShapeDtypeStruct((4, SHARD, 768), low),
            jax.ShapeDtypeStruct(vectors.shape, f32),
            jax.ShapeDtypeStruct(tokens, f32),
            jax.ShapeDtypeStruct(tokens, f32),
        ],
        scratch_shapes=[buf(item.shape, item.dtype) for item in sources]
        + [
            dma((len(sources),)), buf((2,) + tokens, f32), buf((2,) + tokens, low), buf((2,) + tokens, low),
            buf(vectors.shape, f32), buf(vectors.shape, f32), dma((3,)), dma((3,)),
            buf((2, 2, 4, 2, SHARD, 384), low), buf((2, 2, 4, 2, SHARD, 384), low),
            buf((2, 2, 4, SHARD, 384), low),
            buf((4, SHARD, 768), low), buf((4, SHARD, 256), low),
            buf((4, 4, SHARD, 768), low),
            buf((4, SHARD, 768), low), buf((4, SHARD, 768), low),
            buf((2,) + vectors.shape, f32), buf((2,) + vectors.shape, f32), buf((4,) + vectors.shape, f32),
            dma((2, 2)), dma((2, 2)), dma((2, 2)), dma((2, 2)),
            dma((4,)), dma((4,)), dma((3,)), dma((3,)), dma((2, 2)), dma((2, 2)),
            dma((5,)), dma((5,)), dma((5,)), dma((5,)),
        ],
        compiler_params=pltpu.CompilerParams(
            collective_id=1, has_side_effects=True, vmem_limit_bytes=60 * 2**20
        ),
        cost_estimate=pl.CostEstimate(flops=0, bytes_accessed=150 * 10**6, transcendentals=0),
        name="reduce_grads",
    )(*held, *parts, vectors, moments, gain, *sources)
    return whole.reshape(768, 768), other.reshape(768, 768), grads, total, output, d_stream


def newton_kernel(own_ref, other_ref, mask_ref, half_ref, lent_ref, full_ref, current, gram, mix):
    f32, low = jnp.float32, jnp.bfloat16
    rows, cols = current.shape
    tile = 256
    count = rows // tile
    row_ids = lax.broadcasted_iota(jnp.int32, (tile, tile), 0)
    col_ids = lax.broadcasted_iota(jnp.int32, (tile, tile), 1)
    blocks = [pl.ds(at * tile, tile) for at in range(count)]

    wide = own_ref.shape[1]
    for at in range(count):
        for ref, start in ((own_ref, 0), (other_ref, wide)):
            cut = pl.ds(start, wide)
            full_ref[blocks[at], cut] = (ref[blocks[at], :].astype(f32) * mask_ref[:, cut]).astype(low)

    def symmetric(source, store):
        for second in range(count):
            column = dot(source[pl.ds(0, (second + 1) * tile), :], source[blocks[second], :], ((1,), (1,)))
            for first in range(second + 1):
                store(first, second, column[first * tile : (first + 1) * tile])

    def put(ref, first, second, value):
        ref[blocks[first], blocks[second]] = value.astype(low)
        if first != second:
            ref[blocks[second], blocks[first]] = value.T.astype(low)

    firsts = {}
    symmetric(full_ref, lambda first, second, value: firsts.update({(first, second): value}))
    trace = sum(
        jnp.sum(jnp.where(row_ids == col_ids, firsts[at, at], 0.0), keepdims=True) for at in range(count)
    )
    scale = jnp.sqrt(trace) + 1e-07
    inverse, inverse_square = 1.0 / scale, 1.0 / (scale * scale)
    for (first, second), value in firsts.items():
        put(gram, first, second, value * inverse_square)
    for at in range(count):
        current[blocks[at], :] = (full_ref[blocks[at], :].astype(f32) * inverse).astype(low)

    def mixed():
        def store(first, second, value):
            piece = gram[blocks[first], blocks[second]].astype(f32)
            put(mix, first, second, NS_B * piece + NS_C * value)

        symmetric(gram, store)

    def turn(_, carry):
        mixed()

        def update(at, carry):
            here = pl.ds(pl.multiple_of(at * tile, tile), tile)
            held = current[:, here]
            current[:, here] = (NS_A * held.astype(f32) + dot(mix[...], held)).astype(low)
            return carry

        lax.fori_loop(0, cols // tile, update, 0)
        symmetric(current, lambda first, second, value: put(gram, first, second, value))
        return carry

    lax.fori_loop(0, NS_STEPS - 1, turn, 0)
    mixed()
    for at in range(wide // tile + 1):
        here = pl.ds(at * tile, tile)
        held = current[:, here]
        value = (NS_A * held.astype(f32) + dot(mix[...], held)).astype(low)
        if at < wide // tile:
            half_ref[:, here] = value
        else:
            lent_ref[...] = value


def newton(own, other, mask):
    low = jnp.bfloat16
    rows, width = own.shape
    vmem = pl.BlockSpec(memory_space=pltpu.VMEM)
    whole = pltpu.VMEM((rows, 2 * width), low)
    return pl.pallas_call(
        newton_kernel,
        in_specs=[vmem] * 3,
        out_specs=[vmem] * 2,
        out_shape=[jax.ShapeDtypeStruct((rows, width), low), jax.ShapeDtypeStruct((rows, 256), low)],
        scratch_shapes=[whole, whole, pltpu.VMEM((rows, rows), low), pltpu.VMEM((rows, rows), low)],
        compiler_params=pltpu.CompilerParams(vmem_limit_bytes=40 * 2**20),
        cost_estimate=pl.CostEstimate(flops=20 * 10**9, bytes_accessed=4 * 10**6, transcendentals=0),
        name="newton_schulz",
    )(own, other, mask)


def return_kernel(done_ref, lent_ref, back_ref, ready, send, recv):
    x, y, z, _, _, at_z = place()
    greet(at_z)
    small = (z == PLANE_OF["small"]).astype(jnp.float32)
    edge = lent_ref.shape[-1]
    for plane in range(4):
        ready[plane] = done_ref[plane, y, x]
        lent = lent_ref[plane, y, x].astype(jnp.float32) * small
        ready[plane, :, pl.ds(0, edge)] = (
            done_ref[plane, y, x, :, pl.ds(0, edge)].astype(jnp.float32) + lent
        ).astype(ready.dtype)
    copies = []
    for step, peer in enumerate(at_z):
        plane = lax.rem(z + step + 1, 4)
        copies.append(
            remote(ready.at[plane], back_ref.at[z], send.at[step], recv.at[step], peer)
        )
        copies[-1].start()
    back_ref[z] = ready[z]
    for copy in copies:
        copy.wait()


def return_rows(done, lent):
    vmem = pl.BlockSpec(memory_space=pltpu.VMEM)
    dma = pltpu.SemaphoreType.DMA
    return pl.pallas_call(
        return_kernel,
        in_specs=[vmem] * 2,
        out_specs=vmem,
        out_shape=jax.ShapeDtypeStruct((4, SHARD, 768), done.dtype),
        scratch_shapes=[pltpu.VMEM((4, SHARD, 768), done.dtype), dma((3,)), dma((3,))],
        compiler_params=pltpu.CompilerParams(collective_id=2, has_side_effects=True, vmem_limit_bytes=16 * 2**20),
        cost_estimate=pl.CostEstimate(flops=0, bytes_accessed=20 * 10**6, transcendentals=0),
        name="return_rows",
    )(done.reshape(4, 2, 2, SHARD, 768), lent.reshape(4, 2, 2, SHARD, lent.shape[1]))


def orthogonal_owned(own, other, state_width):
    width = own.shape[1]
    small = lax.axis_index("dp") // 4 == PLANE_OF["small"]
    col = jnp.arange(2 * width)[None, :] % width
    keep = (col < state_width) == (lax.axis_index("tensor") == 0)
    half, lent = newton(own, other, (keep | ~small).astype(jnp.float32))
    return half, swap(lent)


def paired_shards(
    stream,
    cotangent,
    positions,
    norm_gain,
    w_gate,
    w_inner,
    w_state,
    w_step,
    conv_inner,
    conv_state,
    head_params,
    gate_gain,
    w_out,
    moment_norm_gain,
    moment_w_gate,
    moment_w_inner,
    moment_w_state,
    moment_w_step,
    moment_conv_inner,
    moment_conv_state,
    moment_head_params,
    moment_gate_gain,
    moment_w_out,
):
    low = jnp.bfloat16
    core = lax.axis_index("tensor")
    room = w_gate.shape[1]
    wide = w_state.shape[1]
    col_width = wide // 2
    heads = w_step.shape[1]
    full_first, full_second, full_out, token_rows, cotangent_rows, first_pre, second_pre, d_normed_out = gather_all(
        w_gate, w_state, w_inner, w_step, w_out.astype(low).T, stream, cotangent, norm_gain[None, :]
    )
    pos = jnp.broadcast_to(positions.astype(jnp.float32)[:, None], (positions.shape[0], 128))
    taps = conv_inner
    taps_s = conv_state
    lanes = jnp.concatenate([pad_cols(head_params, PACK), pad_cols(head_params, 128 - PACK)], axis=1)
    lanes = jnp.pad(lanes, ((0, 5), (0, 0)))
    skip = jnp.repeat(head_params[2], room // heads)[None, :]
    wide_map = expand_matrix()
    scanned, zi, zs, enter, sums = forward_core(
        first_pre, second_pre, d_normed_out, pos, taps, taps_s, lanes, skip, gate_gain[None, :], wide_map
    )
    normed_out, d_gate_pre, d_scan, gain_part = gate_stage(
        first_pre, scanned, d_normed_out, sums, swap(sums), gate_gain[None, :], pos
    )
    out_part = contract_rows(cotangent_rows, normed_out).astype(low)
    gate_part = contract_rows(token_rows, d_gate_pre).astype(low)
    small_moment = pad_cols(jnp.concatenate([moment_w_state, moment_w_step], axis=1), room)
    moment_rows = jnp.stack([moment_w_out.T, moment_w_inner, moment_w_gate, small_moment]).astype(low)
    d_inner, d_state_low, d_step, vectors, held_out, held_gate, moments = backward_core(
        first_pre, second_pre, zi, zs, scanned, d_scan, enter, pos, taps, taps_s, lanes, skip, wide_map, gain_part, out_part, gate_part,
        moment_rows
    )
    col_first = core * col_width
    inner_part = contract_rows(token_rows, d_inner).astype(low)
    small_part = contract_rows(token_rows, jnp.concatenate([d_state_low, d_step], axis=1)).astype(low)
    own, other, grads, vectors, output, d_stream = reduce_all(
        (held_out, held_gate), (inner_part, small_part), vectors, moments, norm_gain[None, :],
        (
            d_gate_pre, d_inner, d_state_low, d_step, normed_out, full_first, full_second, full_out,
            stream, cotangent,
        ),
    )
    grads = grads.astype(jnp.float32)
    grad_gate_w = grads[2]
    grad_inner_w = grads[1]
    grad_out_w = grads[0].T
    grad_state_w = grads[3][:, :col_width]
    grad_step_w = grads[3][:, col_width : col_width + heads]
    grad_conv_inner = vectors[:5]
    grad_gate_gain = vectors[5]
    grad_head = vectors[6:9, :heads]
    grad_conv_state = vectors[9:14, :wide]
    grad_norm = vectors[NORM_ROW]
    m_gate = MU_MAT * moment_w_gate + grad_gate_w
    m_inner = MU_MAT * moment_w_inner + grad_inner_w
    m_state = MU_MAT * moment_w_state + grad_state_w
    m_step = MU_MAT * moment_w_step + grad_step_w
    m_out = MU_MAT * moment_w_out + grad_out_w
    mine = return_rows(*orthogonal_owned(own, other, col_width)).astype(jnp.float32)
    new_gate = w_gate - LR_MAT * spread(D, INNER) * mine[2]
    new_inner = w_inner - LR_MAT * spread(D, INNER) * mine[1]
    new_out = w_out - LR_MAT * spread(INNER, D) * mine[0].T
    new_step = w_step - LR_MAT * spread(D, HEADS) * mine[3][:, col_width : col_width + heads]
    state_slice = lax.dynamic_slice_in_dim(w_state, col_first, col_width, 1)
    new_state = state_slice - LR_MAT * spread(D, 2 * STATE) * mine[3][:, :col_width]
    m_norm = MU_VEC * moment_norm_gain + grad_norm
    m_conv_inner = MU_VEC * moment_conv_inner + grad_conv_inner
    m_conv_state = MU_VEC * moment_conv_state + grad_conv_state
    m_head = MU_VEC * moment_head_params + grad_head
    m_gate_gain = MU_VEC * moment_gate_gain + grad_gate_gain
    return (
        output,
        d_stream,
        grad_norm,
        grad_gate_w,
        grad_inner_w,
        grad_state_w,
        grad_step_w,
        grad_conv_inner,
        grad_conv_state,
        grad_head,
        grad_gate_gain,
        grad_out_w,
        norm_gain - LR_VEC * m_norm,
        new_gate,
        new_inner,
        new_state,
        new_step,
        conv_inner - LR_VEC * m_conv_inner,
        conv_state - LR_VEC * m_conv_state,
        head_params - LR_VEC * m_head,
        gate_gain - LR_VEC * m_gate_gain,
        new_out,
        m_norm,
        m_gate,
        m_inner,
        m_state,
        m_step,
        m_conv_inner,
        m_conv_state,
        m_head,
        m_gate_gain,
        m_out,
    )


def solution(mesh):
    paired = mesh.shape["dp"] == 16 and mesh.shape["tensor"] == 2
    return jax.shard_map(
        paired_shards if paired else shards,
        mesh=mesh,
        in_specs=(
            P(("dp", "tensor"), None),
            P(("dp", "tensor"), None),
            P("dp"),
            P(),
            P("dp", "tensor"),
            P("dp", "tensor"),
            P("dp", None),
            P("dp", "tensor"),
            P(None, "tensor"),
            P(),
            P(None, "tensor"),
            P("tensor"),
            P("tensor", "dp"),
            P(),
            P("dp", "tensor"),
            P("dp", "tensor"),
            P("dp", "tensor"),
            P("dp", "tensor"),
            P(None, "tensor"),
            P(),
            P(None, "tensor"),
            P("tensor"),
            P("tensor", "dp"),
        ),
        out_specs=(
            P(("dp", "tensor"), None),
            P(("dp", "tensor"), None),
            P(),
            P("dp", "tensor"),
            P("dp", "tensor"),
            P("dp", "tensor"),
            P("dp", "tensor"),
            P(None, "tensor"),
            P(),
            P(None, "tensor"),
            P("tensor"),
            P("tensor", "dp"),
            P(),
            P("dp", "tensor"),
            P("dp", "tensor"),
            P("dp", "tensor"),
            P("dp", "tensor"),
            P(None, "tensor"),
            P(),
            P(None, "tensor"),
            P("tensor"),
            P("tensor", "dp"),
            P(),
            P("dp", "tensor"),
            P("dp", "tensor"),
            P("dp", "tensor"),
            P("dp", "tensor"),
            P(None, "tensor"),
            P(),
            P(None, "tensor"),
            P("tensor"),
            P("tensor", "dp"),
        ),
        check_vma=False,
    )
```
